32 devices in a mesh: dp: 2 (over core), row: 4 (over z), col: 4 (over y, x).
Axes of the slice: x: 2, y: 2, z: 4, core: 2. Of those that a mesh axis runs over, the one named last changes fastest.
Arguments:
- tokens: bfloat16 [2, 512, 8192], P(None, 'col', ('dp', 'row')), may hold values from -6 to 6
- cotangent: bfloat16 [2, 512, 8192], P(None, 'col', ('dp', 'row')), may hold values from -6 to 6
- piece_starts: int32 [2, 8, 2], P(None, ('dp', 'col')), may hold values from 0 to 768, as said below
- ln1_gain: bfloat16 [512], P('col'), may hold values from 0.5 to 1.5
- ln1_bias: bfloat16 [512], P('col'), may hold values from -1 to 1
- qkv_weight: bfloat16 [512, 1536], P('col', 'row'), may hold values from -0.25 to 0.25
- content_bias: float32 [8, 64], P('row'), may hold values from -3 to 3
- position_bias: float32 [8, 64], P('row'), may hold values from -3 to 3
- pos_weight: bfloat16 [512, 512], P('col', 'row'), may hold values from -0.25 to 0.25
- out_weight: bfloat16 [512, 512], P('row', 'col'), may hold values from -2 to 2
- ln2_gain: bfloat16 [512], P('col'), may hold values from 0.5 to 1.5
- ln2_bias: bfloat16 [512], P('col'), may hold values from -1 to 1
- up_weight: bfloat16 [512, 2048], P('col', 'row'), may hold values from -0.25 to 0.25
- up_bias: bfloat16 [2048], P('row'), may hold values from -3 to 3
- down_weight: bfloat16 [2048, 512], P('row', 'col'), may hold values from -0.125 to 0.125
- down_bias: bfloat16 [512], P('col'), may hold values from -1 to 1
Outputs:
- output: float32 [2, 512, 8192], P(None, 'col', ('dp', 'row'))
- grad_tokens: float32 [2, 512, 8192], P(None, 'col', ('dp', 'row'))
- grad_ln1_gain: float32 [512], P(('row', 'col', 'dp'))
- grad_ln1_bias: float32 [512], P(('row', 'col', 'dp'))
- grad_qkv_weight: float32 [512, 1536], P('col', ('row', 'dp'))
- grad_content_bias: float32 [8, 64], P('row', ('col', 'dp'))
- grad_position_bias: float32 [8, 64], P('row', ('col', 'dp'))
- grad_pos_weight: float32 [512, 512], P('col', ('row', 'dp'))
- grad_out_weight: float32 [512, 512], P('row', ('col', 'dp'))
- grad_ln2_gain: float32 [512], P(('row', 'col', 'dp'))
- grad_ln2_bias: float32 [512], P(('row', 'col', 'dp'))
- grad_up_weight: float32 [512, 2048], P('col', ('row', 'dp'))
- grad_up_bias: float32 [2048], P(('row', 'col', 'dp'))
- grad_down_weight: float32 [2048, 512], P('row', ('col', 'dp'))
- grad_down_bias: float32 [512], P(('row', 'col', 'dp'))
The draws below stay inside these ranges and needn't reach their ends.
Inputs may be any that keep to these rules, and one draw needn't show every extreme that they name: `piece_starts`: for every sequence, piece p starts between p * (512) and (p + 1) * 512 - 256, so the 2 pieces of 256 positions lie inside the sequence, in order, without intersection. In every micro-batch some sequence has a piece starting at 0 and one ending at the sequence's end.
All inputs are finite; a program needn't handle non-finite values.
Results may differ from the reference program's by a relative error of at most 0.024.
Values may be sent and summed in bfloat16 or wider, within the bound.
A program may use at most 192 MiB of HBM per device.

```python
import jax
import jax.numpy as jnp
from jax import lax

D = 512
H = 8
HD = 64
FF = 2048
SEQ_LEN = 1024
MB = 2
PIECE = 256
NPIECE = 2
SEQS = 8
TOKENS = 8192


def draw_piece_starts(key, part):
    slot_len = SEQ_LEN // NPIECE
    shifts = jax.random.randint(key, (MB, SEQS, NPIECE), 0, slot_len - PIECE + 1, dtype=jnp.int32)
    shifts = shifts.at[:, 0, 0].set(0)
    shifts = shifts.at[:, 0, NPIECE - 1].set(slot_len - PIECE)
    base_pos = jnp.arange(NPIECE, dtype=jnp.int32) * slot_len
    return (base_pos[None, None, :] + shifts).astype(jnp.int32)


def with_spikes(values, rng, source, target, blocks, factor):
    def block_of(axis_at):
        return (jnp.arange(values.shape[axis_at]) // (values.shape[axis_at] // blocks)).reshape((-1,) + (1,) * (values.ndim - 1 - axis_at))

    one_side = jax.random.permutation(rng, blocks)[block_of(target)]
    second = (block_of(target) + blocks // 2) % blocks
    return jnp.where((block_of(source) == one_side) | (block_of(source) == second), factor * values, values)


def levels(stream_key, dims, split, least, largest):
    loudness, own = 1.0, jax.random.fold_in(stream_key, 6)
    for position, blocks in split:
        draws = jnp.exp(jax.random.uniform(jax.random.fold_in(own, position), (blocks,), jnp.float32, least / len(split), largest / len(split)))
        loudness = loudness * jnp.repeat(draws, dims[position] // blocks).reshape([-1 if axis == position else 1 for axis in range(len(dims))])
    return loudness


def bell_draw(stream_key, dims, deviation, most, cuts=(), kind=jnp.bfloat16):
    array = jax.random.normal(stream_key, dims, jnp.float32) * deviation
    if len(cuts) > 0:
        array = levels(stream_key, dims, cuts, -0.22, 0.18) * array
    return jnp.clip(array, min=-most, max=most).astype(kind)


def gaussian_with(own_key, extent, scale, most, split, heavy, held_as=jnp.bfloat16):
    array = scale * jax.random.normal(own_key, extent, jnp.float32)
    if split:
        array = array * levels(own_key, extent, split, -0.22, 0.18)
    return jnp.clip(with_spikes(array, jax.random.fold_in(own_key, 3), *heavy), -most, most).astype(held_as)


def setup_inputs(seed: int = 0) -> dict:
    arg_keys = jax.random.split(jax.random.key(seed), 17)
    tokens = bell_draw(arg_keys[0], (MB, D, TOKENS), 1.0, 6.0, ((1, 4), (2, 8)))
    cotangent = gaussian_with(arg_keys[1], (MB, D, TOKENS), 1.0, 6.0, ((1, 4), (2, 8)), (2, 1, 8, 2.0))
    piece_starts = draw_piece_starts(jax.random.fold_in(arg_keys[16], 71), 0)
    ln1_gain = jnp.clip(1.0 + 0.1 * jax.random.normal(arg_keys[3], (D,), jnp.float32), 0.5, 1.5).astype(jnp.bfloat16)
    ln1_bias = bell_draw(arg_keys[4], (D,), 0.2, 1.0, ((0, 4),))
    qkv_weight = bell_draw(arg_keys[5], (D, 3 * D), D ** -0.5, 0.25, ((0, 4), (1, 4)))
    content_bias = bell_draw(arg_keys[6], (H, HD), 0.5, 3.0, ((0, 4),), jnp.float32)
    position_bias = bell_draw(arg_keys[7], (H, HD), 0.5, 3.0, ((0, 4),), jnp.float32)
    pos_weight = bell_draw(arg_keys[8], (D, D), D ** -0.5, 0.25, ((0, 4), (1, 4)))
    out_weight = bell_draw(arg_keys[9], (D, D), (max(1, D * 16 // SEQ_LEN)) ** -0.5, 2.0, ((0, 4), (1, 4)))
    ln2_gain = jnp.clip(1.0 + 0.1 * jax.random.normal(arg_keys[10], (D,), jnp.float32), 0.5, 1.5).astype(jnp.bfloat16)
    ln2_bias = bell_draw(arg_keys[11], (D,), 0.2, 1.0, ((0, 4),))
    up_weight = bell_draw(arg_keys[12], (D, FF), D ** -0.5, 0.25, ((0, 4), (1, 4)))
    up_bias = bell_draw(arg_keys[13], (FF,), 0.5, 3.0, ((0, 4),))
    down_weight = bell_draw(arg_keys[14], (FF, D), FF ** -0.5, 0.125, ((0, 4), (1, 4)))
    down_bias = bell_draw(arg_keys[15], (D,), 0.2, 1.0, ((0, 4),))
    return dict(tokens=tokens, cotangent=cotangent, piece_starts=piece_starts, ln1_gain=ln1_gain, ln1_bias=ln1_bias, qkv_weight=qkv_weight, content_bias=content_bias, position_bias=position_bias, pos_weight=pos_weight, out_weight=out_weight, ln2_gain=ln2_gain, ln2_bias=ln2_bias, up_weight=up_weight, up_bias=up_bias, down_weight=down_weight, down_bias=down_bias)


@jax.custom_vjp
def low(v):
    return lax.optimization_barrier(v.astype(jnp.bfloat16)).astype(jnp.float32)

@jax.custom_vjp
def low_back(v):
    return v

def low_keep(v):
    return (low(v), None)

def low_pass(kept, grad):
    return (grad,)

def back_keep(v):
    return (v, None)

def back_low(kept, grad):
    return (low(grad),)
low.defvjp(low_keep, low_pass)
low_back.defvjp(back_keep, back_low)
norm_epsilon = 1e-05
big_negative = -1e+30
inv_sqrt_two = 0.7071067811865476
maximum_precision = lax.Precision.HIGHEST

def matmul(left_op, right_op):
    return jnp.dot(left_op, right_op, precision=maximum_precision, preferred_element_type=jnp.float32)

def layer_norm(values, gain, bias):
    mean_row = lax.optimization_barrier(jnp.mean(values, axis=1, keepdims=True))
    square_row = lax.optimization_barrier(jnp.mean(values * values, axis=1, keepdims=True))
    inverse = lax.rsqrt(square_row - mean_row * mean_row + norm_epsilon)
    return (values - mean_row) * inverse * gain + bias

def gelu_exact(values):
    return 0.5 * values * (1.0 + jax.scipy.special.erf(values * inv_sqrt_two))

def sinusoid(seq_len, feature_count):
    offsets = jnp.arange(2 * seq_len - 1, dtype=jnp.float32) - (seq_len - 1)
    frequency = 10000.0 ** (-jnp.arange(0, feature_count, 2, dtype=jnp.float32) / feature_count)
    angles = offsets[:, None] * frequency[None, :]
    return jnp.concatenate([jnp.sin(angles), jnp.cos(angles)], axis=1)

def piece_labels(positions, starts):
    inside = (positions[:, None] >= starts[None, :]) & (positions[:, None] < starts[None, :] + PIECE)
    numbers = jnp.arange(1, starts.shape[0] + 1, dtype=jnp.int32)
    return (lax.optimization_barrier(jnp.sum(jnp.where(inside, numbers[None, :], 0), axis=1)) - 1).astype(jnp.int32)

def layer(params, seq_rows, starts):
    ln1_gain, ln1_bias, qkv_weight, content_bias, position_bias, pos_weight, out_weight, ln2_gain, ln2_bias, up_weight, up_bias, down_weight, down_bias = params
    seq_len = seq_rows.shape[0]
    scaling = HD ** (-0.5)
    normed_one = low(layer_norm(seq_rows, ln1_gain, ln1_bias))
    packed = low_back(low(matmul(normed_one, qkv_weight))).reshape(seq_len, H, 3, HD)
    queries = packed[:, :, 0]
    key_rows = packed[:, :, 1]
    value_rows = packed[:, :, 2]
    query_u = low((queries + content_bias) * scaling)
    query_v = low((queries + position_bias) * scaling)
    table = low(sinusoid(seq_len, D))
    relative = low_back(low(matmul(table, pos_weight))).reshape(2 * seq_len - 1, H, HD)
    block_len = min(512, seq_len)
    positions = jnp.arange(seq_len, dtype=jnp.int32)
    labels = piece_labels(positions, starts)
    shift_index = jnp.arange(block_len, dtype=jnp.int32)[:, None] + (seq_len - 1) - positions[None, :]
    gather_index = jnp.broadcast_to(shift_index[None], (H, block_len, seq_len))

    def attend(offset):
        qu_block = lax.dynamic_slice_in_dim(query_u, offset, block_len, 0)
        query_position_block = lax.dynamic_slice_in_dim(query_v, offset, block_len, 0)
        relative_block = lax.dynamic_slice_in_dim(relative, offset, block_len + seq_len - 1, 0)
        content = jnp.einsum('ihd,jhd->hij', qu_block, key_rows, precision=maximum_precision)
        unshifted_position_scores = jnp.einsum('sgw,egw->gse', query_position_block, relative_block, precision=maximum_precision)
        scores = low_back(content + jnp.take_along_axis(unshifted_position_scores, gather_index, axis=2))
        row_pos = offset + jnp.arange(block_len, dtype=jnp.int32)
        row_labels = lax.dynamic_slice_in_dim(labels, offset, block_len, 0)
        same_piece = (row_labels[:, None] == labels[None, :]) & (row_labels[:, None] >= 0)
        allowed = (positions[None, :] <= row_pos[:, None]) | same_piece
        masked = jnp.where(allowed[None], scores, big_negative)
        row_max = lax.optimization_barrier(jnp.max(masked, axis=2, keepdims=True))
        exponent = jnp.exp(masked - row_max)
        attn_prob = low(exponent / lax.optimization_barrier(jnp.sum(exponent, axis=2, keepdims=True)))
        return jnp.einsum('hij,jhd->ihd', attn_prob, value_rows, precision=maximum_precision)
    offsets = jnp.arange(seq_len // block_len, dtype=jnp.int32) * block_len
    attended = lax.map(jax.checkpoint(attend), offsets)
    attended = low_back(low(attended.reshape(seq_len, H * HD)))
    middle = seq_rows + low_back(matmul(attended, out_weight))
    normed_two = low(layer_norm(middle, ln2_gain, ln2_bias))
    pre_act = low_back(matmul(normed_two, up_weight) + up_bias)
    activated = low(gelu_exact(pre_act))
    return middle + low_back(matmul(activated, down_weight) + down_bias)

def reference(tokens, cotangent, piece_starts, ln1_gain, ln1_bias, qkv_weight, content_bias, position_bias, pos_weight, out_weight, ln2_gain, ln2_bias, up_weight, up_bias, down_weight, down_bias):
    params = tuple((argument.astype(jnp.float32) for argument in (ln1_gain, ln1_bias, qkv_weight, content_bias, position_bias, pos_weight, out_weight, ln2_gain, ln2_bias, up_weight, up_bias, down_weight, down_bias)))
    seq_inputs = jnp.transpose(tokens.astype(jnp.float32), (0, 2, 1)).reshape(MB * SEQS, SEQ_LEN, D)
    seq_cots = jnp.transpose(cotangent.astype(jnp.float32), (0, 2, 1)).reshape(MB * SEQS, SEQ_LEN, D)
    seq_starts = piece_starts.reshape(MB * SEQS, NPIECE)

    def one_sequence(carried, sliced):
        seq_rows, seq_cot, starts = sliced

        def forward(weights, rows_in):
            return layer(weights, rows_in, starts)
        result, pullback = jax.vjp(forward, params, seq_rows)
        grad_params, grad_rows = pullback(seq_cot)
        summed = tuple((left_op + right_op for left_op, right_op in zip(carried, grad_params)))
        return (summed, (result, grad_rows))
    zeros_init = tuple((jnp.zeros_like(param_in) for param_in in params))
    gradients, (results, grad_rows) = lax.scan(one_sequence, zeros_init, (seq_inputs, seq_cots, seq_starts))
    output = jnp.transpose(results.reshape(MB, SEQS * SEQ_LEN, D), (0, 2, 1))
    grad_tokens = jnp.transpose(grad_rows.reshape(MB, SEQS * SEQ_LEN, D), (0, 2, 1))
    return (output, grad_tokens, gradients[0], gradients[1], gradients[2], gradients[3], gradients[4], gradients[5], gradients[6], gradients[7], gradients[8], gradients[9], gradients[10], gradients[11], gradients[12])
```

```python
from functools import reduce

import jax
import jax.numpy as jnp
import numpy as np
from jax import lax
from jax.experimental import pallas as pl
from jax.experimental.pallas import tpu as pltpu
from jax.sharding import PartitionSpec as P

D = 512
SEQ_LEN = 1024
PIECE = 256


norm_epsilon = 1e-05
big_negative = -1e30
inv_sqrt_two = 0.7071067811865476
inv_sqrt_tau = 0.3989422804014327


def contract(left_op, right_op, flipped):
    if flipped:
        return lax.dot_general(
            left_op, right_op, (((1,), (1,)), ((), ())), preferred_element_type=jnp.float32
        )
    return jnp.dot(left_op, right_op, preferred_element_type=jnp.float32)


def outer_sum(left_op, right_op):
    return lax.dot_general(
        left_op, right_op, (((0,), (0,)), ((), ())), preferred_element_type=jnp.float32
    )


def gather_rows(values):
    return lax.all_gather(values, "row", axis=0, tiled=True)


def gather_cols(values):
    return lax.all_gather(values, "col", axis=0, tiled=True)


def sum_over_cols(gathered, weight, flipped):
    share_rows = gathered.shape[0] // lax.axis_size("col")

    def partial_term(offset, amount):
        return contract(gathered, weight, flipped)

    return lax.psum_scatter(
        partial_term(jnp.int32(0), lax.axis_size("col") * share_rows),
        "col",
        scatter_dimension=0,
        tiled=True,
    )


def sum_over_rows(gathered, weight, flipped):
    share_rows = gathered.shape[0] // lax.axis_size("row")

    def partial_term(offset, amount):
        return contract(gathered, weight, flipped)

    return lax.psum_scatter(
        partial_term(jnp.int32(0), lax.axis_size("row") * share_rows),
        "row",
        scatter_dimension=0,
        tiled=True,
    )


def feature_sums(first_sum, second_sum):
    return lax.psum((first_sum, second_sum), "col")


def normalize(values, gain, bias):
    feature_count = values.shape[1] * lax.axis_size("col")
    total_row, square_row = feature_sums(jnp.sum(values, axis=1), jnp.sum(values * values, axis=1))
    mean_row = total_row / feature_count
    inverse = lax.rsqrt(square_row / feature_count - mean_row * mean_row + norm_epsilon)
    scaled = (values - mean_row[:, None]) * inverse[:, None]
    return (scaled * gain + bias, scaled, inverse)


def normalize_back(grad_in, scaled, inverse, gain):
    feature_count = grad_in.shape[1] * lax.axis_size("col")
    shifted = grad_in * gain
    first_sum, second_sum = feature_sums(
        jnp.sum(shifted, axis=1), jnp.sum(shifted * scaled, axis=1)
    )
    back_rows = inverse[:, None] * (
        shifted - first_sum[:, None] / feature_count - scaled * second_sum[:, None] / feature_count
    )
    return (back_rows, jnp.sum(grad_in * scaled, axis=0), jnp.sum(grad_in, axis=0))


def gelu_exact(values):
    return 0.5 * values * (1.0 + jax.scipy.special.erf(values * inv_sqrt_two))


def gelu_slope(values):
    return (
        0.5 * (1.0 + jax.scipy.special.erf(values * inv_sqrt_two))
        + values * jnp.exp(-0.5 * values * values) * inv_sqrt_tau
    )


def sinusoid_table(seq_len, feature_count):
    offsets = jnp.arange(2 * seq_len - 1, dtype=jnp.float32) - (seq_len - 1)
    frequency = 10000.0 ** (-jnp.arange(0, feature_count, 2, dtype=jnp.float32) / feature_count)
    angles = offsets[:, None] * frequency[None, :]
    return jnp.concatenate([jnp.sin(angles), jnp.cos(angles)], axis=1).astype(jnp.bfloat16)


def piece_labels(positions, starts, piece_len):
    inside = (positions[:, None] >= starts[None, :]) & (
        positions[:, None] < starts[None, :] + piece_len
    )
    numbers = jnp.arange(1, starts.shape[0] + 1, dtype=jnp.int32)
    return jnp.sum(jnp.where(inside, numbers[None, :], 0), axis=1) - 1


def block_mask(offset, block_len, labels):
    positions = jnp.arange(labels.shape[0], dtype=jnp.int32)
    row_pos = offset + jnp.arange(block_len, dtype=jnp.int32)
    row_labels = lax.dynamic_slice_in_dim(labels, offset, block_len, 0)
    same_piece = (row_labels[:, None] == labels[None, :]) & (row_labels[:, None] >= 0)
    return (positions[None, :] <= row_pos[:, None]) | same_piece


def skew_rows(unshifted_reversed_scores, key_total):
    head_total, row_total, rel_span = unshifted_reversed_scores.shape
    flattened = unshifted_reversed_scores.reshape(head_total, row_total * rel_span)
    window = lax.slice_in_dim(
        flattened, row_total - 1, row_total - 1 + row_total * (rel_span - 1), axis=1
    )
    return window.reshape(head_total, row_total, rel_span - 1)[:, :, :key_total]


def unskew_rows(grad_pos, rel_span):
    head_total, row_total, key_total = grad_pos.shape
    padded = jnp.pad(grad_pos, ((0, 0), (0, 0), (0, rel_span - 1 - key_total)))
    flattened = padded.reshape(head_total, row_total * (rel_span - 1))
    flattened = jnp.pad(flattened, ((0, 0), (row_total - 1, 1)))
    return flattened.reshape(head_total, row_total, rel_span)


def block_scores(qu_block, query_position_block, key_rows, relative_block, allowed):
    content = jnp.einsum("ihd,jhd->hij", qu_block, key_rows, preferred_element_type=jnp.float32)
    unshifted_reversed_scores = jnp.einsum(
        "sgw,egw->gse", query_position_block, relative_block, preferred_element_type=jnp.float32
    )
    position = skew_rows(unshifted_reversed_scores, key_rows.shape[0])
    return jnp.where(allowed[None], content + position, big_negative)


def attention_forward(query_u, query_v, key_rows, value_rows, relative_rev, labels):
    seq_len, head_count, head_dim = key_rows.shape
    block_len = min(512, seq_len)
    rel_span = block_len + seq_len - 1
    offsets = jnp.arange(seq_len // block_len, dtype=jnp.int32) * block_len

    def attend(offset):
        qu_block = lax.dynamic_slice_in_dim(query_u, offset, block_len, 0)
        query_position_block = lax.dynamic_slice_in_dim(query_v, offset, block_len, 0)
        relative_block = lax.dynamic_slice_in_dim(
            relative_rev, seq_len - block_len - offset, rel_span, 0
        )
        scores = block_scores(
            qu_block,
            query_position_block,
            key_rows,
            relative_block,
            block_mask(offset, block_len, labels),
        )
        row_max = jnp.max(scores, axis=2, keepdims=True)
        log_total = row_max + jnp.log(jnp.sum(jnp.exp(scores - row_max), axis=2, keepdims=True))
        attn_prob = jnp.exp(scores - log_total).astype(jnp.bfloat16)
        result = jnp.einsum(
            "hij,jhd->ihd", attn_prob, value_rows, preferred_element_type=jnp.float32
        )
        return (result, log_total[:, :, 0])

    results, log_totals = lax.map(attend, offsets)
    return (results.reshape(seq_len, head_count * head_dim), log_totals)


def attention_backward(
    query_u, query_v, key_rows, value_rows, relative_rev, labels, log_totals, grad_att
):
    seq_len, head_count, head_dim = key_rows.shape
    block_len = min(512, seq_len)
    rel_span = block_len + seq_len - 1
    offsets = jnp.arange(seq_len // block_len, dtype=jnp.int32) * block_len

    def back_block(carried, sliced):
        grad_keys, grad_values, grad_rel = carried
        offset, log_total = sliced
        rel_start = seq_len - block_len - offset
        qu_block = lax.dynamic_slice_in_dim(query_u, offset, block_len, 0)
        query_position_block = lax.dynamic_slice_in_dim(query_v, offset, block_len, 0)
        relative_block = lax.dynamic_slice_in_dim(relative_rev, rel_start, rel_span, 0)
        scores = block_scores(
            qu_block,
            query_position_block,
            key_rows,
            relative_block,
            block_mask(offset, block_len, labels),
        )
        attn_prob = jnp.exp(scores - log_total[:, :, None])
        low_prob = attn_prob.astype(jnp.bfloat16)
        grad_block = lax.dynamic_slice_in_dim(grad_att, offset, block_len, 0)
        grad_prob = jnp.einsum(
            "ihd,jhd->hij", grad_block, value_rows, preferred_element_type=jnp.float32
        )
        row_inner = jnp.sum(attn_prob * grad_prob, axis=2, keepdims=True)
        grad_scores = (attn_prob * (grad_prob - row_inner)).astype(jnp.bfloat16)
        grad_values = grad_values + jnp.einsum(
            "hij,ihd->jhd", low_prob, grad_block, preferred_element_type=jnp.float32
        )
        grad_keys = grad_keys + jnp.einsum(
            "hij,ihd->jhd", grad_scores, qu_block, preferred_element_type=jnp.float32
        )
        grad_qu = jnp.einsum(
            "hij,jhd->ihd", grad_scores, key_rows, preferred_element_type=jnp.float32
        )
        gradient_unshifted = unskew_rows(grad_scores, rel_span)
        grad_qv = jnp.einsum(
            "qjp,pqr->jqr", gradient_unshifted, relative_block, preferred_element_type=jnp.float32
        )
        rel_part = jnp.einsum(
            "nfx,fne->xne",
            gradient_unshifted,
            query_position_block,
            preferred_element_type=jnp.float32,
        )
        current = lax.dynamic_slice_in_dim(grad_rel, rel_start, rel_span, 0)
        grad_rel = lax.dynamic_update_slice_in_dim(grad_rel, current + rel_part, rel_start, 0)
        return ((grad_keys, grad_values, grad_rel), (grad_qu, grad_qv))

    zero_rows = jnp.zeros((seq_len, head_count, head_dim), jnp.float32)
    zero_rel = jnp.zeros((2 * seq_len - 1, head_count, head_dim), jnp.float32)
    carried, stacked = lax.scan(back_block, (zero_rows, zero_rows, zero_rel), (offsets, log_totals))
    grad_keys, grad_values, grad_rel = carried
    grad_qu = stacked[0].reshape(seq_len, head_count, head_dim)
    grad_qv = stacked[1].reshape(seq_len, head_count, head_dim)
    return (grad_qu, grad_qv, grad_keys, grad_values, grad_rel)


def heads_pass(packed, content_bias, position_bias, relative_rev, labels):
    seq_len = packed.shape[0]
    head_count, head_dim = content_bias.shape
    scaling = head_dim ** (-0.5)
    packed = packed.reshape(seq_len, head_count, 3, head_dim)
    queries = packed[:, :, 0].astype(jnp.float32)
    key_rows = packed[:, :, 1]
    value_rows = packed[:, :, 2]
    query_u = ((queries + content_bias) * scaling).astype(jnp.bfloat16)
    query_v = ((queries + position_bias) * scaling).astype(jnp.bfloat16)
    attended, log_totals = attention_forward(
        query_u, query_v, key_rows, value_rows, relative_rev, labels
    )
    return (attended.astype(jnp.bfloat16), (query_u, query_v, key_rows, value_rows, log_totals))


def heads_back(kept, relative_rev, labels, grad_att):
    query_u, query_v, key_rows, value_rows, log_totals = kept
    seq_len, head_count, head_dim = key_rows.shape
    scaling = head_dim ** (-0.5)
    grad_att = grad_att.reshape(seq_len, head_count, head_dim)
    grad_qu, grad_qv, grad_keys, grad_values, grad_rel = attention_backward(
        query_u, query_v, key_rows, value_rows, relative_rev, labels, log_totals, grad_att
    )
    cbias_part = jnp.sum(grad_qu, axis=0) * scaling
    pbias_part = jnp.sum(grad_qv, axis=0) * scaling
    grad_query = (grad_qu + grad_qv) * scaling
    grad_packed = jnp.stack([grad_query, grad_keys, grad_values], axis=2)
    grad_packed = grad_packed.reshape(seq_len, head_count * 3 * head_dim).astype(jnp.bfloat16)
    rel_low = grad_rel.reshape(2 * seq_len - 1, head_count * head_dim).astype(jnp.bfloat16)
    return (grad_packed, rel_low, cbias_part, pbias_part)


def grid_micro(seq_feats, cot_feats, params, shared):
    (
        ln1_gain,
        ln1_bias,
        qkv_weight,
        content_bias,
        position_bias,
        out_weight,
        ln2_gain,
        ln2_bias,
        up_weight,
        up_bias,
        down_weight,
        down_bias,
    ) = params
    relative_rev, table_rev, labels = shared
    seq_in = seq_feats.astype(jnp.float32).T
    normed_one, scaled_one, inverse_one = normalize(seq_in, ln1_gain, ln1_bias)
    gathered_one = gather_rows(normed_one.astype(jnp.bfloat16))
    packed = sum_over_cols(gathered_one, qkv_weight, False).astype(jnp.bfloat16)
    attended, kept = heads_pass(packed, content_bias, position_bias, relative_rev, labels)
    att_gathered = gather_cols(attended)
    middle = seq_in + sum_over_rows(att_gathered, out_weight, False)
    normed_two, scaled_two, inverse_two = normalize(middle, ln2_gain, ln2_bias)
    gathered_two = gather_rows(normed_two.astype(jnp.bfloat16))
    pre_act = sum_over_cols(gathered_two, up_weight, False) + up_bias
    activated = gelu_exact(pre_act).astype(jnp.bfloat16)
    act_gathered = gather_cols(activated)
    output = middle + sum_over_rows(act_gathered, down_weight, False) + down_bias
    grad_final = cot_feats.T
    gout = grad_final.astype(jnp.float32)
    final_gathered = gather_rows(grad_final)
    grad_act = sum_over_cols(final_gathered, down_weight, True)
    grad_pre = (grad_act * gelu_slope(pre_act)).astype(jnp.bfloat16)
    pre_gathered = gather_cols(grad_pre)
    grad_two = sum_over_rows(pre_gathered, up_weight, True)
    backward_second, gain_two, bias_two = normalize_back(
        grad_two, scaled_two, inverse_two, ln2_gain
    )
    grad_middle = gout + backward_second
    grad_branch = grad_middle.astype(jnp.bfloat16)
    branch_gathered = gather_rows(grad_branch)
    grad_att = sum_over_cols(branch_gathered, out_weight, True).astype(jnp.bfloat16)
    grad_packed, rel_low, cbias_part, pbias_part = heads_back(kept, relative_rev, labels, grad_att)
    packed_gathered = gather_cols(grad_packed)
    grad_one = sum_over_rows(packed_gathered, qkv_weight, True)
    back_one, gain_one, bias_one = normalize_back(grad_one, scaled_one, inverse_one, ln1_gain)
    grad_in = grad_middle + back_one
    collected = (
        outer_sum(gathered_one, packed_gathered),
        outer_sum(att_gathered, branch_gathered),
        outer_sum(gathered_two, pre_gathered),
        outer_sum(act_gathered, final_gathered),
        outer_sum(table_rev, rel_low),
        cbias_part,
        pbias_part,
        jnp.sum(grad_pre.astype(jnp.float32), axis=0),
        gain_one,
        bias_one,
        gain_two,
        bias_two,
        jnp.sum(gout, axis=0),
    )
    return (output.T, grad_in.T, collected)


def embed_heads(part, row_pick, col_count):
    head_count = part.shape[0]
    spread = jnp.transpose(part.reshape(head_count, col_count, -1), (1, 0, 2))
    placed = jnp.where(row_pick[:, None, None, None], spread[None], 0.0)
    return placed.reshape(row_pick.shape[0] * col_count, head_count, -1)


def shards(
    tokens,
    cotangent,
    piece_starts,
    ln1_gain,
    ln1_bias,
    qkv_weight,
    content_bias,
    position_bias,
    pos_weight,
    out_weight,
    ln2_gain,
    ln2_bias,
    up_weight,
    up_bias,
    down_weight,
    down_bias,
):
    micro_count = tokens.shape[0]
    row_count = lax.axis_size("row")
    col_count = lax.axis_size("col")
    grid_cells = row_count * col_count
    head_count, head_dim = content_bias.shape
    pos_cols = lax.all_gather(pos_weight, "col", axis=0, tiled=True)
    table_rev = sinusoid_table(SEQ_LEN, D)[::-1]
    relative_rev = jnp.dot(table_rev, pos_cols, preferred_element_type=jnp.float32).astype(
        jnp.bfloat16
    )
    relative_rev = relative_rev.reshape(2 * SEQ_LEN - 1, head_count, head_dim)
    positions = jnp.arange(SEQ_LEN, dtype=jnp.int32)
    params = (
        ln1_gain,
        ln1_bias,
        qkv_weight,
        content_bias,
        position_bias,
        out_weight,
        ln2_gain,
        ln2_bias,
        up_weight,
        up_bias,
        down_weight,
        down_bias,
    )
    outputs, grad_inputs, part_lists = ([], [], [])
    for micro_idx in range(micro_count):
        labels = piece_labels(positions, piece_starts[micro_idx, 0], PIECE)
        out_feats, grad_feats, collected = grid_micro(
            tokens[micro_idx], cotangent[micro_idx], params, (relative_rev, table_rev, labels)
        )
        outputs.append(out_feats)
        grad_inputs.append(grad_feats)
        part_lists.append(collected)
    totals = [
        reduce(jnp.add, [collected[member] for collected in part_lists]) for member in range(13)
    ]
    (
        acc_qkv,
        acc_out,
        acc_up,
        acc_down,
        acc_pos,
        acc_cbias,
        acc_pbias,
        acc_ubias,
        acc_g1,
        acc_b1,
        acc_g2,
        acc_b2,
        acc_db,
    ) = totals
    row_pick = jnp.arange(row_count, dtype=jnp.int32) == lax.axis_index("row")
    pos_term = jnp.where(row_pick[:, None, None], acc_pos[None], 0.0).reshape(
        row_count * acc_pos.shape[0], -1
    )
    cbias_term = embed_heads(acc_cbias, row_pick, col_count)
    pbias_term = embed_heads(acc_pbias, row_pick, col_count)
    col_pick = jnp.arange(col_count, dtype=jnp.int32) == lax.axis_index("col")
    ubias_term = jnp.where(row_pick[:, None], acc_ubias[None], 0.0).reshape(grid_cells, -1)
    norm_terms = [
        jnp.where(col_pick[:, None], vector[None], 0.0).reshape(grid_cells, -1)
        for vector in (acc_g1, acc_b1, acc_g2, acc_b2, acc_db)
    ]
    sum_pos, sum_cbias, sum_pbias, sum_ubias, sum_g1, sum_b1, sum_g2, second_bias_total, sum_db = (
        lax.psum_scatter(pos_term, ("row", "col"), scatter_dimension=0, tiled=True),
        lax.psum_scatter(cbias_term, ("row", "col"), scatter_dimension=0, tiled=True),
        lax.psum_scatter(pbias_term, ("row", "col"), scatter_dimension=0, tiled=True),
        lax.psum_scatter(ubias_term, ("row", "col"), scatter_dimension=0, tiled=True),
        lax.psum_scatter(norm_terms[0], ("row", "col"), scatter_dimension=0, tiled=True),
        lax.psum_scatter(norm_terms[1], ("row", "col"), scatter_dimension=0, tiled=True),
        lax.psum_scatter(norm_terms[2], ("row", "col"), scatter_dimension=0, tiled=True),
        lax.psum_scatter(norm_terms[3], ("row", "col"), scatter_dimension=0, tiled=True),
        lax.psum_scatter(norm_terms[4], ("row", "col"), scatter_dimension=0, tiled=True),
    )
    sum_qkv, sum_out, sum_up, sum_down = (acc_qkv, acc_out, acc_up, acc_down)
    summed = (
        lax.psum_scatter(
            sum_qkv.astype(jnp.bfloat16), "dp", scatter_dimension=1, tiled=True
        ).astype(jnp.float32),
        lax.psum_scatter(
            sum_out.astype(jnp.bfloat16), "dp", scatter_dimension=1, tiled=True
        ).astype(jnp.float32),
        lax.psum_scatter(sum_up.astype(jnp.bfloat16), "dp", scatter_dimension=1, tiled=True).astype(
            jnp.float32
        ),
        lax.psum_scatter(
            sum_down.astype(jnp.bfloat16), "dp", scatter_dimension=1, tiled=True
        ).astype(jnp.float32),
        lax.psum_scatter(
            sum_pos.astype(jnp.bfloat16), "dp", scatter_dimension=1, tiled=True
        ).astype(jnp.float32),
        lax.psum_scatter(
            sum_cbias.astype(jnp.bfloat16), "dp", scatter_dimension=2, tiled=True
        ).astype(jnp.float32),
        lax.psum_scatter(
            sum_pbias.astype(jnp.bfloat16), "dp", scatter_dimension=2, tiled=True
        ).astype(jnp.float32),
        lax.psum_scatter(
            sum_ubias.astype(jnp.bfloat16), "dp", scatter_dimension=1, tiled=True
        ).astype(jnp.float32),
        lax.psum_scatter(sum_g1.astype(jnp.bfloat16), "dp", scatter_dimension=1, tiled=True).astype(
            jnp.float32
        ),
        lax.psum_scatter(sum_b1.astype(jnp.bfloat16), "dp", scatter_dimension=1, tiled=True).astype(
            jnp.float32
        ),
        lax.psum_scatter(sum_g2.astype(jnp.bfloat16), "dp", scatter_dimension=1, tiled=True).astype(
            jnp.float32
        ),
        lax.psum_scatter(
            second_bias_total.astype(jnp.bfloat16), "dp", scatter_dimension=1, tiled=True
        ).astype(jnp.float32),
        lax.psum_scatter(sum_db.astype(jnp.bfloat16), "dp", scatter_dimension=1, tiled=True).astype(
            jnp.float32
        ),
    )
    (
        grad_qkv_w,
        grad_out_w,
        grad_up_w,
        grad_down_w,
        grad_pos_w,
        grad_cbias,
        grad_pbias,
        grad_ubias,
        grad_g1,
        grad_b1,
        grad_g2,
        grad_b2,
        grad_dbias,
    ) = summed
    output_rows = jnp.stack(outputs, axis=0)
    grad_rows = jnp.stack(grad_inputs, axis=0)
    return (
        output_rows,
        grad_rows,
        grad_g1.reshape(-1),
        grad_b1.reshape(-1),
        grad_qkv_w,
        grad_cbias.reshape(head_count, -1),
        grad_pbias.reshape(head_count, -1),
        grad_pos_w,
        grad_out_w,
        grad_g2.reshape(-1),
        grad_b2.reshape(-1),
        grad_up_w,
        grad_ubias.reshape(-1),
        grad_down_w,
        grad_dbias.reshape(-1),
    )


MESH = pl.DeviceIdType.MESH
F32 = jnp.float32
BF16 = jnp.bfloat16


def aligned(index, size):
    return index if isinstance(index, int) else pl.multiple_of(index, size)


def nt(a, b):
    return lax.dot_general(a, b, (((1,), (1,)), ((), ())), preferred_element_type=F32)


def nn(a, b):
    return lax.dot_general(a, b, (((1,), (0,)), ((), ())), preferred_element_type=F32)


def tn(a, b):
    return lax.dot_general(a, b, (((0,), (0,)), ((), ())), preferred_element_type=F32)


def place():
    k, z, c = lax.axis_index("dp"), lax.axis_index("row"), lax.axis_index("col")
    cx = c + 1 - 2 * lax.rem(c, 2)
    cy = lax.rem(c + 2, 4)
    near = (1 - k) * cx + k * cy
    far = k * cx + (1 - k) * cy
    return k, z, c, near, far


def enter(rows):
    k, z, c, _, _ = place()
    barrier = pltpu.get_barrier_semaphore()
    peers = [(1 - k, z, c)]
    for step in range(1, rows):
        peers.append((k, lax.rem(z + step, rows), c))
    for step in range(1, 4):
        for core in range(2):
            peers.append((0 * k + core, z, lax.rem(c + step, 4)))
    for peer in peers:
        pl.semaphore_signal(barrier, inc=1, device_id=peer, device_id_type=MESH)
    pl.semaphore_wait(barrier, len(peers))


class Sems:
    def __init__(self, send, recv):
        self.send, self.recv, self.next = send, recv, 0
        self.pending = []

    def take(self, count=1):
        first = self.next
        self.next += count
        return first


def remote(sems, src, dst, slot, peer, when=None):
    copy = pltpu.make_async_remote_copy(
        src, dst, sems.send.at[slot], sems.recv.at[slot], device_id=peer, device_id_type=MESH
    )

    def start():
        copy.start()

    def finish():
        copy.wait_send()

    if when is None:
        copy.start()
        sems.pending.append(finish)
    else:
        pl.when(when)(start)
        sems.pending.append(lambda: pl.when(when)(finish))


def arrived(sems, dst, slot):
    pltpu.make_async_copy(dst, dst, sems.recv.at[slot]).wait()


def drain(sems):
    for finish in sems.pending:
        finish()
    sems.pending = []


def tall(row):
    padded = jnp.concatenate([row, jnp.zeros((120, 128), F32)], axis=0)
    return jnp.transpose(padded)


def forward_kernel(
    tok, cot, starts, small_col, small_row, table, wq, wp, wo, wu, wd,
    att, wo_all, wu_all, wd_all, wq_half, wp_half, xt, ct, normed_t, qcat, keys, vals, qv, probs, heads_out, params_col, params_row,
    kcat, own_att, starts_got, send, recv,
):
    rows = wu_all.shape[0]
    cols = wo_all.shape[0]
    half = rows // 2
    k, z, c, near, far = place()
    sems = Sems(send, recv)
    mine = lax.div(z, half) == k
    enter(rows)

    def q_block(cc):
        return wq_half.at[:, pl.ds(aligned(cc * 128, 128), 128), :]

    def p_block(cc):
        return wp_half.at[:, pl.ds(aligned(cc * 128, 128), 128), :]

    def u_block(cc, core=k):
        return wu_all.at[pl.ds(core * half, half), pl.ds(aligned(cc * 128, 128), 128), :]

    def o_block(cc, core=k):
        size = wo_all.shape[1] // 2
        return wo_all.at[cc, pl.ds(aligned(core * size, 128), size), :]

    def d_block(cc, core=k):
        size = wd_all.shape[1] // 2
        return wd_all.at[cc, pl.ds(aligned(core * size, 128), size), :]

    def q_one(i):
        return wq_half.at[i, pl.ds(aligned(c * 128, 128), 128), :]

    def p_one(i):
        return wp_half.at[i, pl.ds(aligned(c * 128, 128), 128), :]

    def u_one(i):
        return wu_all.at[k * half + i, pl.ds(aligned(c * 128, 128), 128), :]

    def o_one(i):
        size = wo_all.shape[1] // rows
        return wo_all.at[c, pl.ds(aligned((k * half + i) * size, 128), size), :]

    def d_one(i):
        size = wd_all.shape[1] // rows
        return wd_all.at[c, pl.ds(aligned((k * half + i) * size, 128), size), :]

    weights = {
        "q": (wq, q_one, q_block), "p": (wp, p_one, p_block), "o": (wo, o_one, o_block),
        "u": (wu, u_one, u_block), "d": (wd, d_one, d_block),
    }
    z_slot = {name: sems.take(2 * half * rows) for name in weights}
    near_slot = {name: sems.take(1) for name in weights}
    far_slot = {name: sems.take(2) for name in weights}
    sib_slot = {name: sems.take(4) for name in weights}

    def z_start(name):
        ref, one, _ = weights[name]
        for i in range(half):
            here = z == k * half + i
            slot = z_slot[name] + i * 2

            @pl.when(here)
            def _(ref=ref, dst=one(i), slot=slot):
                pltpu.make_async_copy(ref, dst, recv.at[slot]).start()

            for step in range(1, rows):
                peer = (k, lax.rem(z + step, rows), c)
                copy = pltpu.make_async_remote_copy(
                    ref, one(i), send.at[z_slot[name] + half * 2 + i * rows + step], recv.at[slot],
                    device_id=peer, device_id_type=MESH,
                )
                pl.when(here)(copy.start)
                sems.pending.append(lambda copy=copy, here=here: pl.when(here)(copy.wait_send))

    def z_done(name):
        _, one, _ = weights[name]
        for i in range(half):
            arrived(sems, one(i), z_slot[name] + i * 2)

    def near_start(name):
        block = weights[name][2]
        remote(sems, block(c), block(c), near_slot[name], (k, z, near))

    def near_done(name):
        arrived(sems, weights[name][2](near), near_slot[name])

    def far_start(name):
        block = weights[name][2]
        remote(sems, block(c), block(c), far_slot[name], (k, z, far))
        remote(sems, block(near), block(near), far_slot[name] + 1, (k, z, far))

    def far_done(name):
        block = weights[name][2]
        arrived(sems, block(far), far_slot[name])
        arrived(sems, block(3 - c), far_slot[name] + 1)

    def sib_start(name):
        block = weights[name][2]
        for cc in range(4):
            remote(sems, block(cc), block(cc), sib_slot[name] + cc, (1 - k, z, c))

    def sib_done(name):
        block = weights[name][2]
        for cc in range(4):
            arrived(sems, block(cc, 1 - k), sib_slot[name] + cc)

    feat = tok.shape[1]
    x_slot = sems.take(4)
    x_send = sems.take(4)
    xf_slot = sems.take(4)

    def x_part(cc, core):
        return xt.at[pl.ds(aligned(cc * feat + core * (feat // 2), 64), feat // 2), :]

    z_start("q")
    for b in range(2):
        target = 2 * b + k
        for core in range(2):
            src = tok.at[b, pl.ds(core * (feat // 2), feat // 2), :]
            dst = x_part(c, core)
            local = jnp.logical_and(target == c, core == k)

            @pl.when(local)
            def _(src=src, dst=dst):
                pltpu.make_async_copy(src, dst, recv.at[x_slot + c]).start()

            copy = pltpu.make_async_remote_copy(
                src, dst, send.at[x_send + 2 * b + core], recv.at[x_slot + c],
                device_id=(0 * k + core, z, target), device_id_type=MESH,
            )
            far_away = jnp.logical_not(local)
            pl.when(far_away)(copy.start)
            sems.pending.append(lambda copy=copy, far_away=far_away: pl.when(far_away)(copy.wait_send))

    g_col = sems.take(4)
    g_row = sems.take(rows)
    for step in range(1, 4):
        peer = (k, z, lax.rem(c + step, 4))
        copy = pltpu.make_async_remote_copy(
            small_col, params_col.at[c], send.at[g_col + step], recv.at[g_col],
            device_id=peer, device_id_type=MESH,
        )
        copy.start()
        sems.pending.append(copy.wait_send)
    pltpu.make_async_copy(small_col, params_col.at[c], recv.at[g_col]).start()
    for step in range(1, rows):
        peer = (k, lax.rem(z + step, rows), c)
        copy = pltpu.make_async_remote_copy(
            small_row, params_row.at[z], send.at[g_row + step], recv.at[g_row],
            device_id=peer, device_id_type=MESH,
        )
        copy.start()
        sems.pending.append(copy.wait_send)
    pltpu.make_async_copy(small_row, params_row.at[z], recv.at[g_row]).start()
    s_slot = sems.take(1)
    s_send = sems.take(4)
    for b in range(2):
        for core in range(2):
            target = 2 * b + k
            owner = c == z
            local = jnp.logical_and(owner, jnp.logical_and(target == c, core == k))
            away = jnp.logical_and(owner, jnp.logical_not(jnp.logical_and(target == c, core == k)))

            @pl.when(local)
            def _():
                pltpu.make_async_copy(starts, starts_got, recv.at[s_slot]).start()

            copy = pltpu.make_async_remote_copy(
                starts, starts_got, send.at[s_send + 2 * b + core], recv.at[s_slot],
                device_id=(0 * k + core, z, target), device_id_type=MESH,
            )
            pl.when(away)(copy.start)
            sems.pending.append(lambda copy=copy, away=away: pl.when(away)(copy.wait_send))

    for name in ("p", "o", "u", "d"):
        z_start(name)

    c_slot = sems.take(4)
    c_send = sems.take(4)
    tok_half = ct.shape[1]
    for b in range(2):
        target = 2 * b + k
        for core in range(2):
            src = cot.at[b, :, pl.ds(core * tok_half, tok_half)]
            dst = ct.at[pl.ds(aligned(c * feat, 128), feat), :]
            local = jnp.logical_and(target == c, core == k)

            @pl.when(local)
            def _(src=src, dst=dst):
                pltpu.make_async_copy(src, dst, recv.at[c_slot + c]).start()

            copy = pltpu.make_async_remote_copy(
                src, dst, send.at[c_send + 2 * b + core], recv.at[c_slot + c],
                device_id=(0 * k + core, z, target), device_id_type=MESH,
            )
            away = jnp.logical_not(local)
            pl.when(away)(copy.start)
            sems.pending.append(lambda copy=copy, away=away: pl.when(away)(copy.wait_send))

    for cc in range(4):
        arrived(sems, x_part(cc, k), x_slot + cc)
        remote(sems, x_part(cc, k), x_part(cc, k), xf_slot + cc, (1 - k, z, c))
    z_done("q")
    near_start("q")
    z_done("p")
    near_start("p")
    arrived(sems, params_col, g_col)
    arrived(sems, params_row, g_row)
    arrived(sems, starts_got, s_slot)
    for cc in range(4):
        arrived(sems, x_part(cc, 1 - k), xf_slot + cc)

    columns = [tall(params_col[cc]) for cc in range(4)]
    gain = jnp.concatenate([col[:, 0:1] for col in columns], axis=0)
    bias = jnp.concatenate([col[:, 1:2] for col in columns], axis=0)
    width = xt.shape[0]
    seq = xt.shape[1]
    piece = PIECE

    @pl.loop(0, seq // 256)
    def _(t):
        here = pl.ds(aligned(t * 256, 256), 256)
        x = xt[:, here].astype(F32)
        mean = jnp.sum(x, axis=0, keepdims=True) * (1.0 / width)
        square = jnp.sum(x * x, axis=0, keepdims=True) * (1.0 / width)
        inverse = lax.rsqrt(square - mean * mean + norm_epsilon)
        normed_t[:, here] = ((x - mean) * inverse * gain + bias).astype(BF16)

    near_done("q")
    far_start("q")
    near_done("p")
    far_start("p")
    for name in ("o", "u", "d"):
        z_done(name)
        near_start(name)

    kcat[:, 0:512] = table[...]
    far_done("q")
    scale = 0.125
    zeros = jnp.zeros((256, 64), F32)
    for i in range(half):
        small = params_row[k * half + i]

        @pl.loop(0, seq // 256)
        def _(t, i=i, small=small):
            here = pl.ds(aligned(t * 256, 256), 256)
            got = tn(normed_t[:, here], wq_half[i])
            for hb in range(2):
                h = 2 * i + hb
                low = got[:, hb * 192 : hb * 192 + 192].astype(BF16).astype(F32)
                query, key, value = low[:, 0:64], low[:, 64:128], low[:, 128:192]
                content = small[4:5, hb * 64 : hb * 64 + 64]
                position = small[5:6, hb * 64 : hb * 64 + 64]
                qcat[h, here, 512:640] = jnp.concatenate(
                    [(query + content) * scale, zeros], axis=1
                ).astype(BF16)
                qv[h, here, :] = ((query + position) * scale).astype(BF16)
                keys[h, here, :] = jnp.concatenate([key, zeros], axis=1).astype(BF16)
                vals[h, here, :] = value.astype(BF16)

    far_done("p")
    for i in range(half):
        for hb in range(2):
            h = 2 * i + hb

            @pl.loop(0, seq // 256)
            def _(t, i=i, hb=hb, h=h):
                here = pl.ds(aligned(t * 256, 256), 256)
                angle = nt(qv[h, here, :], wp_half[i, :, hb * 64 : hb * 64 + 64])
                cosine = table[here, 0:256].astype(F32)
                sine = table[here, 256:512].astype(F32)
                first, second = angle[:, 0:256], angle[:, 256:512]
                qcat[h, here, 0:256] = (first * sine + second * cosine).astype(BF16)
                qcat[h, here, 256:512] = (second * sine - first * cosine).astype(BF16)

    slot_len = seq // 2
    block = 256
    batch = lax.div(c, 2)

    def attend(h, low_row, keys_seen, slot):
        start = starts_got[pl.ds(2 * batch + slot, 1), :][:, 0:1]
        row = low_row + lax.broadcasted_iota(jnp.int32, (block, 1), 0)
        inside = jnp.logical_and(row >= start, row < start + piece)
        limit = jnp.where(inside, start + (piece - 1), row)
        here = pl.ds(aligned(low_row, block), block)
        scores = nt(qcat[h, here, :], kcat[0:keys_seen, :])
        column = slot * slot_len + lax.broadcasted_iota(jnp.int32, (block, slot_len), 1)
        last = jnp.where(column <= limit, scores[:, keys_seen - slot_len :], big_negative)
        top = jnp.max(last, axis=1, keepdims=True)
        if slot == 1:
            top = jnp.maximum(top, jnp.max(scores[:, :slot_len], axis=1, keepdims=True))
        last = jnp.exp(last - top)
        total = jnp.sum(last, axis=1, keepdims=True)
        if slot == 1:
            first = jnp.exp(scores[:, :slot_len] - top)
            total = total + jnp.sum(first, axis=1, keepdims=True)
            whole = jnp.concatenate([first, last], axis=1)
        else:
            whole = last
        low = (whole * (1.0 / total)).astype(BF16)
        probs[h, here, 0:keys_seen] = low
        heads_out[h, here, :] = nn(low, vals[h, 0:keys_seen, :])

    for i in range(half):

        @pl.loop(0, 2)
        def _(hb, i=i):
            h = 2 * i + hb
            kcat[:, 512:640] = keys[h]

            @pl.loop(0, slot_len // block)
            def _(t):
                attend(h, t * block, slot_len, 0)

            @pl.loop(0, slot_len // block)
            def _(t):
                attend(h, slot_len + t * block, seq, 1)

        if i == 0:
            for name in ("o", "u", "d"):
                near_done(name)
                far_start(name)

    for name in ("o", "u"):
        far_done(name)
        sib_start(name)
    mine_cols = jnp.concatenate([heads_out[h] for h in range(2 * half)], axis=1).astype(BF16)
    own_att[...] = mine_cols
    a_slot = sems.take(2)
    span = own_att.shape[1]
    other = pl.ds(aligned((1 - k) * tok_half, tok_half), tok_half)
    own = pl.ds(aligned(k * tok_half, tok_half), tok_half)
    remote(sems, own_att.at[other, :], att.at[:, pl.ds(aligned(k * span, 128), span)], a_slot, (1 - k, z, c))
    pltpu.make_async_copy(
        own_att.at[own, :], att.at[:, pl.ds(aligned(k * span, 128), span)], recv.at[a_slot + 1]
    ).start()
    far_done("d")
    sib_start("d")
    arrived(sems, own_att.at[own, :], a_slot + 1)
    arrived(sems, own_att.at[own, :], a_slot)
    for cc in range(4):
        arrived(sems, ct.at[pl.ds(cc * feat, feat), :], c_slot + cc)
    for name in ("o", "u", "d"):
        sib_done(name)
    drain(sems)


def erf_parts(values):
    erf = lax.erf(values * inv_sqrt_two)
    return 0.5 * (1.0 + erf)


def middle_kernel(
    att, wo_all, wu_all, wd_all, xt, ct, params_col, params_row,
    out_t, grad_mid_t, grad_att, g_up, g_down, g_out, small,
    mid, norm, hat, inv, gout, acc_out, acc_two, tall_norm,
):
    rows, cols = wu_all.shape[0], wo_all.shape[0]
    count = att.shape[0]
    k = lax.axis_index("dp")
    own = pl.ds(aligned(k * count, count), count)

    def line(index):
        return jnp.concatenate([params_col[cc, index : index + 1, :] for cc in range(cols)], axis=1)

    def out_weight():
        return jnp.concatenate([wo_all[cc] for cc in range(cols)], axis=1)

    width = att.shape[1]
    x = jnp.transpose(xt[:, own].astype(F32))
    middle = x + nn(att[...], out_weight())
    mid[...] = middle
    mean = jnp.sum(middle, axis=1, keepdims=True) * (1.0 / width)
    square = jnp.sum(middle * middle, axis=1, keepdims=True) * (1.0 / width)
    inverse = lax.rsqrt(square - mean * mean + norm_epsilon)
    scaled = (middle - mean) * inverse
    hat[...] = scaled
    inv[...] = inverse
    low = (scaled * line(2) + line(3)).astype(BF16)
    norm[...] = low
    tall_norm[...] = jnp.transpose(low)
    gout[...] = jnp.transpose(ct[...])
    acc_out[...] = jnp.zeros_like(acc_out)
    acc_two[...] = jnp.zeros_like(acc_two)
    small[...] = jnp.zeros_like(small)
    hidden = wu_all.shape[2]

    @pl.loop(0, rows)
    def _(r):
        here = pl.ds(aligned(r * hidden, hidden), hidden)
        bias = jnp.concatenate([params_row[r, j : j + 1, :] for j in range(hidden // 128)], axis=1)
        down = jnp.concatenate([wd_all[cc, here, :] for cc in range(cols)], axis=1)
        pre = nn(norm[...], wu_all[r]) + bias
        grad_act = nt(gout[...], down)
        half = erf_parts(pre)
        act = (pre * half).astype(BF16)
        slope = half + pre * jnp.exp(-0.5 * pre * pre) * inv_sqrt_tau
        grad = grad_act * slope
        low_grad = grad.astype(BF16)
        small[pl.ds(5 + r, 1), :] = jnp.sum(low_grad.astype(F32), axis=0, keepdims=True)
        acc_out[...] += nn(act, down)
        acc_two[...] += nt(low_grad, wu_all[r])
        g_up[r] = nn(tall_norm[...], low_grad).astype(BF16)
        found = tn(act, gout[...]).astype(BF16)
        for cc in range(cols):
            g_down[cc, here, :] = found[:, cc * 128 : cc * 128 + 128]

    cotangent = gout[...].astype(F32)
    out_t[...] = jnp.transpose(mid[...] + acc_out[...] + line(4)).astype(BF16)
    two = acc_two[...]
    small[2:3, :] = jnp.sum(two * hat[...], axis=0, keepdims=True)
    small[3:4, :] = jnp.sum(two, axis=0, keepdims=True)
    small[4:5, :] = jnp.sum(cotangent, axis=0, keepdims=True)
    shifted = two * line(2)
    first = jnp.sum(shifted, axis=1, keepdims=True) * (1.0 / width)
    second = jnp.sum(shifted * hat[...], axis=1, keepdims=True) * (1.0 / width)
    grad_mid = cotangent + inv[...] * (shifted - first - hat[...] * second)
    grad_mid_t[...] = jnp.transpose(grad_mid)
    branch = grad_mid.astype(BF16)
    grad_att[...] = nt(branch, out_weight()).astype(BF16)
    found = tn(att[...], branch).astype(BF16)
    for cc in range(cols):
        g_out[cc] = found[:, cc * 128 : cc * 128 + 128]


def backward_kernel(
    out_t, grad_mid_t, grad_att, g_up, g_down, g_out, small, params_col, table, wq_half, wp_half, xt, normed_t,
    qcat, keys, vals, qv, probs, heads_out,
    outs, grads, f_q, f_p, f_o, f_u, f_d, f_small,
    kcat, grad_o, head_grad, turned, turned_k, turned_v, turned_p, one_t, one_low, one_got, grad_x, sum_a, sum_b,
    hs_q, hs_p, hs_o, hs_u, hs_d, r0_o, r0_u, r0_d,
    r1_q, r1_p, r1_o, r1_u, r1_d, r2_q, r2_p, r2_o, r2_u, r2_d, r3_q, r3_p, r3_o, r3_u, r3_d,
    all_small, got_small, got_z, send, recv,
):
    rows, cols = g_up.shape[0], g_out.shape[0]
    half = rows // 2
    k, z, c, near, far = place()
    sems = Sems(send, recv)
    mine = lax.div(z, half) == k
    enter(rows)
    sibling = (1 - k, z, c)

    hs = {
        "q": lambda i, cc: hs_q.at[i, cc], "p": lambda i, cc: hs_p.at[i, cc], "u": lambda i, cc: hs_u.at[i, cc],
        "o": lambda i, cc: hs_o.at[cc, i], "d": lambda i, cc: hs_d.at[cc, i],
    }
    r1 = {"q": r1_q, "p": r1_p, "o": r1_o, "u": r1_u, "d": r1_d}
    r2 = {"q": r2_q, "p": r2_p, "o": r2_o, "u": r2_u, "d": r2_d}
    r3 = {"q": r3_q, "p": r3_p, "o": r3_o, "u": r3_u, "d": r3_d}
    final = {"q": f_q, "p": f_p, "o": f_o, "u": f_u, "d": f_d}
    slots = {}
    for name in ("o", "u", "d", "q", "p"):
        slots[name, "sib"] = sems.take(4)
        slots[name, "one"] = sems.take(2 * half)
        slots[name, "two"] = sems.take(half)
        slots[name, "z"] = sems.take(rows * half)
        slots[name, "last"] = sems.take(1)

    def grad_half(name, core):
        if name == "u":
            return g_up.at[pl.ds(core * half, half)]
        full = g_out if name == "o" else g_down
        size = full.shape[1] // 2
        return full.at[:, pl.ds(aligned(core * size, 128), size), :]

    got0 = {"u": r0_u, "o": r0_o, "d": r0_d}

    def sib_start(name):
        remote(sems, grad_half(name, 1 - k), got0[name], slots[name, "sib"], sibling)

    def sib_done(name):
        arrived(sems, got0[name], slots[name, "sib"])
        if name == "u":
            for i in range(half):
                total = g_up[k * half + i].astype(F32) + r0_u[i].astype(F32)
                hs_u[i] = total.astype(BF16).reshape(hs_u.shape[1:])
        else:
            full = g_out if name == "o" else g_down
            size = full.shape[1] // 2
            to = hs_o if name == "o" else hs_d
            for cc in range(cols):
                part = full[cc, pl.ds(aligned(k * size, 128), size), :]
                total = part.astype(F32) + got0[name][cc].astype(F32)
                to[cc] = total.astype(BF16).reshape(to.shape[1:])

    def one_start(name, i):
        block = hs[name]
        remote(sems, block(i, far), r1[name].at[i, 0], slots[name, "one"] + 2 * i, (k, z, far))
        remote(sems, block(i, 3 - c), r1[name].at[i, 1], slots[name, "one"] + 2 * i + 1, (k, z, far))

    def load(ref):
        return ref[...].astype(F32)

    def one_done(name, i):
        block = hs[name]
        arrived(sems, r1[name].at[i, 1], slots[name, "one"] + 2 * i + 1)
        r1[name][i, 1] = (r1[name][i, 1].astype(F32) + load(block(i, near))).astype(BF16)
        remote(sems, r1[name].at[i, 1], r2[name].at[i], slots[name, "two"] + i, (k, z, near))
        arrived(sems, r1[name].at[i, 0], slots[name, "one"] + 2 * i)
        r1[name][i, 0] = (r1[name][i, 0].astype(F32) + load(block(i, c))).astype(BF16)

    def two_done(name, i):
        arrived(sems, r2[name].at[i], slots[name, "two"] + i)
        r2[name][i] = (r2[name][i].astype(F32) + r1[name][i, 0].astype(F32)).astype(BF16)
        target = k * half + i
        base = slots[name, "z"]
        away = z != target
        copy = pltpu.make_async_remote_copy(
            r2[name].at[i], r3[name].at[z], send.at[base + i], recv.at[base + z],
            device_id=(k, target, c), device_id_type=MESH,
        )
        pl.when(away)(copy.start)
        sems.pending.append(lambda: pl.when(away)(copy.wait_send))

    def z_done(name):
        base = slots[name, "z"]
        to = final[name]

        @pl.when(mine)
        def _():
            total = r2[name][z - k * half].astype(F32)
            for step in range(1, rows):
                source = lax.rem(z + step, rows)
                arrived(sems, r3[name].at[source], base + source)
                total = total + r3[name][source].astype(F32)
            to[...] = total

        copy = pltpu.make_async_remote_copy(
            to, to, send.at[slots[name, "last"]], recv.at[slots[name, "last"]],
            device_id=sibling, device_id_type=MESH,
        )
        pl.when(mine)(copy.start)
        sems.pending.append(lambda: pl.when(mine)(copy.wait_send))

    def last_done(name):
        @pl.when(jnp.logical_not(mine))
        def _():
            arrived(sems, final[name], slots[name, "last"])

    batch, origin = lax.div(c, 2), lax.rem(c, 2)
    feat = outs.shape[2]

    def back_start(src, dst, base):
        for step in range(4):
            cc = lax.rem(c + step, 4)
            part = src.at[pl.ds(aligned(cc * feat, 128), feat), :]
            if step == 0:
                local = origin == k

                @pl.when(local)
                def _():
                    pltpu.make_async_copy(part, dst.at[batch, k], recv.at[base + 2 * batch + k]).start()

                copy = pltpu.make_async_remote_copy(
                    part, dst.at[batch, k], send.at[base + step], recv.at[base + 2 * batch + k],
                    device_id=sibling, device_id_type=MESH,
                )
                away = jnp.logical_not(local)
                pl.when(away)(copy.start)
                sems.pending.append(lambda copy=copy, away=away: pl.when(away)(copy.wait_send))
            else:
                remote(
                    FarSems(sems, base + step, base + 2 * batch + k), part, dst.at[batch, k], None, (origin, z, cc)
                )

    def back_done(dst, base):
        for b in range(2):
            for core in range(2):
                arrived(sems, dst.at[b, core], base + 2 * b + core)

    count = grad_att.shape[0]
    span = grad_o.shape[1]
    own = pl.ds(aligned(k * count, count), count)
    d_slot = sems.take(2)
    remote(sems, grad_att.at[:, pl.ds(aligned((1 - k) * span, 128), span)], grad_o.at[own, :], d_slot, sibling)
    pltpu.make_async_copy(
        grad_att.at[:, pl.ds(aligned(k * span, 128), span)], grad_o.at[own, :], recv.at[d_slot + 1]
    ).start()
    for name in ("u", "d", "o"):
        sib_start(name)
    b_slot = sems.take(4)
    back_start(out_t, outs, b_slot)
    kcat[:, 0:512] = table[...]
    sum_a[...] = jnp.zeros_like(sum_a)
    sum_b[...] = jnp.zeros_like(sum_b)
    arrived(sems, grad_o.at[own, :], d_slot + 1)
    arrived(sems, grad_o.at[own, :], d_slot)
    for h in range(2 * half):
        head_grad[h] = grad_o[:, h * 64 : h * 64 + 64]

    seq = xt.shape[1]
    slot_len = seq // 2
    block = 256

    def attend_back(h, hb, low_row, keys_seen):
        here = pl.ds(aligned(low_row, block), block)
        grad = head_grad[h, here, :]
        low = probs[h, here, 0:keys_seen]
        inner = jnp.sum(grad.astype(F32) * heads_out[h, here, :], axis=1, keepdims=True)
        grad_prob = nt(grad, vals[h, 0:keys_seen, :])
        grad_score = (low.astype(F32) * (grad_prob - inner)).astype(BF16)
        turned_v[:, 0:keys_seen] += tn(grad, low)
        turned_k[:, 0:keys_seen] += tn(qcat[h, here, 512:576], grad_score)
        got = nn(grad_score, kcat[0:keys_seen, :])
        cosine = table[here, 0:256].astype(F32)
        sine = table[here, 256:512].astype(F32)
        first, second = got[:, 0:256], got[:, 256:512]
        angle = jnp.concatenate([first * sine - second * cosine, first * cosine + second * sine], axis=1).astype(BF16)
        return here, got[:, 512:640], angle

    def one_head(i, hb):
        h = 2 * i + hb
        kcat[:, 512:640] = keys[h]
        turned_k[...] = jnp.zeros_like(turned_k)
        turned_v[...] = jnp.zeros_like(turned_v)
        turned_p[...] = jnp.zeros_like(turned_p)
        weight = wp_half[i, :, hb * 64 : hb * 64 + 64]

        def step(low_row, keys_seen):
            here, grad_u, angle = attend_back(h, hb, low_row, keys_seen)
            grad_v = nn(angle, weight)
            turned_p[...] += tn(qv[h, here, :], angle)
            grad_u = grad_u[:, 0:64]
            sum_a[h : h + 1, 0:64] += jnp.sum(grad_u, axis=0, keepdims=True) * 0.125
            sum_b[h : h + 1, 0:64] += jnp.sum(grad_v, axis=0, keepdims=True) * 0.125
            both = jnp.concatenate([(grad_u + grad_v) * 0.125, jnp.zeros((block, 64), F32)], axis=1)
            turned[i, hb * 192 : hb * 192 + 64, here] = jnp.transpose(both)[0:64].astype(BF16)

        @pl.loop(0, slot_len // block)
        def _(t):
            step(t * block, slot_len)

        @pl.loop(0, slot_len // block)
        def _(t):
            step(slot_len + t * block, seq)

        turned[i, hb * 192 + 64 : hb * 192 + 128, :] = turned_k[...].astype(BF16)
        turned[i, hb * 192 + 128 : hb * 192 + 192, :] = turned_v[...].astype(BF16)
        return turned_p[...]

    for i in range(half):
        first = one_head(i, 0)
        if i == 0:
            for name in ("u", "d", "o"):
                sib_done(name)
                for j in range(half):
                    one_start(name, j)
        else:
            for name in ("u", "d", "o"):
                for j in range(half):
                    two_done(name, j)
        second = one_head(i, 1)
        hs_p[i] = jnp.transpose(jnp.concatenate([first, second], axis=0)).astype(BF16).reshape(hs_p.shape[1:])
        hs_q[i] = nt(normed_t[...], turned[i]).astype(BF16).reshape(hs_q.shape[1:])
        if i == 0:
            for name in ("u", "d", "o"):
                for j in range(half):
                    one_done(name, j)
        one_start("q", i)
        one_start("p", i)
        part = nn(wq_half[i], turned[i])
        if i == 0:
            one_t[...] = part
        else:
            one_t[...] += part

    other = pl.ds(aligned((1 - k) * count, count), count)
    one_low[...] = one_t[:, other].astype(BF16)
    e_slot = sems.take(1)
    remote(sems, one_low, one_got, e_slot, sibling)
    for i in range(half):
        one_done("q", i)
        one_done("p", i)
    arrived(sems, one_got, e_slot)
    columns = [tall(params_col[cc]) for cc in range(cols)]
    gain = jnp.concatenate([col[:, 0:1] for col in columns], axis=0)
    width = xt.shape[0]
    one = one_t[:, own] + one_got[...].astype(F32)
    x = xt[:, own].astype(F32)
    mean = jnp.sum(x, axis=0, keepdims=True) * (1.0 / width)
    square = jnp.sum(x * x, axis=0, keepdims=True) * (1.0 / width)
    inverse = lax.rsqrt(square - mean * mean + norm_epsilon)
    scaled = (x - mean) * inverse
    shifted = one * gain
    first = jnp.sum(shifted, axis=0, keepdims=True) * (1.0 / width)
    second = jnp.sum(shifted * scaled, axis=0, keepdims=True) * (1.0 / width)
    grad_x[...] = (grad_mid_t[...] + inverse * (shifted - first - scaled * second)).astype(BF16)
    x_slot = sems.take(4)
    back_start(grad_x, grads, x_slot)
    gain_sum = jnp.sum(one * scaled, axis=1, keepdims=True)
    bias_sum = jnp.sum(one, axis=1, keepdims=True)
    lane = lax.broadcasted_iota(jnp.int32, (width, 128), 1)
    pair = jnp.where(lane == 0, gain_sum, jnp.where(lane == 1, bias_sum, 0.0))
    pair = jnp.transpose(pair)[0:8]
    all_small[0] = small[...]
    all_small[0, 0:2, :] = pair[0:2]

    def spread(sums):
        row = jnp.concatenate([sums[h : h + 1, 0:64] for h in range(2 * half)], axis=1)
        none = jnp.zeros_like(row)
        first_half = jnp.concatenate([row, none], axis=1)
        second_half = jnp.concatenate([none, row], axis=1)
        return jnp.where(k == 0, first_half, second_half)

    all_small[0, 9:10, :] = spread(sum_a[...])
    all_small[0, 10:11, :] = spread(sum_b[...])
    t_slot = sems.take(3)
    v_slot = sems.take(2 * rows)
    remote(sems, all_small.at[0], got_small.at[0], t_slot, sibling)
    for i in range(half):
        two_done("q", i)
        two_done("p", i)
    arrived(sems, got_small.at[0], t_slot)
    all_small[1] = all_small[0] + got_small[0]
    remote(sems, all_small.at[1], got_small.at[1], t_slot + 1, (k, z, near))
    for name in ("u", "d", "o"):
        z_done(name)
    arrived(sems, got_small.at[1], t_slot + 1)
    all_small[2] = all_small[1] + got_small[1]
    remote(sems, all_small.at[2], got_small.at[2], t_slot + 2, (k, z, far))
    arrived(sems, got_small.at[2], t_slot + 2)
    all_small[3] = all_small[2] + got_small[2]
    for step in range(1, rows):
        peer = lax.rem(z + step, rows)
        remote(FarSems(sems, v_slot + rows + step, v_slot + z), all_small.at[3], got_z.at[z], None, (k, peer, c))
    z_done("q")
    z_done("p")
    total = all_small[3]
    for step in range(1, rows):
        source = lax.rem(z + step, rows)
        arrived(sems, got_z.at[source], v_slot + source)
        total = total + got_z[source]
    f_small[...] = total
    back_done(outs, b_slot)
    back_done(grads, x_slot)
    for name in ("u", "d", "o", "q", "p"):
        last_done(name)
    drain(sems)


class FarSems:
    def __init__(self, sems, send_slot, recv_slot):
        self.send = OneSem(sems.send, send_slot)
        self.recv = OneSem(sems.recv, recv_slot)
        self.pending = sems.pending


class OneSem:
    def __init__(self, ref, slot):
        self.ref, self.slot = ref, slot

    @property
    def at(self):
        return self

    def __getitem__(self, _):
        return self.ref.at[self.slot]


def final_kernel(
    outs, grads, f_q, f_p, f_o, f_u, f_d, f_small,
    output, grad_tokens, g1, b1, q_w, c_b, p_b, p_w, o_w, g2, b2, u_w, u_b, d_w, d_b,
):
    k, z, c, _, _ = place()
    for b in range(2):
        for core in range(2):
            size = outs.shape[3]
            output[b, :, core * size : core * size + size] = outs[b, core].astype(F32)
            grad_tokens[b, :, core * size : core * size + size] = grads[b, core].astype(F32)
    for ref, source in ((q_w, f_q), (p_w, f_p), (o_w, f_o), (u_w, f_u), (d_w, f_d)):
        size = ref.shape[1]

        @pl.when(k == 0)
        def _(ref=ref, source=source, size=size):
            ref[...] = source[:, 0:size]

        @pl.when(k == 1)
        def _(ref=ref, source=source, size=size):
            ref[...] = source[:, size : 2 * size]

    width = f_small.shape[1]
    chip = z * 4 + c
    share = g1.shape[1]
    first = pltpu.roll(f_small[0:8, :], lax.rem(width - (chip * 2 + k) * share, width), 1)
    for row, ref in ((0, g1), (1, b1), (2, g2), (3, b2), (4, d_b)):
        ref[...] = first[row : row + 1, 0:share]
    share = u_b.shape[1]
    line = f_small[pl.ds(5 + z, 1), :]
    line = jnp.broadcast_to(line, (8, width))
    u_b[...] = pltpu.roll(line, lax.rem(width - (c * 2 + k) * share, width), 1)[0:1, 0:share]
    heads, share = c_b.shape
    third = pltpu.roll(f_small[8:16, :], lax.rem(2 * width - heads * 64 * z - (c * 2 + k) * share, width), 1)
    for h in range(heads):
        c_b[h : h + 1, :] = third[1:2, h * 64 : h * 64 + share]
        p_b[h : h + 1, :] = third[2:3, h * 64 : h * 64 + share]


def position_table(seq_len, feature_count):
    positions = np.arange(seq_len, dtype=np.float64)
    exponent = -np.arange(0, feature_count, 2, dtype=np.float64) / feature_count
    angles = positions[:, None] * (10000.0**exponent)[None, :]
    return np.concatenate([np.cos(angles), np.sin(angles)], axis=1).astype(jnp.bfloat16)


def fast_shards(
    tokens, cotangent, piece_starts, ln1_gain, ln1_bias, qkv_weight, content_bias, position_bias, pos_weight,
    out_weight, ln2_gain, ln2_bias, up_weight, up_bias, down_weight, down_bias,
):
    rows, cols = lax.axis_size("row"), lax.axis_size("col")
    half = rows // 2
    micro, feat, seq = tokens.shape
    width = feat * cols
    count = seq // 2
    hidden = up_weight.shape[1]
    heads = content_bias.shape[0] * half
    table = jnp.asarray(position_table(seq, width))
    lines = [v.astype(F32)[None] for v in (ln1_gain, ln1_bias, ln2_gain, ln2_bias, down_bias)]
    small_col = jnp.concatenate(lines + [jnp.zeros((3, feat), F32)], axis=0)
    small_row = jnp.concatenate(
        [up_bias.astype(F32).reshape(-1, 128), content_bias.reshape(1, 128), position_bias.reshape(1, 128), jnp.zeros((2, 128), F32)],
        axis=0,
    )
    flat = jnp.pad(piece_starts.reshape(-1), (0, 4))
    starts = jnp.broadcast_to(flat[:, None], (8, 128))
    vm = pl.BlockSpec(memory_space=pltpu.VMEM)
    anywhere = pl.BlockSpec(memory_space=pl.ANY)
    limit = 64 * 1024 * 1024 - 128 * 1024

    def shape(dims, kind=BF16):
        return jax.ShapeDtypeStruct(dims, kind)

    made = pl.pallas_call(
        forward_kernel,
        name="forward",
        out_shape=(
            shape((count, width)),
            shape((cols, width, 128)),
            shape((rows, width, hidden)),
            shape((cols, rows * hidden, 128)),
            shape((half, width, qkv_weight.shape[1])),
            shape((half, width, pos_weight.shape[1])),
            shape((width, seq)),
            shape((width, count)),
            shape((width, seq)),
            shape((heads, seq, width + 128)),
            shape((heads, seq, 128)),
            shape((heads, seq, 64)),
            shape((heads, seq, 64)),
            shape((heads, seq, seq)),
            shape((heads, seq, 64), F32),
            shape((cols, 8, 128), F32),
            shape((rows, 8, 128), F32),
        ),
        in_specs=[anywhere, anywhere, vm, vm, vm, vm] + [anywhere] * 5,
        out_specs=(vm,) * 17,
        scratch_shapes=[
            pltpu.VMEM((seq, width + 128), BF16),
            pltpu.VMEM((seq, heads * 64), BF16),
            pltpu.VMEM((8, 128), jnp.int32),
            pltpu.SemaphoreType.DMA((200,)),
            pltpu.SemaphoreType.DMA((200,)),
        ],
        compiler_params=pltpu.CompilerParams(collective_id=0, has_side_effects=True, vmem_limit_bytes=limit),
    )(tokens, cotangent, starts, small_col, small_row, table, qkv_weight, pos_weight, out_weight, up_weight, down_weight)
    (att, wo_all, wu_all, wd_all, wq_half, wp_half, xt, ct, normed_t, qcat, keys, vals, qv, probs, heads_out, params_col, params_row) = made
    out_t, grad_mid_t, grad_att, g_up, g_down, g_out, small = pl.pallas_call(
        middle_kernel,
        name="middle",
        out_shape=(
            shape((width, count)),
            shape((width, count), F32),
            shape((count, width)),
            shape(wu_all.shape),
            shape(wd_all.shape),
            shape(wo_all.shape),
            shape((16, width), F32),
        ),
        in_specs=[vm] * 8,
        out_specs=(vm,) * 7,
        scratch_shapes=[
            pltpu.VMEM((count, width), F32),
            pltpu.VMEM((count, width), BF16),
            pltpu.VMEM((count, width), F32),
            pltpu.VMEM((count, 1), F32),
            pltpu.VMEM((count, width), BF16),
            pltpu.VMEM((count, width), F32),
            pltpu.VMEM((count, width), F32),
            pltpu.VMEM((width, count), BF16),
        ],
        compiler_params=pltpu.CompilerParams(vmem_limit_bytes=limit),
    )(att, wo_all, wu_all, wd_all, xt, ct, params_col, params_row)
    q_cols, p_cols = qkv_weight.shape[1], pos_weight.shape[1]
    o_rows, d_rows = out_weight.shape[0], down_weight.shape[0]
    blocks = {
        "q": (feat, q_cols), "p": (feat, p_cols), "o": (o_rows, 128), "u": (feat, hidden), "d": (d_rows, 128),
    }
    names = ("q", "p", "o", "u", "d")
    results = pl.pallas_call(
        backward_kernel,
        name="backward",
        out_shape=(
            shape((micro, 2, feat, count)),
            shape((micro, 2, feat, count)),
        )
        + tuple(shape(blocks[name], F32) for name in names)
        + (shape((16, width), F32),),
        in_specs=[vm] * 19,
        out_specs=(vm,) * 8,
        scratch_shapes=[
            pltpu.VMEM((seq, width + 128), BF16),
            pltpu.VMEM((seq, heads * 64), BF16),
            pltpu.VMEM((heads, seq, 64), BF16),
            pltpu.VMEM((half, q_cols, seq), BF16),
            pltpu.VMEM((64, seq), F32),
            pltpu.VMEM((64, seq), F32),
            pltpu.VMEM((64, width), F32),
            pltpu.VMEM((width, seq), F32),
            pltpu.VMEM((width, count), BF16),
            pltpu.VMEM((width, count), BF16),
            pltpu.VMEM((width, count), BF16),
            pltpu.VMEM((8, 128), F32),
            pltpu.VMEM((8, 128), F32),
            pltpu.VMEM((half, cols) + blocks["q"], BF16),
            pltpu.VMEM((half, cols) + blocks["p"], BF16),
            pltpu.VMEM((cols, half) + blocks["o"], BF16),
            pltpu.VMEM((half, cols) + blocks["u"], BF16),
            pltpu.VMEM((cols, half) + blocks["d"], BF16),
            pltpu.VMEM((cols, half * o_rows, 128), BF16),
            pltpu.VMEM((half, width, hidden), BF16),
            pltpu.VMEM((cols, half * d_rows, 128), BF16),
        ]
        + [pltpu.VMEM((half, 2) + blocks[name], BF16) for name in names]
        + [pltpu.VMEM((half,) + blocks[name], BF16) for name in names]
        + [pltpu.VMEM((rows,) + blocks[name], BF16) for name in names]
        + [
            pltpu.VMEM((4, 16, width), F32),
            pltpu.VMEM((3, 16, width), F32),
            pltpu.VMEM((rows, 16, width), F32),
            pltpu.SemaphoreType.DMA((160,)),
            pltpu.SemaphoreType.DMA((160,)),
        ],
        compiler_params=pltpu.CompilerParams(collective_id=1, has_side_effects=True, vmem_limit_bytes=limit),
    )(
        out_t, grad_mid_t, grad_att, g_up, g_down, g_out, small, params_col, table, wq_half, wp_half, xt, normed_t,
        qcat, keys, vals, qv, probs, heads_out,
    )
    devices = 2 * rows * cols
    vec = shape((1, width // devices), F32)
    bias = shape((content_bias.shape[0], 64 // (2 * cols)), F32)
    done = pl.pallas_call(
        final_kernel,
        name="final",
        out_shape=(
            shape(tokens.shape, F32), shape(tokens.shape, F32), vec, vec,
            shape((feat, q_cols // 2), F32), bias, bias, shape((feat, p_cols // 2), F32), shape((o_rows, 64), F32), vec, vec,
            shape((feat, hidden // 2), F32), shape((1, rows * hidden // devices), F32), shape((d_rows, 64), F32), vec,
        ),
        in_specs=[vm] * 8,
        out_specs=(vm,) * 15,
        compiler_params=pltpu.CompilerParams(vmem_limit_bytes=limit),
    )(*results)
    return tuple(v.reshape(-1) if v.shape[0] == 1 else v for v in done)


def solution(mesh):
    in_specs = (
        P(None, "col", ("dp", "row")),
        P(None, "col", ("dp", "row")),
        P(None, ("dp", "col"), None),
        P("col"),
        P("col"),
        P("col", "row"),
        P("row", None),
        P("row", None),
        P("col", "row"),
        P("row", "col"),
        P("col"),
        P("col"),
        P("col", "row"),
        P("row"),
        P("row", "col"),
        P("col"),
    )
    out_specs = (
        P(None, "col", ("dp", "row")),
        P(None, "col", ("dp", "row")),
        P(("row", "col", "dp")),
        P(("row", "col", "dp")),
        P("col", ("row", "dp")),
        P("row", ("col", "dp")),
        P("row", ("col", "dp")),
        P("col", ("row", "dp")),
        P("row", ("col", "dp")),
        P(("row", "col", "dp")),
        P(("row", "col", "dp")),
        P("col", ("row", "dp")),
        P(("row", "col", "dp")),
        P("row", ("col", "dp")),
        P(("row", "col", "dp")),
    )

    def layer(tokens, *others):
        dp, row, col = mesh.shape["dp"], mesh.shape["row"], mesh.shape["col"]
        one_each = tokens.shape[2] == dp * row * SEQ_LEN and tokens.shape[0] * dp == col
        body = fast_shards if one_each and dp == 2 and row == col == 4 else shards
        part = jax.shard_map(body, mesh=mesh, in_specs=in_specs, out_specs=out_specs, check_vma=False)
        return part(tokens, *others)

    return layer
```

```python
from functools import reduce

import jax
import jax.numpy as jnp
import numpy as np
from jax import lax
from jax.experimental import pallas as pl
from jax.experimental.pallas import tpu as pltpu
from jax.sharding import PartitionSpec as P

D = 512
SEQ_LEN = 1024
PIECE = 256


norm_epsilon = 1e-05
big_negative = -1e30
inv_sqrt_two = 0.7071067811865476
inv_sqrt_tau = 0.3989422804014327


def contract(left_op, right_op, flipped):
    if flipped:
        return lax.dot_general(
            left_op, right_op, (((1,), (1,)), ((), ())), preferred_element_type=jnp.float32
        )
    return jnp.dot(left_op, right_op, preferred_element_type=jnp.float32)


def outer_sum(left_op, right_op):
    return lax.dot_general(
        left_op, right_op, (((0,), (0,)), ((), ())), preferred_element_type=jnp.float32
    )


def gather_rows(values):
    return lax.all_gather(values, "row", axis=0, tiled=True)


def gather_cols(values):
    return lax.all_gather(values, "col", axis=0, tiled=True)


def sum_over_cols(gathered, weight, flipped):
    share_rows = gathered.shape[0] // lax.axis_size("col")

    def partial_term(offset, amount):
        return contract(gathered, weight, flipped)

    return lax.psum_scatter(
        partial_term(jnp.int32(0), lax.axis_size("col") * share_rows),
        "col",
        scatter_dimension=0,
        tiled=True,
    )


def sum_over_rows(gathered, weight, flipped):
    share_rows = gathered.shape[0] // lax.axis_size("row")

    def partial_term(offset, amount):
        return contract(gathered, weight, flipped)

    return lax.psum_scatter(
        partial_term(jnp.int32(0), lax.axis_size("row") * share_rows),
        "row",
        scatter_dimension=0,
        tiled=True,
    )


def feature_sums(first_sum, second_sum):
    return lax.psum((first_sum, second_sum), "col")


def normalize(values, gain, bias):
    feature_count = values.shape[1] * lax.axis_size("col")
    total_row, square_row = feature_sums(jnp.sum(values, axis=1), jnp.sum(values * values, axis=1))
    mean_row = total_row / feature_count
    inverse = lax.rsqrt(square_row / feature_count - mean_row * mean_row + norm_epsilon)
    scaled = (values - mean_row[:, None]) * inverse[:, None]
    return (scaled * gain + bias, scaled, inverse)


def normalize_back(grad_in, scaled, inverse, gain):
    feature_count = grad_in.shape[1] * lax.axis_size("col")
    shifted = grad_in * gain
    first_sum, second_sum = feature_sums(
        jnp.sum(shifted, axis=1), jnp.sum(shifted * scaled, axis=1)
    )
    back_rows = inverse[:, None] * (
        shifted - first_sum[:, None] / feature_count - scaled * second_sum[:, None] / feature_count
    )
    return (back_rows, jnp.sum(grad_in * scaled, axis=0), jnp.sum(grad_in, axis=0))


def gelu_exact(values):
    return 0.5 * values * (1.0 + jax.scipy.special.erf(values * inv_sqrt_two))


def gelu_slope(values):
    return (
        0.5 * (1.0 + jax.scipy.special.erf(values * inv_sqrt_two))
        + values * jnp.exp(-0.5 * values * values) * inv_sqrt_tau
    )


def sinusoid_table(seq_len, feature_count):
    offsets = jnp.arange(2 * seq_len - 1, dtype=jnp.float32) - (seq_len - 1)
    frequency = 10000.0 ** (-jnp.arange(0, feature_count, 2, dtype=jnp.float32) / feature_count)
    angles = offsets[:, None] * frequency[None, :]
    return jnp.concatenate([jnp.sin(angles), jnp.cos(angles)], axis=1).astype(jnp.bfloat16)


def piece_labels(positions, starts, piece_len):
    inside = (positions[:, None] >= starts[None, :]) & (
        positions[:, None] < starts[None, :] + piece_len
    )
    numbers = jnp.arange(1, starts.shape[0] + 1, dtype=jnp.int32)
    return jnp.sum(jnp.where(inside, numbers[None, :], 0), axis=1) - 1


def block_mask(offset, block_len, labels):
    positions = jnp.arange(labels.shape[0], dtype=jnp.int32)
    row_pos = offset + jnp.arange(block_len, dtype=jnp.int32)
    row_labels = lax.dynamic_slice_in_dim(labels, offset, block_len, 0)
    same_piece = (row_labels[:, None] == labels[None, :]) & (row_labels[:, None] >= 0)
    return (positions[None, :] <= row_pos[:, None]) | same_piece


def skew_rows(unshifted_reversed_scores, key_total):
    head_total, row_total, rel_span = unshifted_reversed_scores.shape
    flattened = unshifted_reversed_scores.reshape(head_total, row_total * rel_span)
    window = lax.slice_in_dim(
        flattened, row_total - 1, row_total - 1 + row_total * (rel_span - 1), axis=1
    )
    return window.reshape(head_total, row_total, rel_span - 1)[:, :, :key_total]


def unskew_rows(grad_pos, rel_span):
    head_total, row_total, key_total = grad_pos.shape
    padded = jnp.pad(grad_pos, ((0, 0), (0, 0), (0, rel_span - 1 - key_total)))
    flattened = padded.reshape(head_total, row_total * (rel_span - 1))
    flattened = jnp.pad(flattened, ((0, 0), (row_total - 1, 1)))
    return flattened.reshape(head_total, row_total, rel_span)


def block_scores(qu_block, query_position_block, key_rows, relative_block, allowed):
    content = jnp.einsum("ihd,jhd->hij", qu_block, key_rows, preferred_element_type=jnp.float32)
    unshifted_reversed_scores = jnp.einsum(
        "sgw,egw->gse", query_position_block, relative_block, preferred_element_type=jnp.float32
    )
    position = skew_rows(unshifted_reversed_scores, key_rows.shape[0])
    return jnp.where(allowed[None], content + position, big_negative)


def attention_forward(query_u, query_v, key_rows, value_rows, relative_rev, labels):
    seq_len, head_count, head_dim = key_rows.shape
    block_len = min(512, seq_len)
    rel_span = block_len + seq_len - 1
    offsets = jnp.arange(seq_len // block_len, dtype=jnp.int32) * block_len

    def attend(offset):
        qu_block = lax.dynamic_slice_in_dim(query_u, offset, block_len, 0)
        query_position_block = lax.dynamic_slice_in_dim(query_v, offset, block_len, 0)
        relative_block = lax.dynamic_slice_in_dim(
            relative_rev, seq_len - block_len - offset, rel_span, 0
        )
        scores = block_scores(
            qu_block,
            query_position_block,
            key_rows,
            relative_block,
            block_mask(offset, block_len, labels),
        )
        row_max = jnp.max(scores, axis=2, keepdims=True)
        log_total = row_max + jnp.log(jnp.sum(jnp.exp(scores - row_max), axis=2, keepdims=True))
        attn_prob = jnp.exp(scores - log_total).astype(jnp.bfloat16)
        result = jnp.einsum(
            "hij,jhd->ihd", attn_prob, value_rows, preferred_element_type=jnp.float32
        )
        return (result, log_total[:, :, 0])

    results, log_totals = lax.map(attend, offsets)
    return (results.reshape(seq_len, head_count * head_dim), log_totals)


def attention_backward(
    query_u, query_v, key_rows, value_rows, relative_rev, labels, log_totals, grad_att
):
    seq_len, head_count, head_dim = key_rows.shape
    block_len = min(512, seq_len)
    rel_span = block_len + seq_len - 1
    offsets = jnp.arange(seq_len // block_len, dtype=jnp.int32) * block_len

    def back_block(carried, sliced):
        grad_keys, grad_values, grad_rel = carried
        offset, log_total = sliced
        rel_start = seq_len - block_len - offset
        qu_block = lax.dynamic_slice_in_dim(query_u, offset, block_len, 0)
        query_position_block = lax.dynamic_slice_in_dim(query_v, offset, block_len, 0)
        relative_block = lax.dynamic_slice_in_dim(relative_rev, rel_start, rel_span, 0)
        scores = block_scores(
            qu_block,
            query_position_block,
            key_rows,
            relative_block,
            block_mask(offset, block_len, labels),
        )
        attn_prob = jnp.exp(scores - log_total[:, :, None])
        low_prob = attn_prob.astype(jnp.bfloat16)
        grad_block = lax.dynamic_slice_in_dim(grad_att, offset, block_len, 0)
        grad_prob = jnp.einsum(
            "ihd,jhd->hij", grad_block, value_rows, preferred_element_type=jnp.float32
        )
        row_inner = jnp.sum(attn_prob * grad_prob, axis=2, keepdims=True)
        grad_scores = (attn_prob * (grad_prob - row_inner)).astype(jnp.bfloat16)
        grad_values = grad_values + jnp.einsum(
            "hij,ihd->jhd", low_prob, grad_block, preferred_element_type=jnp.float32
        )
        grad_keys = grad_keys + jnp.einsum(
            "hij,ihd->jhd", grad_scores, qu_block, preferred_element_type=jnp.float32
        )
        grad_qu = jnp.einsum(
            "hij,jhd->ihd", grad_scores, key_rows, preferred_element_type=jnp.float32
        )
        gradient_unshifted = unskew_rows(grad_scores, rel_span)
        grad_qv = jnp.einsum(
            "qjp,pqr->jqr", gradient_unshifted, relative_block, preferred_element_type=jnp.float32
        )
        rel_part = jnp.einsum(
            "nfx,fne->xne",
            gradient_unshifted,
            query_position_block,
            preferred_element_type=jnp.float32,
        )
        current = lax.dynamic_slice_in_dim(grad_rel, rel_start, rel_span, 0)
        grad_rel = lax.dynamic_update_slice_in_dim(grad_rel, current + rel_part, rel_start, 0)
        return ((grad_keys, grad_values, grad_rel), (grad_qu, grad_qv))

    zero_rows = jnp.zeros((seq_len, head_count, head_dim), jnp.float32)
    zero_rel = jnp.zeros((2 * seq_len - 1, head_count, head_dim), jnp.float32)
    carried, stacked = lax.scan(back_block, (zero_rows, zero_rows, zero_rel), (offsets, log_totals))
    grad_keys, grad_values, grad_rel = carried
    grad_qu = stacked[0].reshape(seq_len, head_count, head_dim)
    grad_qv = stacked[1].reshape(seq_len, head_count, head_dim)
    return (grad_qu, grad_qv, grad_keys, grad_values, grad_rel)


def heads_pass(packed, content_bias, position_bias, relative_rev, labels):
    seq_len = packed.shape[0]
    head_count, head_dim = content_bias.shape
    scaling = head_dim ** (-0.5)
    packed = packed.reshape(seq_len, head_count, 3, head_dim)
    queries = packed[:, :, 0].astype(jnp.float32)
    key_rows = packed[:, :, 1]
    value_rows = packed[:, :, 2]
    query_u = ((queries + content_bias) * scaling).astype(jnp.bfloat16)
    query_v = ((queries + position_bias) * scaling).astype(jnp.bfloat16)
    attended, log_totals = attention_forward(
        query_u, query_v, key_rows, value_rows, relative_rev, labels
    )
    return (attended.astype(jnp.bfloat16), (query_u, query_v, key_rows, value_rows, log_totals))


def heads_back(kept, relative_rev, labels, grad_att):
    query_u, query_v, key_rows, value_rows, log_totals = kept
    seq_len, head_count, head_dim = key_rows.shape
    scaling = head_dim ** (-0.5)
    grad_att = grad_att.reshape(seq_len, head_count, head_dim)
    grad_qu, grad_qv, grad_keys, grad_values, grad_rel = attention_backward(
        query_u, query_v, key_rows, value_rows, relative_rev, labels, log_totals, grad_att
    )
    cbias_part = jnp.sum(grad_qu, axis=0) * scaling
    pbias_part = jnp.sum(grad_qv, axis=0) * scaling
    grad_query = (grad_qu + grad_qv) * scaling
    grad_packed = jnp.stack([grad_query, grad_keys, grad_values], axis=2)
    grad_packed = grad_packed.reshape(seq_len, head_count * 3 * head_dim).astype(jnp.bfloat16)
    rel_low = grad_rel.reshape(2 * seq_len - 1, head_count * head_dim).astype(jnp.bfloat16)
    return (grad_packed, rel_low, cbias_part, pbias_part)


def grid_micro(seq_feats, cot_feats, params, shared):
    (
        ln1_gain,
        ln1_bias,
        qkv_weight,
        content_bias,
        position_bias,
        out_weight,
        ln2_gain,
        ln2_bias,
        up_weight,
        up_bias,
        down_weight,
        down_bias,
    ) = params
    relative_rev, table_rev, labels = shared
    seq_in = seq_feats.astype(jnp.float32).T
    normed_one, scaled_one, inverse_one = normalize(seq_in, ln1_gain, ln1_bias)
    gathered_one = gather_rows(normed_one.astype(jnp.bfloat16))
    packed = sum_over_cols(gathered_one, qkv_weight, False).astype(jnp.bfloat16)
    attended, kept = heads_pass(packed, content_bias, position_bias, relative_rev, labels)
    att_gathered = gather_cols(attended)
    middle = seq_in + sum_over_rows(att_gathered, out_weight, False)
    normed_two, scaled_two, inverse_two = normalize(middle, ln2_gain, ln2_bias)
    gathered_two = gather_rows(normed_two.astype(jnp.bfloat16))
    pre_act = sum_over_cols(gathered_two, up_weight, False) + up_bias
    activated = gelu_exact(pre_act).astype(jnp.bfloat16)
    act_gathered = gather_cols(activated)
    output = middle + sum_over_rows(act_gathered, down_weight, False) + down_bias
    grad_final = cot_feats.T
    gout = grad_final.astype(jnp.float32)
    final_gathered = gather_rows(grad_final)
    grad_act = sum_over_cols(final_gathered, down_weight, True)
    grad_pre = (grad_act * gelu_slope(pre_act)).astype(jnp.bfloat16)
    pre_gathered = gather_cols(grad_pre)
    grad_two = sum_over_rows(pre_gathered, up_weight, True)
    backward_second, gain_two, bias_two = normalize_back(
        grad_two, scaled_two, inverse_two, ln2_gain
    )
    grad_middle = gout + backward_second
    grad_branch = grad_middle.astype(jnp.bfloat16)
    branch_gathered = gather_rows(grad_branch)
    grad_att = sum_over_cols(branch_gathered, out_weight, True).astype(jnp.bfloat16)
    grad_packed, rel_low, cbias_part, pbias_part = heads_back(kept, relative_rev, labels, grad_att)
    packed_gathered = gather_cols(grad_packed)
    grad_one = sum_over_rows(packed_gathered, qkv_weight, True)
    back_one, gain_one, bias_one = normalize_back(grad_one, scaled_one, inverse_one, ln1_gain)
    grad_in = grad_middle + back_one
    collected = (
        outer_sum(gathered_one, packed_gathered),
        outer_sum(att_gathered, branch_gathered),
        outer_sum(gathered_two, pre_gathered),
        outer_sum(act_gathered, final_gathered),
        outer_sum(table_rev, rel_low),
        cbias_part,
        pbias_part,
        jnp.sum(grad_pre.astype(jnp.float32), axis=0),
        gain_one,
        bias_one,
        gain_two,
        bias_two,
        jnp.sum(gout, axis=0),
    )
    return (output.T, grad_in.T, collected)


def embed_heads(part, row_pick, col_count):
    head_count = part.shape[0]
    spread = jnp.transpose(part.reshape(head_count, col_count, -1), (1, 0, 2))
    placed = jnp.where(row_pick[:, None, None, None], spread[None], 0.0)
    return placed.reshape(row_pick.shape[0] * col_count, head_count, -1)


def shards(
    tokens,
    cotangent,
    piece_starts,
    ln1_gain,
    ln1_bias,
    qkv_weight,
    content_bias,
    position_bias,
    pos_weight,
    out_weight,
    ln2_gain,
    ln2_bias,
    up_weight,
    up_bias,
    down_weight,
    down_bias,
):
    micro_count = tokens.shape[0]
    row_count = lax.axis_size("row")
    col_count = lax.axis_size("col")
    grid_cells = row_count * col_count
    head_count, head_dim = content_bias.shape
    pos_cols = lax.all_gather(pos_weight, "col", axis=0, tiled=True)
    table_rev = sinusoid_table(SEQ_LEN, D)[::-1]
    relative_rev = jnp.dot(table_rev, pos_cols, preferred_element_type=jnp.float32).astype(
        jnp.bfloat16
    )
    relative_rev = relative_rev.reshape(2 * SEQ_LEN - 1, head_count, head_dim)
    positions = jnp.arange(SEQ_LEN, dtype=jnp.int32)
    params = (
        ln1_gain,
        ln1_bias,
        qkv_weight,
        content_bias,
        position_bias,
        out_weight,
        ln2_gain,
        ln2_bias,
        up_weight,
        up_bias,
        down_weight,
        down_bias,
    )
    outputs, grad_inputs, part_lists = ([], [], [])
    for micro_idx in range(micro_count):
        labels = piece_labels(positions, piece_starts[micro_idx, 0], PIECE)
        out_feats, grad_feats, collected = grid_micro(
            tokens[micro_idx], cotangent[micro_idx], params, (relative_rev, table_rev, labels)
        )
        outputs.append(out_feats)
        grad_inputs.append(grad_feats)
        part_lists.append(collected)
    totals = [
        reduce(jnp.add, [collected[member] for collected in part_lists]) for member in range(13)
    ]
    (
        acc_qkv,
        acc_out,
        acc_up,
        acc_down,
        acc_pos,
        acc_cbias,
        acc_pbias,
        acc_ubias,
        acc_g1,
        acc_b1,
        acc_g2,
        acc_b2,
        acc_db,
    ) = totals
    row_pick = jnp.arange(row_count, dtype=jnp.int32) == lax.axis_index("row")
    pos_term = jnp.where(row_pick[:, None, None], acc_pos[None], 0.0).reshape(
        row_count * acc_pos.shape[0], -1
    )
    cbias_term = embed_heads(acc_cbias, row_pick, col_count)
    pbias_term = embed_heads(acc_pbias, row_pick, col_count)
    col_pick = jnp.arange(col_count, dtype=jnp.int32) == lax.axis_index("col")
    ubias_term = jnp.where(row_pick[:, None], acc_ubias[None], 0.0).reshape(grid_cells, -1)
    norm_terms = [
        jnp.where(col_pick[:, None], vector[None], 0.0).reshape(grid_cells, -1)
        for vector in (acc_g1, acc_b1, acc_g2, acc_b2, acc_db)
    ]
    sum_pos, sum_cbias, sum_pbias, sum_ubias, sum_g1, sum_b1, sum_g2, second_bias_total, sum_db = (
        lax.psum_scatter(pos_term, ("row", "col"), scatter_dimension=0, tiled=True),
        lax.psum_scatter(cbias_term, ("row", "col"), scatter_dimension=0, tiled=True),
        lax.psum_scatter(pbias_term, ("row", "col"), scatter_dimension=0, tiled=True),
        lax.psum_scatter(ubias_term, ("row", "col"), scatter_dimension=0, tiled=True),
        lax.psum_scatter(norm_terms[0], ("row", "col"), scatter_dimension=0, tiled=True),
        lax.psum_scatter(norm_terms[1], ("row", "col"), scatter_dimension=0, tiled=True),
        lax.psum_scatter(norm_terms[2], ("row", "col"), scatter_dimension=0, tiled=True),
        lax.psum_scatter(norm_terms[3], ("row", "col"), scatter_dimension=0, tiled=True),
        lax.psum_scatter(norm_terms[4], ("row", "col"), scatter_dimension=0, tiled=True),
    )
    sum_qkv, sum_out, sum_up, sum_down = (acc_qkv, acc_out, acc_up, acc_down)
    summed = (
        lax.psum_scatter(
            sum_qkv.astype(jnp.bfloat16), "dp", scatter_dimension=1, tiled=True
        ).astype(jnp.float32),
        lax.psum_scatter(
            sum_out.astype(jnp.bfloat16), "dp", scatter_dimension=1, tiled=True
        ).astype(jnp.float32),
        lax.psum_scatter(sum_up.astype(jnp.bfloat16), "dp", scatter_dimension=1, tiled=True).astype(
            jnp.float32
        ),
        lax.psum_scatter(
            sum_down.astype(jnp.bfloat16), "dp", scatter_dimension=1, tiled=True
        ).astype(jnp.float32),
        lax.psum_scatter(
            sum_pos.astype(jnp.bfloat16), "dp", scatter_dimension=1, tiled=True
        ).astype(jnp.float32),
        lax.psum_scatter(
            sum_cbias.astype(jnp.bfloat16), "dp", scatter_dimension=2, tiled=True
        ).astype(jnp.float32),
        lax.psum_scatter(
            sum_pbias.astype(jnp.bfloat16), "dp", scatter_dimension=2, tiled=True
        ).astype(jnp.float32),
        lax.psum_scatter(
            sum_ubias.astype(jnp.bfloat16), "dp", scatter_dimension=1, tiled=True
        ).astype(jnp.float32),
        lax.psum_scatter(sum_g1.astype(jnp.bfloat16), "dp", scatter_dimension=1, tiled=True).astype(
            jnp.float32
        ),
        lax.psum_scatter(sum_b1.astype(jnp.bfloat16), "dp", scatter_dimension=1, tiled=True).astype(
            jnp.float32
        ),
        lax.psum_scatter(sum_g2.astype(jnp.bfloat16), "dp", scatter_dimension=1, tiled=True).astype(
            jnp.float32
        ),
        lax.psum_scatter(
            second_bias_total.astype(jnp.bfloat16), "dp", scatter_dimension=1, tiled=True
        ).astype(jnp.float32),
        lax.psum_scatter(sum_db.astype(jnp.bfloat16), "dp", scatter_dimension=1, tiled=True).astype(
            jnp.float32
        ),
    )
    (
        grad_qkv_w,
        grad_out_w,
        grad_up_w,
        grad_down_w,
        grad_pos_w,
        grad_cbias,
        grad_pbias,
        grad_ubias,
        grad_g1,
        grad_b1,
        grad_g2,
        grad_b2,
        grad_dbias,
    ) = summed
    output_rows = jnp.stack(outputs, axis=0)
    grad_rows = jnp.stack(grad_inputs, axis=0)
    return (
        output_rows,
        grad_rows,
        grad_g1.reshape(-1),
        grad_b1.reshape(-1),
        grad_qkv_w,
        grad_cbias.reshape(head_count, -1),
        grad_pbias.reshape(head_count, -1),
        grad_pos_w,
        grad_out_w,
        grad_g2.reshape(-1),
        grad_b2.reshape(-1),
        grad_up_w,
        grad_ubias.reshape(-1),
        grad_down_w,
        grad_dbias.reshape(-1),
    )


MESH = pl.DeviceIdType.MESH
F32 = jnp.float32
BF16 = jnp.bfloat16


def aligned(index, size):
    return index if isinstance(index, int) else pl.multiple_of(index, size)


def nt(a, b):
    return lax.dot_general(a, b, (((1,), (1,)), ((), ())), preferred_element_type=F32)


def nn(a, b):
    return lax.dot_general(a, b, (((1,), (0,)), ((), ())), preferred_element_type=F32)


def tn(a, b):
    return lax.dot_general(a, b, (((0,), (0,)), ((), ())), preferred_element_type=F32)


def place():
    k, z, c = lax.axis_index("dp"), lax.axis_index("row"), lax.axis_index("col")
    cx = c + 1 - 2 * lax.rem(c, 2)
    cy = lax.rem(c + 2, 4)
    near = (1 - k) * cx + k * cy
    far = k * cx + (1 - k) * cy
    return k, z, c, near, far


def enter(rows):
    k, z, c, _, _ = place()
    barrier = pltpu.get_barrier_semaphore()
    peers = [(1 - k, z, c)]
    for step in range(1, rows):
        peers.append((k, lax.rem(z + step, rows), c))
    for step in range(1, 4):
        for core in range(2):
            peers.append((0 * k + core, z, lax.rem(c + step, 4)))
    for peer in peers:
        pl.semaphore_signal(barrier, inc=1, device_id=peer, device_id_type=MESH)
    pl.semaphore_wait(barrier, len(peers))


class Copies:
    def __init__(self, send, recv):
        self.send, self.recv, self.next = send, recv, 0
        self.pending = {}

    def take(self, count=1):
        first = self.next
        self.next += count
        return first

    def push(self, send_slot, build, when=None):
        def copy():
            src, dst, recv_slot, peer = build()
            return pltpu.make_async_remote_copy(
                src, dst, self.send.at[send_slot], self.recv.at[recv_slot], device_id=peer, device_id_type=MESH
            )

        if when is None:
            copy().start()
        else:
            pl.when(when())(lambda: copy().start())
        self.pending[send_slot] = (copy, when)

    def keep(self, src, dst, slot, when=None):
        def go():
            pltpu.make_async_copy(src(), dst(), self.recv.at[slot]).start()

        if when is None:
            go()
        else:
            pl.when(when())(go)

    def arrived(self, dst, slot):
        pltpu.make_async_copy(dst, dst, self.recv.at[slot]).wait()

    def drain(self):
        for copy, when in self.pending.values():
            if when is None:
                copy().wait_send()
            else:
                pl.when(when())(lambda copy=copy: copy().wait_send())


def tall(row):
    padded = jnp.concatenate([row, jnp.zeros((120, 128), F32)], axis=0)
    return jnp.transpose(padded)


def erf_parts(values):
    erf = lax.erf(values * inv_sqrt_two)
    return 0.5 * (1.0 + erf)


def layer_kernel(
    tok, cot, starts, packed, cbias, pbias, table, wq, wp, wo, wu, wd,
    outs, grads, f_q, f_p, f_o, f_u, f_d, f_small,
    att, wo_all, wu_all, wd_all, wq_half, wp_half, wp_head, xt, ct, normed_t, qcat, keys, vals, probs_a, probs_b, heads_out,
    params_col, params_row, cb_all, pb_all, kcat, own_att, starts_got,
    mid, norm, hat, inv, gout, acc_out, acc_two, tall_norm, out_t, grad_mid_t, grad_att, g_up, g_down, g_out, small,
    grad_o, head_grad, turned, turned_k, turned_v, turned_p, one_t, one_low, one_got, grad_x, sums,
    hs_q, hs_p, hs_o, hs_u, hs_d, r0_o, r0_u, r0_d,
    r1_q, r1_p, r1_o, r1_u, r1_d, r2_q, r2_p, r2_o, r2_u, r2_d, r3_q, r3_p, r3_o, r3_u, r3_d,
    all_small, got_small, got_z, send, recv,
):
    rows = wu_all.shape[0]
    cols = wo_all.shape[0]
    half = rows // 2
    heads = 2 * half
    k, z, c, near, far = place()
    opposite = 3 - c
    sibling = (1 - k, z, c)
    io = Copies(send, recv)
    mine = lax.div(z, half) == k
    arrived = io.arrived
    enter(rows)

    def q_block(cc):
        return wq_half.at[:, pl.ds(aligned(cc * 128, 128), 128), :]

    def p_block(cc):
        return wp_half.at[:, pl.ds(aligned(cc * 128, 128), 128), :]

    def u_block(cc, core=k):
        return wu_all.at[pl.ds(core * half, half), pl.ds(aligned(cc * 128, 128), 128), :]

    def o_block(cc, core=k):
        size = wo_all.shape[1] // 2
        return wo_all.at[cc, pl.ds(aligned(core * size, 128), size), :]

    def d_block(cc, core=k):
        size = wd_all.shape[1] // 2
        return wd_all.at[cc, pl.ds(aligned(core * size, 128), size), :]

    def q_one(i):
        return wq_half.at[i, pl.ds(aligned(c * 128, 128), 128), :]

    def p_one(i):
        return wp_half.at[i, pl.ds(aligned(c * 128, 128), 128), :]

    def u_one(i):
        return wu_all.at[k * half + i, pl.ds(aligned(c * 128, 128), 128), :]

    def o_one(i):
        size = wo_all.shape[1] // rows
        return wo_all.at[c, pl.ds(aligned((k * half + i) * size, 128), size), :]

    def d_one(i):
        size = wd_all.shape[1] // rows
        return wd_all.at[c, pl.ds(aligned((k * half + i) * size, 128), size), :]

    weights = {
        "q": (wq, q_one, q_block), "p": (wp, p_one, p_block), "o": (wo, o_one, o_block),
        "u": (wu, u_one, u_block), "d": (wd, d_one, d_block),
    }
    z_slot = {name: io.take(half) for name in weights}
    z_send = {name: io.take(half * rows) for name in weights}
    near_slot = {name: io.take(1) for name in weights}
    far_slot = {name: io.take(2) for name in weights}
    sib_slot = {name: io.take(4) for name in weights}

    def z_start(name):
        ref, one, _ = weights[name]
        for i in range(half):
            slot = z_slot[name] + i

            def here(i=i):
                return z == k * half + i

            io.keep(lambda: ref, lambda i=i: one(i), slot, here)
            for step in range(1, rows):
                io.push(
                    z_send[name] + i * rows + step,
                    lambda i=i, step=step, slot=slot: (ref, one(i), slot, (k, lax.rem(z + step, rows), c)),
                    here,
                )

    def z_done(name):
        _, one, _ = weights[name]
        for i in range(half):
            arrived(one(i), z_slot[name] + i)

    def near_start(name):
        block = weights[name][2]
        io.push(near_slot[name], lambda: (block(c), block(c), near_slot[name], (k, z, near)))

    def near_done(name):
        arrived(weights[name][2](near), near_slot[name])

    def far_start(name):
        block = weights[name][2]
        io.push(far_slot[name], lambda: (block(c), block(c), far_slot[name], (k, z, far)))
        io.push(far_slot[name] + 1, lambda: (block(near), block(near), far_slot[name] + 1, (k, z, far)))

    def far_done(name):
        block = weights[name][2]
        arrived(block(far), far_slot[name])
        arrived(block(3 - c), far_slot[name] + 1)

    def sib_start(name):
        block = weights[name][2]
        for cc in range(4):
            slot = sib_slot[name] + cc
            io.push(slot, lambda cc=cc, slot=slot: (block(cc), block(cc), slot, (1 - k, z, c)))

    def sib_done(name):
        block = weights[name][2]
        for cc in range(4):
            arrived(block(cc, 1 - k), sib_slot[name] + cc)

    feat = tok.shape[1]
    x_slot = io.take(4)
    x_send = io.take(4)
    xf_slot = io.take(4)

    def x_part(cc, core):
        return xt.at[pl.ds(aligned(cc * feat + core * (feat // 2), 64), feat // 2), :]

    def is_local(b, core):
        return jnp.logical_and(2 * b + k == c, core == k)

    z_start("q")
    for b in range(2):
        for core in range(2):

            def src(b=b, core=core):
                return tok.at[b, pl.ds(core * (feat // 2), feat // 2), :]

            def dst(core=core):
                return x_part(c, core)

            io.keep(src, dst, x_slot + c, lambda b=b, core=core: is_local(b, core))
            io.push(
                x_send + 2 * b + core,
                lambda src=src, dst=dst, b=b, core=core: (src(), dst(), x_slot + c, (0 * k + core, z, 2 * b + k)),
                lambda b=b, core=core: jnp.logical_not(is_local(b, core)),
            )
    z_start("p")

    t_slot = io.take(1)
    io.keep(lambda: table, lambda: kcat.at[:, pl.ds(0, table.shape[1])], t_slot)
    g_col = io.take(4)
    g_row = io.take(rows)
    g_cb = io.take(rows)
    g_pb = io.take(rows)
    for step in range(1, 4):
        io.push(
            g_col + step,
            lambda step=step: (packed.at[pl.ds(0, 8)], params_col.at[c], g_col, (k, z, lax.rem(c + step, 4))),
        )
    io.keep(lambda: packed.at[pl.ds(0, 8)], lambda: params_col.at[c], g_col)
    for source, target, slot in ((packed.at[pl.ds(8, 8)], params_row, g_row), (cbias, cb_all, g_cb), (pbias, pb_all, g_pb)):
        for step in range(1, rows):
            io.push(
                slot + step,
                lambda step=step, source=source, target=target, slot=slot: (
                    source, target.at[z], slot, (k, lax.rem(z + step, rows), c)
                ),
            )
        io.keep(lambda source=source: source, lambda target=target: target.at[z], slot)
    s_slot = io.take(1)
    s_send = io.take(4)
    for b in range(2):
        for core in range(2):
            io.keep(
                lambda: starts, lambda: starts_got, s_slot,
                lambda b=b, core=core: jnp.logical_and(c == z, is_local(b, core)),
            )
            io.push(
                s_send + 2 * b + core,
                lambda b=b, core=core: (starts, starts_got, s_slot, (0 * k + core, z, 2 * b + k)),
                lambda b=b, core=core: jnp.logical_and(c == z, jnp.logical_not(is_local(b, core))),
            )
    for name in ("o", "u", "d"):
        z_start(name)

    c_slot = io.take(4)
    c_send = io.take(4)
    count = ct.shape[1]

    def cot_start():
        for b in range(2):
            for core in range(2):

                def src(b=b, core=core):
                    return cot.at[b, :, pl.ds(core * count, count)]

                def dst():
                    return ct.at[pl.ds(aligned(c * feat, 128), feat), :]

                io.keep(src, dst, c_slot + c, lambda b=b, core=core: is_local(b, core))
                io.push(
                    c_send + 2 * b + core,
                    lambda src=src, dst=dst, b=b, core=core: (src(), dst(), c_slot + c, (0 * k + core, z, 2 * b + k)),
                    lambda b=b, core=core: jnp.logical_not(is_local(b, core)),
                )

    for cc in range(4):
        arrived(x_part(cc, k), x_slot + cc)
        io.push(xf_slot + cc, lambda cc=cc: (x_part(cc, k), x_part(cc, k), xf_slot + cc, sibling))
    z_done("q")
    near_start("q")
    z_done("p")
    near_start("p")
    arrived(params_col, g_col)
    arrived(params_row, g_row)
    arrived(cb_all, g_cb)
    arrived(pb_all, g_pb)
    arrived(starts_got, s_slot)
    for cc in range(4):
        arrived(x_part(cc, 1 - k), xf_slot + cc)

    columns = [tall(params_col[cc]) for cc in range(4)]
    gain = jnp.concatenate([col[:, 0:1] for col in columns], axis=0)
    bias = jnp.concatenate([col[:, 1:2] for col in columns], axis=0)
    width = xt.shape[0]
    seq = xt.shape[1]
    piece = PIECE
    blocks = seq // 256

    @pl.loop(0, blocks)
    def _(t):
        here = pl.ds(aligned(t * 256, 256), 256)
        x = xt[:, here].astype(F32)
        mean = jnp.sum(x, axis=0, keepdims=True) * (1.0 / width)
        square = jnp.sum(x * x, axis=0, keepdims=True) * (1.0 / width)
        inverse = lax.rsqrt(square - mean * mean + norm_epsilon)
        normed_t[:, here] = ((x - mean) * inverse * gain + bias).astype(BF16)

    near_done("q")
    far_start("q")
    near_done("p")
    far_start("p")
    cot_start()
    z_done("o")
    near_start("o")
    z_done("u")
    near_start("u")
    far_done("q")
    scale = 0.125
    none = jnp.zeros((256, 64), F32)

    @pl.loop(0, half * blocks)
    def _(n):
        i, t = lax.div(n, blocks), lax.rem(n, blocks)
        here = pl.ds(aligned(t * 256, 256), 256)
        got = tn(normed_t[:, here], wq_half[i])
        for hb in range(2):
            h = 2 * i + hb
            low = got[:, hb * 192 : hb * 192 + 192].astype(BF16).astype(F32)
            query, key, value = low[:, 0:64], low[:, 64:128], low[:, 128:192]
            content = cb_all[k * half + i, hb : hb + 1, :]
            position = pb_all[k * half + i, hb : hb + 1, :]
            qcat[h, here, 512:640] = jnp.concatenate(
                [(query + content) * scale, (query + position) * scale], axis=1
            ).astype(BF16)
            keys[h, here, :] = jnp.concatenate([key, none], axis=1).astype(BF16)
            vals[h, here, :] = value.astype(BF16)

    z_done("d")
    near_start("d")
    far_done("p")
    arrived(kcat.at[:, pl.ds(0, 512)], t_slot)
    for h in range(heads):
        part = wp_half[h // 2, :, (h % 2) * 64 : (h % 2) * 64 + 64]
        wp_head[h] = jnp.concatenate([jnp.zeros_like(part), part], axis=1)

    @pl.loop(0, heads * blocks)
    def _(n):
        h, t = lax.div(n, blocks), lax.rem(n, blocks)
        here = pl.ds(aligned(t * 256, 256), 256)
        angle = nt(qcat[h, here, 512:640], wp_head[h])
        cosine = kcat[here, 0:256].astype(F32)
        sine = kcat[here, 256:512].astype(F32)
        first, second = angle[:, 0:256], angle[:, 256:512]
        qcat[h, here, 0:256] = (first * sine + second * cosine).astype(BF16)
        qcat[h, here, 256:512] = (second * sine - first * cosine).astype(BF16)

    slot_len = seq // 2
    block = 256
    batch = lax.div(c, 2)

    def attend(h, low_row, keys_seen, slot):
        start = starts_got[batch, 0:1, slot : slot + 1]
        row = slot * slot_len + low_row + lax.broadcasted_iota(jnp.int32, (block, 1), 0)
        inside = jnp.logical_and(row >= start, row < start + piece)
        limit = jnp.where(inside, start + (piece - 1), row)
        here = pl.ds(aligned(slot * slot_len + low_row, block), block)
        scores = nt(qcat[h, here, :], kcat[0:keys_seen, :])
        column = slot * slot_len + lax.broadcasted_iota(jnp.int32, (block, slot_len), 1)
        last = jnp.where(column <= limit, scores[:, keys_seen - slot_len :], big_negative)
        top = jnp.max(last, axis=1, keepdims=True)
        if slot == 1:
            top = jnp.maximum(top, jnp.max(scores[:, :slot_len], axis=1, keepdims=True))
        last = jnp.exp(last - top)
        total = jnp.sum(last, axis=1, keepdims=True)
        if slot == 1:
            first = jnp.exp(scores[:, :slot_len] - top)
            total = total + jnp.sum(first, axis=1, keepdims=True)
            whole = jnp.concatenate([first, last], axis=1)
        else:
            whole = last
        low = (whole * (1.0 / total)).astype(BF16)
        probs = (probs_a, probs_b)[slot]
        probs[h, pl.ds(aligned(low_row, block), block), :] = low
        heads_out[h, here, :] = nn(low, vals[h, 0:keys_seen, :]).astype(BF16)

    def stage_zero():
        near_done("o")
        far_start("o")
        near_done("u")
        far_start("u")

    def stage_one():
        near_done("d")
        far_start("d")
        far_done("o")
        sib_start("o")

    def stage_two():
        far_done("u")
        sib_start("u")

    @pl.loop(0, heads)
    def _(h):
        kcat[:, 512:640] = keys[h]

        @pl.loop(0, slot_len // block)
        def _(t):
            attend(h, t * block, slot_len, 0)

        @pl.loop(0, slot_len // block)
        def _(t):
            attend(h, t * block, seq, 1)

        for number, stage in enumerate((stage_zero, stage_one, stage_two)):
            pl.when(h == number)(stage)

    own_att[...] = jnp.concatenate([heads_out[h] for h in range(heads)], axis=1)
    a_slot = io.take(2)
    span = own_att.shape[1]
    other = pl.ds(aligned((1 - k) * count, count), count)
    own = pl.ds(aligned(k * count, count), count)
    att_part = att.at[:, pl.ds(aligned(k * span, 128), span)]
    io.push(a_slot, lambda: (own_att.at[other, :], att_part, a_slot, sibling))
    io.keep(lambda: own_att.at[own, :], lambda: att_part, a_slot + 1)
    far_done("d")
    sib_start("d")
    for cc in range(4):
        arrived(ct.at[pl.ds(cc * feat, feat), :], c_slot + cc)
    gout[...] = jnp.transpose(ct[...])
    sib_done("o")
    arrived(own_att.at[own, :], a_slot + 1)
    arrived(own_att.at[own, :], a_slot)

    def line(index):
        return jnp.concatenate([params_col[cc, index : index + 1, :] for cc in range(cols)], axis=1)

    def out_weight():
        return jnp.concatenate([wo_all[cc] for cc in range(cols)], axis=1)

    x = jnp.transpose(xt[:, own].astype(F32))
    middle = x + nn(att[...], out_weight())
    mid[...] = middle
    mean = jnp.sum(middle, axis=1, keepdims=True) * (1.0 / width)
    square = jnp.sum(middle * middle, axis=1, keepdims=True) * (1.0 / width)
    inverse = lax.rsqrt(square - mean * mean + norm_epsilon)
    scaled = (middle - mean) * inverse
    hat[...] = scaled
    inv[...] = inverse
    low = (scaled * line(2) + line(3)).astype(BF16)
    norm[...] = low
    tall_norm[...] = jnp.transpose(low)
    acc_out[...] = jnp.zeros_like(acc_out)
    acc_two[...] = jnp.zeros_like(acc_two)
    small[...] = jnp.zeros_like(small)
    hidden = wu_all.shape[2]

    @pl.loop(0, rows)
    def _(step):
        r = lax.rem(k * half + step, rows)

        @pl.when(step == half)
        def _():
            for name in ("u", "d"):
                sib_done(name)

        here = pl.ds(aligned(r * hidden, hidden), hidden)
        bias = jnp.concatenate([params_row[r, j : j + 1, :] for j in range(hidden // 128)], axis=1)
        down = jnp.concatenate([wd_all[cc, here, :] for cc in range(cols)], axis=1)
        pre = nn(norm[...], wu_all[r]) + bias
        grad_act = nt(gout[...], down)
        lower = erf_parts(pre)
        act = (pre * lower).astype(BF16)
        slope = lower + pre * jnp.exp(-0.5 * pre * pre) * inv_sqrt_tau
        low_grad = (grad_act * slope).astype(BF16)
        small[pl.ds(5 + r, 1), :] = jnp.sum(low_grad.astype(F32), axis=0, keepdims=True)
        acc_out[...] += nn(act, down)
        acc_two[...] += nt(low_grad, wu_all[r])
        g_up[r] = nn(tall_norm[...], low_grad).astype(BF16)
        found = tn(act, gout[...]).astype(BF16)
        for cc in range(cols):
            g_down[cc, here, :] = found[:, cc * 128 : cc * 128 + 128]

    hs = {
        "q": lambda i, cc: hs_q.at[i, cc], "p": lambda i, cc: hs_p.at[i, cc], "u": lambda i, cc: hs_u.at[i, cc],
        "o": lambda i, cc: hs_o.at[cc, i], "d": lambda i, cc: hs_d.at[cc, i],
    }
    r1 = {"q": r1_q, "p": r1_p, "o": r1_o, "u": r1_u, "d": r1_d}
    r2 = {"q": r2_q, "p": r2_p, "o": r2_o, "u": r2_u, "d": r2_d}
    r3 = {"q": r3_q, "p": r3_p, "o": r3_o, "u": r3_u, "d": r3_d}
    final = {"q": f_q, "p": f_p, "o": f_o, "u": f_u, "d": f_d}
    slots = {}
    for name in ("o", "u", "d", "q", "p"):
        slots[name, "sib"] = io.take(1)
        slots[name, "one"] = io.take(2 * half)
        slots[name, "two"] = io.take(half)
        slots[name, "z"] = io.take(rows)
        slots[name, "last"] = io.take(1)

    def grad_half(name, core):
        if name == "u":
            return g_up.at[pl.ds(core * half, half)]
        full = g_out if name == "o" else g_down
        size = full.shape[1] // 2
        return full.at[:, pl.ds(aligned(core * size, 128), size), :]

    got0 = {"u": r0_u, "o": r0_o, "d": r0_d}

    def grad_sib_start(name):
        slot = slots[name, "sib"]
        io.push(slot, lambda: (grad_half(name, 1 - k), got0[name], slot, sibling))

    def grad_sib_done(name):
        arrived(got0[name], slots[name, "sib"])
        if name == "u":
            for i in range(half):
                total = g_up[k * half + i].astype(F32) + r0_u[i].astype(F32)
                hs_u[i] = total.astype(BF16).reshape(hs_u.shape[1:])
        else:
            full = g_out if name == "o" else g_down
            size = full.shape[1] // 2
            to = hs_o if name == "o" else hs_d
            for cc in range(cols):
                part = full[cc, pl.ds(aligned(k * size, 128), size), :]
                total = part.astype(F32) + got0[name][cc].astype(F32)
                to[cc] = total.astype(BF16).reshape(to.shape[1:])

    def one_start(name, i):
        block = hs[name]
        slot = slots[name, "one"] + 2 * i
        io.push(slot, lambda: (block(i, far), r1[name].at[i, 0], slot, (k, z, far)))
        io.push(slot + 1, lambda: (block(i, 3 - c), r1[name].at[i, 1], slot + 1, (k, z, far)))

    def load(ref):
        return ref[...].astype(F32)

    def one_done(name, i):
        block = hs[name]
        slot = slots[name, "one"] + 2 * i
        arrived(r1[name].at[i, 1], slot + 1)
        r1[name][i, 1] = (r1[name][i, 1].astype(F32) + load(block(i, near))).astype(BF16)
        io.push(
            slots[name, "two"] + i, lambda: (r1[name].at[i, 1], r2[name].at[i], slots[name, "two"] + i, (k, z, near))
        )
        arrived(r1[name].at[i, 0], slot)
        r1[name][i, 0] = (r1[name][i, 0].astype(F32) + load(block(i, c))).astype(BF16)

    def two_done(name, i):
        arrived(r2[name].at[i], slots[name, "two"] + i)
        r2[name][i] = (r2[name][i].astype(F32) + r1[name][i, 0].astype(F32)).astype(BF16)
        base = slots[name, "z"]
        io.push(
            base + i,
            lambda: (r2[name].at[i], r3[name].at[z], base + z, (k, k * half + i, c)),
            lambda: z != k * half + i,
        )

    def grad_z_done(name):
        base = slots[name, "z"]
        to = final[name]

        @pl.when(mine)
        def _():
            total = r2[name][z - k * half].astype(F32)
            for step in range(1, rows):
                source = lax.rem(z + step, rows)
                arrived(r3[name].at[source], base + source)
                total = total + r3[name][source].astype(F32)
            to[...] = total

        slot = slots[name, "last"]
        io.push(slot, lambda: (to, to, slot, sibling), lambda: mine)

    def last_done(name):
        @pl.when(jnp.logical_not(mine))
        def _():
            arrived(final[name], slots[name, "last"])

    origin = lax.rem(c, 2)
    b_slot = {"out": io.take(4), "grad": io.take(4)}

    def back_start(src, dst, base):
        for step in range(4):

            def part(step=step):
                return src.at[pl.ds(aligned(lax.rem(c + step, 4) * feat, 128), feat), :]

            def landing():
                return dst.at[batch, k]

            if step == 0:
                io.keep(part, landing, base + 2 * batch + k, lambda: origin == k)
                io.push(
                    base + step,
                    lambda part=part, landing=landing: (part(), landing(), base + 2 * batch + k, sibling),
                    lambda: origin != k,
                )
            else:
                io.push(
                    base + step,
                    lambda part=part, landing=landing, step=step: (
                        part(), landing(), base + 2 * batch + k, (origin, z, lax.rem(c + step, 4))
                    ),
                )

    def back_done(dst, base):
        for b in range(2):
            for core in range(2):
                arrived(dst.at[b, core], base + 2 * b + core)

    for name in ("u", "d"):
        grad_sib_start(name)
    cotangent = gout[...].astype(F32)
    out_t[...] = jnp.transpose(mid[...] + acc_out[...] + line(4)).astype(BF16)
    back_start(out_t, outs, b_slot["out"])
    two = acc_two[...]
    small[2:3, :] = jnp.sum(two * hat[...], axis=0, keepdims=True)
    small[3:4, :] = jnp.sum(two, axis=0, keepdims=True)
    small[4:5, :] = jnp.sum(cotangent, axis=0, keepdims=True)
    shifted = two * line(2)
    first = jnp.sum(shifted, axis=1, keepdims=True) * (1.0 / width)
    second = jnp.sum(shifted * hat[...], axis=1, keepdims=True) * (1.0 / width)
    grad_mid = cotangent + inv[...] * (shifted - first - hat[...] * second)
    branch = grad_mid.astype(BF16)
    grad_att[...] = nt(branch, out_weight()).astype(BF16)
    e_slot = io.take(2)
    io.push(
        e_slot,
        lambda: (grad_att.at[:, pl.ds(aligned((1 - k) * span, 128), span)], grad_o.at[own, :], e_slot, sibling),
    )
    io.keep(
        lambda: grad_att.at[:, pl.ds(aligned(k * span, 128), span)], lambda: grad_o.at[own, :], e_slot + 1
    )
    grad_mid_t[...] = jnp.transpose(grad_mid)
    found = tn(att[...], branch).astype(BF16)
    for cc in range(cols):
        g_out[cc] = found[:, cc * 128 : cc * 128 + 128]
    grad_sib_start("o")
    sums[...] = jnp.zeros_like(sums)
    arrived(grad_o.at[own, :], e_slot + 1)
    arrived(grad_o.at[own, :], e_slot)
    for h in range(heads):
        head_grad[h] = grad_o[:, h * 64 : h * 64 + 64]
    for name in ("u", "d"):
        grad_sib_done(name)
        for j in range(half):
            one_start(name, j)

    def attend_back(h, low_row, keys_seen, slot):
        at = pl.ds(aligned(low_row, block), block)
        here = pl.ds(aligned(slot * slot_len + low_row, block), block)
        grad = head_grad[h, here, :]
        low = (probs_a, probs_b)[slot][h, at, :]
        inner = jnp.sum(grad.astype(F32) * heads_out[h, here, :].astype(F32), axis=1, keepdims=True)
        grad_prob = nt(grad, vals[h, 0:keys_seen, :])
        grad_score = (low.astype(F32) * (grad_prob - inner)).astype(BF16)
        turned_v[:, 0:keys_seen] += tn(grad, low)
        turned_k[:, 0:keys_seen] += tn(qcat[h, here, 512:576], grad_score)
        got = nn(grad_score, kcat[0:keys_seen, :])
        cosine = kcat[here, 0:256].astype(F32)
        sine = kcat[here, 256:512].astype(F32)
        first, second = got[:, 0:256], got[:, 256:512]
        angle = jnp.concatenate([first * sine - second * cosine, first * cosine + second * sine], axis=1).astype(BF16)
        both = got[:, 512:640] + nn(angle, wp_head[h])
        turned_p[h] += tn(qcat[h, here, 512:640], angle)[64:128]
        sums[pl.ds(h, 1), :] += jnp.sum(both, axis=0, keepdims=True) * 0.125
        query = (both + pltpu.roll(both, 64, 1)) * 0.125
        turned[h, 0:64, here] = jnp.transpose(query)[0:64].astype(BF16)

    def project_back(i):
        pair = jnp.concatenate([turned[2 * i], turned[2 * i + 1]], axis=0)
        hs_q[i] = nt(normed_t[...], pair).astype(BF16).reshape(hs_q.shape[1:])
        one_start("q", i)
        pos = jnp.concatenate([turned_p[2 * i], turned_p[2 * i + 1]], axis=0)
        hs_p[i] = jnp.transpose(pos).astype(BF16).reshape(hs_p.shape[1:])
        one_start("p", i)
        part = nn(wq_half[i], pair)
        if i == 0:
            one_t[...] = part
        else:
            one_t[...] += part

    def back_zero():
        grad_sib_done("o")
        for j in range(half):
            one_start("o", j)

    def back_one():
        project_back(0)
        for name in ("u", "d"):
            for j in range(half):
                one_done(name, j)

    def back_two():
        for j in range(half):
            one_done("o", j)
        for name in ("u", "d"):
            for j in range(half):
                two_done(name, j)

    @pl.loop(0, heads)
    def _(h):
        kcat[:, 512:640] = keys[h]
        turned_k[...] = jnp.zeros_like(turned_k)
        turned_v[...] = jnp.zeros_like(turned_v)
        turned_p[h] = jnp.zeros(turned_p.shape[1:], F32)

        @pl.loop(0, slot_len // block)
        def _(t):
            attend_back(h, t * block, slot_len, 0)

        @pl.loop(0, slot_len // block)
        def _(t):
            attend_back(h, t * block, seq, 1)

        turned[h, 64:128, :] = turned_k[...].astype(BF16)
        turned[h, 128:192, :] = turned_v[...].astype(BF16)
        for number, stage in enumerate((back_zero, back_one, back_two)):
            pl.when(h == number)(stage)

    project_back(1)

    one_low[...] = one_t[:, other].astype(BF16)
    f_slot = io.take(1)
    io.push(f_slot, lambda: (one_low, one_got, f_slot, sibling))
    one_done("q", 0)
    one_done("p", 0)
    for j in range(half):
        two_done("o", j)
    arrived(one_got, f_slot)
    columns = [tall(params_col[cc]) for cc in range(cols)]
    gain = jnp.concatenate([col[:, 0:1] for col in columns], axis=0)
    one = one_t[:, own] + one_got[...].astype(F32)
    x = xt[:, own].astype(F32)
    mean = jnp.sum(x, axis=0, keepdims=True) * (1.0 / width)
    square = jnp.sum(x * x, axis=0, keepdims=True) * (1.0 / width)
    inverse = lax.rsqrt(square - mean * mean + norm_epsilon)
    scaled = (x - mean) * inverse
    shifted = one * gain
    first = jnp.sum(shifted, axis=0, keepdims=True) * (1.0 / width)
    second = jnp.sum(shifted * scaled, axis=0, keepdims=True) * (1.0 / width)
    grad_x[...] = (grad_mid_t[...] + inverse * (shifted - first - scaled * second)).astype(BF16)
    back_start(grad_x, grads, b_slot["grad"])
    gain_sum = jnp.sum(one * scaled, axis=1, keepdims=True)
    bias_sum = jnp.sum(one, axis=1, keepdims=True)
    lane = lax.broadcasted_iota(jnp.int32, (width, 128), 1)
    pair = jnp.where(lane == 0, gain_sum, jnp.where(lane == 1, bias_sum, 0.0))
    pair = jnp.transpose(pair)[0:8]
    all_small[0] = small[...]
    all_small[0, 0:2, :] = pair[0:2]

    def spread(first_lane):
        row = jnp.concatenate([sums[h : h + 1, first_lane : first_lane + 64] for h in range(heads)], axis=1)
        blank = jnp.zeros_like(row)
        return jnp.where(k == 0, jnp.concatenate([row, blank], axis=1), jnp.concatenate([blank, row], axis=1))

    all_small[0, 9:10, :] = spread(0)
    all_small[0, 10:11, :] = spread(64)
    m_slot = io.take(3)
    v_send = io.take(rows)
    v_slot = io.take(rows)
    io.push(m_slot, lambda: (all_small.at[0], got_small.at[0], m_slot, sibling))
    for i in range(half):
        if i > 0:
            one_done("q", i)
            one_done("p", i)
    arrived(got_small.at[0], m_slot)
    all_small[1] = all_small[0] + got_small[0]
    io.push(m_slot + 1, lambda: (all_small.at[1], got_small.at[1], m_slot + 1, (k, z, near)))
    for name in ("u", "d"):
        grad_z_done(name)
    for i in range(half):
        two_done("q", i)
        two_done("p", i)
    arrived(got_small.at[1], m_slot + 1)
    all_small[2] = all_small[1] + got_small[1]
    io.push(m_slot + 2, lambda: (all_small.at[2], got_small.at[2], m_slot + 2, (k, z, far)))
    grad_z_done("o")
    arrived(got_small.at[2], m_slot + 2)
    all_small[3] = all_small[2] + got_small[2]
    for step in range(1, rows):
        io.push(
            v_send + step,
            lambda step=step: (all_small.at[3], got_z.at[z], v_slot + z, (k, lax.rem(z + step, rows), c)),
        )
    grad_z_done("q")
    grad_z_done("p")
    total = all_small[3]
    for step in range(1, rows):
        source = lax.rem(z + step, rows)
        arrived(got_z.at[source], v_slot + source)
        total = total + got_z[source]
    f_small[...] = total
    back_done(outs, b_slot["out"])
    back_done(grads, b_slot["grad"])
    for name in ("u", "d", "o", "q", "p"):
        last_done(name)
    io.drain()


def final_kernel(
    outs, grads, f_q, f_p, f_o, f_u, f_d, f_small,
    output, grad_tokens, g1, b1, q_w, c_b, p_b, p_w, o_w, g2, b2, u_w, u_b, d_w, d_b,
):
    k, z, c, _, _ = place()
    for b in range(2):
        for core in range(2):
            size = outs.shape[3]
            output[b, :, core * size : core * size + size] = outs[b, core].astype(F32)
            grad_tokens[b, :, core * size : core * size + size] = grads[b, core].astype(F32)
    for core in range(2):

        @pl.when(k == core)
        def _(core=core):
            for ref, source in ((q_w, f_q), (p_w, f_p), (o_w, f_o), (d_w, f_d)):
                size = ref.shape[0]
                ref[...] = jnp.transpose(source[:, core * size : core * size + size])
            size = u_w.shape[1]
            u_w[...] = f_u[:, core * size : core * size + size]

    width = f_small.shape[1]
    chip = z * 4 + c
    share = g1.shape[1]
    first = pltpu.roll(f_small[0:8, :], lax.rem(width - (chip * 2 + k) * share, width), 1)
    for row, ref in ((0, g1), (1, b1), (2, g2), (3, b2), (4, d_b)):
        ref[...] = first[row : row + 1, 0:share]
    share = u_b.shape[1]
    line = f_small[pl.ds(5 + z, 1), :]
    line = jnp.broadcast_to(line, (8, width))
    u_b[...] = pltpu.roll(line, lax.rem(width - (c * 2 + k) * share, width), 1)[0:1, 0:share]
    heads, share = c_b.shape
    third = pltpu.roll(f_small[8:16, :], lax.rem(2 * width - heads * 64 * z - (c * 2 + k) * share, width), 1)
    for h in range(heads):
        c_b[h : h + 1, :] = third[1:2, h * 64 : h * 64 + share]
        p_b[h : h + 1, :] = third[2:3, h * 64 : h * 64 + share]


def position_table(seq_len, feature_count):
    positions = np.arange(seq_len, dtype=np.float64)
    exponent = -np.arange(0, feature_count, 2, dtype=np.float64) / feature_count
    angles = positions[:, None] * (10000.0**exponent)[None, :]
    return np.concatenate([np.cos(angles), np.sin(angles)], axis=1).astype(jnp.bfloat16)


def fast_shards(
    tokens, cotangent, piece_starts, ln1_gain, ln1_bias, qkv_weight, content_bias, position_bias, pos_weight,
    out_weight, ln2_gain, ln2_bias, up_weight, up_bias, down_weight, down_bias,
):
    rows, cols = lax.axis_size("row"), lax.axis_size("col")
    half = rows // 2
    micro, feat, seq = tokens.shape
    width = feat * cols
    count = seq // 2
    hidden = up_weight.shape[1]
    heads = content_bias.shape[0] * half
    table = jnp.asarray(position_table(seq, width))
    lines = jnp.concatenate(
        [ln1_gain, ln1_bias, ln2_gain, ln2_bias, down_bias, jnp.zeros((3 * feat,), BF16), up_bias, jnp.zeros((8 * 128 - hidden,), BF16)]
    )
    packed = lines.reshape(16, 128).astype(F32)
    vm = pl.BlockSpec(memory_space=pltpu.VMEM)
    anywhere = pl.BlockSpec(memory_space=pl.ANY)
    limit = 64 * 1024 * 1024 - 128 * 1024

    def shape(dims, kind=BF16):
        return jax.ShapeDtypeStruct(dims, kind)

    def vmem(dims, kind=BF16):
        return pltpu.VMEM(dims, kind)

    q_cols, p_cols = qkv_weight.shape[1], pos_weight.shape[1]
    o_rows, d_rows = out_weight.shape[0], down_weight.shape[0]
    blocks = {
        "q": (feat, q_cols), "p": (feat, p_cols), "o": (o_rows, 128), "u": (feat, hidden), "d": (d_rows, 128),
    }
    names = ("q", "p", "o", "u", "d")
    results = pl.pallas_call(
        layer_kernel,
        name="layer",
        out_shape=(
            shape((micro, 2, feat, count)),
            shape((micro, 2, feat, count)),
        )
        + tuple(shape(blocks[name], F32) for name in names)
        + (shape((16, width), F32),),
        in_specs=[anywhere, anywhere, vm, vm, vm, vm] + [anywhere] * 6,
        out_specs=(vm,) * 8,
        scratch_shapes=[
            vmem((count, width)),
            vmem((cols, width, 128)),
            vmem((rows, width, hidden)),
            vmem((cols, rows * hidden, 128)),
            vmem((half, width, q_cols)),
            vmem((half, width, p_cols)),
            vmem((heads, width, 128)),
            vmem((width, seq)),
            vmem((width, count)),
            vmem((width, seq)),
            vmem((heads, seq, width + 128)),
            vmem((heads, seq, 128)),
            vmem((heads, seq, 64)),
            vmem((heads, count, count)),
            vmem((heads, count, seq)),
            vmem((heads, seq, 64)),
            vmem((cols, 8, 128), F32),
            vmem((rows, 8, 128), F32),
            vmem((rows,) + content_bias.shape, F32),
            vmem((rows,) + position_bias.shape, F32),
            vmem((seq, width + 128)),
            vmem((seq, heads * 64)),
            vmem(piece_starts.shape, jnp.int32),
            vmem((count, width), F32),
            vmem((count, width)),
            vmem((count, width), F32),
            vmem((count, 1), F32),
            vmem((count, width)),
            vmem((count, width), F32),
            vmem((count, width), F32),
            vmem((width, count)),
            vmem((width, count)),
            vmem((width, count), F32),
            vmem((count, width)),
            vmem((rows, width, hidden)),
            vmem((cols, rows * hidden, 128)),
            vmem((cols, width, 128)),
            vmem((16, width), F32),
            vmem((seq, heads * 64)),
            vmem((heads, seq, 64)),
            vmem((heads, 192, seq)),
            vmem((64, seq), F32),
            vmem((64, seq), F32),
            vmem((heads, 64, width), F32),
            vmem((width, seq), F32),
            vmem((width, count)),
            vmem((width, count)),
            vmem((width, count)),
            vmem((8, 128), F32),
            vmem((half, cols) + blocks["q"]),
            vmem((half, cols) + blocks["p"]),
            vmem((cols, half) + blocks["o"]),
            vmem((half, cols) + blocks["u"]),
            vmem((cols, half) + blocks["d"]),
            vmem((cols, half * o_rows, 128)),
            vmem((half, width, hidden)),
            vmem((cols, half * d_rows, 128)),
        ]
        + [vmem((half, 2) + blocks[name]) for name in names]
        + [vmem((half,) + blocks[name]) for name in names]
        + [vmem((rows,) + blocks[name]) for name in names]
        + [
            vmem((4, 16, width), F32),
            vmem((3, 16, width), F32),
            vmem((rows, 16, width), F32),
            pltpu.SemaphoreType.DMA((280,)),
            pltpu.SemaphoreType.DMA((280,)),
        ],
        compiler_params=pltpu.CompilerParams(collective_id=0, has_side_effects=True, vmem_limit_bytes=limit),
    )(
        tokens, cotangent, piece_starts, packed, content_bias, position_bias, table,
        qkv_weight, pos_weight, out_weight, up_weight, down_weight,
    )
    devices = 2 * rows * cols
    vec = shape((1, width // devices), F32)
    bias = shape((content_bias.shape[0], 64 // (2 * cols)), F32)
    done = list(pl.pallas_call(
        final_kernel,
        name="final",
        out_shape=(
            shape(tokens.shape, F32), shape(tokens.shape, F32), vec, vec,
            shape((q_cols // 2, feat), F32), bias, bias, shape((p_cols // 2, feat), F32), shape((64, o_rows), F32), vec, vec,
            shape((feat, hidden // 2), F32), shape((1, rows * hidden // devices), F32), shape((64, d_rows), F32), vec,
        ),
        in_specs=[vm] * 8,
        out_specs=(vm,) * 15,
        compiler_params=pltpu.CompilerParams(vmem_limit_bytes=limit),
    )(*results))
    for index in (4, 7, 8, 13):
        done[index] = done[index].T
    return tuple(v.reshape(-1) if v.shape[0] == 1 else v for v in done)


def solution(mesh):
    in_specs = (
        P(None, "col", ("dp", "row")),
        P(None, "col", ("dp", "row")),
        P(None, ("dp", "col"), None),
        P("col"),
        P("col"),
        P("col", "row"),
        P("row", None),
        P("row", None),
        P("col", "row"),
        P("row", "col"),
        P("col"),
        P("col"),
        P("col", "row"),
        P("row"),
        P("row", "col"),
        P("col"),
    )
    out_specs = (
        P(None, "col", ("dp", "row")),
        P(None, "col", ("dp", "row")),
        P(("row", "col", "dp")),
        P(("row", "col", "dp")),
        P("col", ("row", "dp")),
        P("row", ("col", "dp")),
        P("row", ("col", "dp")),
        P("col", ("row", "dp")),
        P("row", ("col", "dp")),
        P(("row", "col", "dp")),
        P(("row", "col", "dp")),
        P("col", ("row", "dp")),
        P(("row", "col", "dp")),
        P("row", ("col", "dp")),
        P(("row", "col", "dp")),
    )

    def layer(tokens, *others):
        dp, row, col = mesh.shape["dp"], mesh.shape["row"], mesh.shape["col"]
        one_each = tokens.shape[2] == dp * row * SEQ_LEN and tokens.shape[0] * dp == col
        body = fast_shards if one_each and dp == 2 and row == col == 4 else shards
        part = jax.shard_map(body, mesh=mesh, in_specs=in_specs, out_specs=out_specs, check_vma=False)
        return part(tokens, *others)

    return layer
```

```python
from functools import reduce

import jax
import jax.numpy as jnp
import numpy as np
from jax import lax
from jax.experimental import pallas as pl
from jax.experimental.pallas import tpu as pltpu
from jax.sharding import PartitionSpec as P

D = 512
SEQ_LEN = 1024
PIECE = 256


norm_epsilon = 1e-05
big_negative = -1e30
inv_sqrt_two = 0.7071067811865476
inv_sqrt_tau = 0.3989422804014327


def contract(left_op, right_op, flipped):
    if flipped:
        return lax.dot_general(
            left_op, right_op, (((1,), (1,)), ((), ())), preferred_element_type=jnp.float32
        )
    return jnp.dot(left_op, right_op, preferred_element_type=jnp.float32)


def outer_sum(left_op, right_op):
    return lax.dot_general(
        left_op, right_op, (((0,), (0,)), ((), ())), preferred_element_type=jnp.float32
    )


def gather_rows(values):
    return lax.all_gather(values, "row", axis=0, tiled=True)


def gather_cols(values):
    return lax.all_gather(values, "col", axis=0, tiled=True)


def sum_over_cols(gathered, weight, flipped):
    share_rows = gathered.shape[0] // lax.axis_size("col")

    def partial_term(offset, amount):
        return contract(gathered, weight, flipped)

    return lax.psum_scatter(
        partial_term(jnp.int32(0), lax.axis_size("col") * share_rows),
        "col",
        scatter_dimension=0,
        tiled=True,
    )


def sum_over_rows(gathered, weight, flipped):
    share_rows = gathered.shape[0] // lax.axis_size("row")

    def partial_term(offset, amount):
        return contract(gathered, weight, flipped)

    return lax.psum_scatter(
        partial_term(jnp.int32(0), lax.axis_size("row") * share_rows),
        "row",
        scatter_dimension=0,
        tiled=True,
    )


def feature_sums(first_sum, second_sum):
    return lax.psum((first_sum, second_sum), "col")


def normalize(values, gain, bias):
    feature_count = values.shape[1] * lax.axis_size("col")
    total_row, square_row = feature_sums(jnp.sum(values, axis=1), jnp.sum(values * values, axis=1))
    mean_row = total_row / feature_count
    inverse = lax.rsqrt(square_row / feature_count - mean_row * mean_row + norm_epsilon)
    scaled = (values - mean_row[:, None]) * inverse[:, None]
    return (scaled * gain + bias, scaled, inverse)


def normalize_back(grad_in, scaled, inverse, gain):
    feature_count = grad_in.shape[1] * lax.axis_size("col")
    shifted = grad_in * gain
    first_sum, second_sum = feature_sums(
        jnp.sum(shifted, axis=1), jnp.sum(shifted * scaled, axis=1)
    )
    back_rows = inverse[:, None] * (
        shifted - first_sum[:, None] / feature_count - scaled * second_sum[:, None] / feature_count
    )
    return (back_rows, jnp.sum(grad_in * scaled, axis=0), jnp.sum(grad_in, axis=0))


def gelu_exact(values):
    return 0.5 * values * (1.0 + jax.scipy.special.erf(values * inv_sqrt_two))


def gelu_slope(values):
    return (
        0.5 * (1.0 + jax.scipy.special.erf(values * inv_sqrt_two))
        + values * jnp.exp(-0.5 * values * values) * inv_sqrt_tau
    )


def sinusoid_table(seq_len, feature_count):
    offsets = jnp.arange(2 * seq_len - 1, dtype=jnp.float32) - (seq_len - 1)
    frequency = 10000.0 ** (-jnp.arange(0, feature_count, 2, dtype=jnp.float32) / feature_count)
    angles = offsets[:, None] * frequency[None, :]
    return jnp.concatenate([jnp.sin(angles), jnp.cos(angles)], axis=1).astype(jnp.bfloat16)


def piece_labels(positions, starts, piece_len):
    inside = (positions[:, None] >= starts[None, :]) & (
        positions[:, None] < starts[None, :] + piece_len
    )
    numbers = jnp.arange(1, starts.shape[0] + 1, dtype=jnp.int32)
    return jnp.sum(jnp.where(inside, numbers[None, :], 0), axis=1) - 1


def block_mask(offset, block_len, labels):
    positions = jnp.arange(labels.shape[0], dtype=jnp.int32)
    row_pos = offset + jnp.arange(block_len, dtype=jnp.int32)
    row_labels = lax.dynamic_slice_in_dim(labels, offset, block_len, 0)
    same_piece = (row_labels[:, None] == labels[None, :]) & (row_labels[:, None] >= 0)
    return (positions[None, :] <= row_pos[:, None]) | same_piece


def skew_rows(unshifted_reversed_scores, key_total):
    head_total, row_total, rel_span = unshifted_reversed_scores.shape
    flattened = unshifted_reversed_scores.reshape(head_total, row_total * rel_span)
    window = lax.slice_in_dim(
        flattened, row_total - 1, row_total - 1 + row_total * (rel_span - 1), axis=1
    )
    return window.reshape(head_total, row_total, rel_span - 1)[:, :, :key_total]


def unskew_rows(grad_pos, rel_span):
    head_total, row_total, key_total = grad_pos.shape
    padded = jnp.pad(grad_pos, ((0, 0), (0, 0), (0, rel_span - 1 - key_total)))
    flattened = padded.reshape(head_total, row_total * (rel_span - 1))
    flattened = jnp.pad(flattened, ((0, 0), (row_total - 1, 1)))
    return flattened.reshape(head_total, row_total, rel_span)


def block_scores(qu_block, query_position_block, key_rows, relative_block, allowed):
    content = jnp.einsum("ihd,jhd->hij", qu_block, key_rows, preferred_element_type=jnp.float32)
    unshifted_reversed_scores = jnp.einsum(
        "sgw,egw->gse", query_position_block, relative_block, preferred_element_type=jnp.float32
    )
    position = skew_rows(unshifted_reversed_scores, key_rows.shape[0])
    return jnp.where(allowed[None], content + position, big_negative)


def attention_forward(query_u, query_v, key_rows, value_rows, relative_rev, labels):
    seq_len, head_count, head_dim = key_rows.shape
    block_len = min(512, seq_len)
    rel_span = block_len + seq_len - 1
    offsets = jnp.arange(seq_len // block_len, dtype=jnp.int32) * block_len

    def attend(offset):
        qu_block = lax.dynamic_slice_in_dim(query_u, offset, block_len, 0)
        query_position_block = lax.dynamic_slice_in_dim(query_v, offset, block_len, 0)
        relative_block = lax.dynamic_slice_in_dim(
            relative_rev, seq_len - block_len - offset, rel_span, 0
        )
        scores = block_scores(
            qu_block,
            query_position_block,
            key_rows,
            relative_block,
            block_mask(offset, block_len, labels),
        )
        row_max = jnp.max(scores, axis=2, keepdims=True)
        log_total = row_max + jnp.log(jnp.sum(jnp.exp(scores - row_max), axis=2, keepdims=True))
        attn_prob = jnp.exp(scores - log_total).astype(jnp.bfloat16)
        result = jnp.einsum(
            "hij,jhd->ihd", attn_prob, value_rows, preferred_element_type=jnp.float32
        )
        return (result, log_total[:, :, 0])

    results, log_totals = lax.map(attend, offsets)
    return (results.reshape(seq_len, head_count * head_dim), log_totals)


def attention_backward(
    query_u, query_v, key_rows, value_rows, relative_rev, labels, log_totals, grad_att
):
    seq_len, head_count, head_dim = key_rows.shape
    block_len = min(512, seq_len)
    rel_span = block_len + seq_len - 1
    offsets = jnp.arange(seq_len // block_len, dtype=jnp.int32) * block_len

    def back_block(carried, sliced):
        grad_keys, grad_values, grad_rel = carried
        offset, log_total = sliced
        rel_start = seq_len - block_len - offset
        qu_block = lax.dynamic_slice_in_dim(query_u, offset, block_len, 0)
        query_position_block = lax.dynamic_slice_in_dim(query_v, offset, block_len, 0)
        relative_block = lax.dynamic_slice_in_dim(relative_rev, rel_start, rel_span, 0)
        scores = block_scores(
            qu_block,
            query_position_block,
            key_rows,
            relative_block,
            block_mask(offset, block_len, labels),
        )
        attn_prob = jnp.exp(scores - log_total[:, :, None])
        low_prob = attn_prob.astype(jnp.bfloat16)
        grad_block = lax.dynamic_slice_in_dim(grad_att, offset, block_len, 0)
        grad_prob = jnp.einsum(
            "ihd,jhd->hij", grad_block, value_rows, preferred_element_type=jnp.float32
        )
        row_inner = jnp.sum(attn_prob * grad_prob, axis=2, keepdims=True)
        grad_scores = (attn_prob * (grad_prob - row_inner)).astype(jnp.bfloat16)
        grad_values = grad_values + jnp.einsum(
            "hij,ihd->jhd", low_prob, grad_block, preferred_element_type=jnp.float32
        )
        grad_keys = grad_keys + jnp.einsum(
            "hij,ihd->jhd", grad_scores, qu_block, preferred_element_type=jnp.float32
        )
        grad_qu = jnp.einsum(
            "hij,jhd->ihd", grad_scores, key_rows, preferred_element_type=jnp.float32
        )
        gradient_unshifted = unskew_rows(grad_scores, rel_span)
        grad_qv = jnp.einsum(
            "qjp,pqr->jqr", gradient_unshifted, relative_block, preferred_element_type=jnp.float32
        )
        rel_part = jnp.einsum(
            "nfx,fne->xne",
            gradient_unshifted,
            query_position_block,
            preferred_element_type=jnp.float32,
        )
        current = lax.dynamic_slice_in_dim(grad_rel, rel_start, rel_span, 0)
        grad_rel = lax.dynamic_update_slice_in_dim(grad_rel, current + rel_part, rel_start, 0)
        return ((grad_keys, grad_values, grad_rel), (grad_qu, grad_qv))

    zero_rows = jnp.zeros((seq_len, head_count, head_dim), jnp.float32)
    zero_rel = jnp.zeros((2 * seq_len - 1, head_count, head_dim), jnp.float32)
    carried, stacked = lax.scan(back_block, (zero_rows, zero_rows, zero_rel), (offsets, log_totals))
    grad_keys, grad_values, grad_rel = carried
    grad_qu = stacked[0].reshape(seq_len, head_count, head_dim)
    grad_qv = stacked[1].reshape(seq_len, head_count, head_dim)
    return (grad_qu, grad_qv, grad_keys, grad_values, grad_rel)


def heads_pass(packed, content_bias, position_bias, relative_rev, labels):
    seq_len = packed.shape[0]
    head_count, head_dim = content_bias.shape
    scaling = head_dim ** (-0.5)
    packed = packed.reshape(seq_len, head_count, 3, head_dim)
    queries = packed[:, :, 0].astype(jnp.float32)
    key_rows = packed[:, :, 1]
    value_rows = packed[:, :, 2]
    query_u = ((queries + content_bias) * scaling).astype(jnp.bfloat16)
    query_v = ((queries + position_bias) * scaling).astype(jnp.bfloat16)
    attended, log_totals = attention_forward(
        query_u, query_v, key_rows, value_rows, relative_rev, labels
    )
    return (attended.astype(jnp.bfloat16), (query_u, query_v, key_rows, value_rows, log_totals))


def heads_back(kept, relative_rev, labels, grad_att):
    query_u, query_v, key_rows, value_rows, log_totals = kept
    seq_len, head_count, head_dim = key_rows.shape
    scaling = head_dim ** (-0.5)
    grad_att = grad_att.reshape(seq_len, head_count, head_dim)
    grad_qu, grad_qv, grad_keys, grad_values, grad_rel = attention_backward(
        query_u, query_v, key_rows, value_rows, relative_rev, labels, log_totals, grad_att
    )
    cbias_part = jnp.sum(grad_qu, axis=0) * scaling
    pbias_part = jnp.sum(grad_qv, axis=0) * scaling
    grad_query = (grad_qu + grad_qv) * scaling
    grad_packed = jnp.stack([grad_query, grad_keys, grad_values], axis=2)
    grad_packed = grad_packed.reshape(seq_len, head_count * 3 * head_dim).astype(jnp.bfloat16)
    rel_low = grad_rel.reshape(2 * seq_len - 1, head_count * head_dim).astype(jnp.bfloat16)
    return (grad_packed, rel_low, cbias_part, pbias_part)


def grid_micro(seq_feats, cot_feats, params, shared):
    (
        ln1_gain,
        ln1_bias,
        qkv_weight,
        content_bias,
        position_bias,
        out_weight,
        ln2_gain,
        ln2_bias,
        up_weight,
        up_bias,
        down_weight,
        down_bias,
    ) = params
    relative_rev, table_rev, labels = shared
    seq_in = seq_feats.astype(jnp.float32).T
    normed_one, scaled_one, inverse_one = normalize(seq_in, ln1_gain, ln1_bias)
    gathered_one = gather_rows(normed_one.astype(jnp.bfloat16))
    packed = sum_over_cols(gathered_one, qkv_weight, False).astype(jnp.bfloat16)
    attended, kept = heads_pass(packed, content_bias, position_bias, relative_rev, labels)
    att_gathered = gather_cols(attended)
    middle = seq_in + sum_over_rows(att_gathered, out_weight, False)
    normed_two, scaled_two, inverse_two = normalize(middle, ln2_gain, ln2_bias)
    gathered_two = gather_rows(normed_two.astype(jnp.bfloat16))
    pre_act = sum_over_cols(gathered_two, up_weight, False) + up_bias
    activated = gelu_exact(pre_act).astype(jnp.bfloat16)
    act_gathered = gather_cols(activated)
    output = middle + sum_over_rows(act_gathered, down_weight, False) + down_bias
    grad_final = cot_feats.T
    gout = grad_final.astype(jnp.float32)
    final_gathered = gather_rows(grad_final)
    grad_act = sum_over_cols(final_gathered, down_weight, True)
    grad_pre = (grad_act * gelu_slope(pre_act)).astype(jnp.bfloat16)
    pre_gathered = gather_cols(grad_pre)
    grad_two = sum_over_rows(pre_gathered, up_weight, True)
    backward_second, gain_two, bias_two = normalize_back(
        grad_two, scaled_two, inverse_two, ln2_gain
    )
    grad_middle = gout + backward_second
    grad_branch = grad_middle.astype(jnp.bfloat16)
    branch_gathered = gather_rows(grad_branch)
    grad_att = sum_over_cols(branch_gathered, out_weight, True).astype(jnp.bfloat16)
    grad_packed, rel_low, cbias_part, pbias_part = heads_back(kept, relative_rev, labels, grad_att)
    packed_gathered = gather_cols(grad_packed)
    grad_one = sum_over_rows(packed_gathered, qkv_weight, True)
    back_one, gain_one, bias_one = normalize_back(grad_one, scaled_one, inverse_one, ln1_gain)
    grad_in = grad_middle + back_one
    collected = (
        outer_sum(gathered_one, packed_gathered),
        outer_sum(att_gathered, branch_gathered),
        outer_sum(gathered_two, pre_gathered),
        outer_sum(act_gathered, final_gathered),
        outer_sum(table_rev, rel_low),
        cbias_part,
        pbias_part,
        jnp.sum(grad_pre.astype(jnp.float32), axis=0),
        gain_one,
        bias_one,
        gain_two,
        bias_two,
        jnp.sum(gout, axis=0),
    )
    return (output.T, grad_in.T, collected)


def embed_heads(part, row_pick, col_count):
    head_count = part.shape[0]
    spread = jnp.transpose(part.reshape(head_count, col_count, -1), (1, 0, 2))
    placed = jnp.where(row_pick[:, None, None, None], spread[None], 0.0)
    return placed.reshape(row_pick.shape[0] * col_count, head_count, -1)


def shards(
    tokens,
    cotangent,
    piece_starts,
    ln1_gain,
    ln1_bias,
    qkv_weight,
    content_bias,
    position_bias,
    pos_weight,
    out_weight,
    ln2_gain,
    ln2_bias,
    up_weight,
    up_bias,
    down_weight,
    down_bias,
):
    micro_count = tokens.shape[0]
    row_count = lax.axis_size("row")
    col_count = lax.axis_size("col")
    grid_cells = row_count * col_count
    head_count, head_dim = content_bias.shape
    pos_cols = lax.all_gather(pos_weight, "col", axis=0, tiled=True)
    table_rev = sinusoid_table(SEQ_LEN, D)[::-1]
    relative_rev = jnp.dot(table_rev, pos_cols, preferred_element_type=jnp.float32).astype(
        jnp.bfloat16
    )
    relative_rev = relative_rev.reshape(2 * SEQ_LEN - 1, head_count, head_dim)
    positions = jnp.arange(SEQ_LEN, dtype=jnp.int32)
    params = (
        ln1_gain,
        ln1_bias,
        qkv_weight,
        content_bias,
        position_bias,
        out_weight,
        ln2_gain,
        ln2_bias,
        up_weight,
        up_bias,
        down_weight,
        down_bias,
    )
    outputs, grad_inputs, part_lists = ([], [], [])
    for micro_idx in range(micro_count):
        labels = piece_labels(positions, piece_starts[micro_idx, 0], PIECE)
        out_feats, grad_feats, collected = grid_micro(
            tokens[micro_idx], cotangent[micro_idx], params, (relative_rev, table_rev, labels)
        )
        outputs.append(out_feats)
        grad_inputs.append(grad_feats)
        part_lists.append(collected)
    totals = [
        reduce(jnp.add, [collected[member] for collected in part_lists]) for member in range(13)
    ]
    (
        acc_qkv,
        acc_out,
        acc_up,
        acc_down,
        acc_pos,
        acc_cbias,
        acc_pbias,
        acc_ubias,
        acc_g1,
        acc_b1,
        acc_g2,
        acc_b2,
        acc_db,
    ) = totals
    row_pick = jnp.arange(row_count, dtype=jnp.int32) == lax.axis_index("row")
    pos_term = jnp.where(row_pick[:, None, None], acc_pos[None], 0.0).reshape(
        row_count * acc_pos.shape[0], -1
    )
    cbias_term = embed_heads(acc_cbias, row_pick, col_count)
    pbias_term = embed_heads(acc_pbias, row_pick, col_count)
    col_pick = jnp.arange(col_count, dtype=jnp.int32) == lax.axis_index("col")
    ubias_term = jnp.where(row_pick[:, None], acc_ubias[None], 0.0).reshape(grid_cells, -1)
    norm_terms = [
        jnp.where(col_pick[:, None], vector[None], 0.0).reshape(grid_cells, -1)
        for vector in (acc_g1, acc_b1, acc_g2, acc_b2, acc_db)
    ]
    sum_pos, sum_cbias, sum_pbias, sum_ubias, sum_g1, sum_b1, sum_g2, second_bias_total, sum_db = (
        lax.psum_scatter(pos_term, ("row", "col"), scatter_dimension=0, tiled=True),
        lax.psum_scatter(cbias_term, ("row", "col"), scatter_dimension=0, tiled=True),
        lax.psum_scatter(pbias_term, ("row", "col"), scatter_dimension=0, tiled=True),
        lax.psum_scatter(ubias_term, ("row", "col"), scatter_dimension=0, tiled=True),
        lax.psum_scatter(norm_terms[0], ("row", "col"), scatter_dimension=0, tiled=True),
        lax.psum_scatter(norm_terms[1], ("row", "col"), scatter_dimension=0, tiled=True),
        lax.psum_scatter(norm_terms[2], ("row", "col"), scatter_dimension=0, tiled=True),
        lax.psum_scatter(norm_terms[3], ("row", "col"), scatter_dimension=0, tiled=True),
        lax.psum_scatter(norm_terms[4], ("row", "col"), scatter_dimension=0, tiled=True),
    )
    sum_qkv, sum_out, sum_up, sum_down = (acc_qkv, acc_out, acc_up, acc_down)
    summed = (
        lax.psum_scatter(
            sum_qkv.astype(jnp.bfloat16), "dp", scatter_dimension=1, tiled=True
        ).astype(jnp.float32),
        lax.psum_scatter(
            sum_out.astype(jnp.bfloat16), "dp", scatter_dimension=1, tiled=True
        ).astype(jnp.float32),
        lax.psum_scatter(sum_up.astype(jnp.bfloat16), "dp", scatter_dimension=1, tiled=True).astype(
            jnp.float32
        ),
        lax.psum_scatter(
            sum_down.astype(jnp.bfloat16), "dp", scatter_dimension=1, tiled=True
        ).astype(jnp.float32),
        lax.psum_scatter(
            sum_pos.astype(jnp.bfloat16), "dp", scatter_dimension=1, tiled=True
        ).astype(jnp.float32),
        lax.psum_scatter(
            sum_cbias.astype(jnp.bfloat16), "dp", scatter_dimension=2, tiled=True
        ).astype(jnp.float32),
        lax.psum_scatter(
            sum_pbias.astype(jnp.bfloat16), "dp", scatter_dimension=2, tiled=True
        ).astype(jnp.float32),
        lax.psum_scatter(
            sum_ubias.astype(jnp.bfloat16), "dp", scatter_dimension=1, tiled=True
        ).astype(jnp.float32),
        lax.psum_scatter(sum_g1.astype(jnp.bfloat16), "dp", scatter_dimension=1, tiled=True).astype(
            jnp.float32
        ),
        lax.psum_scatter(sum_b1.astype(jnp.bfloat16), "dp", scatter_dimension=1, tiled=True).astype(
            jnp.float32
        ),
        lax.psum_scatter(sum_g2.astype(jnp.bfloat16), "dp", scatter_dimension=1, tiled=True).astype(
            jnp.float32
        ),
        lax.psum_scatter(
            second_bias_total.astype(jnp.bfloat16), "dp", scatter_dimension=1, tiled=True
        ).astype(jnp.float32),
        lax.psum_scatter(sum_db.astype(jnp.bfloat16), "dp", scatter_dimension=1, tiled=True).astype(
            jnp.float32
        ),
    )
    (
        grad_qkv_w,
        grad_out_w,
        grad_up_w,
        grad_down_w,
        grad_pos_w,
        grad_cbias,
        grad_pbias,
        grad_ubias,
        grad_g1,
        grad_b1,
        grad_g2,
        grad_b2,
        grad_dbias,
    ) = summed
    output_rows = jnp.stack(outputs, axis=0)
    grad_rows = jnp.stack(grad_inputs, axis=0)
    return (
        output_rows,
        grad_rows,
        grad_g1.reshape(-1),
        grad_b1.reshape(-1),
        grad_qkv_w,
        grad_cbias.reshape(head_count, -1),
        grad_pbias.reshape(head_count, -1),
        grad_pos_w,
        grad_out_w,
        grad_g2.reshape(-1),
        grad_b2.reshape(-1),
        grad_up_w,
        grad_ubias.reshape(-1),
        grad_down_w,
        grad_dbias.reshape(-1),
    )


MESH = pl.DeviceIdType.MESH
F32 = jnp.float32
BF16 = jnp.bfloat16


def aligned(index, size):
    return index if isinstance(index, int) else pl.multiple_of(index, size)


def nt(a, b):
    return lax.dot_general(a, b, (((1,), (1,)), ((), ())), preferred_element_type=F32)


def nn(a, b):
    return lax.dot_general(a, b, (((1,), (0,)), ((), ())), preferred_element_type=F32)


def tn(a, b):
    return lax.dot_general(a, b, (((0,), (0,)), ((), ())), preferred_element_type=F32)


def place():
    k, z, c = lax.axis_index("dp"), lax.axis_index("row"), lax.axis_index("col")
    cx = c + 1 - 2 * lax.rem(c, 2)
    cy = lax.rem(c + 2, 4)
    near = (1 - k) * cx + k * cy
    far = k * cx + (1 - k) * cy
    return k, z, c, near, far


def enter(rows):
    k, z, c, _, _ = place()
    barrier = pltpu.get_barrier_semaphore()
    peers = [(1 - k, z, c)]
    for step in range(1, rows):
        peers.append((k, lax.rem(z + step, rows), c))
    for step in range(1, 4):
        for core in range(2):
            peers.append((0 * k + core, z, lax.rem(c + step, 4)))
    for peer in peers:
        pl.semaphore_signal(barrier, inc=1, device_id=peer, device_id_type=MESH)
    pl.semaphore_wait(barrier, len(peers))


class Copies:
    def __init__(self, send, recv):
        self.send, self.recv = send, recv
        self.sends, self.recvs = 0, 0
        self.pending = {}

    def leave(self, count=1):
        first = self.sends
        self.sends += count
        return first

    def land(self, count=1):
        first = self.recvs
        self.recvs += count
        return first

    def copy(self, send_slot, build):
        src, dst, recv_slot, peer = build()
        return pltpu.make_async_remote_copy(
            src, dst, self.send.at[send_slot], self.recv.at[recv_slot], device_id=peer, device_id_type=MESH
        )

    def push(self, send_slot, build, when=None):
        if when is None:
            self.copy(send_slot, build).start()
        else:
            pl.when(when())(lambda: self.copy(send_slot, build).start())
        self.later(send_slot, build, when)

    def later(self, send_slot, build, when=None):
        self.pending[send_slot] = (lambda: self.copy(send_slot, build), when)

    def keep(self, src, dst, slot, when=None):
        def go():
            pltpu.make_async_copy(src(), dst(), self.recv.at[slot]).start()

        if when is None:
            go()
        else:
            pl.when(when())(go)

    def arrived(self, dst, slot):
        pltpu.make_async_copy(dst, dst, self.recv.at[slot]).wait()

    def drain(self):
        for copy, when in self.pending.values():
            if when is None:
                copy().wait_send()
            else:
                pl.when(when())(lambda copy=copy: copy().wait_send())


def tall(row):
    padded = jnp.concatenate([row, jnp.zeros((120, 128), F32)], axis=0)
    return jnp.transpose(padded)


def erf_parts(values):
    erf = lax.erf(values * inv_sqrt_two)
    return 0.5 * (1.0 + erf)


def layer_kernel(
    tok, cot, starts, packed, cbias, pbias, table, wq, wp, wo, wu, wd,
    outs, grads, f_qp, f_o, f_u, f_d, f_small,
    att, wo_all, wu_all, wd_all, wq_half, wp_half, wp_head, xt, ct, normed_t, qcat, keys, vals, probs_a, probs_b, heads_out,
    params_col, params_row, cb_all, pb_all, kcat, own_att, starts_got,
    mid, norm, hat, inv, gout, acc_out, acc_two, tall_norm, out_t, grad_mid_t, grad_att, g_up, g_down, g_out, small,
    grad_o, head_grad, turned, turned_k, turned_v, turned_p, one_t, one_low, one_got, grad_x, sums,
    hs_qp, hs_o, hs_u, hs_d, r0_o, r0_u, r0_d, s_d,
    r1_qp, r1_o, r1_u, r1_d, r2_qp, r2_o, r2_u, r2_d, r3_qp, r3_o, r3_u, r3_d,
    all_small, got_sib, got_plane, got_z, send, recv,
):
    rows = wu_all.shape[0]
    cols = wo_all.shape[0]
    half = rows // 2
    heads = 2 * half
    k, z, c, near, far = place()
    opposite = 3 - c
    sibling = (1 - k, z, c)
    io = Copies(send, recv)
    mine = lax.div(z, half) == k
    arrived = io.arrived
    enter(rows)

    def q_block(cc):
        return wq_half.at[:, pl.ds(aligned(cc * 128, 128), 128), :]

    def p_block(cc):
        return wp_half.at[:, pl.ds(aligned(cc * 128, 128), 128), :]

    def u_block(cc, core=k):
        return wu_all.at[pl.ds(core * half, half), pl.ds(aligned(cc * 128, 128), 128), :]

    def o_block(cc, core=k):
        size = wo_all.shape[1] // 2
        return wo_all.at[cc, pl.ds(aligned(core * size, 128), size), :]

    def d_block(cc, core=k):
        size = wd_all.shape[1] // 2
        return wd_all.at[cc, pl.ds(aligned(core * size, 128), size), :]

    def q_one(i):
        return wq_half.at[i, pl.ds(aligned(c * 128, 128), 128), :]

    def p_one(i):
        return wp_half.at[i, pl.ds(aligned(c * 128, 128), 128), :]

    def u_one(i):
        return wu_all.at[k * half + i, pl.ds(aligned(c * 128, 128), 128), :]

    def o_one(i):
        size = wo_all.shape[1] // rows
        return wo_all.at[c, pl.ds(aligned((k * half + i) * size, 128), size), :]

    def d_one(i):
        size = wd_all.shape[1] // rows
        return wd_all.at[c, pl.ds(aligned((k * half + i) * size, 128), size), :]

    weights = {
        "q": (wq, q_one, q_block), "p": (wp, p_one, p_block), "o": (wo, o_one, o_block),
        "u": (wu, u_one, u_block), "d": (wd, d_one, d_block),
    }
    z_slot = {name: io.land(half) for name in weights}
    z_send = {name: io.leave(rows - 1) for name in weights}
    near_slot = {name: (io.leave(), io.land()) for name in weights}
    far_slot = {name: (io.leave(2), io.land(2)) for name in weights}
    sib_slot = {name: (io.leave(), io.land()) for name in ("o", "u", "d")}
    turn = z - k * half

    def z_start(name):
        ref, one, _ = weights[name]
        io.keep(lambda: ref, lambda: one(turn), z_slot[name] + turn, lambda: mine)
        for step in range(1, rows):
            io.push(
                z_send[name] + step - 1,
                lambda step=step: (ref, one(turn), z_slot[name] + turn, (k, lax.rem(z + step, rows), c)),
                lambda: mine,
            )

    def z_done(name):
        _, one, _ = weights[name]
        for i in range(half):
            arrived(one(i), z_slot[name] + i)

    def near_start(name):
        block = weights[name][2]
        leave, land = near_slot[name]
        io.push(leave, lambda: (block(c), block(c), land, (k, z, near)))

    def near_done(name):
        arrived(weights[name][2](near), near_slot[name][1])

    def far_start(name):
        block = weights[name][2]
        leave, land = far_slot[name]
        io.push(leave, lambda: (block(c), block(c), land, (k, z, far)))
        io.push(leave + 1, lambda: (block(near), block(near), land + 1, (k, z, far)))

    def far_done(name):
        block = weights[name][2]
        arrived(block(far), far_slot[name][1])
        arrived(block(opposite), far_slot[name][1] + 1)

    def core_half(name, core):
        if name == "u":
            return wu_all.at[pl.ds(core * half, half)]
        full = wo_all if name == "o" else wd_all
        size = full.shape[1] // 2
        return full.at[:, pl.ds(aligned(core * size, 128), size), :]

    def sib_start(name):
        leave, land = sib_slot[name]
        io.push(leave, lambda: (core_half(name, k), core_half(name, k), land, sibling))

    def sib_done(name):
        arrived(core_half(name, 1 - k), sib_slot[name][1])

    feat = tok.shape[1]
    x_slot = io.land(4)
    x_send = io.leave(4)
    xf_slot = io.land(4)
    xf_send = io.leave(4)

    def x_part(cc, core):
        return xt.at[pl.ds(aligned(cc * feat + core * (feat // 2), 64), feat // 2), :]

    def is_local(b, core):
        return jnp.logical_and(2 * b + k == c, core == k)

    z_start("q")
    for b in range(2):
        for core in range(2):

            def src(b=b, core=core):
                return tok.at[b, pl.ds(core * (feat // 2), feat // 2), :]

            def dst(core=core):
                return x_part(c, core)

            io.keep(src, dst, x_slot + c, lambda b=b, core=core: is_local(b, core))
            io.push(
                x_send + 2 * b + core,
                lambda src=src, dst=dst, b=b, core=core: (src(), dst(), x_slot + c, (0 * k + core, z, 2 * b + k)),
                lambda b=b, core=core: jnp.logical_not(is_local(b, core)),
            )
    z_start("p")

    t_slot = io.land()
    io.keep(lambda: table, lambda: kcat.at[:, pl.ds(0, table.shape[1])], t_slot)
    g_col, g_row, g_cb, g_pb = io.land(), io.land(), io.land(), io.land()
    col_send = io.leave(3)
    for step in range(1, 4):
        io.push(
            col_send + step - 1,
            lambda step=step: (packed.at[pl.ds(0, 8)], params_col.at[c], g_col, (k, z, lax.rem(c + step, 4))),
        )
    io.keep(lambda: packed.at[pl.ds(0, 8)], lambda: params_col.at[c], g_col)
    for source, target, slot in ((packed.at[pl.ds(8, 8)], params_row, g_row), (cbias, cb_all, g_cb), (pbias, pb_all, g_pb)):
        row_send = io.leave(rows - 1)
        for step in range(1, rows):
            io.push(
                row_send + step - 1,
                lambda step=step, source=source, target=target, slot=slot: (
                    source, target.at[z], slot, (k, lax.rem(z + step, rows), c)
                ),
            )
        io.keep(lambda source=source: source, lambda target=target: target.at[z], slot)
    s_slot = io.land()
    s_send = io.leave(4)
    for b in range(2):
        for core in range(2):
            io.keep(
                lambda: starts, lambda: starts_got, s_slot,
                lambda b=b, core=core: jnp.logical_and(c == z, is_local(b, core)),
            )
            io.push(
                s_send + 2 * b + core,
                lambda b=b, core=core: (starts, starts_got, s_slot, (0 * k + core, z, 2 * b + k)),
                lambda b=b, core=core: jnp.logical_and(c == z, jnp.logical_not(is_local(b, core))),
            )
    for name in ("o", "u", "d"):
        z_start(name)

    c_slot = io.land(4)
    c_send = io.leave(4)
    count = ct.shape[1]

    def cot_start():
        for b in range(2):
            for core in range(2):

                def src(b=b, core=core):
                    return cot.at[b, :, pl.ds(core * count, count)]

                def dst():
                    return ct.at[pl.ds(aligned(c * feat, 128), feat), :]

                io.keep(src, dst, c_slot + c, lambda b=b, core=core: is_local(b, core))
                io.push(
                    c_send + 2 * b + core,
                    lambda src=src, dst=dst, b=b, core=core: (src(), dst(), c_slot + c, (0 * k + core, z, 2 * b + k)),
                    lambda b=b, core=core: jnp.logical_not(is_local(b, core)),
                )

    z_done("q")
    near_start("q")
    for cc in range(4):
        arrived(x_part(cc, k), x_slot + cc)
        io.push(xf_send + cc, lambda cc=cc: (x_part(cc, k), x_part(cc, k), xf_slot + cc, sibling))
    z_done("p")
    near_start("p")
    arrived(params_col, g_col)
    arrived(params_row, g_row)
    arrived(cb_all, g_cb)
    arrived(pb_all, g_pb)
    arrived(starts_got, s_slot)
    for cc in range(4):
        arrived(x_part(cc, 1 - k), xf_slot + cc)
    near_done("q")
    far_start("q")

    columns = [tall(params_col[cc]) for cc in range(4)]
    gain = jnp.concatenate([col[:, 0:1] for col in columns], axis=0)
    bias = jnp.concatenate([col[:, 1:2] for col in columns], axis=0)
    width = xt.shape[0]
    seq = xt.shape[1]
    piece = PIECE
    blocks = seq // 256

    @pl.loop(0, blocks)
    def _(t):
        here = pl.ds(aligned(t * 256, 256), 256)
        x = xt[:, here].astype(F32)
        mean = jnp.sum(x, axis=0, keepdims=True) * (1.0 / width)
        square = jnp.sum(x * x, axis=0, keepdims=True) * (1.0 / width)
        inverse = lax.rsqrt(square - mean * mean + norm_epsilon)
        normed_t[:, here] = ((x - mean) * inverse * gain + bias).astype(BF16)

    near_done("p")
    far_start("p")
    z_done("o")
    near_start("o")
    z_done("u")
    near_start("u")
    cot_start()
    far_done("q")
    scale = 0.125
    none = jnp.zeros((256, 64), F32)

    @pl.loop(0, half * blocks)
    def _(n):
        i, t = lax.div(n, blocks), lax.rem(n, blocks)
        here = pl.ds(aligned(t * 256, 256), 256)
        got = tn(normed_t[:, here], wq_half[i])
        for hb in range(2):
            h = 2 * i + hb
            low = got[:, hb * 192 : hb * 192 + 192].astype(BF16).astype(F32)
            query, key, value = low[:, 0:64], low[:, 64:128], low[:, 128:192]
            content = cb_all[k * half + i, hb : hb + 1, :]
            position = pb_all[k * half + i, hb : hb + 1, :]
            qcat[h, here, 512:640] = jnp.concatenate(
                [(query + content) * scale, (query + position) * scale], axis=1
            ).astype(BF16)
            keys[h, here, :] = jnp.concatenate([key, none], axis=1).astype(BF16)
            vals[h, here, :] = value.astype(BF16)

    near_done("o")
    far_start("o")
    z_done("d")
    near_start("d")
    far_done("p")
    arrived(kcat.at[:, pl.ds(0, 512)], t_slot)
    for h in range(heads):
        part = wp_half[h // 2, :, (h % 2) * 64 : (h % 2) * 64 + 64]
        wp_head[h] = jnp.concatenate([jnp.zeros_like(part), part], axis=1)

    @pl.loop(0, heads * blocks)
    def _(n):
        h, t = lax.div(n, blocks), lax.rem(n, blocks)
        here = pl.ds(aligned(t * 256, 256), 256)
        angle = nt(qcat[h, here, 512:640], wp_head[h])
        cosine = kcat[here, 0:256].astype(F32)
        sine = kcat[here, 256:512].astype(F32)
        first, second = angle[:, 0:256], angle[:, 256:512]
        qcat[h, here, 0:256] = (first * sine + second * cosine).astype(BF16)
        qcat[h, here, 256:512] = (second * sine - first * cosine).astype(BF16)

    near_done("u")
    far_start("u")

    slot_len = seq // 2
    block = 256
    batch = lax.div(c, 2)

    def attend(h, low_row, keys_seen, slot):
        start = starts_got[batch, 0:1, slot : slot + 1]
        row = slot * slot_len + low_row + lax.broadcasted_iota(jnp.int32, (block, 1), 0)
        inside = jnp.logical_and(row >= start, row < start + piece)
        limit = jnp.where(inside, start + (piece - 1), row)
        here = pl.ds(aligned(slot * slot_len + low_row, block), block)
        scores = nt(qcat[h, here, :], kcat[0:keys_seen, :])
        column = slot * slot_len + lax.broadcasted_iota(jnp.int32, (block, slot_len), 1)
        last = jnp.where(column <= limit, scores[:, keys_seen - slot_len :], big_negative)
        top = jnp.max(last, axis=1, keepdims=True)
        if slot == 1:
            top = jnp.maximum(top, jnp.max(scores[:, :slot_len], axis=1, keepdims=True))
        last = jnp.exp(last - top)
        total = jnp.sum(last, axis=1, keepdims=True)
        if slot == 1:
            first = jnp.exp(scores[:, :slot_len] - top)
            total = total + jnp.sum(first, axis=1, keepdims=True)
            whole = jnp.concatenate([first, last], axis=1)
        else:
            whole = last
        low = (whole * (1.0 / total)).astype(BF16)
        probs = (probs_a, probs_b)[slot]
        probs[h, pl.ds(aligned(low_row, block), block), :] = low
        heads_out[h, here, :] = nn(low, vals[h, 0:keys_seen, :]).astype(BF16)

    def far_d():
        near_done("d")
        far_start("d")

    def sib_o():
        far_done("o")
        sib_start("o")

    def sib_u():
        far_done("u")
        sib_start("u")

    def ticks(h, slot, t, actions):
        for number, action in actions.items():
            if (number % 4) // 2 == slot:
                pl.when(4 * h + 2 * slot + t == number)(action)

    ahead = {6: far_d, 7: sib_o, 12: sib_u}

    @pl.loop(0, heads)
    def _(h):
        kcat[:, 512:640] = keys[h]

        @pl.loop(0, slot_len // block)
        def _(t):
            attend(h, t * block, slot_len, 0)
            ticks(h, 0, t, ahead)

        @pl.loop(0, slot_len // block)
        def _(t):
            attend(h, t * block, seq, 1)
            ticks(h, 1, t, ahead)

    own_att[...] = jnp.concatenate([heads_out[h] for h in range(heads)], axis=1)
    a_slot, a_send = io.land(2), io.leave()
    span = own_att.shape[1]
    other = pl.ds(aligned((1 - k) * count, count), count)
    own = pl.ds(aligned(k * count, count), count)
    att_part = att.at[:, pl.ds(aligned(k * span, 128), span)]
    io.push(a_send, lambda: (own_att.at[other, :], att_part, a_slot, sibling))
    io.keep(lambda: own_att.at[own, :], lambda: att_part, a_slot + 1)
    for cc in range(4):
        arrived(ct.at[pl.ds(cc * feat, feat), :], c_slot + cc)
    gout[...] = jnp.transpose(ct[...])
    sib_done("o")
    arrived(own_att.at[own, :], a_slot + 1)
    arrived(own_att.at[own, :], a_slot)

    far_done("d")
    sib_start("d")

    def line(index):
        return jnp.concatenate([params_col[cc, index : index + 1, :] for cc in range(cols)], axis=1)

    def out_weight():
        return jnp.concatenate([wo_all[cc] for cc in range(cols)], axis=1)

    x = jnp.transpose(xt[:, own].astype(F32))
    middle = x + nn(att[...], out_weight())
    mid[...] = middle
    mean = jnp.sum(middle, axis=1, keepdims=True) * (1.0 / width)
    square = jnp.sum(middle * middle, axis=1, keepdims=True) * (1.0 / width)
    inverse = lax.rsqrt(square - mean * mean + norm_epsilon)
    scaled = (middle - mean) * inverse
    hat[...] = scaled
    inv[...] = inverse
    low = (scaled * line(2) + line(3)).astype(BF16)
    norm[...] = low
    tall_norm[...] = jnp.transpose(low)
    acc_out[...] = jnp.zeros_like(acc_out)
    acc_two[...] = jnp.zeros_like(acc_two)
    small[...] = jnp.zeros_like(small)
    hidden = wu_all.shape[2]

    part_rows = wd_all.shape[1] // rows // 2
    u0_slot = (io.leave(half), io.land(half))
    o0_slot = (io.leave(), io.land())
    d0_slot = (io.leave(rows), io.land(rows))
    u_slot = {"one": (io.leave(2 * half), io.land(2 * half)), "two": (io.leave(half), io.land(half)), "z": (io.leave(half), io.land(rows))}
    o_slot = {"one": (io.leave(2), io.land(2)), "two": (io.leave(), io.land()), "z": (io.leave(half), io.land(rows))}
    d_slot = {"one": (io.leave(2), io.land(2)), "two": (io.leave(), io.land()), "z": (io.leave(rows), io.land(rows))}
    qp_slot = {
        "one": (io.leave(2 * heads), io.land(2 * heads)), "two": (io.leave(heads), io.land(heads)),
        "z": (io.leave(heads), io.land(2 * rows)),
    }
    last_slot = {name: (io.leave(), io.land()) for name in ("u", "o", "d", "qp")}

    def load(ref):
        return ref[...].astype(F32)

    def add(to, term):
        to[...] = (load(to) + load(term)).astype(BF16)

    def near_on(first, leave, land, target):
        io.push(leave, lambda: (first(), target(), land, (k, z, near)))

    def u_sib(j):
        leave, land = u0_slot
        io.push(leave + j, lambda: (g_up.at[(1 - k) * half + j], r0_u.at[j], land + j, sibling))

    def u_one(j):
        arrived(r0_u.at[j], u0_slot[1] + j)
        total = load(g_up.at[k * half + j]) + load(r0_u.at[j])
        hs_u[j] = total.astype(BF16).reshape(hs_u.shape[1:])
        leave, land = u_slot["one"]
        io.push(leave + 2 * j, lambda: (hs_u.at[j, far], r1_u.at[j, 0], land + 2 * j, (k, z, far)))
        io.push(leave + 2 * j + 1, lambda: (hs_u.at[j, 3 - c], r1_u.at[j, 1], land + 2 * j + 1, (k, z, far)))

    def u_two(j):
        land = u_slot["one"][1] + 2 * j
        arrived(r1_u.at[j, 1], land + 1)
        add(r1_u.at[j, 1], hs_u.at[j, near])
        near_on(lambda: r1_u.at[j, 1], u_slot["two"][0] + j, u_slot["two"][1] + j, lambda: r2_u.at[j])
        arrived(r1_u.at[j, 0], land)
        add(r1_u.at[j, 0], hs_u.at[j, c])

    def u_z(j):
        arrived(r2_u.at[j], u_slot["two"][1] + j)
        add(r2_u.at[j], r1_u.at[j, 0])
        leave, land = u_slot["z"]
        io.push(
            leave + j, lambda: (r2_u.at[j], r3_u.at[z], land + z, (k, k * half + j, c)), lambda: z != k * half + j
        )

    def z_total(total, r3, land, hb=None):
        for step in range(1, rows):
            source = lax.rem(z + step, rows)
            part = r3.at[source] if hb is None else r3.at[hb, source]
            arrived(part, land + source)
            total = total + load(part)
        return total

    def finish(name, to):
        leave, land = last_slot[name]
        io.push(leave, lambda: (to, to, land, sibling), lambda: mine)

    def u_last():
        @pl.when(mine)
        def _():
            f_u[...] = z_total(load(r2_u.at[turn]), r3_u, u_slot["z"][1])

        finish("u", f_u)

    def o_sib():
        leave, land = o0_slot
        size = g_out.shape[1] // 2
        io.push(leave, lambda: (g_out.at[:, pl.ds(aligned((1 - k) * size, 128), size), :], r0_o, land, sibling))

    def o_one():
        arrived(r0_o, o0_slot[1])
        size = g_out.shape[1] // 2
        for cc in range(cols):
            total = load(g_out.at[cc, pl.ds(aligned(k * size, 128), size), :]) + load(r0_o.at[cc])
            hs_o[cc] = total.astype(BF16).reshape(hs_o.shape[1:])
        leave, land = o_slot["one"]
        io.push(leave, lambda: (hs_o.at[far], r1_o.at[0], land, (k, z, far)))
        io.push(leave + 1, lambda: (hs_o.at[3 - c], r1_o.at[1], land + 1, (k, z, far)))

    def o_two():
        land = o_slot["one"][1]
        arrived(r1_o.at[1], land + 1)
        add(r1_o.at[1], hs_o.at[near])
        near_on(lambda: r1_o.at[1], o_slot["two"][0], o_slot["two"][1], lambda: r2_o)
        arrived(r1_o.at[0], land)
        add(r1_o.at[0], hs_o.at[c])

    def o_z():
        arrived(r2_o, o_slot["two"][1])
        add(r2_o, r1_o.at[0])
        leave, land = o_slot["z"]
        for j in range(half):
            io.push(
                leave + j,
                lambda j=j: (r2_o.at[j], r3_o.at[z], land + z, (k, k * half + j, c)),
                lambda j=j: z != k * half + j,
            )

    def o_last():
        @pl.when(mine)
        def _():
            f_o[...] = z_total(load(r2_o.at[turn]), r3_o, o_slot["z"][1])

        finish("o", f_o)

    def d_part(r, core):
        return g_down.at[:, pl.ds(aligned((2 * r + core) * part_rows, 128), part_rows), :]

    def d_sib(r, number):
        leave, land = d0_slot
        io.push(leave + number, lambda: (d_part(r(), 1 - k), r0_d.at[r()], land + r(), sibling))

    def d_z(r, number):
        arrived(r0_d.at[r()], d0_slot[1] + r())
        hs_d[r()] = (load(d_part(r(), k)) + load(r0_d.at[r()])).astype(BF16)
        leave, land = d_slot["z"]
        io.push(leave + number, lambda: (hs_d.at[r()], r3_d.at[z], land + z, (k, r(), c)), lambda: z != r())

    def d_one():
        s_d[...] = z_total(load(hs_d.at[z]), r3_d, d_slot["z"][1]).astype(BF16)
        leave, land = d_slot["one"]
        io.push(leave, lambda: (s_d.at[far], r1_d.at[0], land, (k, z, far)))
        io.push(leave + 1, lambda: (s_d.at[3 - c], r1_d.at[1], land + 1, (k, z, far)))

    def d_two():
        land = d_slot["one"][1]
        arrived(r1_d.at[1], land + 1)
        add(r1_d.at[1], s_d.at[near])
        near_on(lambda: r1_d.at[1], d_slot["two"][0], d_slot["two"][1], lambda: r2_d)
        arrived(r1_d.at[0], land)
        add(r1_d.at[0], s_d.at[c])

    def d_last():
        arrived(r2_d, d_slot["two"][1])
        leave, land = last_slot["d"]
        f_d[pl.ds(aligned(k * part_rows, 128), part_rows), :] = load(r2_d) + load(r1_d.at[0])

        def of_core():
            return f_d.at[pl.ds(aligned(k * part_rows, 128), part_rows), :]

        io.push(leave, lambda: (of_core(), of_core(), land, sibling))

    def qp_builds(h):
        leave, land = qp_slot["one"]
        return (
            (leave + 2 * h, lambda: (hs_qp.at[h, far], r1_qp.at[h, 0], land + 2 * h, (k, z, far))),
            (leave + 2 * h + 1, lambda: (hs_qp.at[h, opposite], r1_qp.at[h, 1], land + 2 * h + 1, (k, z, far))),
        )

    def qp_one(h):
        found = nt(turned[h], normed_t[...]).astype(BF16)
        position = turned_p[h].astype(BF16)
        for cc in range(cols):
            hs_qp[h, cc, 0:192, :] = found[:, cc * 128 : cc * 128 + 128]
            hs_qp[h, cc, 192:256, :] = position[:, cc * 128 : cc * 128 + 128]
        for leave, build in qp_builds(h):
            io.copy(leave, build).start()

    for h in range(heads):
        for leave, build in qp_builds(h):
            io.later(leave, build)

    def qp_two(h):
        land = qp_slot["one"][1] + 2 * h
        arrived(r1_qp.at[h, 1], land + 1)
        add(r1_qp.at[h, 1], hs_qp.at[h, near])
        near_on(lambda: r1_qp.at[h, 1], qp_slot["two"][0] + h, qp_slot["two"][1] + h, lambda: r2_qp.at[h])
        arrived(r1_qp.at[h, 0], land)
        add(r1_qp.at[h, 0], hs_qp.at[h, c])

    def qp_z(h):
        arrived(r2_qp.at[h], qp_slot["two"][1] + h)
        add(r2_qp.at[h], r1_qp.at[h, 0])
        leave, land = qp_slot["z"]
        io.push(
            leave + h,
            lambda: (r2_qp.at[h], r3_qp.at[h % 2, z], land + (h % 2) * rows + z, (k, k * half + h // 2, c)),
            lambda: z != k * half + h // 2,
        )

    def qp_last():
        @pl.when(mine)
        def _():
            for hb in range(2):
                f_qp[hb] = z_total(load(r2_qp.at[2 * turn + hb]), r3_qp, qp_slot["z"][1] + hb * rows, hb)

        finish("qp", f_qp)

    def last_done():
        @pl.when(jnp.logical_not(mine))
        def _():
            for name, to in (("u", f_u), ("o", f_o), ("qp", f_qp)):
                arrived(to, last_slot[name][1])

        arrived(f_d.at[pl.ds(aligned((1 - k) * part_rows, 128), part_rows), :], last_slot["d"][1])

    origin = lax.rem(c, 2)
    out_slot, grad_slot = (io.leave(4), io.land(4)), (io.leave(4), io.land(4))

    def back_start(src, dst, pair):
        leave, base = pair
        for step in range(4):

            def part(step=step):
                return src.at[pl.ds(aligned(lax.rem(c + step, 4) * feat, 128), feat), :]

            def landing():
                return dst.at[batch, k]

            if step == 0:
                io.keep(part, landing, base + 2 * batch + k, lambda: origin == k)
                io.push(
                    leave + step,
                    lambda part=part, landing=landing: (part(), landing(), base + 2 * batch + k, sibling),
                    lambda: origin != k,
                )
            else:
                io.push(
                    leave + step,
                    lambda part=part, landing=landing, step=step: (
                        part(), landing(), base + 2 * batch + k, (origin, z, lax.rem(c + step, 4))
                    ),
                )

    def back_done(dst, pair):
        base = pair[1]
        for b in range(2):
            for core in range(2):
                arrived(dst.at[b, core], base + 2 * b + core)


    def rows_of(number):
        core = k if number % 2 == 0 else 1 - k
        return core * half + number // 2

    def after_one():
        u_sib(0)
        for number in range(2):
            d_sib(lambda number=number: rows_of(number), number)

    def after_two():
        u_one(0)
        for number in range(2):
            d_z(lambda number=number: rows_of(number), number)

    @pl.loop(0, rows)
    def _(step):
        turn_of = lax.rem(step, 2)
        r = ((1 - turn_of) * k + turn_of * (1 - k)) * half + lax.div(step, 2)

        @pl.when(step == 1)
        def _():
            for name in ("u", "d"):
                sib_done(name)

        here = pl.ds(aligned(r * hidden, hidden), hidden)
        bias = jnp.concatenate([params_row[r, j : j + 1, :] for j in range(hidden // 128)], axis=1)
        down = jnp.concatenate([wd_all[cc, here, :] for cc in range(cols)], axis=1)
        pre = nn(norm[...], wu_all[r]) + bias
        grad_act = nt(gout[...], down)
        lower = erf_parts(pre)
        act = (pre * lower).astype(BF16)
        slope = lower + pre * jnp.exp(-0.5 * pre * pre) * inv_sqrt_tau
        low_grad = (grad_act * slope).astype(BF16)
        small[pl.ds(5 + r, 1), :] = jnp.sum(low_grad.astype(F32), axis=0, keepdims=True)
        acc_out[...] += nn(act, down)
        acc_two[...] += nt(low_grad, wu_all[r])
        g_up[r] = nn(tall_norm[...], low_grad).astype(BF16)
        found = tn(act, gout[...]).astype(BF16)
        for cc in range(cols):
            g_down[cc, here, :] = found[:, cc * 128 : cc * 128 + 128]
        pl.when(step == 1)(after_one)
        pl.when(step == 2)(after_two)

    u_sib(1)
    for number in range(2, 4):
        d_sib(lambda number=number: rows_of(number), number)
    cotangent = gout[...].astype(F32)
    out_t[...] = jnp.transpose(mid[...] + acc_out[...] + line(4)).astype(BF16)
    back_start(out_t, outs, out_slot)
    two = acc_two[...]
    small[2:3, :] = jnp.sum(two * hat[...], axis=0, keepdims=True)
    small[3:4, :] = jnp.sum(two, axis=0, keepdims=True)
    small[4:5, :] = jnp.sum(cotangent, axis=0, keepdims=True)
    shifted = two * line(2)
    first = jnp.sum(shifted, axis=1, keepdims=True) * (1.0 / width)
    second = jnp.sum(shifted * hat[...], axis=1, keepdims=True) * (1.0 / width)
    grad_mid = cotangent + inv[...] * (shifted - first - hat[...] * second)
    branch = grad_mid.astype(BF16)
    grad_att[...] = nt(branch, out_weight()).astype(BF16)
    e_slot, e_send = io.land(2), io.leave()
    io.push(
        e_send,
        lambda: (grad_att.at[:, pl.ds(aligned((1 - k) * span, 128), span)], grad_o.at[own, :], e_slot, sibling),
    )
    io.keep(
        lambda: grad_att.at[:, pl.ds(aligned(k * span, 128), span)], lambda: grad_o.at[own, :], e_slot + 1
    )
    grad_mid_t[...] = jnp.transpose(grad_mid)
    found = tn(att[...], branch).astype(BF16)
    for cc in range(cols):
        g_out[cc] = found[:, cc * 128 : cc * 128 + 128]
    o_sib()
    u_one(1)
    for number in range(2, 4):
        d_z(lambda number=number: rows_of(number), number)
    one_t[...] = jnp.zeros_like(one_t)
    sums[...] = jnp.zeros_like(sums)
    arrived(grad_o.at[own, :], e_slot + 1)
    arrived(grad_o.at[own, :], e_slot)
    for h in range(heads):
        head_grad[h] = grad_o[:, h * 64 : h * 64 + 64]

    def attend_back(h, low_row, keys_seen, slot):
        at = pl.ds(aligned(low_row, block), block)
        here = pl.ds(aligned(slot * slot_len + low_row, block), block)
        grad = head_grad[h, here, :]
        low = (probs_a, probs_b)[slot][h, at, :]
        inner = jnp.sum(grad.astype(F32) * heads_out[h, here, :].astype(F32), axis=1, keepdims=True)
        grad_prob = nt(grad, vals[h, 0:keys_seen, :])
        grad_score = (low.astype(F32) * (grad_prob - inner)).astype(BF16)
        turned_v[:, 0:keys_seen] += tn(grad, low)
        turned_k[:, 0:keys_seen] += tn(qcat[h, here, 512:576], grad_score)
        got = nn(grad_score, kcat[0:keys_seen, :])
        cosine = kcat[here, 0:256].astype(F32)
        sine = kcat[here, 256:512].astype(F32)
        first, second = got[:, 0:256], got[:, 256:512]
        angle = jnp.concatenate([first * sine - second * cosine, first * cosine + second * sine], axis=1).astype(BF16)
        both = got[:, 512:640] + nn(angle, wp_head[h])
        turned_p[h] += tn(qcat[h, here, 512:640], angle)[64:128]
        sums[pl.ds(h, 1), :] += jnp.sum(both, axis=0, keepdims=True) * 0.125
        query = (both + pltpu.roll(both, 64, 1)) * 0.125
        turned[h, 0:64, here] = jnp.transpose(query)[0:64].astype(BF16)

    def both(*actions):
        def run():
            for action in actions:
                action()

        return run

    behind = {
        0: both(o_one, lambda: u_two(0)), 6: lambda: u_two(1), 7: o_two, 9: lambda: u_z(0), 10: lambda: qp_two(0),
        11: lambda: u_z(1), 12: o_z, 13: lambda: qp_two(1), 14: lambda: qp_z(0),
    }

    @pl.loop(0, heads)
    def _(h):
        kcat[:, 512:640] = keys[h]
        turned_k[...] = jnp.zeros_like(turned_k)
        turned_v[...] = jnp.zeros_like(turned_v)
        turned_p[h] = jnp.zeros(turned_p.shape[1:], F32)

        @pl.loop(0, slot_len // block)
        def _(t):
            attend_back(h, t * block, slot_len, 0)
            ticks(h, 0, t, behind)

        @pl.loop(0, slot_len // block)
        def _(t):
            attend_back(h, t * block, seq, 1)
            ticks(h, 1, t, behind)

        turned[h, 64:128, :] = turned_k[...].astype(BF16)
        turned[h, 128:192, :] = turned_v[...].astype(BF16)
        qp_one(h)

        @pl.when(lax.rem(h, 2) == 1)
        def _():
            i = lax.div(h, 2)
            pair = jnp.concatenate([turned[2 * i], turned[2 * i + 1]], axis=0)
            one_t[...] += nn(wq_half[i], pair)

    one_low[...] = one_t[:, other].astype(BF16)
    f_slot, f_send = io.land(), io.leave()
    io.push(f_send, lambda: (one_low, one_got, f_slot, sibling))
    qp_two(2)
    qp_z(1)
    arrived(one_got, f_slot)
    columns = [tall(params_col[cc]) for cc in range(cols)]
    gain = jnp.concatenate([col[:, 0:1] for col in columns], axis=0)
    one = one_t[:, own] + one_got[...].astype(F32)
    x = xt[:, own].astype(F32)
    mean = jnp.sum(x, axis=0, keepdims=True) * (1.0 / width)
    square = jnp.sum(x * x, axis=0, keepdims=True) * (1.0 / width)
    inverse = lax.rsqrt(square - mean * mean + norm_epsilon)
    scaled = (x - mean) * inverse
    shifted = one * gain
    first = jnp.sum(shifted, axis=0, keepdims=True) * (1.0 / width)
    second = jnp.sum(shifted * scaled, axis=0, keepdims=True) * (1.0 / width)
    gain_sum = jnp.sum(one * scaled, axis=1, keepdims=True)
    bias_sum = jnp.sum(one, axis=1, keepdims=True)
    lane = lax.broadcasted_iota(jnp.int32, (width, 128), 1)
    pair = jnp.where(lane == 0, gain_sum, jnp.where(lane == 1, bias_sum, 0.0))
    pair = jnp.transpose(pair)[0:8]
    all_small[0] = small[...]
    all_small[0, 0:2, :] = pair[0:2]

    def spread(first_lane):
        row = jnp.concatenate([sums[h : h + 1, first_lane : first_lane + 64] for h in range(heads)], axis=1)
        blank = jnp.zeros_like(row)
        return jnp.where(k == 0, jnp.concatenate([row, blank], axis=1), jnp.concatenate([blank, row], axis=1))

    all_small[0, 9:10, :] = spread(0)
    all_small[0, 10:11, :] = spread(64)
    m_slot, m_send = io.land(), io.leave()
    p_slot, p_send = io.land(), io.leave(3)
    v_slot, v_send = io.land(), io.leave(rows - 1)
    io.push(m_send, lambda: (all_small.at[0], got_sib, m_slot, sibling))
    grad_x[...] = (grad_mid_t[...] + inverse * (shifted - first - scaled * second)).astype(BF16)
    arrived(got_sib, m_slot)
    all_small[1] = all_small[0] + got_sib[...]
    for step in range(1, 4):
        io.push(
            p_send + step - 1, lambda step=step: (all_small.at[1], got_plane.at[c], p_slot, (k, z, lax.rem(c + step, 4)))
        )
    io.keep(lambda: all_small.at[1], lambda: got_plane.at[c], p_slot)
    back_start(grad_x, grads, grad_slot)
    qp_two(3)
    d_one()
    qp_z(2)
    arrived(got_plane, p_slot)
    all_small[2] = (got_plane[0] + got_plane[1]) + (got_plane[2] + got_plane[3])
    for step in range(1, rows):
        io.push(
            v_send + step - 1, lambda step=step: (all_small.at[2], got_z.at[z], v_slot, (k, lax.rem(z + step, rows), c))
        )
    io.keep(lambda: all_small.at[2], lambda: got_z.at[z], v_slot)
    u_last()
    o_last()
    d_two()
    qp_z(3)
    d_last()
    arrived(got_z, v_slot)
    f_small[...] = (got_z[0] + got_z[1]) + (got_z[2] + got_z[3])
    qp_last()
    back_done(outs, out_slot)
    back_done(grads, grad_slot)
    last_done()
    io.drain()


def final_kernel(
    outs, grads, f_qp, f_o, f_u, f_d, f_small,
    output, grad_tokens, g1, b1, q_w, c_b, p_b, p_w, o_w, g2, b2, u_w, u_b, d_w, d_b,
):
    k, z, c, _, _ = place()
    for b in range(2):
        for core in range(2):
            size = outs.shape[3]
            output[b, :, core * size : core * size + size] = outs[b, core].astype(F32)
            grad_tokens[b, :, core * size : core * size + size] = grads[b, core].astype(F32)
    for core in range(2):

        @pl.when(k == core)
        def _(core=core):
            q_w[...] = f_qp[core, 0:192, :]
            p_w[...] = f_qp[core, 192:256, :]
            for ref, source in ((o_w, f_o), (d_w, f_d)):
                size = ref.shape[0]
                ref[...] = jnp.transpose(source[:, core * size : core * size + size])
            size = u_w.shape[1]
            u_w[...] = f_u[:, core * size : core * size + size]

    width = f_small.shape[1]
    chip = z * 4 + c
    share = g1.shape[1]
    first = pltpu.roll(f_small[0:8, :], lax.rem(width - (chip * 2 + k) * share, width), 1)
    for row, ref in ((0, g1), (1, b1), (2, g2), (3, b2), (4, d_b)):
        ref[...] = first[row : row + 1, 0:share]
    share = u_b.shape[1]
    line = f_small[pl.ds(5 + z, 1), :]
    line = jnp.broadcast_to(line, (8, width))
    u_b[...] = pltpu.roll(line, lax.rem(width - (c * 2 + k) * share, width), 1)[0:1, 0:share]
    heads, share = c_b.shape
    third = pltpu.roll(f_small[8:16, :], lax.rem(2 * width - heads * 64 * z - (c * 2 + k) * share, width), 1)
    for h in range(heads):
        c_b[h : h + 1, :] = third[1:2, h * 64 : h * 64 + share]
        p_b[h : h + 1, :] = third[2:3, h * 64 : h * 64 + share]


def position_table(seq_len, feature_count):
    positions = np.arange(seq_len, dtype=np.float64)
    exponent = -np.arange(0, feature_count, 2, dtype=np.float64) / feature_count
    angles = positions[:, None] * (10000.0**exponent)[None, :]
    return np.concatenate([np.cos(angles), np.sin(angles)], axis=1).astype(jnp.bfloat16)


def fast_shards(
    tokens, cotangent, piece_starts, ln1_gain, ln1_bias, qkv_weight, content_bias, position_bias, pos_weight,
    out_weight, ln2_gain, ln2_bias, up_weight, up_bias, down_weight, down_bias,
):
    rows, cols = lax.axis_size("row"), lax.axis_size("col")
    half = rows // 2
    micro, feat, seq = tokens.shape
    width = feat * cols
    count = seq // 2
    hidden = up_weight.shape[1]
    heads = content_bias.shape[0] * half
    table = jnp.asarray(position_table(seq, width))
    lines = [ln1_gain, ln1_bias, ln2_gain, ln2_bias, down_bias]
    places = [(line, index * feat) for index, line in enumerate(lines)] + [(up_bias, 8 * 128)]
    packed = sum(jnp.pad(line.astype(F32), (at, 16 * 128 - at - line.shape[0])) for line, at in places)
    packed = packed.reshape(16, 128)
    vm = pl.BlockSpec(memory_space=pltpu.VMEM)
    anywhere = pl.BlockSpec(memory_space=pl.ANY)
    limit = 64 * 1024 * 1024 - 128 * 1024

    def shape(dims, kind=BF16):
        return jax.ShapeDtypeStruct(dims, kind)

    def vmem(dims, kind=BF16):
        return pltpu.VMEM(dims, kind)

    q_cols, p_cols = qkv_weight.shape[1], pos_weight.shape[1]
    o_rows, d_rows = out_weight.shape[0], down_weight.shape[0]
    qp, part = (256, feat), (d_rows // 2, 128)
    results = pl.pallas_call(
        layer_kernel,
        name="layer",
        out_shape=(
            shape((micro, 2, feat, count)),
            shape((micro, 2, feat, count)),
        )
        + (
            shape((2,) + qp, F32), shape((o_rows, 128), F32), shape((feat, hidden), F32), shape((d_rows, 128), F32),
            shape((16, width), F32),
        ),
        in_specs=[anywhere, anywhere, vm, vm, vm, vm] + [anywhere] * 6,
        out_specs=(vm,) * 7,
        scratch_shapes=[
            vmem((count, width)),
            vmem((cols, width, 128)),
            vmem((rows, width, hidden)),
            vmem((cols, rows * hidden, 128)),
            vmem((half, width, q_cols)),
            vmem((half, width, p_cols)),
            vmem((heads, width, 128)),
            vmem((width, seq)),
            vmem((width, count)),
            vmem((width, seq)),
            vmem((heads, seq, width + 128)),
            vmem((heads, seq, 128)),
            vmem((heads, seq, 64)),
            vmem((heads, count, count)),
            vmem((heads, count, seq)),
            vmem((heads, seq, 64)),
            vmem((cols, 8, 128), F32),
            vmem((rows, 8, 128), F32),
            vmem((rows,) + content_bias.shape, F32),
            vmem((rows,) + position_bias.shape, F32),
            vmem((seq, width + 128)),
            vmem((seq, heads * 64)),
            vmem(piece_starts.shape, jnp.int32),
            vmem((count, width), F32),
            vmem((count, width)),
            vmem((count, width), F32),
            vmem((count, 1), F32),
            vmem((count, width)),
            vmem((count, width), F32),
            vmem((count, width), F32),
            vmem((width, count)),
            vmem((width, count)),
            vmem((width, count), F32),
            vmem((count, width)),
            vmem((rows, width, hidden)),
            vmem((cols, rows * hidden, 128)),
            vmem((cols, width, 128)),
            vmem((16, width), F32),
            vmem((seq, heads * 64)),
            vmem((heads, seq, 64)),
            vmem((heads, 192, seq)),
            vmem((64, seq), F32),
            vmem((64, seq), F32),
            vmem((heads, 64, width), F32),
            vmem((width, seq), F32),
            vmem((width, count)),
            vmem((width, count)),
            vmem((width, count)),
            vmem((8, 128), F32),
            vmem((heads, cols) + qp),
            vmem((cols, half, o_rows, 128)),
            vmem((half, cols, feat, hidden)),
            vmem((rows, cols) + part),
            vmem((cols, half * o_rows, 128)),
            vmem((half, width, hidden)),
            vmem((rows, cols) + part),
            vmem((cols,) + part),
            vmem((heads, 2) + qp),
            vmem((2, half, o_rows, 128)),
            vmem((half, 2, feat, hidden)),
            vmem((2,) + part),
            vmem((heads,) + qp),
            vmem((half, o_rows, 128)),
            vmem((half, feat, hidden)),
            vmem(part),
            vmem((2, rows) + qp),
            vmem((rows, o_rows, 128)),
            vmem((rows, feat, hidden)),
            vmem((rows, cols) + part),
            vmem((3, 16, width), F32),
            vmem((16, width), F32),
            vmem((cols, 16, width), F32),
            vmem((rows, 16, width), F32),
            pltpu.SemaphoreType.DMA((126,)),
            pltpu.SemaphoreType.DMA((117,)),
        ],
        compiler_params=pltpu.CompilerParams(collective_id=0, has_side_effects=True, vmem_limit_bytes=limit),
    )(
        tokens, cotangent, piece_starts, packed, content_bias, position_bias, table,
        qkv_weight, pos_weight, out_weight, up_weight, down_weight,
    )
    devices = 2 * rows * cols
    vec = shape((1, width // devices), F32)
    bias = shape((content_bias.shape[0], 64 // (2 * cols)), F32)
    done = list(pl.pallas_call(
        final_kernel,
        name="final",
        out_shape=(
            shape(tokens.shape, F32), shape(tokens.shape, F32), vec, vec,
            shape((q_cols // 2, feat), F32), bias, bias, shape((p_cols // 2, feat), F32), shape((64, o_rows), F32), vec, vec,
            shape((feat, hidden // 2), F32), shape((1, rows * hidden // devices), F32), shape((64, d_rows), F32), vec,
        ),
        in_specs=[vm] * 7,
        out_specs=(vm,) * 15,
        compiler_params=pltpu.CompilerParams(vmem_limit_bytes=limit),
    )(*results))
    for index in (4, 7, 8, 13):
        done[index] = done[index].T
    return tuple(v.reshape(-1) if v.shape[0] == 1 else v for v in done)


def solution(mesh):
    in_specs = (
        P(None, "col", ("dp", "row")),
        P(None, "col", ("dp", "row")),
        P(None, ("dp", "col"), None),
        P("col"),
        P("col"),
        P("col", "row"),
        P("row", None),
        P("row", None),
        P("col", "row"),
        P("row", "col"),
        P("col"),
        P("col"),
        P("col", "row"),
        P("row"),
        P("row", "col"),
        P("col"),
    )
    out_specs = (
        P(None, "col", ("dp", "row")),
        P(None, "col", ("dp", "row")),
        P(("row", "col", "dp")),
        P(("row", "col", "dp")),
        P("col", ("row", "dp")),
        P("row", ("col", "dp")),
        P("row", ("col", "dp")),
        P("col", ("row", "dp")),
        P("row", ("col", "dp")),
        P(("row", "col", "dp")),
        P(("row", "col", "dp")),
        P("col", ("row", "dp")),
        P(("row", "col", "dp")),
        P("row", ("col", "dp")),
        P(("row", "col", "dp")),
    )

    def layer(tokens, *others):
        dp, row, col = mesh.shape["dp"], mesh.shape["row"], mesh.shape["col"]
        one_each = tokens.shape[2] == dp * row * SEQ_LEN and tokens.shape[0] * dp == col
        body = fast_shards if one_each and dp == 2 and row == col == 4 else shards
        part = jax.shard_map(body, mesh=mesh, in_specs=in_specs, out_specs=out_specs, check_vma=False)
        return part(tokens, *others)

    return layer
```

```python
from functools import reduce

import jax
import jax.numpy as jnp
import numpy as np
from jax import lax
from jax.experimental import pallas as pl
from jax.experimental.pallas import tpu as pltpu
from jax.sharding import PartitionSpec as P

D = 512
SEQ_LEN = 1024
PIECE = 256


norm_epsilon = 1e-05
big_negative = -1e30
inv_sqrt_two = 0.7071067811865476
inv_sqrt_tau = 0.3989422804014327


def contract(left_op, right_op, flipped):
    if flipped:
        return lax.dot_general(
            left_op, right_op, (((1,), (1,)), ((), ())), preferred_element_type=jnp.float32
        )
    return jnp.dot(left_op, right_op, preferred_element_type=jnp.float32)


def outer_sum(left_op, right_op):
    return lax.dot_general(
        left_op, right_op, (((0,), (0,)), ((), ())), preferred_element_type=jnp.float32
    )


def gather_rows(values):
    return lax.all_gather(values, "row", axis=0, tiled=True)


def gather_cols(values):
    return lax.all_gather(values, "col", axis=0, tiled=True)


def sum_over_cols(gathered, weight, flipped):
    share_rows = gathered.shape[0] // lax.axis_size("col")

    def partial_term(offset, amount):
        return contract(gathered, weight, flipped)

    return lax.psum_scatter(
        partial_term(jnp.int32(0), lax.axis_size("col") * share_rows),
        "col",
        scatter_dimension=0,
        tiled=True,
    )


def sum_over_rows(gathered, weight, flipped):
    share_rows = gathered.shape[0] // lax.axis_size("row")

    def partial_term(offset, amount):
        return contract(gathered, weight, flipped)

    return lax.psum_scatter(
        partial_term(jnp.int32(0), lax.axis_size("row") * share_rows),
        "row",
        scatter_dimension=0,
        tiled=True,
    )


def feature_sums(first_sum, second_sum):
    return lax.psum((first_sum, second_sum), "col")


def normalize(values, gain, bias):
    feature_count = values.shape[1] * lax.axis_size("col")
    total_row, square_row = feature_sums(jnp.sum(values, axis=1), jnp.sum(values * values, axis=1))
    mean_row = total_row / feature_count
    inverse = lax.rsqrt(square_row / feature_count - mean_row * mean_row + norm_epsilon)
    scaled = (values - mean_row[:, None]) * inverse[:, None]
    return (scaled * gain + bias, scaled, inverse)


def normalize_back(grad_in, scaled, inverse, gain):
    feature_count = grad_in.shape[1] * lax.axis_size("col")
    shifted = grad_in * gain
    first_sum, second_sum = feature_sums(
        jnp.sum(shifted, axis=1), jnp.sum(shifted * scaled, axis=1)
    )
    back_rows = inverse[:, None] * (
        shifted - first_sum[:, None] / feature_count - scaled * second_sum[:, None] / feature_count
    )
    return (back_rows, jnp.sum(grad_in * scaled, axis=0), jnp.sum(grad_in, axis=0))


def gelu_exact(values):
    return 0.5 * values * (1.0 + jax.scipy.special.erf(values * inv_sqrt_two))


def gelu_slope(values):
    return (
        0.5 * (1.0 + jax.scipy.special.erf(values * inv_sqrt_two))
        + values * jnp.exp(-0.5 * values * values) * inv_sqrt_tau
    )


def sinusoid_table(seq_len, feature_count):
    offsets = jnp.arange(2 * seq_len - 1, dtype=jnp.float32) - (seq_len - 1)
    frequency = 10000.0 ** (-jnp.arange(0, feature_count, 2, dtype=jnp.float32) / feature_count)
    angles = offsets[:, None] * frequency[None, :]
    return jnp.concatenate([jnp.sin(angles), jnp.cos(angles)], axis=1).astype(jnp.bfloat16)


def piece_labels(positions, starts, piece_len):
    inside = (positions[:, None] >= starts[None, :]) & (
        positions[:, None] < starts[None, :] + piece_len
    )
    numbers = jnp.arange(1, starts.shape[0] + 1, dtype=jnp.int32)
    return jnp.sum(jnp.where(inside, numbers[None, :], 0), axis=1) - 1


def block_mask(offset, block_len, labels):
    positions = jnp.arange(labels.shape[0], dtype=jnp.int32)
    row_pos = offset + jnp.arange(block_len, dtype=jnp.int32)
    row_labels = lax.dynamic_slice_in_dim(labels, offset, block_len, 0)
    same_piece = (row_labels[:, None] == labels[None, :]) & (row_labels[:, None] >= 0)
    return (positions[None, :] <= row_pos[:, None]) | same_piece


def skew_rows(unshifted_reversed_scores, key_total):
    head_total, row_total, rel_span = unshifted_reversed_scores.shape
    flattened = unshifted_reversed_scores.reshape(head_total, row_total * rel_span)
    window = lax.slice_in_dim(
        flattened, row_total - 1, row_total - 1 + row_total * (rel_span - 1), axis=1
    )
    return window.reshape(head_total, row_total, rel_span - 1)[:, :, :key_total]


def unskew_rows(grad_pos, rel_span):
    head_total, row_total, key_total = grad_pos.shape
    padded = jnp.pad(grad_pos, ((0, 0), (0, 0), (0, rel_span - 1 - key_total)))
    flattened = padded.reshape(head_total, row_total * (rel_span - 1))
    flattened = jnp.pad(flattened, ((0, 0), (row_total - 1, 1)))
    return flattened.reshape(head_total, row_total, rel_span)


def block_scores(qu_block, query_position_block, key_rows, relative_block, allowed):
    content = jnp.einsum("ihd,jhd->hij", qu_block, key_rows, preferred_element_type=jnp.float32)
    unshifted_reversed_scores = jnp.einsum(
        "sgw,egw->gse", query_position_block, relative_block, preferred_element_type=jnp.float32
    )
    position = skew_rows(unshifted_reversed_scores, key_rows.shape[0])
    return jnp.where(allowed[None], content + position, big_negative)


def attention_forward(query_u, query_v, key_rows, value_rows, relative_rev, labels):
    seq_len, head_count, head_dim = key_rows.shape
    block_len = min(512, seq_len)
    rel_span = block_len + seq_len - 1
    offsets = jnp.arange(seq_len // block_len, dtype=jnp.int32) * block_len

    def attend(offset):
        qu_block = lax.dynamic_slice_in_dim(query_u, offset, block_len, 0)
        query_position_block = lax.dynamic_slice_in_dim(query_v, offset, block_len, 0)
        relative_block = lax.dynamic_slice_in_dim(
            relative_rev, seq_len - block_len - offset, rel_span, 0
        )
        scores = block_scores(
            qu_block,
            query_position_block,
            key_rows,
            relative_block,
            block_mask(offset, block_len, labels),
        )
        row_max = jnp.max(scores, axis=2, keepdims=True)
        log_total = row_max + jnp.log(jnp.sum(jnp.exp(scores - row_max), axis=2, keepdims=True))
        attn_prob = jnp.exp(scores - log_total).astype(jnp.bfloat16)
        result = jnp.einsum(
            "hij,jhd->ihd", attn_prob, value_rows, preferred_element_type=jnp.float32
        )
        return (result, log_total[:, :, 0])

    results, log_totals = lax.map(attend, offsets)
    return (results.reshape(seq_len, head_count * head_dim), log_totals)


def attention_backward(
    query_u, query_v, key_rows, value_rows, relative_rev, labels, log_totals, grad_att
):
    seq_len, head_count, head_dim = key_rows.shape
    block_len = min(512, seq_len)
    rel_span = block_len + seq_len - 1
    offsets = jnp.arange(seq_len // block_len, dtype=jnp.int32) * block_len

    def back_block(carried, sliced):
        grad_keys, grad_values, grad_rel = carried
        offset, log_total = sliced
        rel_start = seq_len - block_len - offset
        qu_block = lax.dynamic_slice_in_dim(query_u, offset, block_len, 0)
        query_position_block = lax.dynamic_slice_in_dim(query_v, offset, block_len, 0)
        relative_block = lax.dynamic_slice_in_dim(relative_rev, rel_start, rel_span, 0)
        scores = block_scores(
            qu_block,
            query_position_block,
            key_rows,
            relative_block,
            block_mask(offset, block_len, labels),
        )
        attn_prob = jnp.exp(scores - log_total[:, :, None])
        low_prob = attn_prob.astype(jnp.bfloat16)
        grad_block = lax.dynamic_slice_in_dim(grad_att, offset, block_len, 0)
        grad_prob = jnp.einsum(
            "ihd,jhd->hij", grad_block, value_rows, preferred_element_type=jnp.float32
        )
        row_inner = jnp.sum(attn_prob * grad_prob, axis=2, keepdims=True)
        grad_scores = (attn_prob * (grad_prob - row_inner)).astype(jnp.bfloat16)
        grad_values = grad_values + jnp.einsum(
            "hij,ihd->jhd", low_prob, grad_block, preferred_element_type=jnp.float32
        )
        grad_keys = grad_keys + jnp.einsum(
            "hij,ihd->jhd", grad_scores, qu_block, preferred_element_type=jnp.float32
        )
        grad_qu = jnp.einsum(
            "hij,jhd->ihd", grad_scores, key_rows, preferred_element_type=jnp.float32
        )
        gradient_unshifted = unskew_rows(grad_scores, rel_span)
        grad_qv = jnp.einsum(
            "qjp,pqr->jqr", gradient_unshifted, relative_block, preferred_element_type=jnp.float32
        )
        rel_part = jnp.einsum(
            "nfx,fne->xne",
            gradient_unshifted,
            query_position_block,
            preferred_element_type=jnp.float32,
        )
        current = lax.dynamic_slice_in_dim(grad_rel, rel_start, rel_span, 0)
        grad_rel = lax.dynamic_update_slice_in_dim(grad_rel, current + rel_part, rel_start, 0)
        return ((grad_keys, grad_values, grad_rel), (grad_qu, grad_qv))

    zero_rows = jnp.zeros((seq_len, head_count, head_dim), jnp.float32)
    zero_rel = jnp.zeros((2 * seq_len - 1, head_count, head_dim), jnp.float32)
    carried, stacked = lax.scan(back_block, (zero_rows, zero_rows, zero_rel), (offsets, log_totals))
    grad_keys, grad_values, grad_rel = carried
    grad_qu = stacked[0].reshape(seq_len, head_count, head_dim)
    grad_qv = stacked[1].reshape(seq_len, head_count, head_dim)
    return (grad_qu, grad_qv, grad_keys, grad_values, grad_rel)


def heads_pass(packed, content_bias, position_bias, relative_rev, labels):
    seq_len = packed.shape[0]
    head_count, head_dim = content_bias.shape
    scaling = head_dim ** (-0.5)
    packed = packed.reshape(seq_len, head_count, 3, head_dim)
    queries = packed[:, :, 0].astype(jnp.float32)
    key_rows = packed[:, :, 1]
    value_rows = packed[:, :, 2]
    query_u = ((queries + content_bias) * scaling).astype(jnp.bfloat16)
    query_v = ((queries + position_bias) * scaling).astype(jnp.bfloat16)
    attended, log_totals = attention_forward(
        query_u, query_v, key_rows, value_rows, relative_rev, labels
    )
    return (attended.astype(jnp.bfloat16), (query_u, query_v, key_rows, value_rows, log_totals))


def heads_back(kept, relative_rev, labels, grad_att):
    query_u, query_v, key_rows, value_rows, log_totals = kept
    seq_len, head_count, head_dim = key_rows.shape
    scaling = head_dim ** (-0.5)
    grad_att = grad_att.reshape(seq_len, head_count, head_dim)
    grad_qu, grad_qv, grad_keys, grad_values, grad_rel = attention_backward(
        query_u, query_v, key_rows, value_rows, relative_rev, labels, log_totals, grad_att
    )
    cbias_part = jnp.sum(grad_qu, axis=0) * scaling
    pbias_part = jnp.sum(grad_qv, axis=0) * scaling
    grad_query = (grad_qu + grad_qv) * scaling
    grad_packed = jnp.stack([grad_query, grad_keys, grad_values], axis=2)
    grad_packed = grad_packed.reshape(seq_len, head_count * 3 * head_dim).astype(jnp.bfloat16)
    rel_low = grad_rel.reshape(2 * seq_len - 1, head_count * head_dim).astype(jnp.bfloat16)
    return (grad_packed, rel_low, cbias_part, pbias_part)


def grid_micro(seq_feats, cot_feats, params, shared):
    (
        ln1_gain,
        ln1_bias,
        qkv_weight,
        content_bias,
        position_bias,
        out_weight,
        ln2_gain,
        ln2_bias,
        up_weight,
        up_bias,
        down_weight,
        down_bias,
    ) = params
    relative_rev, table_rev, labels = shared
    seq_in = seq_feats.astype(jnp.float32).T
    normed_one, scaled_one, inverse_one = normalize(seq_in, ln1_gain, ln1_bias)
    gathered_one = gather_rows(normed_one.astype(jnp.bfloat16))
    packed = sum_over_cols(gathered_one, qkv_weight, False).astype(jnp.bfloat16)
    attended, kept = heads_pass(packed, content_bias, position_bias, relative_rev, labels)
    att_gathered = gather_cols(attended)
    middle = seq_in + sum_over_rows(att_gathered, out_weight, False)
    normed_two, scaled_two, inverse_two = normalize(middle, ln2_gain, ln2_bias)
    gathered_two = gather_rows(normed_two.astype(jnp.bfloat16))
    pre_act = sum_over_cols(gathered_two, up_weight, False) + up_bias
    activated = gelu_exact(pre_act).astype(jnp.bfloat16)
    act_gathered = gather_cols(activated)
    output = middle + sum_over_rows(act_gathered, down_weight, False) + down_bias
    grad_final = cot_feats.T
    gout = grad_final.astype(jnp.float32)
    final_gathered = gather_rows(grad_final)
    grad_act = sum_over_cols(final_gathered, down_weight, True)
    grad_pre = (grad_act * gelu_slope(pre_act)).astype(jnp.bfloat16)
    pre_gathered = gather_cols(grad_pre)
    grad_two = sum_over_rows(pre_gathered, up_weight, True)
    backward_second, gain_two, bias_two = normalize_back(
        grad_two, scaled_two, inverse_two, ln2_gain
    )
    grad_middle = gout + backward_second
    grad_branch = grad_middle.astype(jnp.bfloat16)
    branch_gathered = gather_rows(grad_branch)
    grad_att = sum_over_cols(branch_gathered, out_weight, True).astype(jnp.bfloat16)
    grad_packed, rel_low, cbias_part, pbias_part = heads_back(kept, relative_rev, labels, grad_att)
    packed_gathered = gather_cols(grad_packed)
    grad_one = sum_over_rows(packed_gathered, qkv_weight, True)
    back_one, gain_one, bias_one = normalize_back(grad_one, scaled_one, inverse_one, ln1_gain)
    grad_in = grad_middle + back_one
    collected = (
        outer_sum(gathered_one, packed_gathered),
        outer_sum(att_gathered, branch_gathered),
        outer_sum(gathered_two, pre_gathered),
        outer_sum(act_gathered, final_gathered),
        outer_sum(table_rev, rel_low),
        cbias_part,
        pbias_part,
        jnp.sum(grad_pre.astype(jnp.float32), axis=0),
        gain_one,
        bias_one,
        gain_two,
        bias_two,
        jnp.sum(gout, axis=0),
    )
    return (output.T, grad_in.T, collected)


def embed_heads(part, row_pick, col_count):
    head_count = part.shape[0]
    spread = jnp.transpose(part.reshape(head_count, col_count, -1), (1, 0, 2))
    placed = jnp.where(row_pick[:, None, None, None], spread[None], 0.0)
    return placed.reshape(row_pick.shape[0] * col_count, head_count, -1)


def shards(
    tokens,
    cotangent,
    piece_starts,
    ln1_gain,
    ln1_bias,
    qkv_weight,
    content_bias,
    position_bias,
    pos_weight,
    out_weight,
    ln2_gain,
    ln2_bias,
    up_weight,
    up_bias,
    down_weight,
    down_bias,
):
    micro_count = tokens.shape[0]
    row_count = lax.axis_size("row")
    col_count = lax.axis_size("col")
    grid_cells = row_count * col_count
    head_count, head_dim = content_bias.shape
    pos_cols = lax.all_gather(pos_weight, "col", axis=0, tiled=True)
    table_rev = sinusoid_table(SEQ_LEN, D)[::-1]
    relative_rev = jnp.dot(table_rev, pos_cols, preferred_element_type=jnp.float32).astype(
        jnp.bfloat16
    )
    relative_rev = relative_rev.reshape(2 * SEQ_LEN - 1, head_count, head_dim)
    positions = jnp.arange(SEQ_LEN, dtype=jnp.int32)
    params = (
        ln1_gain,
        ln1_bias,
        qkv_weight,
        content_bias,
        position_bias,
        out_weight,
        ln2_gain,
        ln2_bias,
        up_weight,
        up_bias,
        down_weight,
        down_bias,
    )
    outputs, grad_inputs, part_lists = ([], [], [])
    for micro_idx in range(micro_count):
        labels = piece_labels(positions, piece_starts[micro_idx, 0], PIECE)
        out_feats, grad_feats, collected = grid_micro(
            tokens[micro_idx], cotangent[micro_idx], params, (relative_rev, table_rev, labels)
        )
        outputs.append(out_feats)
        grad_inputs.append(grad_feats)
        part_lists.append(collected)
    totals = [
        reduce(jnp.add, [collected[member] for collected in part_lists]) for member in range(13)
    ]
    (
        acc_qkv,
        acc_out,
        acc_up,
        acc_down,
        acc_pos,
        acc_cbias,
        acc_pbias,
        acc_ubias,
        acc_g1,
        acc_b1,
        acc_g2,
        acc_b2,
        acc_db,
    ) = totals
    row_pick = jnp.arange(row_count, dtype=jnp.int32) == lax.axis_index("row")
    pos_term = jnp.where(row_pick[:, None, None], acc_pos[None], 0.0).reshape(
        row_count * acc_pos.shape[0], -1
    )
    cbias_term = embed_heads(acc_cbias, row_pick, col_count)
    pbias_term = embed_heads(acc_pbias, row_pick, col_count)
    col_pick = jnp.arange(col_count, dtype=jnp.int32) == lax.axis_index("col")
    ubias_term = jnp.where(row_pick[:, None], acc_ubias[None], 0.0).reshape(grid_cells, -1)
    norm_terms = [
        jnp.where(col_pick[:, None], vector[None], 0.0).reshape(grid_cells, -1)
        for vector in (acc_g1, acc_b1, acc_g2, acc_b2, acc_db)
    ]
    sum_pos, sum_cbias, sum_pbias, sum_ubias, sum_g1, sum_b1, sum_g2, second_bias_total, sum_db = (
        lax.psum_scatter(pos_term, ("row", "col"), scatter_dimension=0, tiled=True),
        lax.psum_scatter(cbias_term, ("row", "col"), scatter_dimension=0, tiled=True),
        lax.psum_scatter(pbias_term, ("row", "col"), scatter_dimension=0, tiled=True),
        lax.psum_scatter(ubias_term, ("row", "col"), scatter_dimension=0, tiled=True),
        lax.psum_scatter(norm_terms[0], ("row", "col"), scatter_dimension=0, tiled=True),
        lax.psum_scatter(norm_terms[1], ("row", "col"), scatter_dimension=0, tiled=True),
        lax.psum_scatter(norm_terms[2], ("row", "col"), scatter_dimension=0, tiled=True),
        lax.psum_scatter(norm_terms[3], ("row", "col"), scatter_dimension=0, tiled=True),
        lax.psum_scatter(norm_terms[4], ("row", "col"), scatter_dimension=0, tiled=True),
    )
    sum_qkv, sum_out, sum_up, sum_down = (acc_qkv, acc_out, acc_up, acc_down)
    summed = (
        lax.psum_scatter(
            sum_qkv.astype(jnp.bfloat16), "dp", scatter_dimension=1, tiled=True
        ).astype(jnp.float32),
        lax.psum_scatter(
            sum_out.astype(jnp.bfloat16), "dp", scatter_dimension=1, tiled=True
        ).astype(jnp.float32),
        lax.psum_scatter(sum_up.astype(jnp.bfloat16), "dp", scatter_dimension=1, tiled=True).astype(
            jnp.float32
        ),
        lax.psum_scatter(
            sum_down.astype(jnp.bfloat16), "dp", scatter_dimension=1, tiled=True
        ).astype(jnp.float32),
        lax.psum_scatter(
            sum_pos.astype(jnp.bfloat16), "dp", scatter_dimension=1, tiled=True
        ).astype(jnp.float32),
        lax.psum_scatter(
            sum_cbias.astype(jnp.bfloat16), "dp", scatter_dimension=2, tiled=True
        ).astype(jnp.float32),
        lax.psum_scatter(
            sum_pbias.astype(jnp.bfloat16), "dp", scatter_dimension=2, tiled=True
        ).astype(jnp.float32),
        lax.psum_scatter(
            sum_ubias.astype(jnp.bfloat16), "dp", scatter_dimension=1, tiled=True
        ).astype(jnp.float32),
        lax.psum_scatter(sum_g1.astype(jnp.bfloat16), "dp", scatter_dimension=1, tiled=True).astype(
            jnp.float32
        ),
        lax.psum_scatter(sum_b1.astype(jnp.bfloat16), "dp", scatter_dimension=1, tiled=True).astype(
            jnp.float32
        ),
        lax.psum_scatter(sum_g2.astype(jnp.bfloat16), "dp", scatter_dimension=1, tiled=True).astype(
            jnp.float32
        ),
        lax.psum_scatter(
            second_bias_total.astype(jnp.bfloat16), "dp", scatter_dimension=1, tiled=True
        ).astype(jnp.float32),
        lax.psum_scatter(sum_db.astype(jnp.bfloat16), "dp", scatter_dimension=1, tiled=True).astype(
            jnp.float32
        ),
    )
    (
        grad_qkv_w,
        grad_out_w,
        grad_up_w,
        grad_down_w,
        grad_pos_w,
        grad_cbias,
        grad_pbias,
        grad_ubias,
        grad_g1,
        grad_b1,
        grad_g2,
        grad_b2,
        grad_dbias,
    ) = summed
    output_rows = jnp.stack(outputs, axis=0)
    grad_rows = jnp.stack(grad_inputs, axis=0)
    return (
        output_rows,
        grad_rows,
        grad_g1.reshape(-1),
        grad_b1.reshape(-1),
        grad_qkv_w,
        grad_cbias.reshape(head_count, -1),
        grad_pbias.reshape(head_count, -1),
        grad_pos_w,
        grad_out_w,
        grad_g2.reshape(-1),
        grad_b2.reshape(-1),
        grad_up_w,
        grad_ubias.reshape(-1),
        grad_down_w,
        grad_dbias.reshape(-1),
    )


MESH = pl.DeviceIdType.MESH
F32 = jnp.float32
BF16 = jnp.bfloat16


def aligned(index, size):
    return index if isinstance(index, int) else pl.multiple_of(index, size)


def nt(a, b):
    return lax.dot_general(a, b, (((1,), (1,)), ((), ())), preferred_element_type=F32)


def nn(a, b):
    return lax.dot_general(a, b, (((1,), (0,)), ((), ())), preferred_element_type=F32)


def tn(a, b):
    return lax.dot_general(a, b, (((0,), (0,)), ((), ())), preferred_element_type=F32)


def place():
    k, z, c = lax.axis_index("dp"), lax.axis_index("row"), lax.axis_index("col")
    cx = c + 1 - 2 * lax.rem(c, 2)
    cy = lax.rem(c + 2, 4)
    near = (1 - k) * cx + k * cy
    far = k * cx + (1 - k) * cy
    return k, z, c, near, far


def enter(rows):
    k, z, c, _, _ = place()
    barrier = pltpu.get_barrier_semaphore()
    peers = [(1 - k, z, c)]
    for step in range(1, rows):
        peers.append((k, lax.rem(z + step, rows), c))
    for step in range(1, 4):
        for core in range(2):
            peers.append((0 * k + core, z, lax.rem(c + step, 4)))
    for peer in peers:
        pl.semaphore_signal(barrier, inc=1, device_id=peer, device_id_type=MESH)
    pl.semaphore_wait(barrier, len(peers))


class Copies:
    def __init__(self, send, recv):
        self.send, self.recv = send, recv
        self.sends, self.recvs = 0, 0
        self.pending = {}

    def leave(self, count=1):
        first = self.sends
        self.sends += count
        return first

    def land(self, count=1):
        first = self.recvs
        self.recvs += count
        return first

    def copy(self, send_slot, build):
        src, dst, recv_slot, peer = build()
        return pltpu.make_async_remote_copy(
            src, dst, self.send.at[send_slot], self.recv.at[recv_slot], device_id=peer, device_id_type=MESH
        )

    def push(self, send_slot, build, when=None):
        if when is None:
            self.copy(send_slot, build).start()
        else:
            pl.when(when())(lambda: self.copy(send_slot, build).start())
        self.later(send_slot, build, when)

    def later(self, send_slot, build, when=None):
        self.pending[send_slot] = (lambda: self.copy(send_slot, build), when)

    def keep(self, src, dst, slot, when=None):
        def go():
            pltpu.make_async_copy(src(), dst(), self.recv.at[slot]).start()

        if when is None:
            go()
        else:
            pl.when(when())(go)

    def arrived(self, dst, slot):
        pltpu.make_async_copy(dst, dst, self.recv.at[slot]).wait()

    def drain(self):
        for copy, when in self.pending.values():
            if when is None:
                copy().wait_send()
            else:
                pl.when(when())(lambda copy=copy: copy().wait_send())


def tall(row):
    padded = jnp.concatenate([row, jnp.zeros((120, 128), F32)], axis=0)
    return jnp.transpose(padded)


def erf_parts(values):
    erf = lax.erf(values * inv_sqrt_two)
    return 0.5 * (1.0 + erf)


def layer_kernel(
    tok, cot, starts, packed, cbias, pbias, table, wq, wp, wo, wu, wd,
    outs, grads, f_qp, f_o, f_u, f_d, f_small,
    att, wo_all, wu_all, wd_all, wq_half, wp_half, wp_head, xt, ct, normed_t, qcat, keys, vals, probs_a, probs_b, heads_out,
    params_col, params_row, cb_all, pb_all, kcat, own_att, starts_got,
    mid, norm, hat, inv, gout, acc_out, acc_two, tall_norm, out_t, grad_mid_t, grad_att, g_up, g_down, g_out, small,
    grad_o, head_grad, turned, turned_k, turned_v, turned_p, one_t, one_low, one_got, grad_x, sums,
    hs_qp, hs_o, hs_u, hs_d, r0_o, r0_u, r0_d, s_d,
    r1_qp, r1_o, r1_u, r1_d, r2_qp, r2_o, r2_u, r2_d, r3_qp, r3_o, r3_u, r3_d,
    all_small, got_sib, got_plane, got_z, send, recv,
):
    rows = wu_all.shape[0]
    cols = wo_all.shape[0]
    half = rows // 2
    heads = 2 * half
    k, z, c, near, far = place()
    opposite = 3 - c
    sibling = (1 - k, z, c)
    io = Copies(send, recv)
    mine = lax.div(z, half) == k
    arrived = io.arrived
    enter(rows)

    def q_block(cc, i):
        return wq_half.at[i, pl.ds(aligned(cc * 128, 128), 128), :]

    def p_block(cc, i):
        return wp_half.at[i, pl.ds(aligned(cc * 128, 128), 128), :]

    def u_block(cc, core=k):
        return wu_all.at[pl.ds(core * half, half), pl.ds(aligned(cc * 128, 128), 128), :]

    def o_block(cc, core=k):
        size = wo_all.shape[1] // 2
        return wo_all.at[cc, pl.ds(aligned(core * size, 128), size), :]

    def u_one(i):
        return wu_all.at[k * half + i, pl.ds(aligned(c * 128, 128), 128), :]

    def o_one(i):
        size = wo_all.shape[1] // rows
        return wo_all.at[c, pl.ds(aligned((k * half + i) * size, 128), size), :]

    weights = {
        "q": (wq, lambda i: q_block(c, i), q_block), "p": (wp, lambda i: p_block(c, i), p_block), "o": (wo, o_one, o_block),
        "u": (wu, u_one, u_block),
    }
    z_slot = {name: io.land(half) for name in weights}
    z_send = {name: io.leave(rows - 1) for name in weights}
    near_slot = {name: (io.leave(half), io.land(half)) for name in weights}
    far_slot = {name: (io.leave(2 * half), io.land(2 * half)) for name in weights}
    sib_slot = {name: (io.leave(), io.land()) for name in ("o", "u")}
    turn = z - k * half

    def z_start(name):
        ref, one, _ = weights[name]
        io.keep(lambda: ref, lambda: one(turn), z_slot[name] + turn, lambda: mine)
        for step in range(1, rows):
            io.push(
                z_send[name] + step - 1,
                lambda step=step: (ref, one(turn), z_slot[name] + turn, (k, lax.rem(z + step, rows), c)),
                lambda: mine,
            )

    def z_done(name, i=None):
        _, one, _ = weights[name]
        for number in range(half) if i is None else (i,):
            arrived(one(number), z_slot[name] + number)

    def block_of(name, cc, i):
        block = weights[name][2]
        return block(cc) if i is None else block(cc, i)

    def near_start(name, i=None):
        leave, land = (slot + (i or 0) for slot in near_slot[name])
        io.push(leave, lambda: (block_of(name, c, i), block_of(name, c, i), land, (k, z, near)))

    def near_done(name, i=None):
        arrived(block_of(name, near, i), near_slot[name][1] + (i or 0))

    def far_start(name, i=None):
        leave, land = (slot + 2 * (i or 0) for slot in far_slot[name])
        io.push(leave, lambda: (block_of(name, c, i), block_of(name, c, i), land, (k, z, far)))
        io.push(leave + 1, lambda: (block_of(name, near, i), block_of(name, near, i), land + 1, (k, z, far)))

    def far_done(name, i=None):
        land = far_slot[name][1] + (0 if i is None else 2 * i)
        arrived(block_of(name, far, i), land)
        arrived(block_of(name, opposite, i), land + 1)

    def core_half(name, core):
        if name == "u":
            return wu_all.at[pl.ds(core * half, half)]
        size = wo_all.shape[1] // 2
        return wo_all.at[:, pl.ds(aligned(core * size, 128), size), :]

    def sib_start(name):
        leave, land = sib_slot[name]
        io.push(leave, lambda: (core_half(name, k), core_half(name, k), land, sibling))

    def sib_done(name):
        arrived(core_half(name, 1 - k), sib_slot[name][1])

    part_rows = wd.shape[0] // 2

    def d_cells(zz, core):
        return wd_all.at[:, pl.ds(aligned((2 * zz + core) * part_rows, 128), part_rows), :]

    def d_cell(cc, core=k):
        return wd_all.at[cc, pl.ds(aligned((2 * z + core) * part_rows, 128), part_rows), :]

    def d_own():
        return wd.at[pl.ds(aligned(k * part_rows, 128), part_rows), :]

    d_plane = (io.leave(3), io.land(4))
    d_line = (io.leave(5), io.land(rows))
    d_sibs = (io.leave(rows), io.land(rows))
    relaying = jnp.logical_and(z > 0, z < rows - 1)
    relayed = 2 * (rows - 1) - (rows - 1) * z

    def wd_start():
        leave, land = d_plane
        io.keep(d_own, lambda: d_cell(c), land)
        io.push(leave, lambda: (d_own(), d_cell(c), land + 1, (k, z, near)))
        io.push(leave + 1, lambda: (d_own(), d_cell(c), land + 2, (k, z, far)))

    def wd_far():
        leave, land = d_plane
        arrived(d_cell(near), land + 1)
        io.push(leave + 2, lambda: (d_cell(near), d_cell(near), land + 3, (k, z, far)))

    def wd_sib(number):
        zz = lax.rem(z + number, rows)
        leave, land = d_sibs
        io.push(leave + number, lambda: (d_cells(lax.rem(z + number, rows), k),) * 2 + (land + lax.rem(z + number, rows), sibling))

    def wd_line():
        land = d_plane[1]
        arrived(d_cell(c), land)
        arrived(d_cell(far), land + 2)
        arrived(d_cell(opposite), land + 3)
        leave, land = d_line
        for number, step in enumerate((2, -2, 1, -1)):
            io.push(
                leave + number,
                lambda step=step: (d_cells(z, k), d_cells(z, k), land + z, (k, lax.rem(z + step + rows, rows), c)),
                lambda step=step: jnp.logical_and(z + step >= 0, z + step < rows),
            )
        wd_sib(0)

    def wd_relay():
        leave, land = d_line

        @pl.when(relaying)
        def _():
            arrived(d_cells(relayed, k), land + relayed)

        io.push(
            leave + 4,
            lambda: (d_cells(relayed, k), d_cells(relayed, k), land + relayed, (k, rows - 1 - relayed, c)),
            lambda: relaying,
        )

    def wd_done(number):
        zz = lax.rem(z + number, rows)

        @pl.when(jnp.logical_not(jnp.logical_and(relaying, zz == relayed)))
        def _():
            arrived(d_cells(zz, k), d_line[1] + zz)

        wd_sib(number)

    def wd_all_done():
        for number in range(rows):
            zz = lax.rem(z + number, rows)
            arrived(d_cells(zz, 1 - k), d_sibs[1] + zz)

    feat = tok.shape[1]
    count = xt.shape[1]
    x_slot = io.land(4)
    x_send = io.leave(4)
    n_slot, n_send = io.land(), io.leave()

    def is_local(b, core):
        return jnp.logical_and(2 * b + k == c, core == k)

    def spread_features(source, target, leave, land):
        for b in range(2):
            for core in range(2):

                def src(b=b, core=core):
                    return source.at[b, :, pl.ds(core * count, count)]

                def dst():
                    return target.at[pl.ds(aligned(c * feat, 128), feat), :]

                io.keep(src, dst, land + c, lambda b=b, core=core: is_local(b, core))
                io.push(
                    leave + 2 * b + core,
                    lambda src=src, dst=dst, b=b, core=core: (src(), dst(), land + c, (0 * k + core, z, 2 * b + k)),
                    lambda b=b, core=core: jnp.logical_not(is_local(b, core)),
                )

    z_start("q")
    spread_features(tok, xt, x_send, x_slot)
    z_start("p")

    t_slot = io.land()
    io.keep(lambda: table, lambda: kcat.at[:, pl.ds(0, table.shape[1])], t_slot)
    g_col, g_row, g_cb, g_pb = io.land(), io.land(), io.land(), io.land()
    col_send = io.leave(3)
    for step in range(1, 4):
        io.push(
            col_send + step - 1,
            lambda step=step: (packed.at[pl.ds(0, 8)], params_col.at[c], g_col, (k, z, lax.rem(c + step, 4))),
        )
    io.keep(lambda: packed.at[pl.ds(0, 8)], lambda: params_col.at[c], g_col)
    for source, target, slot in ((packed.at[pl.ds(8, 8)], params_row, g_row), (cbias, cb_all, g_cb), (pbias, pb_all, g_pb)):
        row_send = io.leave(rows - 1)
        for step in range(1, rows):
            io.push(
                row_send + step - 1,
                lambda step=step, source=source, target=target, slot=slot: (
                    source, target.at[z], slot, (k, lax.rem(z + step, rows), c)
                ),
            )
        io.keep(lambda source=source: source, lambda target=target: target.at[z], slot)
    s_slot = io.land()
    s_send = io.leave(4)
    for b in range(2):
        for core in range(2):
            io.keep(
                lambda: starts, lambda: starts_got, s_slot,
                lambda b=b, core=core: jnp.logical_and(c == z, is_local(b, core)),
            )
            io.push(
                s_send + 2 * b + core,
                lambda b=b, core=core: (starts, starts_got, s_slot, (0 * k + core, z, 2 * b + k)),
                lambda b=b, core=core: jnp.logical_and(c == z, jnp.logical_not(is_local(b, core))),
            )
    for name in ("o", "u"):
        z_start(name)

    c_slot = io.land(4)
    c_send = io.leave(4)
    z_done("q", 0)
    near_start("q", 0)
    z_done("p", 0)
    near_start("p", 0)
    wd_start()
    arrived(params_col, g_col)
    arrived(params_row, g_row)
    arrived(cb_all, g_cb)
    arrived(pb_all, g_pb)
    arrived(starts_got, s_slot)
    near_done("q", 0)
    far_start("q", 0)
    for cc in range(4):
        arrived(xt.at[pl.ds(cc * feat, feat), :], x_slot + cc)

    columns = [tall(params_col[cc]) for cc in range(4)]
    gain = jnp.concatenate([col[:, 0:1] for col in columns], axis=0)
    bias = jnp.concatenate([col[:, 1:2] for col in columns], axis=0)
    width = xt.shape[0]
    seq = normed_t.shape[1]
    piece = PIECE
    blocks = seq // 256
    other = pl.ds(aligned((1 - k) * count, count), count)
    own = pl.ds(aligned(k * count, count), count)

    @pl.loop(0, count // 256)
    def _(t):
        x = xt[:, pl.ds(aligned(t * 256, 256), 256)].astype(F32)
        mean = jnp.sum(x, axis=0, keepdims=True) * (1.0 / width)
        square = jnp.sum(x * x, axis=0, keepdims=True) * (1.0 / width)
        inverse = lax.rsqrt(square - mean * mean + norm_epsilon)
        here = pl.ds(aligned(k * count + t * 256, 256), 256)
        normed_t[:, here] = ((x - mean) * inverse * gain + bias).astype(BF16)

    io.push(n_send, lambda: (normed_t.at[:, own], normed_t.at[:, own], n_slot, sibling))
    near_done("p", 0)
    far_start("p", 0)
    wd_far()
    for name in ("q", "p"):
        z_done(name, 1)
        near_start(name, 1)
    z_done("o")
    near_start("o")
    arrived(kcat.at[:, pl.ds(0, 512)], t_slot)
    scale = 0.125
    none = jnp.zeros((256, 64), F32)

    def project(i, number):
        t = lax.rem(k * (blocks // 2) + number, blocks)

        @pl.when(jnp.logical_and(i == 0, number == blocks // 2))
        def _():
            arrived(normed_t.at[:, other], n_slot)

        here = pl.ds(aligned(t * 256, 256), 256)
        got = tn(normed_t[:, here], wq_half[i])
        for hb in range(2):
            h = 2 * i + hb
            low = got[:, hb * 192 : hb * 192 + 192].astype(BF16).astype(F32)
            query, key, value = low[:, 0:64], low[:, 64:128], low[:, 128:192]
            content = cb_all[k * half + i, hb : hb + 1, :]
            position = pb_all[k * half + i, hb : hb + 1, :]
            qcat[h, here, 512:640] = jnp.concatenate(
                [(query + content) * scale, (query + position) * scale], axis=1
            ).astype(BF16)
            keys[h, here, :] = jnp.concatenate([key, none], axis=1).astype(BF16)
            vals[h, here, :] = value.astype(BF16)

    def rotate(i, n):
        h, t = 2 * i + lax.div(n, blocks), lax.rem(n, blocks)
        here = pl.ds(aligned(t * 256, 256), 256)
        angle = nt(qcat[h, here, 512:640], wp_head[h])
        cosine = kcat[here, 0:256].astype(F32)
        sine = kcat[here, 256:512].astype(F32)
        first, second = angle[:, 0:256], angle[:, 256:512]
        qcat[h, here, 0:256] = (first * sine + second * cosine).astype(BF16)
        qcat[h, here, 256:512] = (second * sine - first * cosine).astype(BF16)

    slot_len = seq // 2
    block = 256
    batch = lax.div(c, 2)

    def attend(h, low_row, keys_seen, slot):
        start = starts_got[batch, 0:1, slot : slot + 1]
        row = slot * slot_len + low_row + lax.broadcasted_iota(jnp.int32, (block, 1), 0)
        inside = jnp.logical_and(row >= start, row < start + piece)
        limit = jnp.where(inside, start + (piece - 1), row)
        here = pl.ds(aligned(slot * slot_len + low_row, block), block)
        scores = nt(qcat[h, here, :], kcat[0:keys_seen, :])
        column = slot * slot_len + lax.broadcasted_iota(jnp.int32, (block, slot_len), 1)
        last = jnp.where(column <= limit, scores[:, keys_seen - slot_len :], big_negative)
        top = jnp.max(last, axis=1, keepdims=True)
        if slot == 1:
            top = jnp.maximum(top, jnp.max(scores[:, :slot_len], axis=1, keepdims=True))
        last = jnp.exp(last - top)
        total = jnp.sum(last, axis=1, keepdims=True)
        if slot == 1:
            first = jnp.exp(scores[:, :slot_len] - top)
            total = total + jnp.sum(first, axis=1, keepdims=True)
            whole = jnp.concatenate([first, last], axis=1)
        else:
            whole = last
        low = (whole * (1.0 / total)).astype(BF16)
        probs = (probs_a, probs_b)[slot]
        probs[h, pl.ds(aligned(low_row, block), block), :] = low
        heads_out[h, here, :] = nn(low, vals[h, 0:keys_seen, :]).astype(BF16)

    def sib_o():
        far_done("o")
        sib_start("o")

    def sib_u():
        far_done("u")
        sib_start("u")

    def ticks(h, slot, t, actions):
        for number, action in actions.items():
            if (number % 4) // 2 == slot:
                pl.when(4 * h + 2 * slot + t == number)(action)

    def far_of(name):
        def run():
            near_done(name)
            far_start(name)

        return run

    def projected():
        z_done("u")
        near_start("u")
        wd_line()

    def rotated():
        for name in ("q", "p"):
            near_done(name, 1)
            far_start(name, 1)
        spread_features(cot, ct, c_send, c_slot)

    ahead = {1: far_of("o"), 4: far_of("u"), 9: wd_relay, 11: sib_o, 15: sib_u}

    def one_head(h):
        kcat[:, 512:640] = keys[h]

        @pl.loop(0, slot_len // block)
        def _(t):
            attend(h, t * block, slot_len, 0)
            ticks(h, 0, t, ahead)

        @pl.loop(0, slot_len // block)
        def _(t):
            attend(h, t * block, seq, 1)
            ticks(h, 1, t, ahead)

    @pl.loop(0, half)
    def _(i):
        far_done("q", i)
        pl.loop(0, blocks)(lambda number: project(i, number))
        pl.when(i == 0)(projected)
        far_done("p", i)
        for hb in range(2):
            part = wp_half[i, :, hb * 64 : hb * 64 + 64]
            wp_head[2 * i + hb] = jnp.concatenate([jnp.zeros_like(part), part], axis=1)
        pl.loop(0, 2 * blocks)(lambda n: rotate(i, n))
        pl.when(i == 0)(rotated)
        pl.loop(0, 2)(lambda hb: one_head(2 * i + hb))

    own_att[...] = jnp.concatenate([heads_out[h] for h in range(heads)], axis=1)
    a_slot, a_send = io.land(2), io.leave()
    span = own_att.shape[1]
    att_part = att.at[:, pl.ds(aligned(k * span, 128), span)]
    io.push(a_send, lambda: (own_att.at[other, :], att_part, a_slot, sibling))
    io.keep(lambda: own_att.at[own, :], lambda: att_part, a_slot + 1)
    for cc in range(4):
        arrived(ct.at[pl.ds(cc * feat, feat), :], c_slot + cc)
    gout[...] = jnp.transpose(ct[...])
    sib_done("o")
    arrived(own_att.at[own, :], a_slot + 1)
    arrived(own_att.at[own, :], a_slot)

    for number in range(1, rows):
        wd_done(number)

    def line(index):
        return jnp.concatenate([params_col[cc, index : index + 1, :] for cc in range(cols)], axis=1)

    def out_weight():
        return jnp.concatenate([wo_all[cc] for cc in range(cols)], axis=1)

    x = jnp.transpose(xt[...].astype(F32))
    middle = x + nn(att[...], out_weight())
    mid[...] = middle
    mean = jnp.sum(middle, axis=1, keepdims=True) * (1.0 / width)
    square = jnp.sum(middle * middle, axis=1, keepdims=True) * (1.0 / width)
    inverse = lax.rsqrt(square - mean * mean + norm_epsilon)
    scaled = (middle - mean) * inverse
    hat[...] = scaled
    inv[...] = inverse
    low = (scaled * line(2) + line(3)).astype(BF16)
    norm[...] = low
    tall_norm[...] = jnp.transpose(low)
    acc_out[...] = jnp.zeros_like(acc_out)
    acc_two[...] = jnp.zeros_like(acc_two)
    small[...] = jnp.zeros_like(small)
    hidden = wu_all.shape[2]
    wd_all_done()

    u0_slot = (io.leave(half), io.land(half))
    o0_slot = (io.leave(), io.land())
    d0_slot = (io.leave(rows), io.land(rows))
    u_slot = {"one": (io.leave(2 * half), io.land(2 * half)), "two": (io.leave(half), io.land(half)), "z": (io.leave(half), io.land(rows))}
    o_slot = {"one": (io.leave(2), io.land(2)), "two": (io.leave(), io.land()), "z": (io.leave(half), io.land(rows))}
    d_slot = {"one": (io.leave(2), io.land(2)), "two": (io.leave(), io.land()), "z": (io.leave(rows), io.land(rows))}
    qp_slot = {
        "one": (io.leave(2 * heads), io.land(2 * heads)), "two": (io.leave(heads), io.land(heads)),
        "z": (io.leave(heads), io.land(2 * rows)),
    }
    last_slot = {name: (io.leave(), io.land()) for name in ("u", "o", "d", "qp")}

    def load(ref):
        return ref[...].astype(F32)

    def add(to, term):
        to[...] = (load(to) + load(term)).astype(BF16)

    def near_on(first, leave, land, target):
        io.push(leave, lambda: (first(), target(), land, (k, z, near)))

    def u_sib(j):
        leave, land = u0_slot
        io.push(leave + j, lambda: (g_up.at[(1 - k) * half + j], r0_u.at[j], land + j, sibling))

    def u_one(j):
        arrived(r0_u.at[j], u0_slot[1] + j)
        total = load(g_up.at[k * half + j]) + load(r0_u.at[j])
        hs_u[j] = total.astype(BF16).reshape(hs_u.shape[1:])
        leave, land = u_slot["one"]
        io.push(leave + 2 * j, lambda: (hs_u.at[j, far], r1_u.at[j, 0], land + 2 * j, (k, z, far)))
        io.push(leave + 2 * j + 1, lambda: (hs_u.at[j, 3 - c], r1_u.at[j, 1], land + 2 * j + 1, (k, z, far)))

    def u_two(j):
        land = u_slot["one"][1] + 2 * j
        arrived(r1_u.at[j, 1], land + 1)
        add(r1_u.at[j, 1], hs_u.at[j, near])
        near_on(lambda: r1_u.at[j, 1], u_slot["two"][0] + j, u_slot["two"][1] + j, lambda: r2_u.at[j])
        arrived(r1_u.at[j, 0], land)
        add(r1_u.at[j, 0], hs_u.at[j, c])

    def u_z(j):
        arrived(r2_u.at[j], u_slot["two"][1] + j)
        add(r2_u.at[j], r1_u.at[j, 0])
        leave, land = u_slot["z"]
        io.push(
            leave + j, lambda: (r2_u.at[j], r3_u.at[z], land + z, (k, k * half + j, c)), lambda: z != k * half + j
        )

    def z_total(total, r3, land, hb=None):
        for step in range(1, rows):
            source = lax.rem(z + step, rows)
            part = r3.at[source] if hb is None else r3.at[hb, source]
            arrived(part, land + source)
            total = total + load(part)
        return total

    def finish(name, to):
        leave, land = last_slot[name]
        io.push(leave, lambda: (to, to, land, sibling), lambda: mine)

    def u_last():
        @pl.when(mine)
        def _():
            f_u[...] = z_total(load(r2_u.at[turn]), r3_u, u_slot["z"][1])

        finish("u", f_u)

    def o_sib():
        leave, land = o0_slot
        size = g_out.shape[1] // 2
        io.push(leave, lambda: (g_out.at[:, pl.ds(aligned((1 - k) * size, 128), size), :], r0_o, land, sibling))

    def o_one():
        arrived(r0_o, o0_slot[1])
        size = g_out.shape[1] // 2
        for cc in range(cols):
            total = load(g_out.at[cc, pl.ds(aligned(k * size, 128), size), :]) + load(r0_o.at[cc])
            hs_o[cc] = total.astype(BF16).reshape(hs_o.shape[1:])
        leave, land = o_slot["one"]
        io.push(leave, lambda: (hs_o.at[far], r1_o.at[0], land, (k, z, far)))
        io.push(leave + 1, lambda: (hs_o.at[3 - c], r1_o.at[1], land + 1, (k, z, far)))

    def o_two():
        land = o_slot["one"][1]
        arrived(r1_o.at[1], land + 1)
        add(r1_o.at[1], hs_o.at[near])
        near_on(lambda: r1_o.at[1], o_slot["two"][0], o_slot["two"][1], lambda: r2_o)
        arrived(r1_o.at[0], land)
        add(r1_o.at[0], hs_o.at[c])

    def o_z():
        arrived(r2_o, o_slot["two"][1])
        add(r2_o, r1_o.at[0])
        leave, land = o_slot["z"]
        for j in range(half):
            io.push(
                leave + j,
                lambda j=j: (r2_o.at[j], r3_o.at[z], land + z, (k, k * half + j, c)),
                lambda j=j: z != k * half + j,
            )

    def o_last():
        @pl.when(mine)
        def _():
            f_o[...] = z_total(load(r2_o.at[turn]), r3_o, o_slot["z"][1])

        finish("o", f_o)

    def d_part(r, core):
        return g_down.at[:, pl.ds(aligned((2 * r + core) * part_rows, 128), part_rows), :]

    def d_sib(r, number):
        leave, land = d0_slot
        io.push(leave + number, lambda: (d_part(r(), 1 - k), r0_d.at[r()], land + r(), sibling))

    def d_z(r, number):
        arrived(r0_d.at[r()], d0_slot[1] + r())
        hs_d[r()] = (load(d_part(r(), k)) + load(r0_d.at[r()])).astype(BF16)
        leave, land = d_slot["z"]
        io.push(leave + number, lambda: (hs_d.at[r()], r3_d.at[z], land + z, (k, r(), c)), lambda: z != r())

    def d_one():
        s_d[...] = z_total(load(hs_d.at[z]), r3_d, d_slot["z"][1]).astype(BF16)
        leave, land = d_slot["one"]
        io.push(leave, lambda: (s_d.at[far], r1_d.at[0], land, (k, z, far)))
        io.push(leave + 1, lambda: (s_d.at[3 - c], r1_d.at[1], land + 1, (k, z, far)))

    def d_two():
        land = d_slot["one"][1]
        arrived(r1_d.at[1], land + 1)
        add(r1_d.at[1], s_d.at[near])
        near_on(lambda: r1_d.at[1], d_slot["two"][0], d_slot["two"][1], lambda: r2_d)
        arrived(r1_d.at[0], land)
        add(r1_d.at[0], s_d.at[c])

    def d_last():
        arrived(r2_d, d_slot["two"][1])
        leave, land = last_slot["d"]
        f_d[pl.ds(aligned(k * part_rows, 128), part_rows), :] = load(r2_d) + load(r1_d.at[0])

        def of_core():
            return f_d.at[pl.ds(aligned(k * part_rows, 128), part_rows), :]

        io.push(leave, lambda: (of_core(), of_core(), land, sibling))

    def qp_builds(h):
        leave, land = qp_slot["one"]
        return (
            (leave + 2 * h, lambda: (hs_qp.at[h, far], r1_qp.at[h, 0], land + 2 * h, (k, z, far))),
            (leave + 2 * h + 1, lambda: (hs_qp.at[h, opposite], r1_qp.at[h, 1], land + 2 * h + 1, (k, z, far))),
        )

    def qp_one(h):
        found = nt(turned[h], normed_t[...]).astype(BF16)
        position = turned_p[h].astype(BF16)
        for cc in range(cols):
            hs_qp[h, cc, 0:192, :] = found[:, cc * 128 : cc * 128 + 128]
            hs_qp[h, cc, 192:256, :] = position[:, cc * 128 : cc * 128 + 128]
        for leave, build in qp_builds(h):
            io.copy(leave, build).start()

    for h in range(heads):
        for leave, build in qp_builds(h):
            io.later(leave, build)

    def qp_two(h):
        land = qp_slot["one"][1] + 2 * h
        arrived(r1_qp.at[h, 1], land + 1)
        add(r1_qp.at[h, 1], hs_qp.at[h, near])
        near_on(lambda: r1_qp.at[h, 1], qp_slot["two"][0] + h, qp_slot["two"][1] + h, lambda: r2_qp.at[h])
        arrived(r1_qp.at[h, 0], land)
        add(r1_qp.at[h, 0], hs_qp.at[h, c])

    def qp_z(h):
        arrived(r2_qp.at[h], qp_slot["two"][1] + h)
        add(r2_qp.at[h], r1_qp.at[h, 0])
        leave, land = qp_slot["z"]
        io.push(
            leave + h,
            lambda: (r2_qp.at[h], r3_qp.at[h % 2, z], land + (h % 2) * rows + z, (k, k * half + h // 2, c)),
            lambda: z != k * half + h // 2,
        )

    def qp_last():
        @pl.when(mine)
        def _():
            for hb in range(2):
                f_qp[hb] = z_total(load(r2_qp.at[2 * turn + hb]), r3_qp, qp_slot["z"][1] + hb * rows, hb)

        finish("qp", f_qp)

    def last_done():
        @pl.when(jnp.logical_not(mine))
        def _():
            for name, to in (("u", f_u), ("o", f_o), ("qp", f_qp)):
                arrived(to, last_slot[name][1])

        arrived(f_d.at[pl.ds(aligned((1 - k) * part_rows, 128), part_rows), :], last_slot["d"][1])

    origin = lax.rem(c, 2)
    out_slot, grad_slot = (io.leave(4), io.land(4)), (io.leave(4), io.land(4))

    def back_start(src, dst, pair):
        leave, base = pair
        for step in range(4):

            def part(step=step):
                return src.at[pl.ds(aligned(lax.rem(c + step, 4) * feat, 128), feat), :]

            def landing():
                return dst.at[batch, k]

            if step == 0:
                io.keep(part, landing, base + 2 * batch + k, lambda: origin == k)
                io.push(
                    leave + step,
                    lambda part=part, landing=landing: (part(), landing(), base + 2 * batch + k, sibling),
                    lambda: origin != k,
                )
            else:
                io.push(
                    leave + step,
                    lambda part=part, landing=landing, step=step: (
                        part(), landing(), base + 2 * batch + k, (origin, z, lax.rem(c + step, 4))
                    ),
                )

    def back_done(dst, pair):
        base = pair[1]
        for b in range(2):
            for core in range(2):
                arrived(dst.at[b, core], base + 2 * b + core)


    def rows_of(number):
        core = k if number % 2 == 0 else 1 - k
        return core * half + number // 2

    def after_one():
        u_sib(0)
        for number in range(2):
            d_sib(lambda number=number: rows_of(number), number)

    def after_two():
        u_one(0)
        for number in range(2):
            d_z(lambda number=number: rows_of(number), number)

    @pl.loop(0, rows)
    def _(step):
        turn_of = lax.rem(step, 2)
        r = ((1 - turn_of) * k + turn_of * (1 - k)) * half + lax.div(step, 2)

        @pl.when(step == 1)
        def _():
            sib_done("u")

        here = pl.ds(aligned(r * hidden, hidden), hidden)
        bias = jnp.concatenate([params_row[r, j : j + 1, :] for j in range(hidden // 128)], axis=1)
        down = jnp.concatenate([wd_all[cc, here, :] for cc in range(cols)], axis=1)
        pre = nn(norm[...], wu_all[r]) + bias
        grad_act = nt(gout[...], down)
        lower = erf_parts(pre)
        act = (pre * lower).astype(BF16)
        slope = lower + pre * jnp.exp(-0.5 * pre * pre) * inv_sqrt_tau
        low_grad = (grad_act * slope).astype(BF16)
        small[pl.ds(5 + r, 1), :] = jnp.sum(low_grad.astype(F32), axis=0, keepdims=True)
        acc_out[...] += nn(act, down)
        acc_two[...] += nt(low_grad, wu_all[r])
        g_up[r] = nn(tall_norm[...], low_grad).astype(BF16)
        found = tn(act, gout[...]).astype(BF16)
        for cc in range(cols):
            g_down[cc, here, :] = found[:, cc * 128 : cc * 128 + 128]
        pl.when(step == 1)(after_one)
        pl.when(step == 2)(after_two)

    u_sib(1)
    for number in range(2, 4):
        d_sib(lambda number=number: rows_of(number), number)
    cotangent = gout[...].astype(F32)
    out_t[...] = jnp.transpose(mid[...] + acc_out[...] + line(4)).astype(BF16)
    back_start(out_t, outs, out_slot)
    two = acc_two[...]
    small[2:3, :] = jnp.sum(two * hat[...], axis=0, keepdims=True)
    small[3:4, :] = jnp.sum(two, axis=0, keepdims=True)
    small[4:5, :] = jnp.sum(cotangent, axis=0, keepdims=True)
    shifted = two * line(2)
    first = jnp.sum(shifted, axis=1, keepdims=True) * (1.0 / width)
    second = jnp.sum(shifted * hat[...], axis=1, keepdims=True) * (1.0 / width)
    grad_mid = cotangent + inv[...] * (shifted - first - hat[...] * second)
    branch = grad_mid.astype(BF16)
    grad_att[...] = nt(branch, out_weight()).astype(BF16)
    e_slot, e_send = io.land(2), io.leave()
    io.push(
        e_send,
        lambda: (grad_att.at[:, pl.ds(aligned((1 - k) * span, 128), span)], grad_o.at[own, :], e_slot, sibling),
    )
    io.keep(
        lambda: grad_att.at[:, pl.ds(aligned(k * span, 128), span)], lambda: grad_o.at[own, :], e_slot + 1
    )
    grad_mid_t[...] = jnp.transpose(grad_mid)
    found = tn(att[...], branch).astype(BF16)
    for cc in range(cols):
        g_out[cc] = found[:, cc * 128 : cc * 128 + 128]
    o_sib()
    u_one(1)
    for number in range(2, 4):
        d_z(lambda number=number: rows_of(number), number)
    one_t[...] = jnp.zeros_like(one_t)
    sums[...] = jnp.zeros_like(sums)
    arrived(grad_o.at[own, :], e_slot + 1)
    arrived(grad_o.at[own, :], e_slot)
    for h in range(heads):
        head_grad[h] = grad_o[:, h * 64 : h * 64 + 64]

    def attend_back(h, low_row, keys_seen, slot):
        at = pl.ds(aligned(low_row, block), block)
        here = pl.ds(aligned(slot * slot_len + low_row, block), block)
        grad = head_grad[h, here, :]
        low = (probs_a, probs_b)[slot][h, at, :]
        inner = jnp.sum(grad.astype(F32) * heads_out[h, here, :].astype(F32), axis=1, keepdims=True)
        grad_prob = nt(grad, vals[h, 0:keys_seen, :])
        grad_score = (low.astype(F32) * (grad_prob - inner)).astype(BF16)
        turned_v[:, 0:keys_seen] += tn(grad, low)
        turned_k[:, 0:keys_seen] += tn(qcat[h, here, 512:576], grad_score)
        got = nn(grad_score, kcat[0:keys_seen, :])
        cosine = kcat[here, 0:256].astype(F32)
        sine = kcat[here, 256:512].astype(F32)
        first, second = got[:, 0:256], got[:, 256:512]
        angle = jnp.concatenate([first * sine - second * cosine, first * cosine + second * sine], axis=1).astype(BF16)
        both = got[:, 512:640] + nn(angle, wp_head[h])
        turned_p[h] += tn(qcat[h, here, 512:640], angle)[64:128]
        sums[pl.ds(h, 1), :] += jnp.sum(both, axis=0, keepdims=True) * 0.125
        query = (both + pltpu.roll(both, 64, 1)) * 0.125
        turned[h, 0:64, here] = jnp.transpose(query)[0:64].astype(BF16)

    def both(*actions):
        def run():
            for action in actions:
                action()

        return run

    behind = {
        0: both(o_one, lambda: u_two(0)), 6: lambda: u_two(1), 7: o_two, 9: lambda: u_z(0), 10: lambda: qp_two(0),
        11: lambda: u_z(1), 12: o_z, 13: lambda: qp_two(1), 14: lambda: qp_z(0),
    }

    @pl.loop(0, heads)
    def _(h):
        kcat[:, 512:640] = keys[h]
        turned_k[...] = jnp.zeros_like(turned_k)
        turned_v[...] = jnp.zeros_like(turned_v)
        turned_p[h] = jnp.zeros(turned_p.shape[1:], F32)

        @pl.loop(0, slot_len // block)
        def _(t):
            attend_back(h, t * block, slot_len, 0)
            ticks(h, 0, t, behind)

        @pl.loop(0, slot_len // block)
        def _(t):
            attend_back(h, t * block, seq, 1)
            ticks(h, 1, t, behind)

        turned[h, 64:128, :] = turned_k[...].astype(BF16)
        turned[h, 128:192, :] = turned_v[...].astype(BF16)
        qp_one(h)

        @pl.when(lax.rem(h, 2) == 1)
        def _():
            i = lax.div(h, 2)
            pair = jnp.concatenate([turned[2 * i], turned[2 * i + 1]], axis=0)
            one_t[...] += nn(wq_half[i], pair)

    one_low[...] = one_t[:, other].astype(BF16)
    f_slot, f_send = io.land(), io.leave()
    io.push(f_send, lambda: (one_low, one_got, f_slot, sibling))
    qp_two(2)
    qp_z(1)
    d_one()
    arrived(one_got, f_slot)
    columns = [tall(params_col[cc]) for cc in range(cols)]
    gain = jnp.concatenate([col[:, 0:1] for col in columns], axis=0)
    one = one_t[:, own] + one_got[...].astype(F32)
    x = xt[...].astype(F32)
    mean = jnp.sum(x, axis=0, keepdims=True) * (1.0 / width)
    square = jnp.sum(x * x, axis=0, keepdims=True) * (1.0 / width)
    inverse = lax.rsqrt(square - mean * mean + norm_epsilon)
    scaled = (x - mean) * inverse
    shifted = one * gain
    first = jnp.sum(shifted, axis=0, keepdims=True) * (1.0 / width)
    second = jnp.sum(shifted * scaled, axis=0, keepdims=True) * (1.0 / width)
    gain_sum = jnp.sum(one * scaled, axis=1, keepdims=True)
    bias_sum = jnp.sum(one, axis=1, keepdims=True)
    lane = lax.broadcasted_iota(jnp.int32, (width, 128), 1)
    pair = jnp.where(lane == 0, gain_sum, jnp.where(lane == 1, bias_sum, 0.0))
    pair = jnp.transpose(pair)[0:8]
    all_small[0] = small[...]
    all_small[0, 0:2, :] = pair[0:2]

    def spread(first_lane):
        row = jnp.concatenate([sums[h : h + 1, first_lane : first_lane + 64] for h in range(heads)], axis=1)
        blank = jnp.zeros_like(row)
        return jnp.where(k == 0, jnp.concatenate([row, blank], axis=1), jnp.concatenate([blank, row], axis=1))

    all_small[0, 9:10, :] = spread(0)
    all_small[0, 10:11, :] = spread(64)
    m_slot, m_send = io.land(), io.leave()
    p_slot, p_send = io.land(), io.leave(3)
    v_slot, v_send = io.land(), io.leave(rows - 1)
    io.push(m_send, lambda: (all_small.at[0], got_sib, m_slot, sibling))
    grad_x[...] = (grad_mid_t[...] + inverse * (shifted - first - scaled * second)).astype(BF16)
    arrived(got_sib, m_slot)
    all_small[1] = all_small[0] + got_sib[...]
    for step in range(1, 4):
        io.push(
            p_send + step - 1, lambda step=step: (all_small.at[1], got_plane.at[c], p_slot, (k, z, lax.rem(c + step, 4)))
        )
    io.keep(lambda: all_small.at[1], lambda: got_plane.at[c], p_slot)
    qp_two(3)
    d_two()
    back_start(grad_x, grads, grad_slot)
    qp_z(2)
    arrived(got_plane, p_slot)
    all_small[2] = (got_plane[0] + got_plane[1]) + (got_plane[2] + got_plane[3])
    for step in range(1, rows):
        io.push(
            v_send + step - 1, lambda step=step: (all_small.at[2], got_z.at[z], v_slot, (k, lax.rem(z + step, rows), c))
        )
    io.keep(lambda: all_small.at[2], lambda: got_z.at[z], v_slot)
    u_last()
    o_last()
    qp_z(3)
    d_last()
    arrived(got_z, v_slot)
    f_small[...] = (got_z[0] + got_z[1]) + (got_z[2] + got_z[3])
    qp_last()
    back_done(outs, out_slot)
    back_done(grads, grad_slot)
    last_done()
    io.drain()


def final_kernel(
    outs, grads, f_qp, f_o, f_u, f_d, f_small,
    output, grad_tokens, g1, b1, q_w, c_b, p_b, p_w, o_w, g2, b2, u_w, u_b, d_w, d_b,
):
    k, z, c, _, _ = place()
    for b in range(2):
        for core in range(2):
            size = outs.shape[3]
            output[b, :, core * size : core * size + size] = outs[b, core].astype(F32)
            grad_tokens[b, :, core * size : core * size + size] = grads[b, core].astype(F32)
    for core in range(2):

        @pl.when(k == core)
        def _(core=core):
            q_w[...] = f_qp[core, 0:192, :]
            p_w[...] = f_qp[core, 192:256, :]
            for ref, source in ((o_w, f_o), (d_w, f_d)):
                size = ref.shape[0]
                ref[...] = jnp.transpose(source[:, core * size : core * size + size])
            size = u_w.shape[1]
            u_w[...] = f_u[:, core * size : core * size + size]

    width = f_small.shape[1]
    chip = z * 4 + c
    share = g1.shape[1]
    first = pltpu.roll(f_small[0:8, :], lax.rem(width - (chip * 2 + k) * share, width), 1)
    for row, ref in ((0, g1), (1, b1), (2, g2), (3, b2), (4, d_b)):
        ref[...] = first[row : row + 1, 0:share]
    share = u_b.shape[1]
    line = f_small[pl.ds(5 + z, 1), :]
    line = jnp.broadcast_to(line, (8, width))
    u_b[...] = pltpu.roll(line, lax.rem(width - (c * 2 + k) * share, width), 1)[0:1, 0:share]
    heads, share = c_b.shape
    third = pltpu.roll(f_small[8:16, :], lax.rem(2 * width - heads * 64 * z - (c * 2 + k) * share, width), 1)
    for h in range(heads):
        c_b[h : h + 1, :] = third[1:2, h * 64 : h * 64 + share]
        p_b[h : h + 1, :] = third[2:3, h * 64 : h * 64 + share]


def position_table(seq_len, feature_count):
    positions = np.arange(seq_len, dtype=np.float64)
    exponent = -np.arange(0, feature_count, 2, dtype=np.float64) / feature_count
    angles = positions[:, None] * (10000.0**exponent)[None, :]
    return np.concatenate([np.cos(angles), np.sin(angles)], axis=1).astype(jnp.bfloat16)


def fast_shards(
    tokens, cotangent, piece_starts, ln1_gain, ln1_bias, qkv_weight, content_bias, position_bias, pos_weight,
    out_weight, ln2_gain, ln2_bias, up_weight, up_bias, down_weight, down_bias,
):
    rows, cols = lax.axis_size("row"), lax.axis_size("col")
    half = rows // 2
    micro, feat, seq = tokens.shape
    width = feat * cols
    count = seq // 2
    hidden = up_weight.shape[1]
    heads = content_bias.shape[0] * half
    table = jnp.asarray(position_table(seq, width))
    lines = [ln1_gain, ln1_bias, ln2_gain, ln2_bias, down_bias]
    places = [(line, index * feat) for index, line in enumerate(lines)] + [(up_bias, 8 * 128)]
    packed = sum(jnp.pad(line.astype(F32), (at, 16 * 128 - at - line.shape[0])) for line, at in places)
    packed = packed.reshape(16, 128)
    vm = pl.BlockSpec(memory_space=pltpu.VMEM)
    anywhere = pl.BlockSpec(memory_space=pl.ANY)
    limit = 64 * 1024 * 1024 - 128 * 1024

    def shape(dims, kind=BF16):
        return jax.ShapeDtypeStruct(dims, kind)

    def vmem(dims, kind=BF16):
        return pltpu.VMEM(dims, kind)

    q_cols, p_cols = qkv_weight.shape[1], pos_weight.shape[1]
    o_rows, d_rows = out_weight.shape[0], down_weight.shape[0]
    qp, part = (256, feat), (d_rows // 2, 128)
    results = pl.pallas_call(
        layer_kernel,
        name="layer",
        out_shape=(
            shape((micro, 2, feat, count)),
            shape((micro, 2, feat, count)),
        )
        + (
            shape((2,) + qp, F32), shape((o_rows, 128), F32), shape((feat, hidden), F32), shape((d_rows, 128), F32),
            shape((16, width), F32),
        ),
        in_specs=[anywhere, anywhere, vm, vm, vm, vm] + [anywhere] * 6,
        out_specs=(vm,) * 7,
        scratch_shapes=[
            vmem((count, width)),
            vmem((cols, width, 128)),
            vmem((rows, width, hidden)),
            vmem((cols, rows * hidden, 128)),
            vmem((half, width, q_cols)),
            vmem((half, width, p_cols)),
            vmem((heads, width, 128)),
            vmem((width, count)),
            vmem((width, count)),
            vmem((width, seq)),
            vmem((heads, seq, width + 128)),
            vmem((heads, seq, 128)),
            vmem((heads, seq, 64)),
            vmem((heads, count, count)),
            vmem((heads, count, seq)),
            vmem((heads, seq, 64)),
            vmem((cols, 8, 128), F32),
            vmem((rows, 8, 128), F32),
            vmem((rows,) + content_bias.shape, F32),
            vmem((rows,) + position_bias.shape, F32),
            vmem((seq, width + 128)),
            vmem((seq, heads * 64)),
            vmem(piece_starts.shape, jnp.int32),
            vmem((count, width), F32),
            vmem((count, width)),
            vmem((count, width), F32),
            vmem((count, 1), F32),
            vmem((count, width)),
            vmem((count, width), F32),
            vmem((count, width), F32),
            vmem((width, count)),
            vmem((width, count)),
            vmem((width, count), F32),
            vmem((count, width)),
            vmem((rows, width, hidden)),
            vmem((cols, rows * hidden, 128)),
            vmem((cols, width, 128)),
            vmem((16, width), F32),
            vmem((seq, heads * 64)),
            vmem((heads, seq, 64)),
            vmem((heads, 192, seq)),
            vmem((64, seq), F32),
            vmem((64, seq), F32),
            vmem((heads, 64, width), F32),
            vmem((width, seq), F32),
            vmem((width, count)),
            vmem((width, count)),
            vmem((width, count)),
            vmem((8, 128), F32),
            vmem((heads, cols) + qp),
            vmem((cols, half, o_rows, 128)),
            vmem((half, cols, feat, hidden)),
            vmem((rows, cols) + part),
            vmem((cols, half * o_rows, 128)),
            vmem((half, width, hidden)),
            vmem((rows, cols) + part),
            vmem((cols,) + part),
            vmem((heads, 2) + qp),
            vmem((2, half, o_rows, 128)),
            vmem((half, 2, feat, hidden)),
            vmem((2,) + part),
            vmem((heads,) + qp),
            vmem((half, o_rows, 128)),
            vmem((half, feat, hidden)),
            vmem(part),
            vmem((2, rows) + qp),
            vmem((rows, o_rows, 128)),
            vmem((rows, feat, hidden)),
            vmem((rows, cols) + part),
            vmem((3, 16, width), F32),
            vmem((16, width), F32),
            vmem((cols, 16, width), F32),
            vmem((rows, 16, width), F32),
            pltpu.SemaphoreType.DMA((140,)),
            pltpu.SemaphoreType.DMA((132,)),
        ],
        compiler_params=pltpu.CompilerParams(collective_id=0, has_side_effects=True, vmem_limit_bytes=limit),
    )(
        tokens, cotangent, piece_starts, packed, content_bias, position_bias, table,
        qkv_weight, pos_weight, out_weight, up_weight, down_weight,
    )
    devices = 2 * rows * cols
    vec = shape((1, width // devices), F32)
    bias = shape((content_bias.shape[0], 64 // (2 * cols)), F32)
    done = list(pl.pallas_call(
        final_kernel,
        name="final",
        out_shape=(
            shape(tokens.shape, F32), shape(tokens.shape, F32), vec, vec,
            shape((q_cols // 2, feat), F32), bias, bias, shape((p_cols // 2, feat), F32), shape((64, o_rows), F32), vec, vec,
            shape((feat, hidden // 2), F32), shape((1, rows * hidden // devices), F32), shape((64, d_rows), F32), vec,
        ),
        in_specs=[vm] * 7,
        out_specs=(vm,) * 15,
        compiler_params=pltpu.CompilerParams(vmem_limit_bytes=limit),
    )(*results))
    for index in (4, 7, 8, 13):
        done[index] = done[index].T
    return tuple(v.reshape(-1) if v.shape[0] == 1 else v for v in done)


def solution(mesh):
    in_specs = (
        P(None, "col", ("dp", "row")),
        P(None, "col", ("dp", "row")),
        P(None, ("dp", "col"), None),
        P("col"),
        P("col"),
        P("col", "row"),
        P("row", None),
        P("row", None),
        P("col", "row"),
        P("row", "col"),
        P("col"),
        P("col"),
        P("col", "row"),
        P("row"),
        P("row", "col"),
        P("col"),
    )
    out_specs = (
        P(None, "col", ("dp", "row")),
        P(None, "col", ("dp", "row")),
        P(("row", "col", "dp")),
        P(("row", "col", "dp")),
        P("col", ("row", "dp")),
        P("row", ("col", "dp")),
        P("row", ("col", "dp")),
        P("col", ("row", "dp")),
        P("row", ("col", "dp")),
        P(("row", "col", "dp")),
        P(("row", "col", "dp")),
        P("col", ("row", "dp")),
        P(("row", "col", "dp")),
        P("row", ("col", "dp")),
        P(("row", "col", "dp")),
    )

    def layer(tokens, *others):
        dp, row, col = mesh.shape["dp"], mesh.shape["row"], mesh.shape["col"]
        one_each = tokens.shape[2] == dp * row * SEQ_LEN and tokens.shape[0] * dp == col
        body = fast_shards if one_each and dp == 2 and row == col == 4 else shards
        part = jax.shard_map(body, mesh=mesh, in_specs=in_specs, out_specs=out_specs, check_vma=False)
        return part(tokens, *others)

    return layer
```

```python
from functools import reduce

import jax
import jax.numpy as jnp
import numpy as np
from jax import lax
from jax.experimental import pallas as pl
from jax.experimental.pallas import tpu as pltpu
from jax.sharding import PartitionSpec as P

D = 512
SEQ_LEN = 1024
PIECE = 256


norm_epsilon = 1e-05
big_negative = -1e30
inv_sqrt_two = 0.7071067811865476
inv_sqrt_tau = 0.3989422804014327


def contract(left_op, right_op, flipped):
    if flipped:
        return lax.dot_general(
            left_op, right_op, (((1,), (1,)), ((), ())), preferred_element_type=jnp.float32
        )
    return jnp.dot(left_op, right_op, preferred_element_type=jnp.float32)


def outer_sum(left_op, right_op):
    return lax.dot_general(
        left_op, right_op, (((0,), (0,)), ((), ())), preferred_element_type=jnp.float32
    )


def gather_rows(values):
    return lax.all_gather(values, "row", axis=0, tiled=True)


def gather_cols(values):
    return lax.all_gather(values, "col", axis=0, tiled=True)


def sum_over_cols(gathered, weight, flipped):
    share_rows = gathered.shape[0] // lax.axis_size("col")

    def partial_term(offset, amount):
        return contract(gathered, weight, flipped)

    return lax.psum_scatter(
        partial_term(jnp.int32(0), lax.axis_size("col") * share_rows),
        "col",
        scatter_dimension=0,
        tiled=True,
    )


def sum_over_rows(gathered, weight, flipped):
    share_rows = gathered.shape[0] // lax.axis_size("row")

    def partial_term(offset, amount):
        return contract(gathered, weight, flipped)

    return lax.psum_scatter(
        partial_term(jnp.int32(0), lax.axis_size("row") * share_rows),
        "row",
        scatter_dimension=0,
        tiled=True,
    )


def feature_sums(first_sum, second_sum):
    return lax.psum((first_sum, second_sum), "col")


def normalize(values, gain, bias):
    feature_count = values.shape[1] * lax.axis_size("col")
    total_row, square_row = feature_sums(jnp.sum(values, axis=1), jnp.sum(values * values, axis=1))
    mean_row = total_row / feature_count
    inverse = lax.rsqrt(square_row / feature_count - mean_row * mean_row + norm_epsilon)
    scaled = (values - mean_row[:, None]) * inverse[:, None]
    return (scaled * gain + bias, scaled, inverse)


def normalize_back(grad_in, scaled, inverse, gain):
    feature_count = grad_in.shape[1] * lax.axis_size("col")
    shifted = grad_in * gain
    first_sum, second_sum = feature_sums(
        jnp.sum(shifted, axis=1), jnp.sum(shifted * scaled, axis=1)
    )
    back_rows = inverse[:, None] * (
        shifted - first_sum[:, None] / feature_count - scaled * second_sum[:, None] / feature_count
    )
    return (back_rows, jnp.sum(grad_in * scaled, axis=0), jnp.sum(grad_in, axis=0))


def gelu_exact(values):
    return 0.5 * values * (1.0 + jax.scipy.special.erf(values * inv_sqrt_two))


def gelu_slope(values):
    return (
        0.5 * (1.0 + jax.scipy.special.erf(values * inv_sqrt_two))
        + values * jnp.exp(-0.5 * values * values) * inv_sqrt_tau
    )


def sinusoid_table(seq_len, feature_count):
    offsets = jnp.arange(2 * seq_len - 1, dtype=jnp.float32) - (seq_len - 1)
    frequency = 10000.0 ** (-jnp.arange(0, feature_count, 2, dtype=jnp.float32) / feature_count)
    angles = offsets[:, None] * frequency[None, :]
    return jnp.concatenate([jnp.sin(angles), jnp.cos(angles)], axis=1).astype(jnp.bfloat16)


def piece_labels(positions, starts, piece_len):
    inside = (positions[:, None] >= starts[None, :]) & (
        positions[:, None] < starts[None, :] + piece_len
    )
    numbers = jnp.arange(1, starts.shape[0] + 1, dtype=jnp.int32)
    return jnp.sum(jnp.where(inside, numbers[None, :], 0), axis=1) - 1


def block_mask(offset, block_len, labels):
    positions = jnp.arange(labels.shape[0], dtype=jnp.int32)
    row_pos = offset + jnp.arange(block_len, dtype=jnp.int32)
    row_labels = lax.dynamic_slice_in_dim(labels, offset, block_len, 0)
    same_piece = (row_labels[:, None] == labels[None, :]) & (row_labels[:, None] >= 0)
    return (positions[None, :] <= row_pos[:, None]) | same_piece


def skew_rows(unshifted_reversed_scores, key_total):
    head_total, row_total, rel_span = unshifted_reversed_scores.shape
    flattened = unshifted_reversed_scores.reshape(head_total, row_total * rel_span)
    window = lax.slice_in_dim(
        flattened, row_total - 1, row_total - 1 + row_total * (rel_span - 1), axis=1
    )
    return window.reshape(head_total, row_total, rel_span - 1)[:, :, :key_total]


def unskew_rows(grad_pos, rel_span):
    head_total, row_total, key_total = grad_pos.shape
    padded = jnp.pad(grad_pos, ((0, 0), (0, 0), (0, rel_span - 1 - key_total)))
    flattened = padded.reshape(head_total, row_total * (rel_span - 1))
    flattened = jnp.pad(flattened, ((0, 0), (row_total - 1, 1)))
    return flattened.reshape(head_total, row_total, rel_span)


def block_scores(qu_block, query_position_block, key_rows, relative_block, allowed):
    content = jnp.einsum("ihd,jhd->hij", qu_block, key_rows, preferred_element_type=jnp.float32)
    unshifted_reversed_scores = jnp.einsum(
        "sgw,egw->gse", query_position_block, relative_block, preferred_element_type=jnp.float32
    )
    position = skew_rows(unshifted_reversed_scores, key_rows.shape[0])
    return jnp.where(allowed[None], content + position, big_negative)


def attention_forward(query_u, query_v, key_rows, value_rows, relative_rev, labels):
    seq_len, head_count, head_dim = key_rows.shape
    block_len = min(512, seq_len)
    rel_span = block_len + seq_len - 1
    offsets = jnp.arange(seq_len // block_len, dtype=jnp.int32) * block_len

    def attend(offset):
        qu_block = lax.dynamic_slice_in_dim(query_u, offset, block_len, 0)
        query_position_block = lax.dynamic_slice_in_dim(query_v, offset, block_len, 0)
        relative_block = lax.dynamic_slice_in_dim(
            relative_rev, seq_len - block_len - offset, rel_span, 0
        )
        scores = block_scores(
            qu_block,
            query_position_block,
            key_rows,
            relative_block,
            block_mask(offset, block_len, labels),
        )
        row_max = jnp.max(scores, axis=2, keepdims=True)
        log_total = row_max + jnp.log(jnp.sum(jnp.exp(scores - row_max), axis=2, keepdims=True))
        attn_prob = jnp.exp(scores - log_total).astype(jnp.bfloat16)
        result = jnp.einsum(
            "hij,jhd->ihd", attn_prob, value_rows, preferred_element_type=jnp.float32
        )
        return (result, log_total[:, :, 0])

    results, log_totals = lax.map(attend, offsets)
    return (results.reshape(seq_len, head_count * head_dim), log_totals)


def attention_backward(
    query_u, query_v, key_rows, value_rows, relative_rev, labels, log_totals, grad_att
):
    seq_len, head_count, head_dim = key_rows.shape
    block_len = min(512, seq_len)
    rel_span = block_len + seq_len - 1
    offsets = jnp.arange(seq_len // block_len, dtype=jnp.int32) * block_len

    def back_block(carried, sliced):
        grad_keys, grad_values, grad_rel = carried
        offset, log_total = sliced
        rel_start = seq_len - block_len - offset
        qu_block = lax.dynamic_slice_in_dim(query_u, offset, block_len, 0)
        query_position_block = lax.dynamic_slice_in_dim(query_v, offset, block_len, 0)
        relative_block = lax.dynamic_slice_in_dim(relative_rev, rel_start, rel_span, 0)
        scores = block_scores(
            qu_block,
            query_position_block,
            key_rows,
            relative_block,
            block_mask(offset, block_len, labels),
        )
        attn_prob = jnp.exp(scores - log_total[:, :, None])
        low_prob = attn_prob.astype(jnp.bfloat16)
        grad_block = lax.dynamic_slice_in_dim(grad_att, offset, block_len, 0)
        grad_prob = jnp.einsum(
            "ihd,jhd->hij", grad_block, value_rows, preferred_element_type=jnp.float32
        )
        row_inner = jnp.sum(attn_prob * grad_prob, axis=2, keepdims=True)
        grad_scores = (attn_prob * (grad_prob - row_inner)).astype(jnp.bfloat16)
        grad_values = grad_values + jnp.einsum(
            "hij,ihd->jhd", low_prob, grad_block, preferred_element_type=jnp.float32
        )
        grad_keys = grad_keys + jnp.einsum(
            "hij,ihd->jhd", grad_scores, qu_block, preferred_element_type=jnp.float32
        )
        grad_qu = jnp.einsum(
            "hij,jhd->ihd", grad_scores, key_rows, preferred_element_type=jnp.float32
        )
        gradient_unshifted = unskew_rows(grad_scores, rel_span)
        grad_qv = jnp.einsum(
            "qjp,pqr->jqr", gradient_unshifted, relative_block, preferred_element_type=jnp.float32
        )
        rel_part = jnp.einsum(
            "nfx,fne->xne",
            gradient_unshifted,
            query_position_block,
            preferred_element_type=jnp.float32,
        )
        current = lax.dynamic_slice_in_dim(grad_rel, rel_start, rel_span, 0)
        grad_rel = lax.dynamic_update_slice_in_dim(grad_rel, current + rel_part, rel_start, 0)
        return ((grad_keys, grad_values, grad_rel), (grad_qu, grad_qv))

    zero_rows = jnp.zeros((seq_len, head_count, head_dim), jnp.float32)
    zero_rel = jnp.zeros((2 * seq_len - 1, head_count, head_dim), jnp.float32)
    carried, stacked = lax.scan(back_block, (zero_rows, zero_rows, zero_rel), (offsets, log_totals))
    grad_keys, grad_values, grad_rel = carried
    grad_qu = stacked[0].reshape(seq_len, head_count, head_dim)
    grad_qv = stacked[1].reshape(seq_len, head_count, head_dim)
    return (grad_qu, grad_qv, grad_keys, grad_values, grad_rel)


def heads_pass(packed, content_bias, position_bias, relative_rev, labels):
    seq_len = packed.shape[0]
    head_count, head_dim = content_bias.shape
    scaling = head_dim ** (-0.5)
    packed = packed.reshape(seq_len, head_count, 3, head_dim)
    queries = packed[:, :, 0].astype(jnp.float32)
    key_rows = packed[:, :, 1]
    value_rows = packed[:, :, 2]
    query_u = ((queries + content_bias) * scaling).astype(jnp.bfloat16)
    query_v = ((queries + position_bias) * scaling).astype(jnp.bfloat16)
    attended, log_totals = attention_forward(
        query_u, query_v, key_rows, value_rows, relative_rev, labels
    )
    return (attended.astype(jnp.bfloat16), (query_u, query_v, key_rows, value_rows, log_totals))


def heads_back(kept, relative_rev, labels, grad_att):
    query_u, query_v, key_rows, value_rows, log_totals = kept
    seq_len, head_count, head_dim = key_rows.shape
    scaling = head_dim ** (-0.5)
    grad_att = grad_att.reshape(seq_len, head_count, head_dim)
    grad_qu, grad_qv, grad_keys, grad_values, grad_rel = attention_backward(
        query_u, query_v, key_rows, value_rows, relative_rev, labels, log_totals, grad_att
    )
    cbias_part = jnp.sum(grad_qu, axis=0) * scaling
    pbias_part = jnp.sum(grad_qv, axis=0) * scaling
    grad_query = (grad_qu + grad_qv) * scaling
    grad_packed = jnp.stack([grad_query, grad_keys, grad_values], axis=2)
    grad_packed = grad_packed.reshape(seq_len, head_count * 3 * head_dim).astype(jnp.bfloat16)
    rel_low = grad_rel.reshape(2 * seq_len - 1, head_count * head_dim).astype(jnp.bfloat16)
    return (grad_packed, rel_low, cbias_part, pbias_part)


def grid_micro(seq_feats, cot_feats, params, shared):
    (
        ln1_gain,
        ln1_bias,
        qkv_weight,
        content_bias,
        position_bias,
        out_weight,
        ln2_gain,
        ln2_bias,
        up_weight,
        up_bias,
        down_weight,
        down_bias,
    ) = params
    relative_rev, table_rev, labels = shared
    seq_in = seq_feats.astype(jnp.float32).T
    normed_one, scaled_one, inverse_one = normalize(seq_in, ln1_gain, ln1_bias)
    gathered_one = gather_rows(normed_one.astype(jnp.bfloat16))
    packed = sum_over_cols(gathered_one, qkv_weight, False).astype(jnp.bfloat16)
    attended, kept = heads_pass(packed, content_bias, position_bias, relative_rev, labels)
    att_gathered = gather_cols(attended)
    middle = seq_in + sum_over_rows(att_gathered, out_weight, False)
    normed_two, scaled_two, inverse_two = normalize(middle, ln2_gain, ln2_bias)
    gathered_two = gather_rows(normed_two.astype(jnp.bfloat16))
    pre_act = sum_over_cols(gathered_two, up_weight, False) + up_bias
    activated = gelu_exact(pre_act).astype(jnp.bfloat16)
    act_gathered = gather_cols(activated)
    output = middle + sum_over_rows(act_gathered, down_weight, False) + down_bias
    grad_final = cot_feats.T
    gout = grad_final.astype(jnp.float32)
    final_gathered = gather_rows(grad_final)
    grad_act = sum_over_cols(final_gathered, down_weight, True)
    grad_pre = (grad_act * gelu_slope(pre_act)).astype(jnp.bfloat16)
    pre_gathered = gather_cols(grad_pre)
    grad_two = sum_over_rows(pre_gathered, up_weight, True)
    backward_second, gain_two, bias_two = normalize_back(
        grad_two, scaled_two, inverse_two, ln2_gain
    )
    grad_middle = gout + backward_second
    grad_branch = grad_middle.astype(jnp.bfloat16)
    branch_gathered = gather_rows(grad_branch)
    grad_att = sum_over_cols(branch_gathered, out_weight, True).astype(jnp.bfloat16)
    grad_packed, rel_low, cbias_part, pbias_part = heads_back(kept, relative_rev, labels, grad_att)
    packed_gathered = gather_cols(grad_packed)
    grad_one = sum_over_rows(packed_gathered, qkv_weight, True)
    back_one, gain_one, bias_one = normalize_back(grad_one, scaled_one, inverse_one, ln1_gain)
    grad_in = grad_middle + back_one
    collected = (
        outer_sum(gathered_one, packed_gathered),
        outer_sum(att_gathered, branch_gathered),
        outer_sum(gathered_two, pre_gathered),
        outer_sum(act_gathered, final_gathered),
        outer_sum(table_rev, rel_low),
        cbias_part,
        pbias_part,
        jnp.sum(grad_pre.astype(jnp.float32), axis=0),
        gain_one,
        bias_one,
        gain_two,
        bias_two,
        jnp.sum(gout, axis=0),
    )
    return (output.T, grad_in.T, collected)


def embed_heads(part, row_pick, col_count):
    head_count = part.shape[0]
    spread = jnp.transpose(part.reshape(head_count, col_count, -1), (1, 0, 2))
    placed = jnp.where(row_pick[:, None, None, None], spread[None], 0.0)
    return placed.reshape(row_pick.shape[0] * col_count, head_count, -1)


def shards(
    tokens,
    cotangent,
    piece_starts,
    ln1_gain,
    ln1_bias,
    qkv_weight,
    content_bias,
    position_bias,
    pos_weight,
    out_weight,
    ln2_gain,
    ln2_bias,
    up_weight,
    up_bias,
    down_weight,
    down_bias,
):
    micro_count = tokens.shape[0]
    row_count = lax.axis_size("row")
    col_count = lax.axis_size("col")
    grid_cells = row_count * col_count
    head_count, head_dim = content_bias.shape
    pos_cols = lax.all_gather(pos_weight, "col", axis=0, tiled=True)
    table_rev = sinusoid_table(SEQ_LEN, D)[::-1]
    relative_rev = jnp.dot(table_rev, pos_cols, preferred_element_type=jnp.float32).astype(
        jnp.bfloat16
    )
    relative_rev = relative_rev.reshape(2 * SEQ_LEN - 1, head_count, head_dim)
    positions = jnp.arange(SEQ_LEN, dtype=jnp.int32)
    params = (
        ln1_gain,
        ln1_bias,
        qkv_weight,
        content_bias,
        position_bias,
        out_weight,
        ln2_gain,
        ln2_bias,
        up_weight,
        up_bias,
        down_weight,
        down_bias,
    )
    outputs, grad_inputs, part_lists = ([], [], [])
    for micro_idx in range(micro_count):
        labels = piece_labels(positions, piece_starts[micro_idx, 0], PIECE)
        out_feats, grad_feats, collected = grid_micro(
            tokens[micro_idx], cotangent[micro_idx], params, (relative_rev, table_rev, labels)
        )
        outputs.append(out_feats)
        grad_inputs.append(grad_feats)
        part_lists.append(collected)
    totals = [
        reduce(jnp.add, [collected[member] for collected in part_lists]) for member in range(13)
    ]
    (
        acc_qkv,
        acc_out,
        acc_up,
        acc_down,
        acc_pos,
        acc_cbias,
        acc_pbias,
        acc_ubias,
        acc_g1,
        acc_b1,
        acc_g2,
        acc_b2,
        acc_db,
    ) = totals
    row_pick = jnp.arange(row_count, dtype=jnp.int32) == lax.axis_index("row")
    pos_term = jnp.where(row_pick[:, None, None], acc_pos[None], 0.0).reshape(
        row_count * acc_pos.shape[0], -1
    )
    cbias_term = embed_heads(acc_cbias, row_pick, col_count)
    pbias_term = embed_heads(acc_pbias, row_pick, col_count)
    col_pick = jnp.arange(col_count, dtype=jnp.int32) == lax.axis_index("col")
    ubias_term = jnp.where(row_pick[:, None], acc_ubias[None], 0.0).reshape(grid_cells, -1)
    norm_terms = [
        jnp.where(col_pick[:, None], vector[None], 0.0).reshape(grid_cells, -1)
        for vector in (acc_g1, acc_b1, acc_g2, acc_b2, acc_db)
    ]
    sum_pos, sum_cbias, sum_pbias, sum_ubias, sum_g1, sum_b1, sum_g2, second_bias_total, sum_db = (
        lax.psum_scatter(pos_term, ("row", "col"), scatter_dimension=0, tiled=True),
        lax.psum_scatter(cbias_term, ("row", "col"), scatter_dimension=0, tiled=True),
        lax.psum_scatter(pbias_term, ("row", "col"), scatter_dimension=0, tiled=True),
        lax.psum_scatter(ubias_term, ("row", "col"), scatter_dimension=0, tiled=True),
        lax.psum_scatter(norm_terms[0], ("row", "col"), scatter_dimension=0, tiled=True),
        lax.psum_scatter(norm_terms[1], ("row", "col"), scatter_dimension=0, tiled=True),
        lax.psum_scatter(norm_terms[2], ("row", "col"), scatter_dimension=0, tiled=True),
        lax.psum_scatter(norm_terms[3], ("row", "col"), scatter_dimension=0, tiled=True),
        lax.psum_scatter(norm_terms[4], ("row", "col"), scatter_dimension=0, tiled=True),
    )
    sum_qkv, sum_out, sum_up, sum_down = (acc_qkv, acc_out, acc_up, acc_down)
    summed = (
        lax.psum_scatter(
            sum_qkv.astype(jnp.bfloat16), "dp", scatter_dimension=1, tiled=True
        ).astype(jnp.float32),
        lax.psum_scatter(
            sum_out.astype(jnp.bfloat16), "dp", scatter_dimension=1, tiled=True
        ).astype(jnp.float32),
        lax.psum_scatter(sum_up.astype(jnp.bfloat16), "dp", scatter_dimension=1, tiled=True).astype(
            jnp.float32
        ),
        lax.psum_scatter(
            sum_down.astype(jnp.bfloat16), "dp", scatter_dimension=1, tiled=True
        ).astype(jnp.float32),
        lax.psum_scatter(
            sum_pos.astype(jnp.bfloat16), "dp", scatter_dimension=1, tiled=True
        ).astype(jnp.float32),
        lax.psum_scatter(
            sum_cbias.astype(jnp.bfloat16), "dp", scatter_dimension=2, tiled=True
        ).astype(jnp.float32),
        lax.psum_scatter(
            sum_pbias.astype(jnp.bfloat16), "dp", scatter_dimension=2, tiled=True
        ).astype(jnp.float32),
        lax.psum_scatter(
            sum_ubias.astype(jnp.bfloat16), "dp", scatter_dimension=1, tiled=True
        ).astype(jnp.float32),
        lax.psum_scatter(sum_g1.astype(jnp.bfloat16), "dp", scatter_dimension=1, tiled=True).astype(
            jnp.float32
        ),
        lax.psum_scatter(sum_b1.astype(jnp.bfloat16), "dp", scatter_dimension=1, tiled=True).astype(
            jnp.float32
        ),
        lax.psum_scatter(sum_g2.astype(jnp.bfloat16), "dp", scatter_dimension=1, tiled=True).astype(
            jnp.float32
        ),
        lax.psum_scatter(
            second_bias_total.astype(jnp.bfloat16), "dp", scatter_dimension=1, tiled=True
        ).astype(jnp.float32),
        lax.psum_scatter(sum_db.astype(jnp.bfloat16), "dp", scatter_dimension=1, tiled=True).astype(
            jnp.float32
        ),
    )
    (
        grad_qkv_w,
        grad_out_w,
        grad_up_w,
        grad_down_w,
        grad_pos_w,
        grad_cbias,
        grad_pbias,
        grad_ubias,
        grad_g1,
        grad_b1,
        grad_g2,
        grad_b2,
        grad_dbias,
    ) = summed
    output_rows = jnp.stack(outputs, axis=0)
    grad_rows = jnp.stack(grad_inputs, axis=0)
    return (
        output_rows,
        grad_rows,
        grad_g1.reshape(-1),
        grad_b1.reshape(-1),
        grad_qkv_w,
        grad_cbias.reshape(head_count, -1),
        grad_pbias.reshape(head_count, -1),
        grad_pos_w,
        grad_out_w,
        grad_g2.reshape(-1),
        grad_b2.reshape(-1),
        grad_up_w,
        grad_ubias.reshape(-1),
        grad_down_w,
        grad_dbias.reshape(-1),
    )


MESH = pl.DeviceIdType.MESH
F32 = jnp.float32
BF16 = jnp.bfloat16


def aligned(index, size):
    return index if isinstance(index, int) else pl.multiple_of(index, size)


def nt(a, b):
    return lax.dot_general(a, b, (((1,), (1,)), ((), ())), preferred_element_type=F32)


def nn(a, b):
    return lax.dot_general(a, b, (((1,), (0,)), ((), ())), preferred_element_type=F32)


def tn(a, b):
    return lax.dot_general(a, b, (((0,), (0,)), ((), ())), preferred_element_type=F32)


def place():
    k, z, c = lax.axis_index("dp"), lax.axis_index("row"), lax.axis_index("col")
    cx = c + 1 - 2 * lax.rem(c, 2)
    cy = lax.rem(c + 2, 4)
    near = (1 - k) * cx + k * cy
    far = k * cx + (1 - k) * cy
    return k, z, c, near, far


def enter(rows):
    k, z, c, _, _ = place()
    barrier = pltpu.get_barrier_semaphore()
    peers = [(1 - k, z, c)]
    for step in range(1, rows):
        peers.append((k, lax.rem(z + step, rows), c))
    for step in range(1, 4):
        for core in range(2):
            peers.append((0 * k + core, z, lax.rem(c + step, 4)))
    for peer in peers:
        pl.semaphore_signal(barrier, inc=1, device_id=peer, device_id_type=MESH)
    pl.semaphore_wait(barrier, len(peers))


class Copies:
    def __init__(self, send, recv):
        self.send, self.recv = send, recv
        self.sends, self.recvs = 0, 0
        self.pending = {}

    def leave(self, count=1):
        first = self.sends
        self.sends += count
        return first

    def land(self, count=1):
        first = self.recvs
        self.recvs += count
        return first

    def copy(self, send_slot, build):
        src, dst, recv_slot, peer = build()
        return pltpu.make_async_remote_copy(
            src, dst, self.send.at[send_slot], self.recv.at[recv_slot], device_id=peer, device_id_type=MESH
        )

    def push(self, send_slot, build, when=None):
        if when is None:
            self.copy(send_slot, build).start()
        else:
            pl.when(when())(lambda: self.copy(send_slot, build).start())
        self.later(send_slot, build, when)

    def later(self, send_slot, build, when=None):
        self.pending[send_slot] = (lambda: self.copy(send_slot, build), when)

    def keep(self, src, dst, slot, when=None):
        def go():
            pltpu.make_async_copy(src(), dst(), self.recv.at[slot]).start()

        if when is None:
            go()
        else:
            pl.when(when())(go)

    def arrived(self, dst, slot):
        pltpu.make_async_copy(dst, dst, self.recv.at[slot]).wait()

    def drain(self):
        for copy, when in self.pending.values():
            if when is None:
                copy().wait_send()
            else:
                pl.when(when())(lambda copy=copy: copy().wait_send())


def tall(row):
    padded = jnp.concatenate([row, jnp.zeros((120, 128), F32)], axis=0)
    return jnp.transpose(padded)


def erf_parts(values):
    erf = lax.erf(values * inv_sqrt_two)
    return 0.5 * (1.0 + erf)


def layer_kernel(
    tok, cot, starts, packed, cbias, pbias, table, wq, wp, wo, wu, wd,
    outs, grads, f_qp, f_o, f_u, f_d, f_small,
    att, wo_all, wu_all, wd_all, wq_half, wp_half, wp_head, xt, ct, normed_t, qcat, keys, vals, probs_a, probs_b, heads_out,
    params_col, params_row, cb_all, pb_all, kcat, own_att, starts_got,
    mid, norm, hat, inv, gout, acc_out, acc_two, tall_norm, out_t, grad_mid_t, grad_att, g_up, g_down, g_out, small,
    grad_o, head_grad, turned, turned_k, turned_v, turned_p, one_t, one_low, one_got, grad_x, sums,
    hs_qp, hs_o, hs_u, hs_d, r0_o, r0_u, r0_d, s_d,
    r1_qp, r1_o, r1_u, r1_d, r2_qp, r2_o, r2_u, r2_d, r3_qp, r3_o, r3_u, r3_d,
    all_small, got_sib, got_plane, got_z, send, recv,
):
    rows = wu_all.shape[0]
    cols = wo_all.shape[0]
    half = rows // 2
    heads = 2 * half
    k, z, c, near, far = place()
    opposite = 3 - c
    sibling = (1 - k, z, c)
    io = Copies(send, recv)
    mine = lax.div(z, half) == k
    arrived = io.arrived
    enter(rows)

    def q_block(cc, i):
        return wq_half.at[i, pl.ds(aligned(cc * 128, 128), 128), :]

    def p_block(cc, i):
        return wp_half.at[i, pl.ds(aligned(cc * 128, 128), 128), :]

    def u_block(cc, core=k):
        return wu_all.at[pl.ds(core * half, half), pl.ds(aligned(cc * 128, 128), 128), :]

    def o_block(cc, core=k):
        size = wo_all.shape[1] // 2
        return wo_all.at[cc, pl.ds(aligned(core * size, 128), size), :]

    def u_one(i):
        return wu_all.at[k * half + i, pl.ds(aligned(c * 128, 128), 128), :]

    def o_one(i):
        size = wo_all.shape[1] // rows
        return wo_all.at[c, pl.ds(aligned((k * half + i) * size, 128), size), :]

    weights = {
        "q": (wq, lambda i: q_block(c, i), q_block), "p": (wp, lambda i: p_block(c, i), p_block), "o": (wo, o_one, o_block),
        "u": (wu, u_one, u_block),
    }
    z_slot = {name: io.land(half) for name in weights}
    z_send = {name: io.leave(rows - 1) for name in weights}
    near_slot = {name: (io.leave(half), io.land(half)) for name in weights}
    far_slot = {name: (io.leave(2 * half), io.land(2 * half)) for name in weights}
    sib_slot = {name: (io.leave(), io.land()) for name in ("o", "u")}
    turn = z - k * half

    def z_start(name):
        ref, one, _ = weights[name]
        io.keep(lambda: ref, lambda: one(turn), z_slot[name] + turn, lambda: mine)
        for step in range(1, rows):
            io.push(
                z_send[name] + step - 1,
                lambda step=step: (ref, one(turn), z_slot[name] + turn, (k, lax.rem(z + step, rows), c)),
                lambda: mine,
            )

    def z_done(name, i=None):
        _, one, _ = weights[name]
        for number in range(half) if i is None else (i,):
            arrived(one(number), z_slot[name] + number)

    def block_of(name, cc, i):
        block = weights[name][2]
        return block(cc) if i is None else block(cc, i)

    def near_start(name, i=None):
        leave, land = (slot + (i or 0) for slot in near_slot[name])
        io.push(leave, lambda: (block_of(name, c, i), block_of(name, c, i), land, (k, z, near)))

    def near_done(name, i=None):
        arrived(block_of(name, near, i), near_slot[name][1] + (i or 0))

    def far_start(name, i=None):
        leave, land = (slot + 2 * (i or 0) for slot in far_slot[name])
        io.push(leave, lambda: (block_of(name, c, i), block_of(name, c, i), land, (k, z, far)))
        io.push(leave + 1, lambda: (block_of(name, near, i), block_of(name, near, i), land + 1, (k, z, far)))

    def far_done(name, i=None):
        land = far_slot[name][1] + (0 if i is None else 2 * i)
        arrived(block_of(name, far, i), land)
        arrived(block_of(name, opposite, i), land + 1)

    def core_half(name, core):
        if name == "u":
            return wu_all.at[pl.ds(core * half, half)]
        size = wo_all.shape[1] // 2
        return wo_all.at[:, pl.ds(aligned(core * size, 128), size), :]

    def sib_start(name):
        leave, land = sib_slot[name]
        io.push(leave, lambda: (core_half(name, k), core_half(name, k), land, sibling))

    def sib_done(name):
        arrived(core_half(name, 1 - k), sib_slot[name][1])

    part_rows = wd.shape[0] // 2

    def d_cells(zz, core):
        return wd_all.at[:, pl.ds(aligned((2 * zz + core) * part_rows, 128), part_rows), :]

    def d_cell(cc, core=k):
        return wd_all.at[cc, pl.ds(aligned((2 * z + core) * part_rows, 128), part_rows), :]

    def d_own():
        return wd.at[pl.ds(aligned(k * part_rows, 128), part_rows), :]

    d_plane = (io.leave(3), io.land(4))
    d_line = (io.leave(5), io.land(rows))
    d_sibs = (io.leave(rows), io.land(rows))
    relaying = jnp.logical_and(z > 0, z < rows - 1)
    relayed = 2 * (rows - 1) - (rows - 1) * z

    def wd_start():
        leave, land = d_plane
        io.keep(d_own, lambda: d_cell(c), land)
        io.push(leave, lambda: (d_own(), d_cell(c), land + 1, (k, z, near)))
        io.push(leave + 1, lambda: (d_own(), d_cell(c), land + 2, (k, z, far)))

    def wd_far():
        leave, land = d_plane
        arrived(d_cell(near), land + 1)
        io.push(leave + 2, lambda: (d_cell(near), d_cell(near), land + 3, (k, z, far)))

    def wd_sib(number):
        zz = lax.rem(z + number, rows)
        leave, land = d_sibs
        io.push(leave + number, lambda: (d_cells(lax.rem(z + number, rows), k),) * 2 + (land + lax.rem(z + number, rows), sibling))

    def wd_line():
        land = d_plane[1]
        arrived(d_cell(c), land)
        arrived(d_cell(far), land + 2)
        arrived(d_cell(opposite), land + 3)
        leave, land = d_line
        for number, step in enumerate((2, -2, 1, -1)):
            io.push(
                leave + number,
                lambda step=step: (d_cells(z, k), d_cells(z, k), land + z, (k, lax.rem(z + step + rows, rows), c)),
                lambda step=step: jnp.logical_and(z + step >= 0, z + step < rows),
            )
        wd_sib(0)

    def wd_relay():
        leave, land = d_line

        @pl.when(relaying)
        def _():
            arrived(d_cells(relayed, k), land + relayed)

        io.push(
            leave + 4,
            lambda: (d_cells(relayed, k), d_cells(relayed, k), land + relayed, (k, rows - 1 - relayed, c)),
            lambda: relaying,
        )

    def wd_done(number):
        zz = lax.rem(z + number, rows)

        @pl.when(jnp.logical_not(jnp.logical_and(relaying, zz == relayed)))
        def _():
            arrived(d_cells(zz, k), d_line[1] + zz)

        wd_sib(number)

    def wd_all_done():
        for number in range(rows):
            zz = lax.rem(z + number, rows)
            arrived(d_cells(zz, 1 - k), d_sibs[1] + zz)

    feat = tok.shape[1]
    count = xt.shape[1]
    x_slot = io.land(4)
    x_send = io.leave(4)
    n_slot, n_send = io.land(), io.leave()

    def is_local(b, core):
        return jnp.logical_and(2 * b + k == c, core == k)

    def spread_features(source, target, leave, land):
        for b in range(2):
            for core in range(2):

                def src(b=b, core=core):
                    return source.at[b, :, pl.ds(core * count, count)]

                def dst():
                    return target.at[pl.ds(aligned(c * feat, 128), feat), :]

                io.keep(src, dst, land + c, lambda b=b, core=core: is_local(b, core))
                io.push(
                    leave + 2 * b + core,
                    lambda src=src, dst=dst, b=b, core=core: (src(), dst(), land + c, (0 * k + core, z, 2 * b + k)),
                    lambda b=b, core=core: jnp.logical_not(is_local(b, core)),
                )

    z_start("q")
    spread_features(tok, xt, x_send, x_slot)
    z_start("p")

    t_slot = io.land()
    io.keep(lambda: table, lambda: kcat.at[:, pl.ds(0, table.shape[1])], t_slot)
    g_col, g_row, g_cb, g_pb = io.land(), io.land(), io.land(), io.land()
    col_send = io.leave(3)
    for step in range(1, 4):
        io.push(
            col_send + step - 1,
            lambda step=step: (packed.at[pl.ds(0, 8)], params_col.at[c], g_col, (k, z, lax.rem(c + step, 4))),
        )
    io.keep(lambda: packed.at[pl.ds(0, 8)], lambda: params_col.at[c], g_col)
    for source, target, slot in ((packed.at[pl.ds(8, 8)], params_row, g_row), (cbias, cb_all, g_cb), (pbias, pb_all, g_pb)):
        row_send = io.leave(rows - 1)
        for step in range(1, rows):
            io.push(
                row_send + step - 1,
                lambda step=step, source=source, target=target, slot=slot: (
                    source, target.at[z], slot, (k, lax.rem(z + step, rows), c)
                ),
            )
        io.keep(lambda source=source: source, lambda target=target: target.at[z], slot)
    s_slot = io.land()
    s_send = io.leave(4)
    for b in range(2):
        for core in range(2):
            io.keep(
                lambda: starts, lambda: starts_got, s_slot,
                lambda b=b, core=core: jnp.logical_and(c == z, is_local(b, core)),
            )
            io.push(
                s_send + 2 * b + core,
                lambda b=b, core=core: (starts, starts_got, s_slot, (0 * k + core, z, 2 * b + k)),
                lambda b=b, core=core: jnp.logical_and(c == z, jnp.logical_not(is_local(b, core))),
            )
    for name in ("o", "u"):
        z_start(name)

    c_slot = io.land(4)
    c_send = io.leave(4)
    z_done("q", 0)
    near_start("q", 0)
    z_done("p", 0)
    near_start("p", 0)
    wd_start()
    arrived(params_col, g_col)
    arrived(params_row, g_row)
    arrived(cb_all, g_cb)
    arrived(pb_all, g_pb)
    arrived(starts_got, s_slot)
    near_done("q", 0)
    far_start("q", 0)
    for cc in range(4):
        arrived(xt.at[pl.ds(cc * feat, feat), :], x_slot + cc)

    columns = [tall(params_col[cc]) for cc in range(4)]
    gain = jnp.concatenate([col[:, 0:1] for col in columns], axis=0)
    bias = jnp.concatenate([col[:, 1:2] for col in columns], axis=0)
    width = xt.shape[0]
    seq = normed_t.shape[1]
    piece = PIECE
    blocks = seq // 256
    other = pl.ds(aligned((1 - k) * count, count), count)
    own = pl.ds(aligned(k * count, count), count)

    @pl.loop(0, count // 256)
    def _(t):
        x = xt[:, pl.ds(aligned(t * 256, 256), 256)].astype(F32)
        mean = jnp.sum(x, axis=0, keepdims=True) * (1.0 / width)
        square = jnp.sum(x * x, axis=0, keepdims=True) * (1.0 / width)
        inverse = lax.rsqrt(square - mean * mean + norm_epsilon)
        here = pl.ds(aligned(k * count + t * 256, 256), 256)
        normed_t[:, here] = ((x - mean) * inverse * gain + bias).astype(BF16)

    io.push(n_send, lambda: (normed_t.at[:, own], normed_t.at[:, own], n_slot, sibling))
    near_done("p", 0)
    far_start("p", 0)
    wd_far()
    for name in ("q", "p"):
        z_done(name, 1)
        near_start(name, 1)
    z_done("o")
    near_start("o")
    arrived(kcat.at[:, pl.ds(0, 512)], t_slot)
    scale = 0.125
    none = jnp.zeros((256, 64), F32)

    def project(i, number):
        t = lax.rem(k * (blocks // 2) + number, blocks)

        @pl.when(jnp.logical_and(i == 0, number == blocks // 2))
        def _():
            arrived(normed_t.at[:, other], n_slot)

        here = pl.ds(aligned(t * 256, 256), 256)
        got = tn(normed_t[:, here], wq_half[i])
        for hb in range(2):
            h = 2 * i + hb
            low = got[:, hb * 192 : hb * 192 + 192].astype(BF16).astype(F32)
            query, key, value = low[:, 0:64], low[:, 64:128], low[:, 128:192]
            content = cb_all[k * half + i, hb : hb + 1, :]
            position = pb_all[k * half + i, hb : hb + 1, :]
            qcat[h, here, 512:640] = jnp.concatenate(
                [(query + content) * scale, (query + position) * scale], axis=1
            ).astype(BF16)
            keys[h, here, :] = jnp.concatenate([key, none], axis=1).astype(BF16)
            vals[h, here, :] = value.astype(BF16)

    def rotate(i, n):
        h, t = 2 * i + lax.div(n, blocks), lax.rem(n, blocks)
        here = pl.ds(aligned(t * 256, 256), 256)
        angle = nt(qcat[h, here, 512:640], wp_head[h])
        cosine = kcat[here, 0:256].astype(F32)
        sine = kcat[here, 256:512].astype(F32)
        first, second = angle[:, 0:256], angle[:, 256:512]
        qcat[h, here, 0:256] = (first * sine + second * cosine).astype(BF16)
        qcat[h, here, 256:512] = (second * sine - first * cosine).astype(BF16)

    slot_len = seq // 2
    block = 256
    batch = lax.div(c, 2)

    def attend(h, low_row, keys_seen, slot):
        start = starts_got[batch, 0:1, slot : slot + 1]
        row = slot * slot_len + low_row + lax.broadcasted_iota(jnp.int32, (block, 1), 0)
        inside = jnp.logical_and(row >= start, row < start + piece)
        limit = jnp.where(inside, start + (piece - 1), row)
        here = pl.ds(aligned(slot * slot_len + low_row, block), block)
        scores = nt(qcat[h, here, :], kcat[0:keys_seen, :])
        column = slot * slot_len + lax.broadcasted_iota(jnp.int32, (block, slot_len), 1)
        last = jnp.where(column <= limit, scores[:, keys_seen - slot_len :], big_negative)
        top = jnp.max(last, axis=1, keepdims=True)
        if slot == 1:
            top = jnp.maximum(top, jnp.max(scores[:, :slot_len], axis=1, keepdims=True))
        last = jnp.exp(last - top)
        total = jnp.sum(last, axis=1, keepdims=True)
        if slot == 1:
            first = jnp.exp(scores[:, :slot_len] - top)
            total = total + jnp.sum(first, axis=1, keepdims=True)
            whole = jnp.concatenate([first, last], axis=1)
        else:
            whole = last
        low = (whole * (1.0 / total)).astype(BF16)
        probs = (probs_a, probs_b)[slot]
        probs[h, pl.ds(aligned(low_row, block), block), :] = low
        heads_out[h, here, :] = nn(low, vals[h, 0:keys_seen, :]).astype(BF16)

    def sib_o():
        far_done("o")
        sib_start("o")

    def sib_u():
        far_done("u")
        sib_start("u")

    def ticks(h, slot, t, actions):
        for number, action in actions.items():
            if (number % 4) // 2 == slot and (not isinstance(t, int) or number % 2 == t):
                pl.when(4 * h + 2 * slot + t == number)(action)

    def far_of(name):
        def run():
            near_done(name)
            far_start(name)

        return run

    def projected():
        wd_line()

    def rotated():
        spread_features(cot, ct, c_send, c_slot)

    ahead = {1: far_of("o"), 4: far_of("u"), 9: wd_relay, 11: sib_o, 15: sib_u}

    def one_head(h):
        kcat[:, 512:640] = keys[h]

        for t in range(slot_len // block):
            attend(h, t * block, slot_len, 0)
        for t in range(slot_len // block):
            ticks(h, 0, t, ahead)
        for t in range(slot_len // block):
            attend(h, t * block, seq, 1)
        for t in range(slot_len // block):
            ticks(h, 1, t, ahead)

    for name in ("q", "p"):
        near_done(name, 1)
        far_start(name, 1)
    z_done("u")
    near_start("u")

    @pl.loop(0, half)
    def _(i):
        far_done("q", i)
        pl.loop(0, blocks)(lambda number: project(i, number))
        pl.when(i == 0)(projected)
        far_done("p", i)
        for hb in range(2):
            part = wp_half[i, :, hb * 64 : hb * 64 + 64]
            wp_head[2 * i + hb] = jnp.concatenate([jnp.zeros_like(part), part], axis=1)
        pl.loop(0, 2 * blocks)(lambda n: rotate(i, n))
        pl.when(i == 0)(rotated)
        pl.loop(0, 2)(lambda hb: one_head(2 * i + hb))

    own_att[...] = jnp.concatenate([heads_out[h] for h in range(heads)], axis=1)
    a_slot, a_send = io.land(2), io.leave()
    span = own_att.shape[1]
    att_part = att.at[:, pl.ds(aligned(k * span, 128), span)]
    io.push(a_send, lambda: (own_att.at[other, :], att_part, a_slot, sibling))
    io.keep(lambda: own_att.at[own, :], lambda: att_part, a_slot + 1)
    for cc in range(4):
        arrived(ct.at[pl.ds(cc * feat, feat), :], c_slot + cc)
    gout[...] = jnp.transpose(ct[...])
    sib_done("o")
    arrived(own_att.at[own, :], a_slot + 1)
    arrived(own_att.at[own, :], a_slot)

    for number in range(1, rows):
        wd_done(number)

    def line(index):
        return jnp.concatenate([params_col[cc, index : index + 1, :] for cc in range(cols)], axis=1)

    def out_weight():
        return jnp.concatenate([wo_all[cc] for cc in range(cols)], axis=1)

    x = jnp.transpose(xt[...].astype(F32))
    middle = x + nn(att[...], out_weight())
    mid[...] = middle
    mean = jnp.sum(middle, axis=1, keepdims=True) * (1.0 / width)
    square = jnp.sum(middle * middle, axis=1, keepdims=True) * (1.0 / width)
    inverse = lax.rsqrt(square - mean * mean + norm_epsilon)
    scaled = (middle - mean) * inverse
    hat[...] = scaled
    inv[...] = inverse
    low = (scaled * line(2) + line(3)).astype(BF16)
    norm[...] = low
    tall_norm[...] = jnp.transpose(low)
    acc_out[...] = jnp.zeros_like(acc_out)
    acc_two[...] = jnp.zeros_like(acc_two)
    small[...] = jnp.zeros_like(small)
    hidden = wu_all.shape[2]
    wd_all_done()

    u0_slot = (io.leave(half), io.land(half))
    o0_slot = (io.leave(), io.land())
    d0_slot = (io.leave(rows), io.land(rows))
    u_slot = {"one": (io.leave(2 * half), io.land(2 * half)), "two": (io.leave(half), io.land(half)), "z": (io.leave(half), io.land(rows))}
    o_slot = {"one": (io.leave(2), io.land(2)), "two": (io.leave(), io.land()), "z": (io.leave(half), io.land(rows))}
    d_slot = {"one": (io.leave(2), io.land(2)), "two": (io.leave(), io.land()), "z": (io.leave(rows), io.land(rows))}
    qp_slot = {
        "one": (io.leave(2 * heads), io.land(2 * heads)), "two": (io.leave(heads), io.land(heads)),
        "z": (io.leave(heads), io.land(2 * rows)),
    }
    last_slot = {name: (io.leave(), io.land()) for name in ("u", "o", "d", "qp")}

    def load(ref):
        return ref[...].astype(F32)

    def add(to, term):
        to[...] = (load(to) + load(term)).astype(BF16)

    def near_on(first, leave, land, target):
        io.push(leave, lambda: (first(), target(), land, (k, z, near)))

    def u_sib(j):
        leave, land = u0_slot
        io.push(leave + j, lambda: (g_up.at[(1 - k) * half + j], r0_u.at[j], land + j, sibling))

    def u_one(j):
        arrived(r0_u.at[j], u0_slot[1] + j)
        total = load(g_up.at[k * half + j]) + load(r0_u.at[j])
        hs_u[j] = total.astype(BF16).reshape(hs_u.shape[1:])
        leave, land = u_slot["one"]
        io.push(leave + 2 * j, lambda: (hs_u.at[j, far], r1_u.at[j, 0], land + 2 * j, (k, z, far)))
        io.push(leave + 2 * j + 1, lambda: (hs_u.at[j, 3 - c], r1_u.at[j, 1], land + 2 * j + 1, (k, z, far)))

    def u_two(j):
        land = u_slot["one"][1] + 2 * j
        arrived(r1_u.at[j, 1], land + 1)
        add(r1_u.at[j, 1], hs_u.at[j, near])
        near_on(lambda: r1_u.at[j, 1], u_slot["two"][0] + j, u_slot["two"][1] + j, lambda: r2_u.at[j])
        arrived(r1_u.at[j, 0], land)
        add(r1_u.at[j, 0], hs_u.at[j, c])

    def u_z(j):
        arrived(r2_u.at[j], u_slot["two"][1] + j)
        add(r2_u.at[j], r1_u.at[j, 0])
        leave, land = u_slot["z"]
        io.push(
            leave + j, lambda: (r2_u.at[j], r3_u.at[z], land + z, (k, k * half + j, c)), lambda: z != k * half + j
        )

    def z_total(total, r3, land, hb=None):
        for step in range(1, rows):
            source = lax.rem(z + step, rows)
            part = r3.at[source] if hb is None else r3.at[hb, source]
            arrived(part, land + source)
            total = total + load(part)
        return total

    def finish(name, to):
        leave, land = last_slot[name]
        io.push(leave, lambda: (to, to, land, sibling), lambda: mine)

    def u_last():
        @pl.when(mine)
        def _():
            f_u[...] = z_total(load(r2_u.at[turn]), r3_u, u_slot["z"][1])

        finish("u", f_u)

    def o_sib():
        leave, land = o0_slot
        size = g_out.shape[1] // 2
        io.push(leave, lambda: (g_out.at[:, pl.ds(aligned((1 - k) * size, 128), size), :], r0_o, land, sibling))

    def o_one():
        arrived(r0_o, o0_slot[1])
        size = g_out.shape[1] // 2
        for cc in range(cols):
            total = load(g_out.at[cc, pl.ds(aligned(k * size, 128), size), :]) + load(r0_o.at[cc])
            hs_o[cc] = total.astype(BF16).reshape(hs_o.shape[1:])
        leave, land = o_slot["one"]
        io.push(leave, lambda: (hs_o.at[far], r1_o.at[0], land, (k, z, far)))
        io.push(leave + 1, lambda: (hs_o.at[3 - c], r1_o.at[1], land + 1, (k, z, far)))

    def o_two():
        land = o_slot["one"][1]
        arrived(r1_o.at[1], land + 1)
        add(r1_o.at[1], hs_o.at[near])
        near_on(lambda: r1_o.at[1], o_slot["two"][0], o_slot["two"][1], lambda: r2_o)
        arrived(r1_o.at[0], land)
        add(r1_o.at[0], hs_o.at[c])

    def o_z():
        arrived(r2_o, o_slot["two"][1])
        add(r2_o, r1_o.at[0])
        leave, land = o_slot["z"]
        for j in range(half):
            io.push(
                leave + j,
                lambda j=j: (r2_o.at[j], r3_o.at[z], land + z, (k, k * half + j, c)),
                lambda j=j: z != k * half + j,
            )

    def o_last():
        @pl.when(mine)
        def _():
            f_o[...] = z_total(load(r2_o.at[turn]), r3_o, o_slot["z"][1])

        finish("o", f_o)

    def d_part(r, core):
        return g_down.at[:, pl.ds(aligned((2 * r + core) * part_rows, 128), part_rows), :]

    def d_sib(r, number):
        leave, land = d0_slot
        io.push(leave + number, lambda: (d_part(r(), 1 - k), r0_d.at[r()], land + r(), sibling))

    def d_z(r, number):
        arrived(r0_d.at[r()], d0_slot[1] + r())
        hs_d[r()] = (load(d_part(r(), k)) + load(r0_d.at[r()])).astype(BF16)
        leave, land = d_slot["z"]
        io.push(leave + number, lambda: (hs_d.at[r()], r3_d.at[z], land + z, (k, r(), c)), lambda: z != r())

    def d_one():
        s_d[...] = z_total(load(hs_d.at[z]), r3_d, d_slot["z"][1]).astype(BF16)
        leave, land = d_slot["one"]
        io.push(leave, lambda: (s_d.at[far], r1_d.at[0], land, (k, z, far)))
        io.push(leave + 1, lambda: (s_d.at[3 - c], r1_d.at[1], land + 1, (k, z, far)))

    def d_two():
        land = d_slot["one"][1]
        arrived(r1_d.at[1], land + 1)
        add(r1_d.at[1], s_d.at[near])
        near_on(lambda: r1_d.at[1], d_slot["two"][0], d_slot["two"][1], lambda: r2_d)
        arrived(r1_d.at[0], land)
        add(r1_d.at[0], s_d.at[c])

    def d_last():
        arrived(r2_d, d_slot["two"][1])
        leave, land = last_slot["d"]
        f_d[pl.ds(aligned(k * part_rows, 128), part_rows), :] = load(r2_d) + load(r1_d.at[0])

        def of_core():
            return f_d.at[pl.ds(aligned(k * part_rows, 128), part_rows), :]

        io.push(leave, lambda: (of_core(), of_core(), land, sibling))

    def qp_builds(h):
        leave, land = qp_slot["one"]
        return (
            (leave + 2 * h, lambda: (hs_qp.at[h, far], r1_qp.at[h, 0], land + 2 * h, (k, z, far))),
            (leave + 2 * h + 1, lambda: (hs_qp.at[h, opposite], r1_qp.at[h, 1], land + 2 * h + 1, (k, z, far))),
        )

    def qp_one(h):
        found = nt(turned[h], normed_t[...]).astype(BF16)
        position = turned_p[h].astype(BF16)
        for cc in range(cols):
            hs_qp[h, cc, 0:192, :] = found[:, cc * 128 : cc * 128 + 128]
            hs_qp[h, cc, 192:256, :] = position[:, cc * 128 : cc * 128 + 128]
        for leave, build in qp_builds(h):
            io.copy(leave, build).start()

    for h in range(heads):
        for leave, build in qp_builds(h):
            io.later(leave, build)

    def qp_two(h):
        land = qp_slot["one"][1] + 2 * h
        arrived(r1_qp.at[h, 1], land + 1)
        add(r1_qp.at[h, 1], hs_qp.at[h, near])
        near_on(lambda: r1_qp.at[h, 1], qp_slot["two"][0] + h, qp_slot["two"][1] + h, lambda: r2_qp.at[h])
        arrived(r1_qp.at[h, 0], land)
        add(r1_qp.at[h, 0], hs_qp.at[h, c])

    def qp_z(h):
        arrived(r2_qp.at[h], qp_slot["two"][1] + h)
        add(r2_qp.at[h], r1_qp.at[h, 0])
        leave, land = qp_slot["z"]
        io.push(
            leave + h,
            lambda: (r2_qp.at[h], r3_qp.at[h % 2, z], land + (h % 2) * rows + z, (k, k * half + h // 2, c)),
            lambda: z != k * half + h // 2,
        )

    def qp_last():
        @pl.when(mine)
        def _():
            for hb in range(2):
                f_qp[hb] = z_total(load(r2_qp.at[2 * turn + hb]), r3_qp, qp_slot["z"][1] + hb * rows, hb)

        finish("qp", f_qp)

    def last_done():
        @pl.when(jnp.logical_not(mine))
        def _():
            for name, to in (("u", f_u), ("o", f_o), ("qp", f_qp)):
                arrived(to, last_slot[name][1])

        arrived(f_d.at[pl.ds(aligned((1 - k) * part_rows, 128), part_rows), :], last_slot["d"][1])

    origin = lax.rem(c, 2)
    out_slot, grad_slot = (io.leave(4), io.land(4)), (io.leave(4), io.land(4))

    def back_start(src, dst, pair):
        leave, base = pair
        for step in range(4):

            def part(step=step):
                return src.at[pl.ds(aligned(lax.rem(c + step, 4) * feat, 128), feat), :]

            def landing():
                return dst.at[batch, k]

            if step == 0:
                io.keep(part, landing, base + 2 * batch + k, lambda: origin == k)
                io.push(
                    leave + step,
                    lambda part=part, landing=landing: (part(), landing(), base + 2 * batch + k, sibling),
                    lambda: origin != k,
                )
            else:
                io.push(
                    leave + step,
                    lambda part=part, landing=landing, step=step: (
                        part(), landing(), base + 2 * batch + k, (origin, z, lax.rem(c + step, 4))
                    ),
                )

    def back_done(dst, pair):
        base = pair[1]
        for b in range(2):
            for core in range(2):
                arrived(dst.at[b, core], base + 2 * b + core)


    def rows_of(number):
        core = k if number % 2 == 0 else 1 - k
        return core * half + number // 2

    def after_one():
        u_sib(0)
        for number in range(2):
            d_sib(lambda number=number: rows_of(number), number)

    def after_two():
        u_one(0)
        for number in range(2):
            d_z(lambda number=number: rows_of(number), number)

    @pl.loop(0, rows)
    def _(step):
        turn_of = lax.rem(step, 2)
        r = ((1 - turn_of) * k + turn_of * (1 - k)) * half + lax.div(step, 2)

        @pl.when(step == 1)
        def _():
            sib_done("u")

        here = pl.ds(aligned(r * hidden, hidden), hidden)
        bias = jnp.concatenate([params_row[r, j : j + 1, :] for j in range(hidden // 128)], axis=1)
        down = jnp.concatenate([wd_all[cc, here, :] for cc in range(cols)], axis=1)
        pre = nn(norm[...], wu_all[r]) + bias
        grad_act = nt(gout[...], down)
        lower = erf_parts(pre)
        act = (pre * lower).astype(BF16)
        slope = lower + pre * jnp.exp(-0.5 * pre * pre) * inv_sqrt_tau
        low_grad = (grad_act * slope).astype(BF16)
        small[pl.ds(5 + r, 1), :] = jnp.sum(low_grad.astype(F32), axis=0, keepdims=True)
        acc_out[...] += nn(act, down)
        acc_two[...] += nt(low_grad, wu_all[r])
        g_up[r] = nn(tall_norm[...], low_grad).astype(BF16)
        found = tn(act, gout[...]).astype(BF16)
        for cc in range(cols):
            g_down[cc, here, :] = found[:, cc * 128 : cc * 128 + 128]
        pl.when(step == 1)(after_one)
        pl.when(step == 2)(after_two)

    u_sib(1)
    for number in range(2, 4):
        d_sib(lambda number=number: rows_of(number), number)
    cotangent = gout[...].astype(F32)
    out_t[...] = jnp.transpose(mid[...] + acc_out[...] + line(4)).astype(BF16)
    back_start(out_t, outs, out_slot)
    two = acc_two[...]
    small[2:3, :] = jnp.sum(two * hat[...], axis=0, keepdims=True)
    small[3:4, :] = jnp.sum(two, axis=0, keepdims=True)
    small[4:5, :] = jnp.sum(cotangent, axis=0, keepdims=True)
    shifted = two * line(2)
    first = jnp.sum(shifted, axis=1, keepdims=True) * (1.0 / width)
    second = jnp.sum(shifted * hat[...], axis=1, keepdims=True) * (1.0 / width)
    grad_mid = cotangent + inv[...] * (shifted - first - hat[...] * second)
    branch = grad_mid.astype(BF16)
    grad_att[...] = nt(branch, out_weight()).astype(BF16)
    e_slot, e_send = io.land(2), io.leave()
    io.push(
        e_send,
        lambda: (grad_att.at[:, pl.ds(aligned((1 - k) * span, 128), span)], grad_o.at[own, :], e_slot, sibling),
    )
    io.keep(
        lambda: grad_att.at[:, pl.ds(aligned(k * span, 128), span)], lambda: grad_o.at[own, :], e_slot + 1
    )
    grad_mid_t[...] = jnp.transpose(grad_mid)
    found = tn(att[...], branch).astype(BF16)
    for cc in range(cols):
        g_out[cc] = found[:, cc * 128 : cc * 128 + 128]
    o_sib()
    u_one(1)
    for number in range(2, 4):
        d_z(lambda number=number: rows_of(number), number)
    one_t[...] = jnp.zeros_like(one_t)
    sums[...] = jnp.zeros_like(sums)
    arrived(grad_o.at[own, :], e_slot + 1)
    arrived(grad_o.at[own, :], e_slot)
    for h in range(heads):
        head_grad[h] = grad_o[:, h * 64 : h * 64 + 64]

    def attend_back(h, low_row, keys_seen, slot):
        at = pl.ds(aligned(low_row, block), block)
        here = pl.ds(aligned(slot * slot_len + low_row, block), block)
        grad = head_grad[h, here, :]
        low = (probs_a, probs_b)[slot][h, at, :]
        inner = jnp.sum(grad.astype(F32) * heads_out[h, here, :].astype(F32), axis=1, keepdims=True)
        grad_prob = nt(grad, vals[h, 0:keys_seen, :])
        grad_score = (low.astype(F32) * (grad_prob - inner)).astype(BF16)
        turned_v[:, 0:keys_seen] += tn(grad, low)
        turned_k[:, 0:keys_seen] += tn(qcat[h, here, 512:576], grad_score)
        got = nn(grad_score, kcat[0:keys_seen, :])
        cosine = kcat[here, 0:256].astype(F32)
        sine = kcat[here, 256:512].astype(F32)
        first, second = got[:, 0:256], got[:, 256:512]
        angle = jnp.concatenate([first * sine - second * cosine, first * cosine + second * sine], axis=1).astype(BF16)
        both = got[:, 512:640] + nn(angle, wp_head[h])
        turned_p[h] += tn(qcat[h, here, 512:640], angle)[64:128]
        sums[pl.ds(h, 1), :] += jnp.sum(both, axis=0, keepdims=True) * 0.125
        query = (both + pltpu.roll(both, 64, 1)) * 0.125
        turned[h, 0:64, here] = jnp.transpose(query)[0:64].astype(BF16)

    def both(*actions):
        def run():
            for action in actions:
                action()

        return run

    behind = {
        0: both(o_one, lambda: u_two(0)), 6: lambda: u_two(1), 7: o_two, 9: lambda: u_z(0), 10: lambda: qp_two(0),
        11: lambda: u_z(1), 12: o_z, 13: lambda: qp_two(1), 14: lambda: qp_z(0),
    }

    @pl.loop(0, heads)
    def _(h):
        kcat[:, 512:640] = keys[h]
        turned_k[...] = jnp.zeros_like(turned_k)
        turned_v[...] = jnp.zeros_like(turned_v)
        turned_p[h] = jnp.zeros(turned_p.shape[1:], F32)

        for t in range(slot_len // block):
            attend_back(h, t * block, slot_len, 0)
        for t in range(slot_len // block):
            ticks(h, 0, t, behind)
        for t in range(slot_len // block):
            attend_back(h, t * block, seq, 1)
        for t in range(slot_len // block):
            ticks(h, 1, t, behind)

        turned[h, 64:128, :] = turned_k[...].astype(BF16)
        turned[h, 128:192, :] = turned_v[...].astype(BF16)
        qp_one(h)

        @pl.when(lax.rem(h, 2) == 1)
        def _():
            i = lax.div(h, 2)
            pair = jnp.concatenate([turned[2 * i], turned[2 * i + 1]], axis=0)
            one_t[...] += nn(wq_half[i], pair)

    one_low[...] = one_t[:, other].astype(BF16)
    f_slot, f_send = io.land(), io.leave()
    io.push(f_send, lambda: (one_low, one_got, f_slot, sibling))
    qp_two(2)
    qp_z(1)
    d_one()
    arrived(one_got, f_slot)
    columns = [tall(params_col[cc]) for cc in range(cols)]
    gain = jnp.concatenate([col[:, 0:1] for col in columns], axis=0)
    one = one_t[:, own] + one_got[...].astype(F32)
    x = xt[...].astype(F32)
    mean = jnp.sum(x, axis=0, keepdims=True) * (1.0 / width)
    square = jnp.sum(x * x, axis=0, keepdims=True) * (1.0 / width)
    inverse = lax.rsqrt(square - mean * mean + norm_epsilon)
    scaled = (x - mean) * inverse
    shifted = one * gain
    first = jnp.sum(shifted, axis=0, keepdims=True) * (1.0 / width)
    second = jnp.sum(shifted * scaled, axis=0, keepdims=True) * (1.0 / width)
    gain_sum = jnp.sum(one * scaled, axis=1, keepdims=True)
    bias_sum = jnp.sum(one, axis=1, keepdims=True)
    lane = lax.broadcasted_iota(jnp.int32, (width, 128), 1)
    pair = jnp.where(lane == 0, gain_sum, jnp.where(lane == 1, bias_sum, 0.0))
    pair = jnp.transpose(pair)[0:8]
    all_small[0] = small[...]
    all_small[0, 0:2, :] = pair[0:2]

    def spread(first_lane):
        row = jnp.concatenate([sums[h : h + 1, first_lane : first_lane + 64] for h in range(heads)], axis=1)
        blank = jnp.zeros_like(row)
        return jnp.where(k == 0, jnp.concatenate([row, blank], axis=1), jnp.concatenate([blank, row], axis=1))

    all_small[0, 9:10, :] = spread(0)
    all_small[0, 10:11, :] = spread(64)
    m_slot, m_send = io.land(), io.leave()
    p_slot, p_send = io.land(), io.leave(3)
    v_slot, v_send = io.land(), io.leave(rows - 1)
    io.push(m_send, lambda: (all_small.at[0], got_sib, m_slot, sibling))
    grad_x[...] = (grad_mid_t[...] + inverse * (shifted - first - scaled * second)).astype(BF16)
    arrived(got_sib, m_slot)
    all_small[1] = all_small[0] + got_sib[...]
    for step in range(1, 4):
        io.push(
            p_send + step - 1, lambda step=step: (all_small.at[1], got_plane.at[c], p_slot, (k, z, lax.rem(c + step, 4)))
        )
    io.keep(lambda: all_small.at[1], lambda: got_plane.at[c], p_slot)
    qp_two(3)
    d_two()
    back_start(grad_x, grads, grad_slot)
    qp_z(2)
    arrived(got_plane, p_slot)
    all_small[2] = (got_plane[0] + got_plane[1]) + (got_plane[2] + got_plane[3])
    for step in range(1, rows):
        io.push(
            v_send + step - 1, lambda step=step: (all_small.at[2], got_z.at[z], v_slot, (k, lax.rem(z + step, rows), c))
        )
    io.keep(lambda: all_small.at[2], lambda: got_z.at[z], v_slot)
    u_last()
    o_last()
    qp_z(3)
    d_last()
    arrived(got_z, v_slot)
    f_small[...] = (got_z[0] + got_z[1]) + (got_z[2] + got_z[3])
    qp_last()
    back_done(outs, out_slot)
    back_done(grads, grad_slot)
    last_done()
    io.drain()


def final_kernel(
    outs, grads, f_qp, f_o, f_u, f_d, f_small,
    output, grad_tokens, g1, b1, q_w, c_b, p_b, p_w, o_w, g2, b2, u_w, u_b, d_w, d_b,
):
    k, z, c, _, _ = place()
    for b in range(2):
        for core in range(2):
            size = outs.shape[3]
            output[b, :, core * size : core * size + size] = outs[b, core].astype(F32)
            grad_tokens[b, :, core * size : core * size + size] = grads[b, core].astype(F32)
    for core in range(2):

        @pl.when(k == core)
        def _(core=core):
            q_w[...] = f_qp[core, 0:192, :]
            p_w[...] = f_qp[core, 192:256, :]
            for ref, source in ((o_w, f_o), (d_w, f_d)):
                size = ref.shape[0]
                ref[...] = jnp.transpose(source[:, core * size : core * size + size])
            size = u_w.shape[1]
            u_w[...] = f_u[:, core * size : core * size + size]

    width = f_small.shape[1]
    chip = z * 4 + c
    share = g1.shape[1]
    first = pltpu.roll(f_small[0:8, :], lax.rem(width - (chip * 2 + k) * share, width), 1)
    for row, ref in ((0, g1), (1, b1), (2, g2), (3, b2), (4, d_b)):
        ref[...] = first[row : row + 1, 0:share]
    share = u_b.shape[1]
    line = f_small[pl.ds(5 + z, 1), :]
    line = jnp.broadcast_to(line, (8, width))
    u_b[...] = pltpu.roll(line, lax.rem(width - (c * 2 + k) * share, width), 1)[0:1, 0:share]
    heads, share = c_b.shape
    third = pltpu.roll(f_small[8:16, :], lax.rem(2 * width - heads * 64 * z - (c * 2 + k) * share, width), 1)
    for h in range(heads):
        c_b[h : h + 1, :] = third[1:2, h * 64 : h * 64 + share]
        p_b[h : h + 1, :] = third[2:3, h * 64 : h * 64 + share]


def position_table(seq_len, feature_count):
    positions = np.arange(seq_len, dtype=np.float64)
    exponent = -np.arange(0, feature_count, 2, dtype=np.float64) / feature_count
    angles = positions[:, None] * (10000.0**exponent)[None, :]
    return np.concatenate([np.cos(angles), np.sin(angles)], axis=1).astype(jnp.bfloat16)


def fast_shards(
    tokens, cotangent, piece_starts, ln1_gain, ln1_bias, qkv_weight, content_bias, position_bias, pos_weight,
    out_weight, ln2_gain, ln2_bias, up_weight, up_bias, down_weight, down_bias,
):
    rows, cols = lax.axis_size("row"), lax.axis_size("col")
    half = rows // 2
    micro, feat, seq = tokens.shape
    width = feat * cols
    count = seq // 2
    hidden = up_weight.shape[1]
    heads = content_bias.shape[0] * half
    table = jnp.asarray(position_table(seq, width))
    lines = [ln1_gain, ln1_bias, ln2_gain, ln2_bias, down_bias]
    places = [(line, index * feat) for index, line in enumerate(lines)] + [(up_bias, 8 * 128)]
    packed = sum(jnp.pad(line.astype(F32), (at, 16 * 128 - at - line.shape[0])) for line, at in places)
    packed = packed.reshape(16, 128)
    vm = pl.BlockSpec(memory_space=pltpu.VMEM)
    anywhere = pl.BlockSpec(memory_space=pl.ANY)
    limit = 64 * 1024 * 1024 - 128 * 1024

    def shape(dims, kind=BF16):
        return jax.ShapeDtypeStruct(dims, kind)

    def vmem(dims, kind=BF16):
        return pltpu.VMEM(dims, kind)

    q_cols, p_cols = qkv_weight.shape[1], pos_weight.shape[1]
    o_rows, d_rows = out_weight.shape[0], down_weight.shape[0]
    qp, part = (256, feat), (d_rows // 2, 128)
    results = pl.pallas_call(
        layer_kernel,
        name="layer",
        out_shape=(
            shape((micro, 2, feat, count)),
            shape((micro, 2, feat, count)),
        )
        + (
            shape((2,) + qp, F32), shape((o_rows, 128), F32), shape((feat, hidden), F32), shape((d_rows, 128), F32),
            shape((16, width), F32),
        ),
        in_specs=[anywhere, anywhere, vm, vm, vm, vm] + [anywhere] * 6,
        out_specs=(anywhere, anywhere) + (vm,) * 5,
        scratch_shapes=[
            vmem((count, width)),
            vmem((cols, width, 128)),
            vmem((rows, width, hidden)),
            vmem((cols, rows * hidden, 128)),
            vmem((half, width, q_cols)),
            vmem((half, width, p_cols)),
            vmem((heads, width, 128)),
            vmem((width, count)),
            vmem((width, count)),
            vmem((width, seq)),
            vmem((heads, seq, width + 128)),
            vmem((heads, seq, 128)),
            vmem((heads, seq, 64)),
            vmem((heads, count, count)),
            vmem((heads, count, seq)),
            vmem((heads, seq, 64)),
            vmem((cols, 8, 128), F32),
            vmem((rows, 8, 128), F32),
            vmem((rows,) + content_bias.shape, F32),
            vmem((rows,) + position_bias.shape, F32),
            vmem((seq, width + 128)),
            vmem((seq, heads * 64)),
            vmem(piece_starts.shape, jnp.int32),
            vmem((count, width), F32),
            vmem((count, width)),
            vmem((count, width), F32),
            vmem((count, 1), F32),
            vmem((count, width)),
            vmem((count, width), F32),
            vmem((count, width), F32),
            vmem((width, count)),
            vmem((width, count)),
            vmem((width, count), F32),
            vmem((count, width)),
            vmem((rows, width, hidden)),
            vmem((cols, rows * hidden, 128)),
            vmem((cols, width, 128)),
            vmem((16, width), F32),
            vmem((seq, heads * 64)),
            vmem((heads, seq, 64)),
            vmem((heads, 192, seq)),
            vmem((64, seq), F32),
            vmem((64, seq), F32),
            vmem((heads, 64, width), F32),
            vmem((width, seq), F32),
            vmem((width, count)),
            vmem((width, count)),
            vmem((width, count)),
            vmem((8, 128), F32),
            vmem((heads, cols) + qp),
            vmem((cols, half, o_rows, 128)),
            vmem((half, cols, feat, hidden)),
            vmem((rows, cols) + part),
            vmem((cols, half * o_rows, 128)),
            vmem((half, width, hidden)),
            vmem((rows, cols) + part),
            vmem((cols,) + part),
            vmem((heads, 2) + qp),
            vmem((2, half, o_rows, 128)),
            vmem((half, 2, feat, hidden)),
            vmem((2,) + part),
            vmem((heads,) + qp),
            vmem((half, o_rows, 128)),
            vmem((half, feat, hidden)),
            vmem(part),
            vmem((2, rows) + qp),
            vmem((rows, o_rows, 128)),
            vmem((rows, feat, hidden)),
            vmem((rows, cols) + part),
            vmem((3, 16, width), F32),
            vmem((16, width), F32),
            vmem((cols, 16, width), F32),
            vmem((rows, 16, width), F32),
            pltpu.SemaphoreType.DMA((140,)),
            pltpu.SemaphoreType.DMA((132,)),
        ],
        compiler_params=pltpu.CompilerParams(collective_id=0, has_side_effects=True, vmem_limit_bytes=limit),
    )(
        tokens, cotangent, piece_starts, packed, content_bias, position_bias, table,
        qkv_weight, pos_weight, out_weight, up_weight, down_weight,
    )
    devices = 2 * rows * cols
    vec = shape((1, width // devices), F32)
    bias = shape((content_bias.shape[0], 64 // (2 * cols)), F32)
    done = list(pl.pallas_call(
        final_kernel,
        name="final",
        out_shape=(
            shape(tokens.shape, F32), shape(tokens.shape, F32), vec, vec,
            shape((q_cols // 2, feat), F32), bias, bias, shape((p_cols // 2, feat), F32), shape((64, o_rows), F32), vec, vec,
            shape((feat, hidden // 2), F32), shape((1, rows * hidden // devices), F32), shape((64, d_rows), F32), vec,
        ),
        in_specs=[vm] * 7,
        out_specs=(vm,) * 15,
        compiler_params=pltpu.CompilerParams(vmem_limit_bytes=limit),
    )(*results))
    for index in (4, 7, 8, 13):
        done[index] = done[index].T
    return tuple(v.reshape(-1) if v.shape[0] == 1 else v for v in done)


def solution(mesh):
    in_specs = (
        P(None, "col", ("dp", "row")),
        P(None, "col", ("dp", "row")),
        P(None, ("dp", "col"), None),
        P("col"),
        P("col"),
        P("col", "row"),
        P("row", None),
        P("row", None),
        P("col", "row"),
        P("row", "col"),
        P("col"),
        P("col"),
        P("col", "row"),
        P("row"),
        P("row", "col"),
        P("col"),
    )
    out_specs = (
        P(None, "col", ("dp", "row")),
        P(None, "col", ("dp", "row")),
        P(("row", "col", "dp")),
        P(("row", "col", "dp")),
        P("col", ("row", "dp")),
        P("row", ("col", "dp")),
        P("row", ("col", "dp")),
        P("col", ("row", "dp")),
        P("row", ("col", "dp")),
        P(("row", "col", "dp")),
        P(("row", "col", "dp")),
        P("col", ("row", "dp")),
        P(("row", "col", "dp")),
        P("row", ("col", "dp")),
        P(("row", "col", "dp")),
    )

    def layer(tokens, *others):
        dp, row, col = mesh.shape["dp"], mesh.shape["row"], mesh.shape["col"]
        one_each = tokens.shape[2] == dp * row * SEQ_LEN and tokens.shape[0] * dp == col
        body = fast_shards if one_each and dp == 2 and row == col == 4 else shards
        part = jax.shard_map(body, mesh=mesh, in_specs=in_specs, out_specs=out_specs, check_vma=False)
        return part(tokens, *others)

    return layer
```

```python
from functools import reduce

import jax
import jax.numpy as jnp
import numpy as np
from jax import lax
from jax.experimental import pallas as pl
from jax.experimental.pallas import tpu as pltpu
from jax.sharding import PartitionSpec as P

D = 512
SEQ_LEN = 1024
PIECE = 256


norm_epsilon = 1e-05
big_negative = -1e30
inv_sqrt_two = 0.7071067811865476
inv_sqrt_tau = 0.3989422804014327


def contract(left_op, right_op, flipped):
    if flipped:
        return lax.dot_general(
            left_op, right_op, (((1,), (1,)), ((), ())), preferred_element_type=jnp.float32
        )
    return jnp.dot(left_op, right_op, preferred_element_type=jnp.float32)


def outer_sum(left_op, right_op):
    return lax.dot_general(
        left_op, right_op, (((0,), (0,)), ((), ())), preferred_element_type=jnp.float32
    )


def gather_rows(values):
    return lax.all_gather(values, "row", axis=0, tiled=True)


def gather_cols(values):
    return lax.all_gather(values, "col", axis=0, tiled=True)


def sum_over_cols(gathered, weight, flipped):
    share_rows = gathered.shape[0] // lax.axis_size("col")

    def partial_term(offset, amount):
        return contract(gathered, weight, flipped)

    return lax.psum_scatter(
        partial_term(jnp.int32(0), lax.axis_size("col") * share_rows),
        "col",
        scatter_dimension=0,
        tiled=True,
    )


def sum_over_rows(gathered, weight, flipped):
    share_rows = gathered.shape[0] // lax.axis_size("row")

    def partial_term(offset, amount):
        return contract(gathered, weight, flipped)

    return lax.psum_scatter(
        partial_term(jnp.int32(0), lax.axis_size("row") * share_rows),
        "row",
        scatter_dimension=0,
        tiled=True,
    )


def feature_sums(first_sum, second_sum):
    return lax.psum((first_sum, second_sum), "col")


def normalize(values, gain, bias):
    feature_count = values.shape[1] * lax.axis_size("col")
    total_row, square_row = feature_sums(jnp.sum(values, axis=1), jnp.sum(values * values, axis=1))
    mean_row = total_row / feature_count
    inverse = lax.rsqrt(square_row / feature_count - mean_row * mean_row + norm_epsilon)
    scaled = (values - mean_row[:, None]) * inverse[:, None]
    return (scaled * gain + bias, scaled, inverse)


def normalize_back(grad_in, scaled, inverse, gain):
    feature_count = grad_in.shape[1] * lax.axis_size("col")
    shifted = grad_in * gain
    first_sum, second_sum = feature_sums(
        jnp.sum(shifted, axis=1), jnp.sum(shifted * scaled, axis=1)
    )
    back_rows = inverse[:, None] * (
        shifted - first_sum[:, None] / feature_count - scaled * second_sum[:, None] / feature_count
    )
    return (back_rows, jnp.sum(grad_in * scaled, axis=0), jnp.sum(grad_in, axis=0))


def gelu_exact(values):
    return 0.5 * values * (1.0 + jax.scipy.special.erf(values * inv_sqrt_two))


def gelu_slope(values):
    return (
        0.5 * (1.0 + jax.scipy.special.erf(values * inv_sqrt_two))
        + values * jnp.exp(-0.5 * values * values) * inv_sqrt_tau
    )


def sinusoid_table(seq_len, feature_count):
    offsets = jnp.arange(2 * seq_len - 1, dtype=jnp.float32) - (seq_len - 1)
    frequency = 10000.0 ** (-jnp.arange(0, feature_count, 2, dtype=jnp.float32) / feature_count)
    angles = offsets[:, None] * frequency[None, :]
    return jnp.concatenate([jnp.sin(angles), jnp.cos(angles)], axis=1).astype(jnp.bfloat16)


def piece_labels(positions, starts, piece_len):
    inside = (positions[:, None] >= starts[None, :]) & (
        positions[:, None] < starts[None, :] + piece_len
    )
    numbers = jnp.arange(1, starts.shape[0] + 1, dtype=jnp.int32)
    return jnp.sum(jnp.where(inside, numbers[None, :], 0), axis=1) - 1


def block_mask(offset, block_len, labels):
    positions = jnp.arange(labels.shape[0], dtype=jnp.int32)
    row_pos = offset + jnp.arange(block_len, dtype=jnp.int32)
    row_labels = lax.dynamic_slice_in_dim(labels, offset, block_len, 0)
    same_piece = (row_labels[:, None] == labels[None, :]) & (row_labels[:, None] >= 0)
    return (positions[None, :] <= row_pos[:, None]) | same_piece


def skew_rows(unshifted_reversed_scores, key_total):
    head_total, row_total, rel_span = unshifted_reversed_scores.shape
    flattened = unshifted_reversed_scores.reshape(head_total, row_total * rel_span)
    window = lax.slice_in_dim(
        flattened, row_total - 1, row_total - 1 + row_total * (rel_span - 1), axis=1
    )
    return window.reshape(head_total, row_total, rel_span - 1)[:, :, :key_total]


def unskew_rows(grad_pos, rel_span):
    head_total, row_total, key_total = grad_pos.shape
    padded = jnp.pad(grad_pos, ((0, 0), (0, 0), (0, rel_span - 1 - key_total)))
    flattened = padded.reshape(head_total, row_total * (rel_span - 1))
    flattened = jnp.pad(flattened, ((0, 0), (row_total - 1, 1)))
    return flattened.reshape(head_total, row_total, rel_span)


def block_scores(qu_block, query_position_block, key_rows, relative_block, allowed):
    content = jnp.einsum("ihd,jhd->hij", qu_block, key_rows, preferred_element_type=jnp.float32)
    unshifted_reversed_scores = jnp.einsum(
        "sgw,egw->gse", query_position_block, relative_block, preferred_element_type=jnp.float32
    )
    position = skew_rows(unshifted_reversed_scores, key_rows.shape[0])
    return jnp.where(allowed[None], content + position, big_negative)


def attention_forward(query_u, query_v, key_rows, value_rows, relative_rev, labels):
    seq_len, head_count, head_dim = key_rows.shape
    block_len = min(512, seq_len)
    rel_span = block_len + seq_len - 1
    offsets = jnp.arange(seq_len // block_len, dtype=jnp.int32) * block_len

    def attend(offset):
        qu_block = lax.dynamic_slice_in_dim(query_u, offset, block_len, 0)
        query_position_block = lax.dynamic_slice_in_dim(query_v, offset, block_len, 0)
        relative_block = lax.dynamic_slice_in_dim(
            relative_rev, seq_len - block_len - offset, rel_span, 0
        )
        scores = block_scores(
            qu_block,
            query_position_block,
            key_rows,
            relative_block,
            block_mask(offset, block_len, labels),
        )
        row_max = jnp.max(scores, axis=2, keepdims=True)
        log_total = row_max + jnp.log(jnp.sum(jnp.exp(scores - row_max), axis=2, keepdims=True))
        attn_prob = jnp.exp(scores - log_total).astype(jnp.bfloat16)
        result = jnp.einsum(
            "hij,jhd->ihd", attn_prob, value_rows, preferred_element_type=jnp.float32
        )
        return (result, log_total[:, :, 0])

    results, log_totals = lax.map(attend, offsets)
    return (results.reshape(seq_len, head_count * head_dim), log_totals)


def attention_backward(
    query_u, query_v, key_rows, value_rows, relative_rev, labels, log_totals, grad_att
):
    seq_len, head_count, head_dim = key_rows.shape
    block_len = min(512, seq_len)
    rel_span = block_len + seq_len - 1
    offsets = jnp.arange(seq_len // block_len, dtype=jnp.int32) * block_len

    def back_block(carried, sliced):
        grad_keys, grad_values, grad_rel = carried
        offset, log_total = sliced
        rel_start = seq_len - block_len - offset
        qu_block = lax.dynamic_slice_in_dim(query_u, offset, block_len, 0)
        query_position_block = lax.dynamic_slice_in_dim(query_v, offset, block_len, 0)
        relative_block = lax.dynamic_slice_in_dim(relative_rev, rel_start, rel_span, 0)
        scores = block_scores(
            qu_block,
            query_position_block,
            key_rows,
            relative_block,
            block_mask(offset, block_len, labels),
        )
        attn_prob = jnp.exp(scores - log_total[:, :, None])
        low_prob = attn_prob.astype(jnp.bfloat16)
        grad_block = lax.dynamic_slice_in_dim(grad_att, offset, block_len, 0)
        grad_prob = jnp.einsum(
            "ihd,jhd->hij", grad_block, value_rows, preferred_element_type=jnp.float32
        )
        row_inner = jnp.sum(attn_prob * grad_prob, axis=2, keepdims=True)
        grad_scores = (attn_prob * (grad_prob - row_inner)).astype(jnp.bfloat16)
        grad_values = grad_values + jnp.einsum(
            "hij,ihd->jhd", low_prob, grad_block, preferred_element_type=jnp.float32
        )
        grad_keys = grad_keys + jnp.einsum(
            "hij,ihd->jhd", grad_scores, qu_block, preferred_element_type=jnp.float32
        )
        grad_qu = jnp.einsum(
            "hij,jhd->ihd", grad_scores, key_rows, preferred_element_type=jnp.float32
        )
        gradient_unshifted = unskew_rows(grad_scores, rel_span)
        grad_qv = jnp.einsum(
            "qjp,pqr->jqr", gradient_unshifted, relative_block, preferred_element_type=jnp.float32
        )
        rel_part = jnp.einsum(
            "nfx,fne->xne",
            gradient_unshifted,
            query_position_block,
            preferred_element_type=jnp.float32,
        )
        current = lax.dynamic_slice_in_dim(grad_rel, rel_start, rel_span, 0)
        grad_rel = lax.dynamic_update_slice_in_dim(grad_rel, current + rel_part, rel_start, 0)
        return ((grad_keys, grad_values, grad_rel), (grad_qu, grad_qv))

    zero_rows = jnp.zeros((seq_len, head_count, head_dim), jnp.float32)
    zero_rel = jnp.zeros((2 * seq_len - 1, head_count, head_dim), jnp.float32)
    carried, stacked = lax.scan(back_block, (zero_rows, zero_rows, zero_rel), (offsets, log_totals))
    grad_keys, grad_values, grad_rel = carried
    grad_qu = stacked[0].reshape(seq_len, head_count, head_dim)
    grad_qv = stacked[1].reshape(seq_len, head_count, head_dim)
    return (grad_qu, grad_qv, grad_keys, grad_values, grad_rel)


def heads_pass(packed, content_bias, position_bias, relative_rev, labels):
    seq_len = packed.shape[0]
    head_count, head_dim = content_bias.shape
    scaling = head_dim ** (-0.5)
    packed = packed.reshape(seq_len, head_count, 3, head_dim)
    queries = packed[:, :, 0].astype(jnp.float32)
    key_rows = packed[:, :, 1]
    value_rows = packed[:, :, 2]
    query_u = ((queries + content_bias) * scaling).astype(jnp.bfloat16)
    query_v = ((queries + position_bias) * scaling).astype(jnp.bfloat16)
    attended, log_totals = attention_forward(
        query_u, query_v, key_rows, value_rows, relative_rev, labels
    )
    return (attended.astype(jnp.bfloat16), (query_u, query_v, key_rows, value_rows, log_totals))


def heads_back(kept, relative_rev, labels, grad_att):
    query_u, query_v, key_rows, value_rows, log_totals = kept
    seq_len, head_count, head_dim = key_rows.shape
    scaling = head_dim ** (-0.5)
    grad_att = grad_att.reshape(seq_len, head_count, head_dim)
    grad_qu, grad_qv, grad_keys, grad_values, grad_rel = attention_backward(
        query_u, query_v, key_rows, value_rows, relative_rev, labels, log_totals, grad_att
    )
    cbias_part = jnp.sum(grad_qu, axis=0) * scaling
    pbias_part = jnp.sum(grad_qv, axis=0) * scaling
    grad_query = (grad_qu + grad_qv) * scaling
    grad_packed = jnp.stack([grad_query, grad_keys, grad_values], axis=2)
    grad_packed = grad_packed.reshape(seq_len, head_count * 3 * head_dim).astype(jnp.bfloat16)
    rel_low = grad_rel.reshape(2 * seq_len - 1, head_count * head_dim).astype(jnp.bfloat16)
    return (grad_packed, rel_low, cbias_part, pbias_part)


def grid_micro(seq_feats, cot_feats, params, shared):
    (
        ln1_gain,
        ln1_bias,
        qkv_weight,
        content_bias,
        position_bias,
        out_weight,
        ln2_gain,
        ln2_bias,
        up_weight,
        up_bias,
        down_weight,
        down_bias,
    ) = params
    relative_rev, table_rev, labels = shared
    seq_in = seq_feats.astype(jnp.float32).T
    normed_one, scaled_one, inverse_one = normalize(seq_in, ln1_gain, ln1_bias)
    gathered_one = gather_rows(normed_one.astype(jnp.bfloat16))
    packed = sum_over_cols(gathered_one, qkv_weight, False).astype(jnp.bfloat16)
    attended, kept = heads_pass(packed, content_bias, position_bias, relative_rev, labels)
    att_gathered = gather_cols(attended)
    middle = seq_in + sum_over_rows(att_gathered, out_weight, False)
    normed_two, scaled_two, inverse_two = normalize(middle, ln2_gain, ln2_bias)
    gathered_two = gather_rows(normed_two.astype(jnp.bfloat16))
    pre_act = sum_over_cols(gathered_two, up_weight, False) + up_bias
    activated = gelu_exact(pre_act).astype(jnp.bfloat16)
    act_gathered = gather_cols(activated)
    output = middle + sum_over_rows(act_gathered, down_weight, False) + down_bias
    grad_final = cot_feats.T
    gout = grad_final.astype(jnp.float32)
    final_gathered = gather_rows(grad_final)
    grad_act = sum_over_cols(final_gathered, down_weight, True)
    grad_pre = (grad_act * gelu_slope(pre_act)).astype(jnp.bfloat16)
    pre_gathered = gather_cols(grad_pre)
    grad_two = sum_over_rows(pre_gathered, up_weight, True)
    backward_second, gain_two, bias_two = normalize_back(
        grad_two, scaled_two, inverse_two, ln2_gain
    )
    grad_middle = gout + backward_second
    grad_branch = grad_middle.astype(jnp.bfloat16)
    branch_gathered = gather_rows(grad_branch)
    grad_att = sum_over_cols(branch_gathered, out_weight, True).astype(jnp.bfloat16)
    grad_packed, rel_low, cbias_part, pbias_part = heads_back(kept, relative_rev, labels, grad_att)
    packed_gathered = gather_cols(grad_packed)
    grad_one = sum_over_rows(packed_gathered, qkv_weight, True)
    back_one, gain_one, bias_one = normalize_back(grad_one, scaled_one, inverse_one, ln1_gain)
    grad_in = grad_middle + back_one
    collected = (
        outer_sum(gathered_one, packed_gathered),
        outer_sum(att_gathered, branch_gathered),
        outer_sum(gathered_two, pre_gathered),
        outer_sum(act_gathered, final_gathered),
        outer_sum(table_rev, rel_low),
        cbias_part,
        pbias_part,
        jnp.sum(grad_pre.astype(jnp.float32), axis=0),
        gain_one,
        bias_one,
        gain_two,
        bias_two,
        jnp.sum(gout, axis=0),
    )
    return (output.T, grad_in.T, collected)


def embed_heads(part, row_pick, col_count):
    head_count = part.shape[0]
    spread = jnp.transpose(part.reshape(head_count, col_count, -1), (1, 0, 2))
    placed = jnp.where(row_pick[:, None, None, None], spread[None], 0.0)
    return placed.reshape(row_pick.shape[0] * col_count, head_count, -1)


def shards(
    tokens,
    cotangent,
    piece_starts,
    ln1_gain,
    ln1_bias,
    qkv_weight,
    content_bias,
    position_bias,
    pos_weight,
    out_weight,
    ln2_gain,
    ln2_bias,
    up_weight,
    up_bias,
    down_weight,
    down_bias,
):
    micro_count = tokens.shape[0]
    row_count = lax.axis_size("row")
    col_count = lax.axis_size("col")
    grid_cells = row_count * col_count
    head_count, head_dim = content_bias.shape
    pos_cols = lax.all_gather(pos_weight, "col", axis=0, tiled=True)
    table_rev = sinusoid_table(SEQ_LEN, D)[::-1]
    relative_rev = jnp.dot(table_rev, pos_cols, preferred_element_type=jnp.float32).astype(
        jnp.bfloat16
    )
    relative_rev = relative_rev.reshape(2 * SEQ_LEN - 1, head_count, head_dim)
    positions = jnp.arange(SEQ_LEN, dtype=jnp.int32)
    params = (
        ln1_gain,
        ln1_bias,
        qkv_weight,
        content_bias,
        position_bias,
        out_weight,
        ln2_gain,
        ln2_bias,
        up_weight,
        up_bias,
        down_weight,
        down_bias,
    )
    outputs, grad_inputs, part_lists = ([], [], [])
    for micro_idx in range(micro_count):
        labels = piece_labels(positions, piece_starts[micro_idx, 0], PIECE)
        out_feats, grad_feats, collected = grid_micro(
            tokens[micro_idx], cotangent[micro_idx], params, (relative_rev, table_rev, labels)
        )
        outputs.append(out_feats)
        grad_inputs.append(grad_feats)
        part_lists.append(collected)
    totals = [
        reduce(jnp.add, [collected[member] for collected in part_lists]) for member in range(13)
    ]
    (
        acc_qkv,
        acc_out,
        acc_up,
        acc_down,
        acc_pos,
        acc_cbias,
        acc_pbias,
        acc_ubias,
        acc_g1,
        acc_b1,
        acc_g2,
        acc_b2,
        acc_db,
    ) = totals
    row_pick = jnp.arange(row_count, dtype=jnp.int32) == lax.axis_index("row")
    pos_term = jnp.where(row_pick[:, None, None], acc_pos[None], 0.0).reshape(
        row_count * acc_pos.shape[0], -1
    )
    cbias_term = embed_heads(acc_cbias, row_pick, col_count)
    pbias_term = embed_heads(acc_pbias, row_pick, col_count)
    col_pick = jnp.arange(col_count, dtype=jnp.int32) == lax.axis_index("col")
    ubias_term = jnp.where(row_pick[:, None], acc_ubias[None], 0.0).reshape(grid_cells, -1)
    norm_terms = [
        jnp.where(col_pick[:, None], vector[None], 0.0).reshape(grid_cells, -1)
        for vector in (acc_g1, acc_b1, acc_g2, acc_b2, acc_db)
    ]
    sum_pos, sum_cbias, sum_pbias, sum_ubias, sum_g1, sum_b1, sum_g2, second_bias_total, sum_db = (
        lax.psum_scatter(pos_term, ("row", "col"), scatter_dimension=0, tiled=True),
        lax.psum_scatter(cbias_term, ("row", "col"), scatter_dimension=0, tiled=True),
        lax.psum_scatter(pbias_term, ("row", "col"), scatter_dimension=0, tiled=True),
        lax.psum_scatter(ubias_term, ("row", "col"), scatter_dimension=0, tiled=True),
        lax.psum_scatter(norm_terms[0], ("row", "col"), scatter_dimension=0, tiled=True),
        lax.psum_scatter(norm_terms[1], ("row", "col"), scatter_dimension=0, tiled=True),
        lax.psum_scatter(norm_terms[2], ("row", "col"), scatter_dimension=0, tiled=True),
        lax.psum_scatter(norm_terms[3], ("row", "col"), scatter_dimension=0, tiled=True),
        lax.psum_scatter(norm_terms[4], ("row", "col"), scatter_dimension=0, tiled=True),
    )
    sum_qkv, sum_out, sum_up, sum_down = (acc_qkv, acc_out, acc_up, acc_down)
    summed = (
        lax.psum_scatter(
            sum_qkv.astype(jnp.bfloat16), "dp", scatter_dimension=1, tiled=True
        ).astype(jnp.float32),
        lax.psum_scatter(
            sum_out.astype(jnp.bfloat16), "dp", scatter_dimension=1, tiled=True
        ).astype(jnp.float32),
        lax.psum_scatter(sum_up.astype(jnp.bfloat16), "dp", scatter_dimension=1, tiled=True).astype(
            jnp.float32
        ),
        lax.psum_scatter(
            sum_down.astype(jnp.bfloat16), "dp", scatter_dimension=1, tiled=True
        ).astype(jnp.float32),
        lax.psum_scatter(
            sum_pos.astype(jnp.bfloat16), "dp", scatter_dimension=1, tiled=True
        ).astype(jnp.float32),
        lax.psum_scatter(
            sum_cbias.astype(jnp.bfloat16), "dp", scatter_dimension=2, tiled=True
        ).astype(jnp.float32),
        lax.psum_scatter(
            sum_pbias.astype(jnp.bfloat16), "dp", scatter_dimension=2, tiled=True
        ).astype(jnp.float32),
        lax.psum_scatter(
            sum_ubias.astype(jnp.bfloat16), "dp", scatter_dimension=1, tiled=True
        ).astype(jnp.float32),
        lax.psum_scatter(sum_g1.astype(jnp.bfloat16), "dp", scatter_dimension=1, tiled=True).astype(
            jnp.float32
        ),
        lax.psum_scatter(sum_b1.astype(jnp.bfloat16), "dp", scatter_dimension=1, tiled=True).astype(
            jnp.float32
        ),
        lax.psum_scatter(sum_g2.astype(jnp.bfloat16), "dp", scatter_dimension=1, tiled=True).astype(
            jnp.float32
        ),
        lax.psum_scatter(
            second_bias_total.astype(jnp.bfloat16), "dp", scatter_dimension=1, tiled=True
        ).astype(jnp.float32),
        lax.psum_scatter(sum_db.astype(jnp.bfloat16), "dp", scatter_dimension=1, tiled=True).astype(
            jnp.float32
        ),
    )
    (
        grad_qkv_w,
        grad_out_w,
        grad_up_w,
        grad_down_w,
        grad_pos_w,
        grad_cbias,
        grad_pbias,
        grad_ubias,
        grad_g1,
        grad_b1,
        grad_g2,
        grad_b2,
        grad_dbias,
    ) = summed
    output_rows = jnp.stack(outputs, axis=0)
    grad_rows = jnp.stack(grad_inputs, axis=0)
    return (
        output_rows,
        grad_rows,
        grad_g1.reshape(-1),
        grad_b1.reshape(-1),
        grad_qkv_w,
        grad_cbias.reshape(head_count, -1),
        grad_pbias.reshape(head_count, -1),
        grad_pos_w,
        grad_out_w,
        grad_g2.reshape(-1),
        grad_b2.reshape(-1),
        grad_up_w,
        grad_ubias.reshape(-1),
        grad_down_w,
        grad_dbias.reshape(-1),
    )


MESH = pl.DeviceIdType.MESH
F32 = jnp.float32
BF16 = jnp.bfloat16


def aligned(index, size):
    return index if isinstance(index, int) else pl.multiple_of(index, size)


def nt(a, b):
    return lax.dot_general(a, b, (((1,), (1,)), ((), ())), preferred_element_type=F32)


def nn(a, b):
    return lax.dot_general(a, b, (((1,), (0,)), ((), ())), preferred_element_type=F32)


def tn(a, b):
    return lax.dot_general(a, b, (((0,), (0,)), ((), ())), preferred_element_type=F32)


def place():
    k, z, c = lax.axis_index("dp"), lax.axis_index("row"), lax.axis_index("col")
    cx = c + 1 - 2 * lax.rem(c, 2)
    cy = lax.rem(c + 2, 4)
    near = (1 - k) * cx + k * cy
    far = k * cx + (1 - k) * cy
    return k, z, c, near, far


def enter(rows):
    k, z, c, _, _ = place()
    barrier = pltpu.get_barrier_semaphore()
    peers = [(1 - k, z, c)]
    for step in range(1, rows):
        peers.append((k, lax.rem(z + step, rows), c))
    for step in range(1, 4):
        for core in range(2):
            peers.append((0 * k + core, z, lax.rem(c + step, 4)))
    for peer in peers:
        pl.semaphore_signal(barrier, inc=1, device_id=peer, device_id_type=MESH)
    pl.semaphore_wait(barrier, len(peers))


class Copies:
    def __init__(self, send, recv):
        self.send, self.recv = send, recv
        self.sends, self.recvs = 0, 0
        self.pending = {}

    def leave(self, count=1):
        first = self.sends
        self.sends += count
        return first

    def land(self, count=1):
        first = self.recvs
        self.recvs += count
        return first

    def copy(self, send_slot, build):
        src, dst, recv_slot, peer = build()
        return pltpu.make_async_remote_copy(
            src, dst, self.send.at[send_slot], self.recv.at[recv_slot], device_id=peer, device_id_type=MESH
        )

    def push(self, send_slot, build, when=None):
        if when is None:
            self.copy(send_slot, build).start()
        else:
            pl.when(when())(lambda: self.copy(send_slot, build).start())
        self.later(send_slot, build, when)

    def later(self, send_slot, build, when=None):
        self.pending[send_slot] = (lambda: self.copy(send_slot, build), when)

    def keep(self, src, dst, slot, when=None):
        def go():
            pltpu.make_async_copy(src(), dst(), self.recv.at[slot]).start()

        if when is None:
            go()
        else:
            pl.when(when())(go)

    def arrived(self, dst, slot):
        pltpu.make_async_copy(dst, dst, self.recv.at[slot]).wait()

    def drain(self):
        for copy, when in self.pending.values():
            if when is None:
                copy().wait_send()
            else:
                pl.when(when())(lambda copy=copy: copy().wait_send())


def tall(row):
    padded = jnp.concatenate([row, jnp.zeros((120, 128), F32)], axis=0)
    return jnp.transpose(padded)


def erf_parts(values):
    erf = lax.erf(values * inv_sqrt_two)
    return 0.5 * (1.0 + erf)


def layer_kernel(
    tok, cot, starts, packed, cbias, pbias, table, wq, wp, wo, wu, wd,
    outs, grads, f_qp, f_o, f_u, f_d, f_small,
    att, wo_all, wu_all, wd_all, wq_half, wp_half, wp_head, xt, ct, normed_t, qcat, keys, vals, probs_a, probs_b, heads_out, inverse_sum,
    params_col, params_row, cb_all, pb_all, kcat, own_att, starts_got,
    mid, norm, hat, inv, gout, acc_out, acc_two, tall_norm, out_t, grad_mid_t, grad_att, g_up, g_down, g_out, small,
    grad_o, head_grad, turned, turned_k, turned_v, turned_p, one_t, one_low, one_got, grad_x, sums,
    hs_qp, hs_o, hs_u, hs_d, r0_o, r0_u, r0_d, s_d,
    r1_qp, r1_o, r1_u, r1_d, r2_qp, r2_o, r2_u, r2_d, r3_qp, r3_o, r3_u, r3_d,
    all_small, got_sib, got_plane, got_z, send, recv,
):
    rows = wu_all.shape[0]
    cols = wo_all.shape[0]
    half = rows // 2
    heads = 2 * half
    k, z, c, near, far = place()
    opposite = 3 - c
    sibling = (1 - k, z, c)
    io = Copies(send, recv)
    mine = lax.div(z, half) == k
    arrived = io.arrived
    enter(rows)

    def q_block(cc, i):
        return wq_half.at[i, pl.ds(aligned(cc * 128, 128), 128), :]

    def p_block(cc, i):
        return wp_half.at[i, pl.ds(aligned(cc * 128, 128), 128), :]

    def u_block(cc, core=k):
        return wu_all.at[pl.ds(core * half, half), pl.ds(aligned(cc * 128, 128), 128), :]

    def o_block(cc, core=k):
        size = wo_all.shape[1] // 2
        return wo_all.at[cc, pl.ds(aligned(core * size, 128), size), :]

    def u_one(i):
        return wu_all.at[k * half + i, pl.ds(aligned(c * 128, 128), 128), :]

    def o_one(i):
        size = wo_all.shape[1] // rows
        return wo_all.at[c, pl.ds(aligned((k * half + i) * size, 128), size), :]

    weights = {
        "q": (wq, lambda i: q_block(c, i), q_block), "p": (wp, lambda i: p_block(c, i), p_block), "o": (wo, o_one, o_block),
        "u": (wu, u_one, u_block),
    }
    z_slot = {name: io.land(half) for name in weights}
    z_send = {name: io.leave(rows - 1) for name in weights}
    near_slot = {name: (io.leave(half), io.land(half)) for name in weights}
    far_slot = {name: (io.leave(2 * half), io.land(2 * half)) for name in weights}
    sib_slot = {name: (io.leave(), io.land()) for name in ("o", "u")}
    turn = z - k * half

    def z_start(name):
        ref, one, _ = weights[name]
        io.keep(lambda: ref, lambda: one(turn), z_slot[name] + turn, lambda: mine)
        for step in range(1, rows):
            io.push(
                z_send[name] + step - 1,
                lambda step=step: (ref, one(turn), z_slot[name] + turn, (k, lax.rem(z + step, rows), c)),
                lambda: mine,
            )

    def z_done(name, i=None):
        _, one, _ = weights[name]
        for number in range(half) if i is None else (i,):
            arrived(one(number), z_slot[name] + number)

    def block_of(name, cc, i):
        block = weights[name][2]
        return block(cc) if i is None else block(cc, i)

    def near_start(name, i=None):
        leave, land = (slot + (i or 0) for slot in near_slot[name])
        io.push(leave, lambda: (block_of(name, c, i), block_of(name, c, i), land, (k, z, near)))

    def near_done(name, i=None):
        arrived(block_of(name, near, i), near_slot[name][1] + (i or 0))

    def far_start(name, i=None):
        leave, land = (slot + 2 * (i or 0) for slot in far_slot[name])
        io.push(leave, lambda: (block_of(name, c, i), block_of(name, c, i), land, (k, z, far)))
        io.push(leave + 1, lambda: (block_of(name, near, i), block_of(name, near, i), land + 1, (k, z, far)))

    def far_done(name, i=None):
        land = far_slot[name][1] + (0 if i is None else 2 * i)
        arrived(block_of(name, far, i), land)
        arrived(block_of(name, opposite, i), land + 1)

    def core_half(name, core):
        if name == "u":
            return wu_all.at[pl.ds(core * half, half)]
        size = wo_all.shape[1] // 2
        return wo_all.at[:, pl.ds(aligned(core * size, 128), size), :]

    def sib_start(name):
        leave, land = sib_slot[name]
        io.push(leave, lambda: (core_half(name, k), core_half(name, k), land, sibling))

    def sib_done(name):
        arrived(core_half(name, 1 - k), sib_slot[name][1])

    part_rows = wd.shape[0] // 2

    def d_cells(zz, core):
        return wd_all.at[:, pl.ds(aligned((2 * zz + core) * part_rows, 128), part_rows), :]

    def d_cell(cc, core=k):
        return wd_all.at[cc, pl.ds(aligned((2 * z + core) * part_rows, 128), part_rows), :]

    def d_own():
        return wd.at[pl.ds(aligned(k * part_rows, 128), part_rows), :]

    d_plane = (io.leave(3), io.land(4))
    d_line = (io.leave(5), io.land(rows))
    d_sibs = (io.leave(rows), io.land(rows))
    relaying = jnp.logical_and(z > 0, z < rows - 1)
    relayed = 2 * (rows - 1) - (rows - 1) * z

    def wd_start():
        leave, land = d_plane
        io.keep(d_own, lambda: d_cell(c), land)
        io.push(leave, lambda: (d_own(), d_cell(c), land + 1, (k, z, near)))
        io.push(leave + 1, lambda: (d_own(), d_cell(c), land + 2, (k, z, far)))

    def wd_far():
        leave, land = d_plane
        arrived(d_cell(near), land + 1)
        io.push(leave + 2, lambda: (d_cell(near), d_cell(near), land + 3, (k, z, far)))

    def wd_sib(number):
        zz = lax.rem(z + number, rows)
        leave, land = d_sibs
        io.push(leave + number, lambda: (d_cells(lax.rem(z + number, rows), k),) * 2 + (land + lax.rem(z + number, rows), sibling))

    def wd_line():
        land = d_plane[1]
        arrived(d_cell(c), land)
        arrived(d_cell(far), land + 2)
        arrived(d_cell(opposite), land + 3)
        leave, land = d_line
        for number, step in enumerate((2, -2, 1, -1)):
            io.push(
                leave + number,
                lambda step=step: (d_cells(z, k), d_cells(z, k), land + z, (k, lax.rem(z + step + rows, rows), c)),
                lambda step=step: jnp.logical_and(z + step >= 0, z + step < rows),
            )
        wd_sib(0)

    def wd_relay():
        leave, land = d_line

        @pl.when(relaying)
        def _():
            arrived(d_cells(relayed, k), land + relayed)

        io.push(
            leave + 4,
            lambda: (d_cells(relayed, k), d_cells(relayed, k), land + relayed, (k, rows - 1 - relayed, c)),
            lambda: relaying,
        )

    def wd_done(number):
        zz = lax.rem(z + number, rows)

        @pl.when(jnp.logical_not(jnp.logical_and(relaying, zz == relayed)))
        def _():
            arrived(d_cells(zz, k), d_line[1] + zz)

        wd_sib(number)

    def wd_all_done():
        for number in range(rows):
            zz = lax.rem(z + number, rows)
            arrived(d_cells(zz, 1 - k), d_sibs[1] + zz)

    feat = tok.shape[1]
    count = xt.shape[1]
    x_slot = io.land(4)
    x_send = io.leave(4)
    n_slot, n_send = io.land(), io.leave()

    def is_local(b, core):
        return jnp.logical_and(2 * b + k == c, core == k)

    def spread_features(source, target, leave, land):
        for b in range(2):
            for core in range(2):

                def src(b=b, core=core):
                    return source.at[b, :, pl.ds(core * count, count)]

                def dst():
                    return target.at[pl.ds(aligned(c * feat, 128), feat), :]

                io.keep(src, dst, land + c, lambda b=b, core=core: is_local(b, core))
                io.push(
                    leave + 2 * b + core,
                    lambda src=src, dst=dst, b=b, core=core: (src(), dst(), land + c, (0 * k + core, z, 2 * b + k)),
                    lambda b=b, core=core: jnp.logical_not(is_local(b, core)),
                )

    z_start("q")
    spread_features(tok, xt, x_send, x_slot)
    z_start("p")

    t_slot = io.land()
    io.keep(lambda: table, lambda: kcat.at[:, pl.ds(0, table.shape[1])], t_slot)
    g_col, g_row, g_cb, g_pb = io.land(), io.land(), io.land(), io.land()
    col_send = io.leave(3)
    for step in range(1, 4):
        io.push(
            col_send + step - 1,
            lambda step=step: (packed.at[pl.ds(0, 8)], params_col.at[c], g_col, (k, z, lax.rem(c + step, 4))),
        )
    io.keep(lambda: packed.at[pl.ds(0, 8)], lambda: params_col.at[c], g_col)
    for source, target, slot in ((packed.at[pl.ds(8, 8)], params_row, g_row), (cbias, cb_all, g_cb), (pbias, pb_all, g_pb)):
        row_send = io.leave(rows - 1)
        for step in range(1, rows):
            io.push(
                row_send + step - 1,
                lambda step=step, source=source, target=target, slot=slot: (
                    source, target.at[z], slot, (k, lax.rem(z + step, rows), c)
                ),
            )
        io.keep(lambda source=source: source, lambda target=target: target.at[z], slot)
    s_slot = io.land()
    s_send = io.leave(4)
    for b in range(2):
        for core in range(2):
            io.keep(
                lambda: starts, lambda: starts_got, s_slot,
                lambda b=b, core=core: jnp.logical_and(c == z, is_local(b, core)),
            )
            io.push(
                s_send + 2 * b + core,
                lambda b=b, core=core: (starts, starts_got, s_slot, (0 * k + core, z, 2 * b + k)),
                lambda b=b, core=core: jnp.logical_and(c == z, jnp.logical_not(is_local(b, core))),
            )
    for name in ("o", "u"):
        z_start(name)

    c_slot = io.land(4)
    c_send = io.leave(4)
    z_done("q", 0)
    near_start("q", 0)
    z_done("p", 0)
    near_start("p", 0)
    wd_start()
    arrived(params_col, g_col)
    arrived(params_row, g_row)
    arrived(cb_all, g_cb)
    arrived(pb_all, g_pb)
    arrived(starts_got, s_slot)
    near_done("q", 0)
    far_start("q", 0)
    for cc in range(4):
        arrived(xt.at[pl.ds(cc * feat, feat), :], x_slot + cc)

    columns = [tall(params_col[cc]) for cc in range(4)]
    gain = jnp.concatenate([col[:, 0:1] for col in columns], axis=0)
    bias = jnp.concatenate([col[:, 1:2] for col in columns], axis=0)
    width = xt.shape[0]
    seq = normed_t.shape[1]
    piece = PIECE
    blocks = seq // 256
    other = pl.ds(aligned((1 - k) * count, count), count)
    own = pl.ds(aligned(k * count, count), count)

    @pl.loop(0, count // 256)
    def _(t):
        x = xt[:, pl.ds(aligned(t * 256, 256), 256)].astype(F32)
        mean = jnp.sum(x, axis=0, keepdims=True) * (1.0 / width)
        square = jnp.sum(x * x, axis=0, keepdims=True) * (1.0 / width)
        inverse = lax.rsqrt(square - mean * mean + norm_epsilon)
        here = pl.ds(aligned(k * count + t * 256, 256), 256)
        normed_t[:, here] = ((x - mean) * inverse * gain + bias).astype(BF16)

    io.push(n_send, lambda: (normed_t.at[:, own], normed_t.at[:, own], n_slot, sibling))
    near_done("p", 0)
    far_start("p", 0)
    wd_far()
    for name in ("q", "p"):
        z_done(name, 1)
        near_start(name, 1)
    z_done("o")
    near_start("o")
    arrived(kcat.at[:, pl.ds(0, 512)], t_slot)
    scale = 0.125
    none = jnp.zeros((256, 64), F32)

    def project(i, number):
        t = lax.rem(k * (blocks // 2) + number, blocks)

        @pl.when(jnp.logical_and(i == 0, number == blocks // 2))
        def _():
            arrived(normed_t.at[:, other], n_slot)

        here = pl.ds(aligned(t * 256, 256), 256)
        got = tn(normed_t[:, here], wq_half[i])
        for hb in range(2):
            h = 2 * i + hb
            low = got[:, hb * 192 : hb * 192 + 192].astype(BF16).astype(F32)
            query, key, value = low[:, 0:64], low[:, 64:128], low[:, 128:192]
            content = cb_all[k * half + i, hb : hb + 1, :]
            position = pb_all[k * half + i, hb : hb + 1, :]
            qcat[h, here, 512:640] = jnp.concatenate(
                [(query + content) * scale, (query + position) * scale], axis=1
            ).astype(BF16)
            keys[h, here, :] = jnp.concatenate([key, none], axis=1).astype(BF16)
            vals[h, here, :] = value.astype(BF16)

    def rotate(i, n):
        h, t = 2 * i + lax.div(n, blocks), lax.rem(n, blocks)
        here = pl.ds(aligned(t * 256, 256), 256)
        angle = nt(qcat[h, here, 512:640], wp_head[h])
        cosine = kcat[here, 0:256].astype(F32)
        sine = kcat[here, 256:512].astype(F32)
        first, second = angle[:, 0:256], angle[:, 256:512]
        qcat[h, here, 0:256] = (first * sine + second * cosine).astype(BF16)
        qcat[h, here, 256:512] = (second * sine - first * cosine).astype(BF16)

    slot_len = seq // 2
    block = 256
    batch = lax.div(c, 2)

    def attend(h, low_row, keys_seen, slot):
        start = starts_got[batch, 0:1, slot : slot + 1]
        row = slot * slot_len + low_row + lax.broadcasted_iota(jnp.int32, (block, 1), 0)
        inside = jnp.logical_and(row >= start, row < start + piece)
        limit = jnp.where(inside, start + (piece - 1), row)
        here = pl.ds(aligned(slot * slot_len + low_row, block), block)
        scores = nt(qcat[h, here, :], kcat[0:keys_seen, :])
        column = slot * slot_len + lax.broadcasted_iota(jnp.int32, (block, slot_len), 1)
        last = jnp.where(column <= limit, scores[:, keys_seen - slot_len :], big_negative)
        top = jnp.max(last, axis=1, keepdims=True)
        if slot == 1:
            top = jnp.maximum(top, jnp.max(scores[:, :slot_len], axis=1, keepdims=True))
        last = jnp.exp(last - top)
        total = jnp.sum(last, axis=1, keepdims=True)
        if slot == 1:
            first = jnp.exp(scores[:, :slot_len] - top)
            total = total + jnp.sum(first, axis=1, keepdims=True)
            low = jnp.concatenate([first.astype(BF16), last.astype(BF16)], axis=1)
        else:
            low = last.astype(BF16)
        inverse = 1.0 / total
        probs = (probs_a, probs_b)[slot]
        probs[h, pl.ds(aligned(low_row, block), block), :] = low
        inverse_sum[h, here, :] = inverse
        heads_out[h, here, :] = (nn(low, vals[h, 0:keys_seen, :]) * inverse).astype(BF16)

    def sib_o():
        far_done("o")
        sib_start("o")

    def sib_u():
        far_done("u")
        sib_start("u")

    def ticks(h, slot, t, actions):
        for number, action in actions.items():
            if (number % 4) // 2 == slot and (not isinstance(t, int) or number % 2 == t):
                pl.when(4 * h + 2 * slot + t == number)(action)

    def far_of(name):
        def run():
            near_done(name)
            far_start(name)

        return run

    def projected():
        wd_line()

    def rotated():
        spread_features(cot, ct, c_send, c_slot)

    ahead = {1: far_of("o"), 4: far_of("u"), 9: wd_relay, 11: sib_o, 15: sib_u}

    def one_head(h):
        kcat[:, 512:640] = keys[h]

        for t in range(slot_len // block):
            attend(h, t * block, slot_len, 0)
        for t in range(slot_len // block):
            ticks(h, 0, t, ahead)
        for t in range(slot_len // block):
            attend(h, t * block, seq, 1)
        for t in range(slot_len // block):
            ticks(h, 1, t, ahead)

    for name in ("q", "p"):
        near_done(name, 1)
        far_start(name, 1)
    z_done("u")
    near_start("u")

    @pl.loop(0, half)
    def _(i):
        far_done("q", i)
        pl.loop(0, blocks)(lambda number: project(i, number))
        pl.when(i == 0)(projected)
        far_done("p", i)
        for hb in range(2):
            part = wp_half[i, :, hb * 64 : hb * 64 + 64]
            wp_head[2 * i + hb] = jnp.concatenate([jnp.zeros_like(part), part], axis=1)
        pl.loop(0, 2 * blocks)(lambda n: rotate(i, n))
        pl.when(i == 0)(rotated)
        pl.loop(0, 2)(lambda hb: one_head(2 * i + hb))

    own_att[...] = jnp.concatenate([heads_out[h] for h in range(heads)], axis=1)
    a_slot, a_send = io.land(2), io.leave()
    span = own_att.shape[1]
    att_part = att.at[:, pl.ds(aligned(k * span, 128), span)]
    io.push(a_send, lambda: (own_att.at[other, :], att_part, a_slot, sibling))
    io.keep(lambda: own_att.at[own, :], lambda: att_part, a_slot + 1)
    for cc in range(4):
        arrived(ct.at[pl.ds(cc * feat, feat), :], c_slot + cc)
    gout[...] = jnp.transpose(ct[...])
    sib_done("o")
    arrived(own_att.at[own, :], a_slot + 1)
    arrived(own_att.at[own, :], a_slot)

    for number in range(1, rows):
        wd_done(number)

    def line(index):
        return jnp.concatenate([params_col[cc, index : index + 1, :] for cc in range(cols)], axis=1)

    def out_weight():
        return jnp.concatenate([wo_all[cc] for cc in range(cols)], axis=1)

    x = jnp.transpose(xt[...].astype(F32))
    middle = x + nn(att[...], out_weight())
    mid[...] = middle
    mean = jnp.sum(middle, axis=1, keepdims=True) * (1.0 / width)
    square = jnp.sum(middle * middle, axis=1, keepdims=True) * (1.0 / width)
    inverse = lax.rsqrt(square - mean * mean + norm_epsilon)
    scaled = (middle - mean) * inverse
    hat[...] = scaled
    inv[...] = inverse
    low = (scaled * line(2) + line(3)).astype(BF16)
    norm[...] = low
    tall_norm[...] = jnp.transpose(low)
    acc_out[...] = jnp.zeros_like(acc_out)
    acc_two[...] = jnp.zeros_like(acc_two)
    small[...] = jnp.zeros_like(small)
    hidden = wu_all.shape[2]
    wd_all_done()

    u0_slot = (io.leave(half), io.land(half))
    o0_slot = (io.leave(), io.land())
    d0_slot = (io.leave(rows), io.land(rows))
    u_slot = {"one": (io.leave(2 * half), io.land(2 * half)), "two": (io.leave(half), io.land(half)), "z": (io.leave(half), io.land(rows))}
    o_slot = {"one": (io.leave(2), io.land(2)), "two": (io.leave(), io.land()), "z": (io.leave(half), io.land(rows))}
    d_slot = {"one": (io.leave(2), io.land(2)), "two": (io.leave(), io.land()), "z": (io.leave(rows), io.land(rows))}
    qp_slot = {
        "one": (io.leave(2 * heads), io.land(2 * heads)), "two": (io.leave(heads), io.land(heads)),
        "z": (io.leave(heads), io.land(2 * rows)),
    }
    last_slot = {name: (io.leave(), io.land()) for name in ("u", "o", "d", "qp")}

    def load(ref):
        return ref[...].astype(F32)

    def add(to, term):
        to[...] = (load(to) + load(term)).astype(BF16)

    def near_on(first, leave, land, target):
        io.push(leave, lambda: (first(), target(), land, (k, z, near)))

    def u_sib(j):
        leave, land = u0_slot
        io.push(leave + j, lambda: (g_up.at[(1 - k) * half + j], r0_u.at[j], land + j, sibling))

    def u_one(j):
        arrived(r0_u.at[j], u0_slot[1] + j)
        total = load(g_up.at[k * half + j]) + load(r0_u.at[j])
        hs_u[j] = total.astype(BF16).reshape(hs_u.shape[1:])
        leave, land = u_slot["one"]
        io.push(leave + 2 * j, lambda: (hs_u.at[j, far], r1_u.at[j, 0], land + 2 * j, (k, z, far)))
        io.push(leave + 2 * j + 1, lambda: (hs_u.at[j, 3 - c], r1_u.at[j, 1], land + 2 * j + 1, (k, z, far)))

    def u_two(j):
        land = u_slot["one"][1] + 2 * j
        arrived(r1_u.at[j, 1], land + 1)
        add(r1_u.at[j, 1], hs_u.at[j, near])
        near_on(lambda: r1_u.at[j, 1], u_slot["two"][0] + j, u_slot["two"][1] + j, lambda: r2_u.at[j])
        arrived(r1_u.at[j, 0], land)
        add(r1_u.at[j, 0], hs_u.at[j, c])

    def u_z(j):
        arrived(r2_u.at[j], u_slot["two"][1] + j)
        add(r2_u.at[j], r1_u.at[j, 0])
        leave, land = u_slot["z"]
        io.push(
            leave + j, lambda: (r2_u.at[j], r3_u.at[z], land + z, (k, k * half + j, c)), lambda: z != k * half + j
        )

    def z_total(total, r3, land, hb=None):
        for step in range(1, rows):
            source = lax.rem(z + step, rows)
            part = r3.at[source] if hb is None else r3.at[hb, source]
            arrived(part, land + source)
            total = total + load(part)
        return total

    def finish(name, to):
        leave, land = last_slot[name]
        io.push(leave, lambda: (to, to, land, sibling), lambda: mine)

    def u_last():
        @pl.when(mine)
        def _():
            f_u[...] = z_total(load(r2_u.at[turn]), r3_u, u_slot["z"][1])

        finish("u", f_u)

    def o_sib():
        leave, land = o0_slot
        size = g_out.shape[1] // 2
        io.push(leave, lambda: (g_out.at[:, pl.ds(aligned((1 - k) * size, 128), size), :], r0_o, land, sibling))

    def o_one():
        arrived(r0_o, o0_slot[1])
        size = g_out.shape[1] // 2
        for cc in range(cols):
            total = load(g_out.at[cc, pl.ds(aligned(k * size, 128), size), :]) + load(r0_o.at[cc])
            hs_o[cc] = total.astype(BF16).reshape(hs_o.shape[1:])
        leave, land = o_slot["one"]
        io.push(leave, lambda: (hs_o.at[far], r1_o.at[0], land, (k, z, far)))
        io.push(leave + 1, lambda: (hs_o.at[3 - c], r1_o.at[1], land + 1, (k, z, far)))

    def o_two():
        land = o_slot["one"][1]
        arrived(r1_o.at[1], land + 1)
        add(r1_o.at[1], hs_o.at[near])
        near_on(lambda: r1_o.at[1], o_slot["two"][0], o_slot["two"][1], lambda: r2_o)
        arrived(r1_o.at[0], land)
        add(r1_o.at[0], hs_o.at[c])

    def o_z():
        arrived(r2_o, o_slot["two"][1])
        add(r2_o, r1_o.at[0])
        leave, land = o_slot["z"]
        for j in range(half):
            io.push(
                leave + j,
                lambda j=j: (r2_o.at[j], r3_o.at[z], land + z, (k, k * half + j, c)),
                lambda j=j: z != k * half + j,
            )

    def o_last():
        @pl.when(mine)
        def _():
            f_o[...] = z_total(load(r2_o.at[turn]), r3_o, o_slot["z"][1])

        finish("o", f_o)

    def d_part(r, core):
        return g_down.at[:, pl.ds(aligned((2 * r + core) * part_rows, 128), part_rows), :]

    def d_sib(r, number):
        leave, land = d0_slot
        io.push(leave + number, lambda: (d_part(r(), 1 - k), r0_d.at[r()], land + r(), sibling))

    def d_z(r, number):
        arrived(r0_d.at[r()], d0_slot[1] + r())
        hs_d[r()] = (load(d_part(r(), k)) + load(r0_d.at[r()])).astype(BF16)
        leave, land = d_slot["z"]
        io.push(leave + number, lambda: (hs_d.at[r()], r3_d.at[z], land + z, (k, r(), c)), lambda: z != r())

    def d_one():
        s_d[...] = z_total(load(hs_d.at[z]), r3_d, d_slot["z"][1]).astype(BF16)
        leave, land = d_slot["one"]
        io.push(leave, lambda: (s_d.at[far], r1_d.at[0], land, (k, z, far)))
        io.push(leave + 1, lambda: (s_d.at[3 - c], r1_d.at[1], land + 1, (k, z, far)))

    def d_two():
        land = d_slot["one"][1]
        arrived(r1_d.at[1], land + 1)
        add(r1_d.at[1], s_d.at[near])
        near_on(lambda: r1_d.at[1], d_slot["two"][0], d_slot["two"][1], lambda: r2_d)
        arrived(r1_d.at[0], land)
        add(r1_d.at[0], s_d.at[c])

    def d_last():
        arrived(r2_d, d_slot["two"][1])
        leave, land = last_slot["d"]
        f_d[pl.ds(aligned(k * part_rows, 128), part_rows), :] = load(r2_d) + load(r1_d.at[0])

        def of_core():
            return f_d.at[pl.ds(aligned(k * part_rows, 128), part_rows), :]

        io.push(leave, lambda: (of_core(), of_core(), land, sibling))

    def qp_builds(h):
        leave, land = qp_slot["one"]
        return (
            (leave + 2 * h, lambda: (hs_qp.at[h, far], r1_qp.at[h, 0], land + 2 * h, (k, z, far))),
            (leave + 2 * h + 1, lambda: (hs_qp.at[h, opposite], r1_qp.at[h, 1], land + 2 * h + 1, (k, z, far))),
        )

    def qp_one(h):
        found = nt(turned[h], normed_t[...]).astype(BF16)
        position = turned_p[h].astype(BF16)
        for cc in range(cols):
            hs_qp[h, cc, 0:192, :] = found[:, cc * 128 : cc * 128 + 128]
            hs_qp[h, cc, 192:256, :] = position[:, cc * 128 : cc * 128 + 128]
        for leave, build in qp_builds(h):
            io.copy(leave, build).start()

    for h in range(heads):
        for leave, build in qp_builds(h):
            io.later(leave, build)

    def qp_two(h):
        land = qp_slot["one"][1] + 2 * h
        arrived(r1_qp.at[h, 1], land + 1)
        add(r1_qp.at[h, 1], hs_qp.at[h, near])
        near_on(lambda: r1_qp.at[h, 1], qp_slot["two"][0] + h, qp_slot["two"][1] + h, lambda: r2_qp.at[h])
        arrived(r1_qp.at[h, 0], land)
        add(r1_qp.at[h, 0], hs_qp.at[h, c])

    def qp_z(h):
        arrived(r2_qp.at[h], qp_slot["two"][1] + h)
        add(r2_qp.at[h], r1_qp.at[h, 0])
        leave, land = qp_slot["z"]
        io.push(
            leave + h,
            lambda: (r2_qp.at[h], r3_qp.at[h % 2, z], land + (h % 2) * rows + z, (k, k * half + h // 2, c)),
            lambda: z != k * half + h // 2,
        )

    def qp_last():
        @pl.when(mine)
        def _():
            for hb in range(2):
                f_qp[hb] = z_total(load(r2_qp.at[2 * turn + hb]), r3_qp, qp_slot["z"][1] + hb * rows, hb)

        finish("qp", f_qp)

    def last_done():
        @pl.when(jnp.logical_not(mine))
        def _():
            for name, to in (("u", f_u), ("o", f_o), ("qp", f_qp)):
                arrived(to, last_slot[name][1])

        arrived(f_d.at[pl.ds(aligned((1 - k) * part_rows, 128), part_rows), :], last_slot["d"][1])

    origin = lax.rem(c, 2)
    out_slot, grad_slot = (io.leave(4), io.land(4)), (io.leave(4), io.land(4))

    def back_start(src, dst, pair):
        leave, base = pair
        for step in range(4):

            def part(step=step):
                return src.at[pl.ds(aligned(lax.rem(c + step, 4) * feat, 128), feat), :]

            def landing():
                return dst.at[batch, k]

            if step == 0:
                io.keep(part, landing, base + 2 * batch + k, lambda: origin == k)
                io.push(
                    leave + step,
                    lambda part=part, landing=landing: (part(), landing(), base + 2 * batch + k, sibling),
                    lambda: origin != k,
                )
            else:
                io.push(
                    leave + step,
                    lambda part=part, landing=landing, step=step: (
                        part(), landing(), base + 2 * batch + k, (origin, z, lax.rem(c + step, 4))
                    ),
                )

    def back_done(dst, pair):
        base = pair[1]
        for b in range(2):
            for core in range(2):
                arrived(dst.at[b, core], base + 2 * b + core)


    def rows_of(number):
        core = k if number % 2 == 0 else 1 - k
        return core * half + number // 2

    def after_one():
        u_sib(0)
        for number in range(2):
            d_sib(lambda number=number: rows_of(number), number)

    def after_two():
        u_one(0)
        for number in range(2):
            d_z(lambda number=number: rows_of(number), number)

    @pl.loop(0, rows)
    def _(step):
        turn_of = lax.rem(step, 2)
        r = ((1 - turn_of) * k + turn_of * (1 - k)) * half + lax.div(step, 2)

        @pl.when(step == 1)
        def _():
            sib_done("u")

        here = pl.ds(aligned(r * hidden, hidden), hidden)
        bias = jnp.concatenate([params_row[r, j : j + 1, :] for j in range(hidden // 128)], axis=1)
        down = jnp.concatenate([wd_all[cc, here, :] for cc in range(cols)], axis=1)
        pre = nn(norm[...], wu_all[r]) + bias
        grad_act = nt(gout[...], down)
        lower = erf_parts(pre)
        act = (pre * lower).astype(BF16)
        slope = lower + pre * jnp.exp(-0.5 * pre * pre) * inv_sqrt_tau
        low_grad = (grad_act * slope).astype(BF16)
        small[pl.ds(5 + r, 1), :] = jnp.sum(low_grad.astype(F32), axis=0, keepdims=True)
        acc_out[...] += nn(act, down)
        acc_two[...] += nt(low_grad, wu_all[r])
        g_up[r] = nn(tall_norm[...], low_grad).astype(BF16)
        found = tn(act, gout[...]).astype(BF16)
        for cc in range(cols):
            g_down[cc, here, :] = found[:, cc * 128 : cc * 128 + 128]
        pl.when(step == 1)(after_one)
        pl.when(step == 2)(after_two)

    u_sib(1)
    for number in range(2, 4):
        d_sib(lambda number=number: rows_of(number), number)
    cotangent = gout[...].astype(F32)
    out_t[...] = jnp.transpose(mid[...] + acc_out[...] + line(4)).astype(BF16)
    back_start(out_t, outs, out_slot)
    two = acc_two[...]
    small[2:3, :] = jnp.sum(two * hat[...], axis=0, keepdims=True)
    small[3:4, :] = jnp.sum(two, axis=0, keepdims=True)
    small[4:5, :] = jnp.sum(cotangent, axis=0, keepdims=True)
    shifted = two * line(2)
    first = jnp.sum(shifted, axis=1, keepdims=True) * (1.0 / width)
    second = jnp.sum(shifted * hat[...], axis=1, keepdims=True) * (1.0 / width)
    grad_mid = cotangent + inv[...] * (shifted - first - hat[...] * second)
    branch = grad_mid.astype(BF16)
    grad_att[...] = nt(branch, out_weight()).astype(BF16)
    e_slot, e_send = io.land(2), io.leave()
    io.push(
        e_send,
        lambda: (grad_att.at[:, pl.ds(aligned((1 - k) * span, 128), span)], grad_o.at[own, :], e_slot, sibling),
    )
    io.keep(
        lambda: grad_att.at[:, pl.ds(aligned(k * span, 128), span)], lambda: grad_o.at[own, :], e_slot + 1
    )
    grad_mid_t[...] = jnp.transpose(grad_mid)
    found = tn(att[...], branch).astype(BF16)
    for cc in range(cols):
        g_out[cc] = found[:, cc * 128 : cc * 128 + 128]
    o_sib()
    u_one(1)
    for number in range(2, 4):
        d_z(lambda number=number: rows_of(number), number)
    one_t[...] = jnp.zeros_like(one_t)
    sums[...] = jnp.zeros_like(sums)
    arrived(grad_o.at[own, :], e_slot + 1)
    arrived(grad_o.at[own, :], e_slot)
    for h in range(heads):
        head_grad[h] = grad_o[:, h * 64 : h * 64 + 64]

    def attend_back(h, low_row, keys_seen, slot):
        at = pl.ds(aligned(low_row, block), block)
        here = pl.ds(aligned(slot * slot_len + low_row, block), block)
        grad = (head_grad[h, here, :].astype(F32) * inverse_sum[h, here, :]).astype(BF16)
        low = (probs_a, probs_b)[slot][h, at, :]
        inner = jnp.sum(grad.astype(F32) * heads_out[h, here, :].astype(F32), axis=1, keepdims=True)
        grad_prob = nt(grad, vals[h, 0:keys_seen, :])
        grad_score = (low.astype(F32) * (grad_prob - inner)).astype(BF16)
        turned_v[:, 0:keys_seen] += tn(grad, low)
        turned_k[:, 0:keys_seen] += tn(qcat[h, here, 512:576], grad_score)
        got = nn(grad_score, kcat[0:keys_seen, :])
        cosine = kcat[here, 0:256].astype(F32)
        sine = kcat[here, 256:512].astype(F32)
        first, second = got[:, 0:256], got[:, 256:512]
        angle = jnp.concatenate([first * sine - second * cosine, first * cosine + second * sine], axis=1).astype(BF16)
        both = got[:, 512:640] + nn(angle, wp_head[h])
        turned_p[h] += tn(qcat[h, here, 512:640], angle)[64:128]
        sums[pl.ds(h, 1), :] += jnp.sum(both, axis=0, keepdims=True) * 0.125
        query = (both + pltpu.roll(both, 64, 1)) * 0.125
        turned[h, 0:64, here] = jnp.transpose(query)[0:64].astype(BF16)

    def both(*actions):
        def run():
            for action in actions:
                action()

        return run

    behind = {
        0: both(o_one, lambda: u_two(0)), 6: lambda: u_two(1), 8: both(o_two, lambda: u_z(0)), 10: lambda: qp_two(0),
        11: lambda: u_z(1), 13: both(o_z, lambda: qp_two(1)), 15: lambda: qp_z(0),
    }

    @pl.loop(0, heads)
    def _(h):
        kcat[:, 512:640] = keys[h]
        turned_k[...] = jnp.zeros_like(turned_k)
        turned_v[...] = jnp.zeros_like(turned_v)
        turned_p[h] = jnp.zeros(turned_p.shape[1:], F32)

        for t in range(slot_len // block):
            attend_back(h, t * block, slot_len, 0)
        for t in range(slot_len // block):
            ticks(h, 0, t, behind)
        for t in range(slot_len // block):
            attend_back(h, t * block, seq, 1)
        for t in range(slot_len // block):
            ticks(h, 1, t, behind)

        turned[h, 64:128, :] = turned_k[...].astype(BF16)
        turned[h, 128:192, :] = turned_v[...].astype(BF16)
        qp_one(h)

        @pl.when(lax.rem(h, 2) == 1)
        def _():
            i = lax.div(h, 2)
            pair = jnp.concatenate([turned[2 * i], turned[2 * i + 1]], axis=0)
            one_t[...] += nn(wq_half[i], pair)

    one_low[...] = one_t[:, other].astype(BF16)
    f_slot, f_send = io.land(), io.leave()
    io.push(f_send, lambda: (one_low, one_got, f_slot, sibling))
    qp_two(2)
    qp_z(1)
    d_one()
    arrived(one_got, f_slot)
    columns = [tall(params_col[cc]) for cc in range(cols)]
    gain = jnp.concatenate([col[:, 0:1] for col in columns], axis=0)
    one = one_t[:, own] + one_got[...].astype(F32)
    x = xt[...].astype(F32)
    mean = jnp.sum(x, axis=0, keepdims=True) * (1.0 / width)
    square = jnp.sum(x * x, axis=0, keepdims=True) * (1.0 / width)
    inverse = lax.rsqrt(square - mean * mean + norm_epsilon)
    scaled = (x - mean) * inverse
    shifted = one * gain
    first = jnp.sum(shifted, axis=0, keepdims=True) * (1.0 / width)
    second = jnp.sum(shifted * scaled, axis=0, keepdims=True) * (1.0 / width)
    gain_sum = jnp.sum(one * scaled, axis=1, keepdims=True)
    bias_sum = jnp.sum(one, axis=1, keepdims=True)
    lane = lax.broadcasted_iota(jnp.int32, (width, 128), 1)
    pair = jnp.where(lane == 0, gain_sum, jnp.where(lane == 1, bias_sum, 0.0))
    pair = jnp.transpose(pair)[0:8]
    all_small[0] = small[...]
    all_small[0, 0:2, :] = pair[0:2]

    def spread(first_lane):
        row = jnp.concatenate([sums[h : h + 1, first_lane : first_lane + 64] for h in range(heads)], axis=1)
        blank = jnp.zeros_like(row)
        return jnp.where(k == 0, jnp.concatenate([row, blank], axis=1), jnp.concatenate([blank, row], axis=1))

    all_small[0, 9:10, :] = spread(0)
    all_small[0, 10:11, :] = spread(64)
    m_slot, m_send = io.land(), io.leave()
    p_slot, p_send = io.land(), io.leave(3)
    v_slot, v_send = io.land(), io.leave(rows - 1)
    io.push(m_send, lambda: (all_small.at[0], got_sib, m_slot, sibling))
    grad_x[...] = (grad_mid_t[...] + inverse * (shifted - first - scaled * second)).astype(BF16)
    arrived(got_sib, m_slot)
    all_small[1] = all_small[0] + got_sib[...]
    for step in range(1, 4):
        io.push(
            p_send + step - 1, lambda step=step: (all_small.at[1], got_plane.at[c], p_slot, (k, z, lax.rem(c + step, 4)))
        )
    io.keep(lambda: all_small.at[1], lambda: got_plane.at[c], p_slot)
    qp_two(3)
    d_two()
    back_start(grad_x, grads, grad_slot)
    qp_z(2)
    arrived(got_plane, p_slot)
    all_small[2] = (got_plane[0] + got_plane[1]) + (got_plane[2] + got_plane[3])
    for step in range(1, rows):
        io.push(
            v_send + step - 1, lambda step=step: (all_small.at[2], got_z.at[z], v_slot, (k, lax.rem(z + step, rows), c))
        )
    io.keep(lambda: all_small.at[2], lambda: got_z.at[z], v_slot)
    u_last()
    o_last()
    qp_z(3)
    d_last()
    arrived(got_z, v_slot)
    f_small[...] = (got_z[0] + got_z[1]) + (got_z[2] + got_z[3])
    qp_last()
    back_done(outs, out_slot)
    back_done(grads, grad_slot)
    last_done()
    io.drain()


def final_kernel(
    outs, grads, f_qp, f_o, f_u, f_d, f_small,
    output, grad_tokens, g1, b1, q_w, c_b, p_b, p_w, o_w, g2, b2, u_w, u_b, d_w, d_b,
):
    k, z, c, _, _ = place()
    for b in range(2):
        for core in range(2):
            size = outs.shape[3]
            output[b, :, core * size : core * size + size] = outs[b, core].astype(F32)
            grad_tokens[b, :, core * size : core * size + size] = grads[b, core].astype(F32)
    for core in range(2):

        @pl.when(k == core)
        def _(core=core):
            q_w[...] = f_qp[core, 0:192, :]
            p_w[...] = f_qp[core, 192:256, :]
            for ref, source in ((o_w, f_o), (d_w, f_d)):
                size = ref.shape[0]
                ref[...] = jnp.transpose(source[:, core * size : core * size + size])
            size = u_w.shape[1]
            u_w[...] = f_u[:, core * size : core * size + size]

    width = f_small.shape[1]
    chip = z * 4 + c
    share = g1.shape[1]
    first = pltpu.roll(f_small[0:8, :], lax.rem(width - (chip * 2 + k) * share, width), 1)
    for row, ref in ((0, g1), (1, b1), (2, g2), (3, b2), (4, d_b)):
        ref[...] = first[row : row + 1, 0:share]
    share = u_b.shape[1]
    line = f_small[pl.ds(5 + z, 1), :]
    line = jnp.broadcast_to(line, (8, width))
    u_b[...] = pltpu.roll(line, lax.rem(width - (c * 2 + k) * share, width), 1)[0:1, 0:share]
    heads, share = c_b.shape
    third = pltpu.roll(f_small[8:16, :], lax.rem(2 * width - heads * 64 * z - (c * 2 + k) * share, width), 1)
    for h in range(heads):
        c_b[h : h + 1, :] = third[1:2, h * 64 : h * 64 + share]
        p_b[h : h + 1, :] = third[2:3, h * 64 : h * 64 + share]


def position_table(seq_len, feature_count):
    positions = np.arange(seq_len, dtype=np.float64)
    exponent = -np.arange(0, feature_count, 2, dtype=np.float64) / feature_count
    angles = positions[:, None] * (10000.0**exponent)[None, :]
    return np.concatenate([np.cos(angles), np.sin(angles)], axis=1).astype(jnp.bfloat16)


def fast_shards(
    tokens, cotangent, piece_starts, ln1_gain, ln1_bias, qkv_weight, content_bias, position_bias, pos_weight,
    out_weight, ln2_gain, ln2_bias, up_weight, up_bias, down_weight, down_bias,
):
    rows, cols = lax.axis_size("row"), lax.axis_size("col")
    half = rows // 2
    micro, feat, seq = tokens.shape
    width = feat * cols
    count = seq // 2
    hidden = up_weight.shape[1]
    heads = content_bias.shape[0] * half
    table = jnp.asarray(position_table(seq, width))
    lines = [ln1_gain, ln1_bias, ln2_gain, ln2_bias, down_bias]
    places = [(line, index * feat) for index, line in enumerate(lines)] + [(up_bias, 8 * 128)]
    packed = sum(jnp.pad(line.astype(F32), (at, 16 * 128 - at - line.shape[0])) for line, at in places)
    packed = packed.reshape(16, 128)
    vm = pl.BlockSpec(memory_space=pltpu.VMEM)
    anywhere = pl.BlockSpec(memory_space=pl.ANY)
    limit = 64 * 1024 * 1024 - 128 * 1024

    def shape(dims, kind=BF16):
        return jax.ShapeDtypeStruct(dims, kind)

    def vmem(dims, kind=BF16):
        return pltpu.VMEM(dims, kind)

    q_cols, p_cols = qkv_weight.shape[1], pos_weight.shape[1]
    o_rows, d_rows = out_weight.shape[0], down_weight.shape[0]
    qp, part = (256, feat), (d_rows // 2, 128)
    results = pl.pallas_call(
        layer_kernel,
        name="layer",
        out_shape=(
            shape((micro, 2, feat, count)),
            shape((micro, 2, feat, count)),
        )
        + (
            shape((2,) + qp, F32), shape((o_rows, 128), F32), shape((feat, hidden), F32), shape((d_rows, 128), F32),
            shape((16, width), F32),
        ),
        in_specs=[anywhere, anywhere, vm, vm, vm, vm] + [anywhere] * 6,
        out_specs=(anywhere, anywhere) + (vm,) * 5,
        scratch_shapes=[
            vmem((count, width)),
            vmem((cols, width, 128)),
            vmem((rows, width, hidden)),
            vmem((cols, rows * hidden, 128)),
            vmem((half, width, q_cols)),
            vmem((half, width, p_cols)),
            vmem((heads, width, 128)),
            vmem((width, count)),
            vmem((width, count)),
            vmem((width, seq)),
            vmem((heads, seq, width + 128)),
            vmem((heads, seq, 128)),
            vmem((heads, seq, 64)),
            vmem((heads, count, count)),
            vmem((heads, count, seq)),
            vmem((heads, seq, 64)),
            vmem((heads, seq, 1), F32),
            vmem((cols, 8, 128), F32),
            vmem((rows, 8, 128), F32),
            vmem((rows,) + content_bias.shape, F32),
            vmem((rows,) + position_bias.shape, F32),
            vmem((seq, width + 128)),
            vmem((seq, heads * 64)),
            vmem(piece_starts.shape, jnp.int32),
            vmem((count, width), F32),
            vmem((count, width)),
            vmem((count, width), F32),
            vmem((count, 1), F32),
            vmem((count, width)),
            vmem((count, width), F32),
            vmem((count, width), F32),
            vmem((width, count)),
            vmem((width, count)),
            vmem((width, count), F32),
            vmem((count, width)),
            vmem((rows, width, hidden)),
            vmem((cols, rows * hidden, 128)),
            vmem((cols, width, 128)),
            vmem((16, width), F32),
            vmem((seq, heads * 64)),
            vmem((heads, seq, 64)),
            vmem((heads, 192, seq)),
            vmem((64, seq), F32),
            vmem((64, seq), F32),
            vmem((heads, 64, width), F32),
            vmem((width, seq), F32),
            vmem((width, count)),
            vmem((width, count)),
            vmem((width, count)),
            vmem((8, 128), F32),
            vmem((heads, cols) + qp),
            vmem((cols, half, o_rows, 128)),
            vmem((half, cols, feat, hidden)),
            vmem((rows, cols) + part),
            vmem((cols, half * o_rows, 128)),
            vmem((half, width, hidden)),
            vmem((rows, cols) + part),
            vmem((cols,) + part),
            vmem((heads, 2) + qp),
            vmem((2, half, o_rows, 128)),
            vmem((half, 2, feat, hidden)),
            vmem((2,) + part),
            vmem((heads,) + qp),
            vmem((half, o_rows, 128)),
            vmem((half, feat, hidden)),
            vmem(part),
            vmem((2, rows) + qp),
            vmem((rows, o_rows, 128)),
            vmem((rows, feat, hidden)),
            vmem((rows, cols) + part),
            vmem((3, 16, width), F32),
            vmem((16, width), F32),
            vmem((cols, 16, width), F32),
            vmem((rows, 16, width), F32),
            pltpu.SemaphoreType.DMA((140,)),
            pltpu.SemaphoreType.DMA((132,)),
        ],
        compiler_params=pltpu.CompilerParams(collective_id=0, has_side_effects=True, vmem_limit_bytes=limit),
    )(
        tokens, cotangent, piece_starts, packed, content_bias, position_bias, table,
        qkv_weight, pos_weight, out_weight, up_weight, down_weight,
    )
    devices = 2 * rows * cols
    vec = shape((1, width // devices), F32)
    bias = shape((content_bias.shape[0], 64 // (2 * cols)), F32)
    done = list(pl.pallas_call(
        final_kernel,
        name="final",
        out_shape=(
            shape(tokens.shape, F32), shape(tokens.shape, F32), vec, vec,
            shape((q_cols // 2, feat), F32), bias, bias, shape((p_cols // 2, feat), F32), shape((64, o_rows), F32), vec, vec,
            shape((feat, hidden // 2), F32), shape((1, rows * hidden // devices), F32), shape((64, d_rows), F32), vec,
        ),
        in_specs=[vm] * 7,
        out_specs=(vm,) * 15,
        compiler_params=pltpu.CompilerParams(vmem_limit_bytes=limit),
    )(*results))
    for index in (4, 7, 8, 13):
        done[index] = done[index].T
    return tuple(v.reshape(-1) if v.shape[0] == 1 else v for v in done)


def solution(mesh):
    in_specs = (
        P(None, "col", ("dp", "row")),
        P(None, "col", ("dp", "row")),
        P(None, ("dp", "col"), None),
        P("col"),
        P("col"),
        P("col", "row"),
        P("row", None),
        P("row", None),
        P("col", "row"),
        P("row", "col"),
        P("col"),
        P("col"),
        P("col", "row"),
        P("row"),
        P("row", "col"),
        P("col"),
    )
    out_specs = (
        P(None, "col", ("dp", "row")),
        P(None, "col", ("dp", "row")),
        P(("row", "col", "dp")),
        P(("row", "col", "dp")),
        P("col", ("row", "dp")),
        P("row", ("col", "dp")),
        P("row", ("col", "dp")),
        P("col", ("row", "dp")),
        P("row", ("col", "dp")),
        P(("row", "col", "dp")),
        P(("row", "col", "dp")),
        P("col", ("row", "dp")),
        P(("row", "col", "dp")),
        P("row", ("col", "dp")),
        P(("row", "col", "dp")),
    )

    def layer(tokens, *others):
        dp, row, col = mesh.shape["dp"], mesh.shape["row"], mesh.shape["col"]
        one_each = tokens.shape[2] == dp * row * SEQ_LEN and tokens.shape[0] * dp == col
        body = fast_shards if one_each and dp == 2 and row == col == 4 else shards
        part = jax.shard_map(body, mesh=mesh, in_specs=in_specs, out_specs=out_specs, check_vma=False)
        return part(tokens, *others)

    return layer
```
